32 devices in a mesh: tower: 2 (over x), dp: 4 (over y, core), mp: 4 (over z).
Axes of the slice: x: 2, y: 2, z: 4, core: 2. Of those that a mesh axis runs over, the one named last changes fastest.
Arguments:
- tower_in: bfloat16 [2, 4608, 768], P('tower', ('dp', 'mp')), may hold values from -6 to 6
- out_cot: bfloat16 [2, 4608, 768], P('tower', ('dp', 'mp')), may hold values from -6 to 6
- segment_ids: int32 [72, 64], P('dp'), may hold values from 0 to 3, never falling along the last dimension, each value on 1 to 32 neighbouring positions
- row_image: int32 [72], P('dp'), may hold values from 0 to 1
- attn_qkv: bfloat16 [2, 3, 768, 768], P('tower', None, None, 'mp'), may hold values from -0.21875 to 0.21875
- attn_out: bfloat16 [2, 768, 768], P('tower', 'mp'), may hold values from -0.625 to 0.625
- mlp_in: bfloat16 [2, 768, 3072], P('tower', None, 'mp'), may hold values from -0.21875 to 0.21875
- mlp_out: bfloat16 [2, 3072, 768], P('tower', 'mp'), may hold values from -0.109375 to 0.109375
- cross_proj: bfloat16 [2, 2, 768, 768], P('tower', None, None, 'mp'), may hold values from -0.3125 to 0.3125
- qv_bias: float32 [2, 2, 768], P('tower'), may hold values from -3 to 3
- out_bias: float32 [2, 768], P('tower'), may hold values from -1.75 to 1.75
- mlp_bias_in: float32 [2, 3072], P('tower'), may hold values from -3 to 3
- mlp_bias_out: float32 [2, 768], P('tower'), may hold values from -1.75 to 1.75
- norm_gain: float32 [2, 3, 768], P('tower'), may hold values from 0.25 to 1.75
- norm_bias: float32 [2, 3, 768], P('tower'), may hold values from -1.75 to 1.75
Outputs:
- tower_out: bfloat16 [2, 4608, 768], P('tower', ('dp', 'mp'))
- tower_in_grad: bfloat16 [2, 4608, 768], P('tower', ('dp', 'mp'))
- qkv_grad: float32 [2, 3, 768, 768], P('tower', None, 'dp', 'mp')
- attn_out_grad: float32 [2, 768, 768], P('tower', 'mp', 'dp')
- mlp_in_grad: float32 [2, 768, 3072], P('tower', 'dp', 'mp')
- mlp_out_grad: float32 [2, 3072, 768], P('tower', 'mp', 'dp')
- cross_grad: float32 [2, 2, 768, 768], P('tower', None, 'dp', 'mp')
- qv_bias_grad: float32 [2, 2, 768], P('tower')
- out_bias_grad: float32 [2, 768], P('tower')
- mlp_bias_in_grad: float32 [2, 3072], P('tower')
- mlp_bias_out_grad: float32 [2, 768], P('tower')
- norm_gain_grad: float32 [2, 3, 768], P('tower')
- norm_bias_grad: float32 [2, 3, 768], P('tower')
The draws below stay inside these ranges and needn't reach their ends.
Inputs may be any that keep to these rules, and one draw needn't show every extreme that they name: `segment_ids`: within a caption row of 64 tokens the numbers never fall. Row r and image i belong to one group where r // 18 == i // 2; row_image counts images within the group.
All inputs are finite; a program needn't handle non-finite values.
Results may differ from the reference program's by a relative error of at most 0.03.
Values may be sent and summed in bfloat16 or wider, within the bound.
A program may use at most 192 MiB of HBM per device.

```python
import math
import jax
import jax.numpy as jnp
import numpy as np
from jax import lax

D = 768
HEADS = 12
HDIM = 64
FF = 3072
PATCH = 576
LTXT = 64
IMG_DEV = 2
ROWS_DEV = 18
ROWS = 72
TOKENS = 4608


def place_ends(result, own_key, low, largest):
    index_at = [jax.random.randint(jax.random.fold_in(own_key, axis), (), 0, length) for axis, length in enumerate(result.shape)]
    longest = result.shape.index(max(result.shape))
    next_to = index_at[:longest] + [(index_at[longest] + 1) % result.shape[longest]] + index_at[longest + 1:]
    return result.at[tuple(index_at)].set(low).at[tuple(next_to)].set(largest)


def block_levels(stream_key, extent, split, smallest, top_value):
    def one(axis_at, parts):
        heights = jax.random.uniform(jax.random.fold_in(jax.random.fold_in(stream_key, 6), axis_at), (parts,), jnp.float32, smallest / len(split), top_value / len(split))
        return jnp.repeat(jnp.exp(heights), extent[axis_at] // parts).reshape((-1,) + (1,) * (len(extent) - axis_at - 1))

    level = one(*split[0])
    for cut in split[1:]:
        level = level * one(*cut)
    return level


def profile(count, total, limit, lean):
    loads = [(1 << 20) // math.isqrt(standing ** lean) + 1 for standing in range(2, count + 1)]
    spare, counts = total - limit - (count - 1), [1] * (count - 1)
    while spare > 0:
        free = [i for i in range(count - 1) if counts[i] < limit]
        mass, remaining = sum([loads[i] for i in free]), spare
        for i in free:
            more = min(limit - counts[i], max(1, remaining * loads[i] // mass), spare)
            counts[i] = counts[i] + more
            spare = spare - more
    return np.array([limit] + counts)


def uneven_parts(own_key, amount, total, reach, lean):
    if amount == 2:
        one = jax.random.randint(own_key, (), max(1, total - reach), min(reach, total - 1) + 1)
        return jnp.stack([one, total - one])
    lengths = jnp.asarray(profile(amount, total, reach, lean), jnp.int32)
    couples = (amount - 1) // 2
    source_of, sink = lengths[1:1 + 2 * couples:2], lengths[2:2 + 2 * couples:2]
    slack = jnp.minimum(source_of - 1, reach - sink)
    passed = jax.random.randint(jax.random.fold_in(own_key, 1), (couples,), 0, 1 << 20) % (slack + 1)
    lengths = lengths.at[1:1 + 2 * couples:2].set(source_of - passed).at[2:2 + 2 * couples:2].set(sink + passed)
    return lengths[jax.random.permutation(jax.random.fold_in(own_key, 2), amount)]


def noise(own_key, shape, width, limit, cuts=(), dtype=jnp.bfloat16):
    result = jax.random.normal(own_key, shape, jnp.float32) * width
    if len(cuts) > 0:
        result = block_levels(own_key, shape, cuts, -0.22, 0.18) * result
    return jnp.clip(result, min=-limit, max=limit).astype(dtype)


def setup_inputs(seed: int = 0) -> dict:
    seeds = jax.random.split(jax.random.key(seed), 16)
    tower_in = noise(seeds[0], (2, TOKENS, D), 1.0, 6.0, ((0, 2), (1, 16)))
    out_cot = noise(seeds[1], (2, TOKENS, D), 1.0, 6.0, ((0, 2), (1, 16)))
    segment_ids = jax.vmap(lambda own: jnp.searchsorted(jnp.cumsum(uneven_parts(own, 4, LTXT, LTXT // 2, 2)), jnp.arange(LTXT), side="right"))(jax.random.split(seeds[2], ROWS)).reshape((ROWS, LTXT)).astype(jnp.int32)
    row_image = place_ends(jax.random.randint(seeds[3], (ROWS,), 0, IMG_DEV), jax.random.fold_in(seeds[3], 1), 0, IMG_DEV - 1).astype(jnp.int32)
    attn_qkv = noise(seeds[4], (2, 3, D, D), D ** -0.5, 0.21875, ((0, 2), (3, 4)))
    attn_out = noise(seeds[5], (2, D, D), (D // 8) ** -0.5, 0.625, ((0, 2), (1, 4)))
    mlp_in = noise(seeds[6], (2, D, FF), D ** -0.5, 0.21875, ((0, 2), (2, 4)))
    mlp_out = noise(seeds[7], (2, FF, D), FF ** -0.5, 0.109375, ((0, 2), (1, 4)))
    cross_proj = noise(seeds[8], (2, 2, D, D), (D // 2) ** -0.5, 0.3125, ((0, 2), (3, 4)))
    qv_bias = noise(seeds[9], (2, 2, D), 0.5, 3.0, ((0, 2),), jnp.float32)
    out_bias = noise(seeds[10], (2, D), 0.3, 1.75, ((0, 2),), jnp.float32)
    mlp_bias_in = noise(seeds[11], (2, FF), 0.5, 3.0, ((0, 2),), jnp.float32)
    mlp_bias_out = noise(seeds[12], (2, D), 0.3, 1.75, ((0, 2),), jnp.float32)
    norm_gain = jnp.clip(1.0 + 0.15 * jax.random.normal(seeds[13], (2, 3, D), jnp.float32), 0.25, 1.75)
    norm_bias = noise(seeds[14], (2, 3, D), 0.3, 1.75, ((0, 2),), jnp.float32)
    return dict(tower_in=tower_in, out_cot=out_cot, segment_ids=segment_ids, row_image=row_image, attn_qkv=attn_qkv, attn_out=attn_out, mlp_in=mlp_in, mlp_out=mlp_out, cross_proj=cross_proj, qv_bias=qv_bias, out_bias=out_bias, mlp_bias_in=mlp_bias_in, mlp_bias_out=mlp_bias_out, norm_gain=norm_gain, norm_bias=norm_bias)


HIGH = lax.Precision.HIGHEST
EPS = 1e-06
NEG = -1e+30

@jax.custom_vjp
def low(v):
    return lax.optimization_barrier(v.astype(jnp.bfloat16)).astype(jnp.float32)

@jax.custom_vjp
def low_back(v):
    return v

def low_keep(v):
    return (low(v), None)

def low_pass(kept, grad):
    return (grad,)

def back_keep(v):
    return (v, None)

def back_low(kept, grad):
    return (low(grad),)
low.defvjp(low_keep, low_pass)
low_back.defvjp(back_keep, back_low)

def rounded(values):
    return low(low_back(values))

def matmul(left, right):
    return jnp.dot(left, right, precision=HIGH)

def norm_rows(values, gain_vec, shift_vec):
    center = values - lax.optimization_barrier(jnp.mean(values, axis=-1, keepdims=True))
    spread = lax.optimization_barrier(jnp.mean(center * center, axis=-1, keepdims=True))
    return center * lax.rsqrt(spread + EPS) * gain_vec + shift_vec

def self_heads(queries, key_rows, value_rows, seg_blocks, causal):
    blocks = queries.shape[0] // PATCH
    shape_four = (blocks, PATCH, HEADS, HDIM)
    places = jnp.arange(PATCH)
    same_row = places[:, None] // LTXT == places[None, :] // LTXT
    earlier = places[None, :] <= places[:, None]

    def one_block(block_items):
        q_blk, k_blk, v_blk, seg_row = block_items
        scores = low_back(jnp.einsum('qhe,khe->hqk', q_blk, k_blk, precision=HIGH) * HDIM ** (-0.5))
        if causal:
            allowed = same_row & earlier & (seg_row[:, None] == seg_row[None, :])
            scores = jnp.where(allowed[None], scores, NEG)
        weights_p = low(jax.nn.softmax(scores, axis=-1))
        return rounded(jnp.einsum('hqk,khe->qhe', weights_p, v_blk, precision=HIGH))
    mixed_rows = lax.map(jax.checkpoint(one_block), (queries.reshape(shape_four), key_rows.reshape(shape_four), value_rows.reshape(shape_four), seg_blocks))
    return mixed_rows.reshape(queries.shape)

def cross_heads(queries, key_rows, value_rows, row_image):
    groups = queries.shape[0] // (ROWS_DEV * LTXT)
    q_grp = queries.reshape(groups, ROWS_DEV, LTXT, HEADS, HDIM)
    k_grp = key_rows.reshape(groups, IMG_DEV, PATCH, HEADS, HDIM)
    v_grp = value_rows.reshape(groups, IMG_DEV, PATCH, HEADS, HDIM)
    pick_grp = row_image.reshape(groups, ROWS_DEV)

    def one_group(group_items):
        q_one, k_one, v_one, pick_one = group_items
        key_pick = jnp.take(k_one, pick_one, axis=0)
        val_pick = jnp.take(v_one, pick_one, axis=0)
        scores = low_back(jnp.einsum('rqhe,rkhe->rhqk', q_one, key_pick, precision=HIGH) * HDIM ** (-0.5))
        weights_p = low(jax.nn.softmax(scores, axis=-1))
        return rounded(jnp.einsum('rhqk,rkhe->rqhe', weights_p, val_pick, precision=HIGH))
    mixed_rows = lax.map(jax.checkpoint(one_group), (q_grp, k_grp, v_grp, pick_grp))
    return mixed_rows.reshape(queries.shape)

def reference(tower_in, out_cot, segment_ids, row_image, attn_qkv, attn_out, mlp_in, mlp_out, cross_proj, qv_bias, out_bias, mlp_bias_in, mlp_bias_out, norm_gain, norm_bias):
    seg_blocks = segment_ids.reshape(-1, PATCH)

    def forward(stream_in, qkv_w, out_w, in_w, mlp_w, cross_w, bias_qv, bias_out, bias_in, bias_mlp, gains, shifts):

        def attention_part(stream, tower, causal):
            act_one = low(norm_rows(stream, gains[tower, 0], shifts[tower, 0]))
            queries = rounded(matmul(act_one, qkv_w[tower, 0]) + bias_qv[tower, 0])
            key_rows = rounded(matmul(act_one, qkv_w[tower, 1]))
            value_rows = rounded(matmul(act_one, qkv_w[tower, 2]) + bias_qv[tower, 1])
            mixed_rows = self_heads(queries, key_rows, value_rows, seg_blocks, causal)
            return stream + low_back(matmul(mixed_rows, out_w[tower]) + bias_out[tower])

        def feed_part(stream, tower):
            act_two = low(norm_rows(stream, gains[tower, 1], shifts[tower, 1]))
            pre_act = low_back(matmul(act_two, in_w[tower]) + bias_in[tower])
            hidden = low(jax.nn.gelu(pre_act, approximate=True))
            return stream + low_back(matmul(hidden, mlp_w[tower]) + bias_mlp[tower])
        enc_one = attention_part(stream_in[0], 0, False)
        enc_out = feed_part(enc_one, 0)
        image_act = low(norm_rows(enc_out, gains[0, 2], shifts[0, 2]))
        image_keys = rounded(matmul(image_act, cross_w[0, 0]))
        image_vals = rounded(matmul(image_act, cross_w[0, 1]))
        dec_one = attention_part(stream_in[1], 1, True)
        cross_act = low(norm_rows(dec_one, gains[1, 2], shifts[1, 2]))
        cross_query = rounded(matmul(cross_act, cross_w[1, 0]))
        cross_mix = cross_heads(cross_query, image_keys, image_vals, row_image)
        dec_two = dec_one + low_back(matmul(cross_mix, cross_w[1, 1].T))
        dec_out = feed_part(dec_two, 1)
        return jnp.stack([enc_out, dec_out])
    floats = (tower_in.astype(jnp.float32), attn_qkv.astype(jnp.float32), attn_out.astype(jnp.float32), mlp_in.astype(jnp.float32), mlp_out.astype(jnp.float32), cross_proj.astype(jnp.float32), qv_bias.astype(jnp.float32), out_bias.astype(jnp.float32), mlp_bias_in.astype(jnp.float32), mlp_bias_out.astype(jnp.float32), norm_gain.astype(jnp.float32), norm_bias.astype(jnp.float32))
    outputs, pullback = jax.vjp(forward, *floats)
    grads = pullback(out_cot.astype(jnp.float32))
    return (outputs.astype(jnp.bfloat16), grads[0].astype(jnp.bfloat16), grads[1], grads[2], grads[3], grads[4], grads[5], grads[6], grads[7], grads[8], grads[9], grads[10], grads[11])
```

```python
import functools

import jax
import jax.numpy as jnp
from jax import lax
from jax.experimental import pallas as pl
from jax.experimental.pallas import tpu as pltpu
from jax.sharding import PartitionSpec as P

HDIM = 64
PATCH = 576
LTXT = 64
EPS = 1e-06
NEG = -1e30
LANES = 128
MESH = pl.DeviceIdType.MESH
F32 = jnp.float32
BF16 = jnp.bfloat16
VMEM_LIMIT = 60 * 1024 * 1024


def norm_parts(values):
    center = values - jnp.mean(values, axis=-1, keepdims=True)
    spread = jnp.mean(center * center, axis=-1, keepdims=True)
    scale = lax.rsqrt(spread + EPS)
    return (center * scale, scale)


def norm_rows(values, gain_vec, shift_vec):
    unit, _ = norm_parts(values)
    return unit * gain_vec + shift_vec


def norm_back(values, gain_vec, grad_normed):
    unit, scale = norm_parts(values)
    inner = grad_normed * gain_vec
    mean_one = jnp.mean(inner, axis=-1, keepdims=True)
    mean_two = jnp.mean(inner * unit, axis=-1, keepdims=True)
    back = (inner - mean_one - unit * mean_two) * scale
    return (back, jnp.sum(grad_normed * unit, axis=0), jnp.sum(grad_normed, axis=0))


def gelu_tanh(values):
    return jax.nn.gelu(values, approximate=True)


def dot_rows(left, right):
    return lax.dot_general(left, right, (((1,), (1,)), ((), ())), preferred_element_type=F32)


def dot_first(left, right):
    return lax.dot_general(left, right, (((0,), (0,)), ((), ())), preferred_element_type=F32)


def dot_plain(left, right):
    return lax.dot_general(left, right, (((1,), (0,)), ((), ())), preferred_element_type=F32)


def stack_heads(block, low_lanes):
    wide = block.astype(F32)
    return jnp.concatenate([jnp.where(low_lanes, wide, 0.0), jnp.where(low_lanes, 0.0, wide)], axis=0)


def merge_heads(pair, low_lanes):
    return jnp.where(low_lanes, pair[:LTXT], pair[LTXT:])


def low_half():
    return lax.broadcasted_iota(jnp.int32, (LTXT, LANES), 1) < HDIM


def causal_mask(seg_col, seg_row):
    key_at = lax.broadcasted_iota(jnp.int32, (LTXT, LANES), 0)
    query_at = lax.broadcasted_iota(jnp.int32, (LTXT, LANES), 1) % LTXT
    return jnp.logical_and(key_at <= query_at, seg_col == seg_row)


def key_block(mode, ref, r, picks):
    if mode == "image":
        return ref[...]
    if mode == "text":
        return ref[pl.ds(pl.multiple_of(r * LTXT, LTXT), LTXT), :]
    return ref[picks[r]]


def attend_kernel(mode, rows, scale, *refs):
    if mode == "cross":
        picks, q_ref, k_ref, v_ref, o_ref, l_ref = refs
    elif mode == "text":
        picks = None
        q_ref, k_ref, v_ref, segc_ref, segr_ref, o_ref, l_ref = refs
    else:
        picks = None
        q_ref, k_ref, v_ref, o_ref, l_ref = refs
    low = low_half()

    def step(r, carry):
        at = pl.ds(pl.multiple_of(r * LTXT, LTXT), LTXT)
        queries = (stack_heads(q_ref[at, :], low) * scale).astype(BF16)
        keys = key_block(mode, k_ref, r, picks)
        vals = key_block(mode, v_ref, r, picks)
        scores = dot_rows(keys, queries)
        if mode == "text":
            scores = jnp.where(causal_mask(segc_ref[at, :], segr_ref[pl.ds(r, 1), :]), scores, NEG)
        top = jnp.max(scores, axis=0, keepdims=True)
        grown = jnp.exp(scores - top)
        total = jnp.sum(grown, axis=0, keepdims=True)
        weights = (grown * (1.0 / total)).astype(BF16)
        mixed = dot_first(weights, vals)
        o_ref[at, :] = merge_heads(mixed, low).astype(BF16)
        l_ref[0, pl.ds(r, 1), :] = top + jnp.log(total)
        return carry

    lax.fori_loop(0, rows, step, 0, unroll=3)


def attend_back_kernel(mode, rows, scale, pairs, *refs):
    if mode == "cross":
        picks, q_ref, k_ref, v_ref, g_ref, l_ref, dq_ref, dk_ref, dv_ref, dk_acc, dv_acc = refs
    elif mode == "text":
        picks = None
        q_ref, k_ref, v_ref, g_ref, l_ref, segc_ref, segr_ref, d_ref, dk_acc, dv_acc = refs
    else:
        picks = None
        q_ref, k_ref, v_ref, g_ref, l_ref, d_ref, dk_acc, dv_acc = refs
    low = low_half()
    pair = pl.program_id(0)
    if mode != "text":
        dk_acc[...] = jnp.zeros_like(dk_acc)
        dv_acc[...] = jnp.zeros_like(dv_acc)

    def lanes(part):
        return pl.ds(pl.multiple_of((part * pairs + pair) * LANES, LANES), LANES)

    def step(r, carry):
        at = pl.ds(pl.multiple_of(r * LTXT, LTXT), LTXT)
        queries = (stack_heads(q_ref[at, :], low) * scale).astype(BF16)
        grads = stack_heads(g_ref[at, :], low).astype(BF16)
        keys = key_block(mode, k_ref, r, picks)
        vals = key_block(mode, v_ref, r, picks)
        scores = dot_rows(keys, queries)
        if mode == "text":
            scores = jnp.where(causal_mask(segc_ref[at, :], segr_ref[pl.ds(r, 1), :]), scores, NEG)
        weights = jnp.exp(scores - l_ref[0, pl.ds(r, 1), :])
        grad_w = dot_rows(vals, grads)
        row_dot = jnp.sum(weights * grad_w, axis=0, keepdims=True)
        grad_s = (weights * (grad_w - row_dot)).astype(BF16)
        grad_q = merge_heads(dot_first(grad_s, keys), low) * scale
        grad_k = dot_plain(grad_s, queries)
        grad_v = dot_plain(weights.astype(BF16), grads)
        if mode == "cross":
            dq_ref[at, :] = grad_q.astype(BF16)
            dk_acc[picks[r]] += grad_k
            dv_acc[picks[r]] += grad_v
        elif mode == "text":
            d_ref[at, lanes(0)] = grad_q.astype(BF16)
            d_ref[at, lanes(1)] = grad_k.astype(BF16)
            d_ref[at, lanes(2)] = grad_v.astype(BF16)
        else:
            d_ref[at, lanes(0)] = grad_q.astype(BF16)
            dk_acc[...] += grad_k
            dv_acc[...] += grad_v
        return carry

    lax.fori_loop(0, rows, step, 0)
    if mode == "cross":
        dk_ref[...] = dk_acc[...].astype(BF16)
        dv_ref[...] = dv_acc[...].astype(BF16)
    elif mode == "image":
        d_ref[:, lanes(1)] = dk_acc[...].astype(BF16)
        d_ref[:, lanes(2)] = dv_acc[...].astype(BF16)


def column(part, pairs, rows):
    return pl.BlockSpec((rows, LANES), lambda i, *_: (0, part * pairs + i))


def whole(shape):
    return pl.BlockSpec(shape, lambda i, *_: (0,) * len(shape))


def tops_spec():
    return pl.BlockSpec((1, 16, LANES), lambda i, *_: (i, 0, 0))


def self_cost(tokens, heads, products, mode):
    keys = PATCH if mode != "text" else LTXT
    return pl.CostEstimate(
        flops=2 * products * 2 * tokens * keys * HDIM * heads,
        bytes_accessed=8 * tokens * heads * HDIM,
        transcendentals=tokens * keys * heads,
    )


def kernel_params():
    return pltpu.CompilerParams(vmem_limit_bytes=VMEM_LIMIT)


def self_attend(mode, packed, seg_col, seg_row, scale):
    tokens = packed.shape[0]
    pairs = packed.shape[1] // (3 * LANES)
    rows = tokens // LTXT
    specs = [column(part, pairs, tokens) for part in range(3)]
    extra = ()
    if mode == "text":
        specs += [whole(seg_col.shape), whole(seg_row.shape)]
        extra = (seg_col, seg_row)
    return pl.pallas_call(
        functools.partial(attend_kernel, mode, rows, scale),
        grid=(pairs,),
        in_specs=specs,
        out_specs=[column(0, pairs, tokens), tops_spec()],
        out_shape=[
            jax.ShapeDtypeStruct((tokens, pairs * LANES), BF16),
            jax.ShapeDtypeStruct((pairs, 16, LANES), F32),
        ],
        compiler_params=kernel_params(),
        cost_estimate=self_cost(tokens, 2 * pairs, 2, mode),
        name="attend_" + mode,
    )(packed, packed, packed, *extra)


def self_attend_back(mode, packed, grads, tops, seg_col, seg_row, scale):
    tokens = packed.shape[0]
    pairs = packed.shape[1] // (3 * LANES)
    rows = tokens // LTXT
    specs = [column(part, pairs, tokens) for part in range(3)] + [column(0, pairs, tokens), tops_spec()]
    extra = ()
    if mode == "text":
        specs += [whole(seg_col.shape), whole(seg_row.shape)]
        extra = (seg_col, seg_row)
    return pl.pallas_call(
        functools.partial(attend_back_kernel, mode, rows, scale, pairs),
        grid=(pairs,),
        in_specs=specs,
        out_specs=whole(packed.shape),
        out_shape=jax.ShapeDtypeStruct(packed.shape, BF16),
        scratch_shapes=[pltpu.VMEM((tokens, LANES), F32), pltpu.VMEM((tokens, LANES), F32)],
        compiler_params=kernel_params(),
        cost_estimate=self_cost(tokens, 2 * pairs, 5, mode),
        name="attend_back_" + mode,
    )(packed, packed, packed, grads, tops, *extra)


def image_block(images, keys):
    return pl.BlockSpec((images, keys, LANES), lambda i, *_: (0, 0, i))


def cross_attend(queries, keys, vals, picks, scale):
    tokens, wide = queries.shape
    pairs = wide // LANES
    images, key_rows, _ = keys.shape
    grid = pltpu.PrefetchScalarGridSpec(
        num_scalar_prefetch=1,
        grid=(pairs,),
        in_specs=[column(0, pairs, tokens), image_block(images, key_rows), image_block(images, key_rows)],
        out_specs=[column(0, pairs, tokens), tops_spec()],
    )
    return pl.pallas_call(
        functools.partial(attend_kernel, "cross", tokens // LTXT, scale),
        grid_spec=grid,
        out_shape=[
            jax.ShapeDtypeStruct((tokens, wide), BF16),
            jax.ShapeDtypeStruct((pairs, 16, LANES), F32),
        ],
        compiler_params=kernel_params(),
        cost_estimate=self_cost(tokens, 2 * pairs, 2, "cross"),
        name="attend_cross",
    )(picks, queries, keys, vals)


def cross_attend_back(queries, keys, vals, grads, tops, picks, scale):
    tokens, wide = queries.shape
    pairs = wide // LANES
    images, key_rows, _ = keys.shape
    grid = pltpu.PrefetchScalarGridSpec(
        num_scalar_prefetch=1,
        grid=(pairs,),
        in_specs=[
            column(0, pairs, tokens),
            image_block(images, key_rows),
            image_block(images, key_rows),
            column(0, pairs, tokens),
            tops_spec(),
        ],
        out_specs=[column(0, pairs, tokens), image_block(images, key_rows), image_block(images, key_rows)],
        scratch_shapes=[pltpu.VMEM((images, key_rows, LANES), F32)] * 2,
    )
    return pl.pallas_call(
        functools.partial(attend_back_kernel, "cross", tokens // LTXT, scale, pairs),
        grid_spec=grid,
        out_shape=[
            jax.ShapeDtypeStruct((tokens, wide), BF16),
            jax.ShapeDtypeStruct(keys.shape, BF16),
            jax.ShapeDtypeStruct(keys.shape, BF16),
        ],
        compiler_params=kernel_params(),
        cost_estimate=self_cost(tokens, 2 * pairs, 5, "cross"),
        name="attend_back_cross",
    )(picks, queries, keys, vals, grads, tops)


def gather_kernel(pieces, n_src, *refs):
    srcs = refs[:n_src]
    outs = refs[n_src : 2 * n_src]
    stages = refs[2 * n_src : 3 * n_src]
    send_sem, recv_sem, local_sem, twin_send, twin_recv, = refs[3 * n_src :]
    tower = lax.axis_index("tower")
    dp = lax.axis_index("dp")
    z = lax.axis_index("mp")
    core = lax.rem(dp, 2)
    line = dp // 2
    place = z + core * (3 - 2 * z)
    ahead = z + 1 - 2 * core
    behind = z - 1 + 2 * core
    other = dp + 2 - 4 * line
    slot_of = (core, 1 - core)
    is_text = tower == 1
    cross = n_src - 1

    barrier = pltpu.get_barrier_semaphore()

    @pl.when(z > 0)
    def _():
        pl.semaphore_signal(barrier, inc=1, device_id={"mp": z - 1}, device_id_type=MESH)

    @pl.when(z < 3)
    def _():
        pl.semaphore_signal(barrier, inc=1, device_id={"mp": z + 1}, device_id_type=MESH)

    pl.semaphore_signal(barrier, inc=1, device_id={"dp": other}, device_id_type=MESH)
    pl.semaphore_signal(barrier, inc=1, device_id={"tower": 1 - tower}, device_id_type=MESH)

    @pl.when(jnp.logical_or(z == 0, z == 3))
    def _():
        pl.semaphore_wait(barrier, 3)

    @pl.when(jnp.logical_and(z > 0, z < 3))
    def _():
        pl.semaphore_wait(barrier, 4)

    def spot(piece, slot, half):
        which, first, start, size, far = piece
        part = size // 2
        count = srcs[which].shape[0]
        return outs[which].at[pl.ds(first, count), slot, pl.ds(start + half * part, part), :]

    def own(piece):
        which, first, start, size, far = piece
        part = size // 2
        if far:
            return outs[which].at[pl.ds(first, srcs[which].shape[0]), lax.rem(z, 2), pl.ds(start + line * part, part), :]
        return srcs[which].at[:, pl.ds(start + line * part, part), :]

    def move(k, source, slot, half, kind, arrive, target):
        return pltpu.make_async_remote_copy(
            src_ref=source,
            dst_ref=spot(pieces[k], slot, half),
            send_sem=send_sem.at[k, kind],
            recv_sem=recv_sem.at[k, arrive],
            device_id=target,
            device_id_type=MESH,
        )

    def twin_copy():
        slot = lax.rem(z, 2)
        return pltpu.make_async_remote_copy(
            src_ref=srcs[cross],
            dst_ref=outs[cross].at[pl.ds(0, srcs[cross].shape[0]), slot],
            send_sem=twin_send,
            recv_sem=twin_recv,
            device_id={"tower": 1 - tower},
            device_id_type=MESH,
        )

    holder = place <= 1

    @pl.when(jnp.logical_and(holder, tower == 0))
    def _():
        twin_copy().start()

    def local_in(i):
        return pltpu.make_async_copy(srcs[i], stages[i], local_sem.at[i, 0])

    def local_out(i):
        first = outs[i].shape[0] - srcs[i].shape[0]
        return pltpu.make_async_copy(stages[i], outs[i].at[pl.ds(first, srcs[i].shape[0]), lax.rem(z, 2)], local_sem.at[i, 1])

    def gate(piece, cond):
        which = piece[0]
        return jnp.logical_and(cond, is_text) if which == cross else cond

    def send_own(k):
        piece = pieces[k]

        @pl.when(gate(piece, place == 0))
        def _():
            move(k, own(piece), slot_of[0], line, 0, 0, {"mp": ahead}).start()

        @pl.when(gate(piece, place == 1))
        def _():
            move(k, own(piece), slot_of[1], line, 1, 1, {"mp": ahead}).start()
            move(k, own(piece), slot_of[1], line, 2, 1, {"mp": behind}).start()

    for k, piece in enumerate(pieces):
        if not piece[4]:
            send_own(k)

    @pl.when(holder)
    def _():
        for i in range(n_src):
            local_in(i).start()
        for i in range(n_src):
            local_in(i).wait()
            local_out(i).start()

    def pass_on(k):
        piece = pieces[k]
        if piece[4]:

            @pl.when(jnp.logical_and(holder, is_text))
            def _():
                twin_copy().wait_recv()

            send_own(k)

        @pl.when(gate(piece, place >= 1))
        def _():
            here = spot(piece, slot_of[0], line)
            move(k, here, slot_of[0], line, 0, 0, {"mp": z}).wait_recv()
            move(k, here, slot_of[0], line, 3, 2, {"dp": other}).start()

        @pl.when(gate(piece, jnp.logical_and(place >= 1, place <= 2)))
        def _():
            here = spot(piece, slot_of[0], line)
            move(k, here, slot_of[0], line, 0, 0, {"mp": ahead}).start()

        @pl.when(gate(piece, place != 1))
        def _():
            here = spot(piece, slot_of[1], line)
            move(k, here, slot_of[1], line, 1, 1, {"mp": z}).wait_recv()
            move(k, here, slot_of[1], line, 4, 3, {"dp": other}).start()

        @pl.when(gate(piece, place == 2))
        def _():
            here = spot(piece, slot_of[1], line)
            move(k, here, slot_of[1], line, 1, 1, {"mp": ahead}).start()

    for k in range(len(pieces)):
        pass_on(k)

    def finish(k):
        piece = pieces[k]

        @pl.when(gate(piece, place <= 2))
        def _():
            move(k, spot(piece, slot_of[0], line), slot_of[0], line, 0, 0, {"mp": z}).wait_send()

        @pl.when(gate(piece, jnp.logical_and(place >= 1, place <= 2)))
        def _():
            move(k, spot(piece, slot_of[1], line), slot_of[1], line, 1, 1, {"mp": z}).wait_send()

        @pl.when(gate(piece, place == 1))
        def _():
            move(k, spot(piece, slot_of[1], line), slot_of[1], line, 2, 1, {"mp": z}).wait_send()

        @pl.when(gate(piece, place >= 1))
        def _():
            made = move(k, spot(piece, slot_of[0], 1 - line), slot_of[0], 1 - line, 3, 2, {"dp": dp})
            made.wait_send()
            made.wait_recv()

        @pl.when(gate(piece, place != 1))
        def _():
            made = move(k, spot(piece, slot_of[1], 1 - line), slot_of[1], 1 - line, 4, 3, {"dp": dp})
            made.wait_send()
            made.wait_recv()

    for k in range(len(pieces)):
        finish(k)

    @pl.when(holder)
    def _():
        for i in range(n_src):
            local_out(i).wait()

    @pl.when(jnp.logical_and(holder, tower == 0))
    def _():
        twin_copy().wait_send()


def gather_weights(shards):
    n_src = len(shards)
    outs = [
        jax.ShapeDtypeStruct(((2 if i == n_src - 1 else 1) * s.shape[0], 2) + s.shape[1:], BF16)
        for i, s in enumerate(shards)
    ]
    pieces = []
    for i, s in enumerate(shards):
        rows = s.shape[1]
        if i == n_src - 1:
            pieces.append((i, s.shape[0], 0, rows, False))
            pieces.insert(2, (i, 0, 0, rows, True))
        else:
            cut = rows if rows <= 192 else rows // 2
            pieces += [(i, 0, at, cut, False) for at in range(0, rows, cut)]
    n = len(pieces)
    any_spec = pl.BlockSpec(memory_space=pl.ANY)
    return pl.pallas_call(
        functools.partial(gather_kernel, tuple(pieces), n_src),
        in_specs=[any_spec] * n_src,
        out_specs=[any_spec] * n_src,
        out_shape=outs,
        scratch_shapes=[pltpu.VMEM(s.shape, BF16) for s in shards]
        + [
            pltpu.SemaphoreType.DMA((n, 5)),
            pltpu.SemaphoreType.DMA((n, 4)),
            pltpu.SemaphoreType.DMA((n_src, 2)),
            pltpu.SemaphoreType.DMA,
            pltpu.SemaphoreType.DMA,
        ],
        compiler_params=pltpu.CompilerParams(
            collective_id=0, has_side_effects=True, vmem_limit_bytes=VMEM_LIMIT
        ),
        name="gather_weights",
    )(*shards)


TILE = 32


def reduce_kernel(pieces, flags, n_src, with_smalls, *refs):
    it = iter(refs)
    srcs = [next(it) for _ in range(n_src)]
    small_in = next(it) if with_smalls else None
    outs = [next(it) for _ in range(n_src)]
    small_out = next(it) if with_smalls else None
    mine = [next(it) for _ in range(n_src)]
    near = [next(it) for _ in range(n_src)]
    far = [next(it) for _ in range(n_src)]
    if with_smalls:
        small_near, small_all = next(it), next(it)
        small_sem = next(it)
    local_sem, y_send, y_recv, z_send, z_recv, c_send, c_recv = it
    tower = lax.axis_index("tower")
    dp = lax.axis_index("dp")
    z = lax.axis_index("mp")
    core = lax.rem(dp, 2)
    line = dp // 2
    other = dp + 2 - 4 * line
    partner = dp + 1 - 2 * core
    holder = z // 2 == core
    slot = lax.rem(z, 2)
    half = srcs[0].shape[3] // 2

    barrier = pltpu.get_barrier_semaphore()
    pl.semaphore_signal(barrier, inc=1, device_id={"dp": other}, device_id_type=MESH)
    pl.semaphore_signal(barrier, inc=1, device_id={"dp": partner}, device_id_type=MESH)
    for away in range(1, 4):
        pl.semaphore_signal(barrier, inc=1, device_id={"mp": lax.rem(z + away, 4)}, device_id_type=MESH)
    pl.semaphore_wait(barrier, 5)

    def gate(piece, cond=None):
        flag = flags[piece[0]]
        if flag is None:
            return cond
        here = tower == flag
        return here if cond is None else jnp.logical_and(cond, here)

    def guarded(cond, run):
        if cond is None:
            run()
        else:
            pl.when(cond)(run)

    def rows_of(piece):
        return pl.ds(piece[1], piece[2])

    def to_line(k):
        which = pieces[k][0]
        rows = rows_of(pieces[k])
        return pltpu.make_async_remote_copy(
            src_ref=srcs[which].at[:, :, rows, pl.ds(pl.multiple_of((1 - line) * half, LANES), half)],
            dst_ref=near[which].at[:, :, rows, :],
            send_sem=y_send.at[k],
            recv_sem=y_recv.at[k],
            device_id={"dp": other},
            device_id_type=MESH,
        )

    def to_mine(k):
        which = pieces[k][0]
        rows = rows_of(pieces[k])
        return pltpu.make_async_copy(
            srcs[which].at[:, :, rows, pl.ds(pl.multiple_of(line * half, LANES), half)],
            mine[which].at[:, :, rows, :],
            local_sem.at[k],
        )

    def to_chip(k, shard, seat):
        which = pieces[k][0]
        rows = rows_of(pieces[k])
        target = 2 * core + shard
        return pltpu.make_async_remote_copy(
            src_ref=mine[which].at[:, shard, rows, :],
            dst_ref=far[which].at[seat, :, rows, :],
            send_sem=z_send.at[k, shard],
            recv_sem=z_recv.at[k, seat],
            device_id={"mp": target},
            device_id_type=MESH,
        )

    def to_core(k):
        which = pieces[k][0]
        rows = rows_of(pieces[k])
        return pltpu.make_async_remote_copy(
            src_ref=outs[which].at[:, rows, :],
            dst_ref=outs[which].at[:, rows, :],
            send_sem=c_send.at[k],
            recv_sem=c_recv.at[k],
            device_id={"dp": partner},
            device_id_type=MESH,
        )

    def seat_of(shard):
        return lax.rem(z - (2 * core + shard) + 4, 4) - 1

    for k, piece in enumerate(pieces):

        def begin(k=k):
            to_line(k).start()
            to_mine(k).start()

        guarded(gate(piece), begin)

    if with_smalls:
        small_line = pltpu.make_async_remote_copy(
            src_ref=small_in,
            dst_ref=small_near,
            send_sem=small_sem.at[0],
            recv_sem=small_sem.at[1],
            device_id={"dp": other},
            device_id_type=MESH,
        )
        small_line.start()

        def small_move(away):
            return pltpu.make_async_remote_copy(
                src_ref=small_all.at[z],
                dst_ref=small_all.at[z],
                send_sem=small_sem.at[1 + away],
                recv_sem=small_sem.at[4 + away],
                device_id={"mp": lax.rem(z + away, 4)},
                device_id_type=MESH,
            )

        def small_got(away):
            sender = lax.rem(z + 4 - away, 4)
            return pltpu.make_async_remote_copy(
                src_ref=small_all.at[sender],
                dst_ref=small_all.at[sender],
                send_sem=small_sem.at[1 + away],
                recv_sem=small_sem.at[4 + away],
                device_id={"mp": lax.rem(z + away, 4)},
                device_id_type=MESH,
            )

        def small_core(which):
            return pltpu.make_async_remote_copy(
                src_ref=small_out.at[which],
                dst_ref=small_out.at[which],
                send_sem=small_sem.at[8],
                recv_sem=small_sem.at[9],
                device_id={"dp": partner},
                device_id_type=MESH,
            )

        small_line.wait()
        small_all[z] = small_in[...] + small_near[...]

    for k, piece in enumerate(pieces):
        which, start, size = piece
        count = srcs[which].shape[0]

        def add_near(k=k, which=which, start=start, size=size, count=count):
            to_mine(k).wait()
            to_line(k).wait_recv()

            @pl.loop(0, size // TILE)
            def _(i):
                rows = pl.ds(pl.multiple_of(start + i * TILE, TILE), TILE)
                for a in range(count):
                    for b in range(2):
                        total = mine[which][a, b, rows, :].astype(F32) + near[which][a, b, rows, :].astype(F32)
                        mine[which][a, b, rows, :] = total.astype(BF16)

            for shard in range(2):

                @pl.when(z != 2 * core + shard)
                def _(shard=shard):
                    to_chip(k, shard, seat_of(shard)).start()

        guarded(gate(piece), add_near)
        if with_smalls and k == 0:
            for away in range(1, 4):
                small_move(away).start()

    for k, piece in enumerate(pieces):
        which, start, size = piece
        count = srcs[which].shape[0]

        def add_far(k=k, which=which, start=start, size=size, count=count):
            for seat in range(3):
                to_chip(k, 0, seat).wait_recv()

            @pl.loop(0, size // TILE)
            def _(i):
                rows = pl.ds(pl.multiple_of(start + i * TILE, TILE), TILE)
                for a in range(count):
                    total = mine[which][a, slot, rows, :].astype(F32)
                    for seat in range(3):
                        total = total + far[which][seat, a, rows, :].astype(F32)
                    outs[which][a, rows, :] = total.astype(BF16)

            to_core(k).start()

        guarded(gate(piece, holder), add_far)

    if with_smalls:
        for away in range(1, 4):
            small_got(away).wait_recv()
        small_out[core] = ((small_all[0] + small_all[1]) + small_all[2]) + small_all[3]
        small_core(core).start()

    for k, piece in enumerate(pieces):

        def ended(k=k):
            to_line(k).wait_send()
            for shard in range(2):

                @pl.when(z != 2 * core + shard)
                def _(shard=shard):
                    to_chip(k, shard, 0).wait_send()

            @pl.when(holder)
            def _():
                to_core(k).wait_send()

            @pl.when(jnp.logical_not(holder))
            def _():
                to_core(k).wait_recv()

        guarded(gate(piece), ended)

    if with_smalls:
        for away in range(1, 4):
            small_move(away).wait_send()
        small_core(core).wait_send()
        small_core(1 - core).wait_recv()


def reduce_grads(grads, flags, smalls, collective_id):
    n_src = len(grads)
    pieces = []
    for i, g in enumerate(grads):
        rows = g.shape[2]
        cut = rows if rows <= 192 else rows // 2
        pieces += [(i, at, cut) for at in range(0, rows, cut)]
    n = len(pieces)
    half = grads[0].shape[3] // 2
    any_spec = pl.BlockSpec(memory_space=pl.ANY)
    vmem_spec = pl.BlockSpec(memory_space=pltpu.VMEM)
    in_specs = [any_spec] * n_src
    out_shape = [jax.ShapeDtypeStruct((g.shape[0], g.shape[2], half), BF16) for g in grads]
    out_specs = [vmem_spec] * n_src
    args = list(grads)
    with_smalls = smalls is not None
    scratch = (
        [pltpu.VMEM(g.shape[:3] + (half,), BF16) for g in grads] * 2
        + [pltpu.VMEM((3, g.shape[0], g.shape[2], half), BF16) for g in grads]
    )
    if with_smalls:
        in_specs.append(vmem_spec)
        out_specs.append(vmem_spec)
        out_shape.append(jax.ShapeDtypeStruct((2,) + smalls.shape, F32))
        args.append(smalls)
        scratch += [
            pltpu.VMEM(smalls.shape, F32),
            pltpu.VMEM((4,) + smalls.shape, F32),
            pltpu.SemaphoreType.DMA((10,)),
        ]
    scratch += [
        pltpu.SemaphoreType.DMA((n,)),
        pltpu.SemaphoreType.DMA((n,)),
        pltpu.SemaphoreType.DMA((n,)),
        pltpu.SemaphoreType.DMA((n, 2)),
        pltpu.SemaphoreType.DMA((n, 3)),
        pltpu.SemaphoreType.DMA((n,)),
        pltpu.SemaphoreType.DMA((n,)),
    ]
    return pl.pallas_call(
        functools.partial(reduce_kernel, tuple(pieces), tuple(flags), n_src, with_smalls),
        in_specs=in_specs,
        out_specs=out_specs,
        out_shape=out_shape,
        scratch_shapes=scratch,
        compiler_params=pltpu.CompilerParams(
            collective_id=collective_id, has_side_effects=True, vmem_limit_bytes=VMEM_LIMIT
        ),
        name="reduce_grads_%d" % collective_id,
    )(*args)


def gather_plain(shards):
    core = lax.rem(lax.axis_index("dp"), 2)
    outs = []
    for i, s in enumerate(shards):
        if i == len(shards) - 1:
            s = jnp.concatenate([lax.ppermute(s, "tower", [(0, 1)]), s], axis=0)
        full = lax.all_gather(s, "mp", axis=1, tiled=False)
        outs.append(lax.dynamic_slice_in_dim(full, 2 * core, 2, 1))
    return outs


def reduce_plain(grads, smalls):
    dp = lax.axis_index("dp")
    core = lax.rem(dp, 2)
    outs = []
    for g in grads:
        n, _, rows, wide = g.shape
        full = jnp.zeros((n, 4, rows, wide), BF16)
        full = lax.dynamic_update_slice(full, g, (0, 2 * core, 0, 0))
        part = lax.psum_scatter(full, "mp", scatter_dimension=1, tiled=False)
        part = lax.psum_scatter(part, "dp", scatter_dimension=2, tiled=True)
        outs.append(part)
    if smalls is None:
        return outs
    both = jnp.zeros((2,) + smalls.shape, F32)
    both = lax.dynamic_update_slice(both, smalls[None], (core, 0, 0))
    return outs + [lax.psum(both, ("dp", "mp"))]


def body(
    tower_in,
    out_cot,
    segment_ids,
    row_image,
    attn_qkv,
    attn_out,
    mlp_in,
    mlp_out,
    cross_proj,
    qv_bias,
    out_bias,
    mlp_bias_in,
    mlp_bias_out,
    norm_gain,
    norm_bias,
):
    lines = lax.axis_size("dp") // 2
    depth = lax.axis_size("mp")
    devices = lax.axis_size("dp")
    is_enc = lax.axis_index("tower") == 0
    dp = lax.axis_index("dp")
    z = lax.axis_index("mp")
    core = lax.rem(dp, 2)
    side = lax.rem(z, 2)
    group = z // 2
    direct = lines == 2
    assert depth == 4
    quarter = tower_in.shape[1]
    tokens = 2 * quarter
    assert tokens == PATCH
    width = tower_in.shape[2]
    head_cols = 2 * attn_qkv.shape[3]
    hidden = 2 * mlp_in.shape[2]
    scale_qk = HDIM ** (-0.5)

    out_moves, back_moves = [], []
    for d in range(devices):
        for place in range(depth):
            here = d * depth + place
            there = (d - d % 2 + place % 2) * depth + 2 * (d % 2) + place // 2
            out_moves.append((here, there))
            back_moves.append((there, here))

    def swap_cores(x):
        return lax.ppermute(x, "dp", [(i, i ^ 1) for i in range(devices)])

    def both_cores(own):
        other = swap_cores(own)
        return jnp.where(core == 0, jnp.concatenate([own, other], -2), jnp.concatenate([other, own], -2))

    def own_rows(full):
        return lax.dynamic_slice_in_dim(full, core * quarter, quarter, full.ndim - 2)

    def add_cores(part):
        low = lax.reduce_precision(part, 8, 7).astype(BF16)
        return low.astype(F32) + swap_cores(low).astype(F32)

    shards = [
        jnp.swapaxes(attn_qkv[0], 1, 2),
        attn_out,
        mlp_in,
        mlp_out,
        jnp.swapaxes(cross_proj[0], 1, 2),
    ]
    gathered = gather_weights(shards) if direct else gather_plain(shards)
    w_qkv = gathered[0].reshape(3 * head_cols, width)
    w_out = gathered[1].reshape(head_cols, width)
    w_in = gathered[2][0]
    w_mlp = gathered[3].reshape(hidden, width)
    w_cross = gathered[4].reshape(4, head_cols, width)
    bias_qv = lax.dynamic_slice_in_dim(qv_bias[0], core * head_cols, head_cols, 1)
    bias_packed = jnp.concatenate([bias_qv[0], jnp.zeros_like(bias_qv[0]), bias_qv[1]])
    bias_in = lax.dynamic_slice_in_dim(mlp_bias_in[0], core * hidden, hidden, 0)
    gains = norm_gain[0]
    shifts = norm_bias[0]

    stream_low = both_cores(lax.ppermute(tower_in[0], ("dp", "mp"), out_moves))
    cot_low = both_cores(lax.ppermute(out_cot[0], ("dp", "mp"), out_moves))
    stream = stream_low.astype(F32)
    rows_dev = segment_ids.shape[0]
    rows = rows_dev // 2
    segs = jnp.where(core == group, segment_ids, swap_cores(segment_ids))
    segs = lax.dynamic_slice_in_dim(segs, rows * side, rows, 0)
    picks = jnp.where(core == group, row_image, swap_cores(row_image))
    picks = lax.dynamic_slice_in_dim(picks, rows * side, rows, 0)
    seg_row = jnp.pad(jnp.concatenate([segs, segs], axis=1), ((0, 16 - rows), (0, 0)))
    seg_col = jnp.broadcast_to(segs.reshape(rows * LTXT, 1), (rows * LTXT, LANES))

    act_one = norm_rows(stream, gains[0], shifts[0]).astype(BF16)
    packed = (dot_rows(act_one, w_qkv) + bias_packed).astype(BF16)
    mixed, tops = lax.cond(
        is_enc,
        lambda p: tuple(self_attend("image", p, seg_col, seg_row, scale_qk)),
        lambda p: tuple(self_attend("text", p, seg_col, seg_row, scale_qk)),
        packed,
    )
    stream_one = stream + add_cores(dot_plain(mixed, w_out)) + out_bias[0]

    def feed_in(values):
        act = norm_rows(values, gains[1], shifts[1]).astype(BF16)
        pre = jnp.concatenate([dot_plain(act, w_in[0]), dot_plain(act, w_in[1])], axis=1) + bias_in
        return (act, pre, gelu_tanh(pre).astype(BF16))

    def feed_out(hid):
        return add_cores(dot_plain(hid, w_mlp)) + mlp_bias_out[0]

    act_enc, pre_enc, hid_enc = feed_in(stream_one)
    out_enc = stream_one + feed_out(hid_enc)
    base_three = jnp.where(is_enc, out_enc, stream_one)
    act_three = norm_rows(base_three, gains[2], shifts[2]).astype(BF16)

    near_half = lax.ppermute(own_rows(act_three), "tower", [(0, 1)])
    far_half = lax.ppermute(near_half, "mp", [(i, i ^ 1) for i in range(depth)])
    halves = jnp.where(side == 0, jnp.stack([near_half, far_half]), jnp.stack([far_half, near_half]))
    images = both_cores(halves)

    cross_q = dot_rows(act_three, w_cross[2]).astype(BF16)
    flat_images = images.reshape(2 * tokens, width)
    cross_k = dot_rows(flat_images, w_cross[0]).astype(BF16).reshape(2, tokens, head_cols)
    cross_v = dot_rows(flat_images, w_cross[1]).astype(BF16).reshape(2, tokens, head_cols)
    cross_mix, cross_tops = cross_attend(cross_q, cross_k, cross_v, picks, scale_qk)
    stream_two = stream_one + add_cores(dot_plain(cross_mix, w_cross[3]))

    act_dec, pre_dec, hid_dec = feed_in(stream_two)
    out_dec = stream_two + feed_out(hid_dec)
    tower_out = own_rows(jnp.where(is_enc, out_enc, out_dec).astype(BF16))
    tower_out = lax.ppermute(tower_out, ("dp", "mp"), back_moves)

    def feed_back(grad_low, pre):
        grad_hid = dot_rows(grad_low, w_mlp)
        _, pullback = jax.vjp(gelu_tanh, pre)
        grad_pre = pullback(grad_hid)[0].astype(BF16)
        cols = hidden // 2
        part = dot_rows(grad_pre[:, :cols], w_in[0]) + dot_rows(grad_pre[:, cols:], w_in[1])
        return (grad_pre, add_cores(part))

    def feed_grads(grad_low, act, grad_pre, hid):
        g_in = dot_first(grad_pre, act).astype(BF16)
        g_mlp = dot_first(hid, grad_low).astype(BF16)
        return (
            g_in.reshape(1, 2, hidden // 2, width),
            g_mlp.reshape(1, 2, hidden // 2, width),
        )

    cot = cot_low.astype(F32)
    grad_pre_dec, back_in = feed_back(cot_low, pre_dec)
    back_a, gain_a, shift_a = norm_back(stream_two, gains[1], back_in)
    grad_two = cot + back_a
    grad_two_low = grad_two.astype(BF16)

    grad_mix = dot_rows(grad_two_low, w_cross[3]).astype(BF16)
    grad_q, grad_k, grad_v = cross_attend_back(
        cross_q, cross_k, cross_v, grad_mix, cross_tops, picks, scale_qk
    )
    flat_k = grad_k.reshape(2 * tokens, head_cols)
    flat_v = grad_v.reshape(2 * tokens, head_cols)
    part_images = dot_plain(flat_k, w_cross[0]) + dot_plain(flat_v, w_cross[1])
    part_low = part_images.astype(BF16).reshape(2, 2, quarter, width)
    give = lax.dynamic_index_in_dim(part_low, 1 - core, 1, keepdims=False)
    keep = lax.dynamic_index_in_dim(part_low, core, 1, keepdims=False)
    pair_sum = (keep.astype(F32) + swap_cores(give).astype(F32)).astype(BF16)
    give = lax.dynamic_index_in_dim(pair_sum, 1 - side, 0, keepdims=False)
    keep = lax.dynamic_index_in_dim(pair_sum, side, 0, keepdims=False)
    got = lax.ppermute(give, "mp", [(i, i ^ 1) for i in range(depth)])
    image_sum = (keep.astype(F32) + got.astype(F32)).astype(BF16)
    image_back = both_cores(lax.ppermute(image_sum, "tower", [(1, 0)])).astype(F32)
    query_back = add_cores(dot_plain(grad_q, w_cross[2]))

    g_cross = jnp.concatenate(
        [
            dot_first(flat_k, flat_images).astype(BF16),
            dot_first(flat_v, flat_images).astype(BF16),
            dot_first(grad_q, act_three).astype(BF16),
            dot_first(cross_mix, grad_two_low).astype(BF16),
        ],
        axis=0,
    ).reshape(4, 2, head_cols // 2, width)

    back_three, gain_three, shift_three = norm_back(
        base_three, gains[2], jnp.where(is_enc, image_back, query_back)
    )
    grad_enc = cot + back_three
    grad_enc_low = grad_enc.astype(BF16)
    grad_pre_enc, back_in = feed_back(grad_enc_low, pre_enc)
    back_b, gain_b, shift_b = norm_back(stream_one, gains[1], back_in)
    grad_one = jnp.where(is_enc, grad_enc + back_b, grad_two + back_three)
    grad_one_low = grad_one.astype(BF16)

    feed_low = jnp.where(is_enc, grad_enc_low, cot_low)
    feed_pre = jnp.where(is_enc, grad_pre_enc, grad_pre_dec)
    g_in, g_mlp = feed_grads(
        feed_low,
        jnp.where(is_enc, act_enc, act_dec),
        feed_pre,
        jnp.where(is_enc, hid_enc, hid_dec),
    )

    g_out = dot_first(mixed, grad_one_low).astype(BF16).reshape(1, 2, head_cols // 2, width)
    grad_mixed = dot_rows(grad_one_low, w_out).astype(BF16)
    grad_packed = lax.cond(
        is_enc,
        lambda p, g, t: self_attend_back("image", p, g, t, seg_col, seg_row, scale_qk),
        lambda p, g, t: self_attend_back("text", p, g, t, seg_col, seg_row, scale_qk),
        packed,
        grad_mixed,
        tops,
    )
    g_qkv = dot_first(grad_packed, act_one).astype(BF16).reshape(3, 2, head_cols // 2, width)
    back_in = add_cores(dot_plain(grad_packed, w_qkv))
    back_one, gain_one, shift_one = norm_back(stream, gains[0], back_in)
    grad_in = own_rows((grad_one + back_one).astype(BF16))
    grad_in = lax.ppermute(grad_in, ("dp", "mp"), back_moves)

    packed_sum = jnp.sum(grad_packed, axis=0, dtype=F32)
    shared = [
        jnp.sum(grad_one_low, axis=0, dtype=F32),
        jnp.sum(feed_low, axis=0, dtype=F32),
        gain_one,
        jnp.where(is_enc, gain_b, gain_a),
        gain_three,
        shift_one,
        jnp.where(is_enc, shift_b, shift_a),
        shift_three,
    ]
    by_core = [
        packed_sum[:head_cols],
        packed_sum[2 * head_cols :],
        jnp.sum(feed_pre, axis=0, dtype=F32),
    ]
    smalls = jnp.concatenate(shared + by_core)
    used = smalls.shape[0]
    lines_of = -(-used // (8 * LANES)) * 8
    smalls = jnp.pad(smalls, (0, lines_of * LANES - used)).reshape(lines_of, LANES)

    grads = [g_qkv, g_out, g_in, g_mlp, g_cross]
    flags = [None, None, None, None, 1]
    if direct:
        sums = reduce_grads(grads, flags, smalls, 1)

        def own_cols(x):
            cut = x.shape[2] // 2
            return jnp.where(core == 0, x[:, :, :cut], x[:, :, cut:])

        *sums, total = sums
        sums = [own_cols(s) for s in sums]
    else:
        *sums, total = reduce_plain(grads, smalls)
    s_qkv, s_out, s_in, s_mlp, s_cross = sums
    from_text = lax.ppermute(s_cross[:2], "tower", [(1, 0)])
    s_cross = jnp.where(is_enc, from_text, s_cross[2:])

    def turned(x):
        return jnp.swapaxes(x, 1, 2).astype(F32)

    cross_pair = jnp.stack(
        [
            s_cross[0].T,
            s_cross[1].T,
        ]
    ).astype(F32)
    total = total.reshape(2, lines_of * LANES)
    first = total[0]
    pieces = [first[i * width : (i + 1) * width] for i in range(8)]
    at = 8 * width
    parts = total[:, at:]
    qv_total = jnp.stack(
        [
            parts[:, :head_cols].reshape(-1),
            parts[:, head_cols : 2 * head_cols].reshape(-1),
        ]
    )
    in_total = parts[:, 2 * head_cols : 2 * head_cols + hidden].reshape(-1)
    return (
        tower_out[None],
        grad_in[None],
        turned(s_qkv)[None],
        s_out.astype(F32),
        turned(s_in),
        s_mlp.astype(F32),
        cross_pair[None],
        qv_total[None],
        pieces[0][None],
        in_total[None],
        pieces[1][None],
        jnp.stack(pieces[2:5])[None],
        jnp.stack(pieces[5:8])[None],
    )


def solution(mesh):
    return jax.shard_map(
        body,
        mesh=mesh,
        in_specs=(
            P("tower", ("dp", "mp"), None),
            P("tower", ("dp", "mp"), None),
            P("dp", None),
            P("dp"),
            P("tower", None, None, "mp"),
            P("tower", "mp", None),
            P("tower", None, "mp"),
            P("tower", "mp", None),
            P("tower", None, None, "mp"),
            P("tower", None, None),
            P("tower", None),
            P("tower", None),
            P("tower", None),
            P("tower", None, None),
            P("tower", None, None),
        ),
        out_specs=(
            P("tower", ("dp", "mp"), None),
            P("tower", ("dp", "mp"), None),
            P("tower", None, "dp", "mp"),
            P("tower", "mp", "dp"),
            P("tower", "dp", "mp"),
            P("tower", "mp", "dp"),
            P("tower", None, "dp", "mp"),
            P("tower", None, None),
            P("tower", None),
            P("tower", None),
            P("tower", None),
            P("tower", None, None),
            P("tower", None, None),
        ),
        check_vma=False,
    )
```

```python
import functools

import jax
import jax.numpy as jnp
from jax import lax
from jax.experimental import pallas as pl
from jax.experimental.pallas import tpu as pltpu
from jax.sharding import PartitionSpec as P

HDIM = 64
PATCH = 576
LTXT = 64
EPS = 1e-06
NEG = -1e30
LANES = 128
MESH = pl.DeviceIdType.MESH
F32 = jnp.float32
BF16 = jnp.bfloat16
VMEM_LIMIT = 60 * 1024 * 1024


def norm_parts(values):
    center = values - jnp.mean(values, axis=-1, keepdims=True)
    spread = jnp.mean(center * center, axis=-1, keepdims=True)
    scale = lax.rsqrt(spread + EPS)
    return (center * scale, scale)


def norm_rows(values, gain_vec, shift_vec):
    unit, _ = norm_parts(values)
    return unit * gain_vec + shift_vec


def norm_back(values, gain_vec, grad_normed):
    unit, scale = norm_parts(values)
    inner = grad_normed * gain_vec
    mean_one = jnp.mean(inner, axis=-1, keepdims=True)
    mean_two = jnp.mean(inner * unit, axis=-1, keepdims=True)
    back = (inner - mean_one - unit * mean_two) * scale
    return (back, jnp.sum(grad_normed * unit, axis=0), jnp.sum(grad_normed, axis=0))


def gelu_tanh(values):
    return jax.nn.gelu(values, approximate=True)


def dot_rows(left, right):
    return lax.dot_general(left, right, (((1,), (1,)), ((), ())), preferred_element_type=F32)


def dot_first(left, right):
    return lax.dot_general(left, right, (((0,), (0,)), ((), ())), preferred_element_type=F32)


def dot_plain(left, right):
    return lax.dot_general(left, right, (((1,), (0,)), ((), ())), preferred_element_type=F32)


def stack_heads(block, low_lanes):
    wide = block.astype(F32)
    return jnp.concatenate([jnp.where(low_lanes, wide, 0.0), jnp.where(low_lanes, 0.0, wide)], axis=0)


def merge_heads(pair, low_lanes):
    return jnp.where(low_lanes, pair[:LTXT], pair[LTXT:])


def low_half():
    return lax.broadcasted_iota(jnp.int32, (LTXT, LANES), 1) < HDIM


def causal_mask(seg_col, seg_row):
    key_at = lax.broadcasted_iota(jnp.int32, (LTXT, LANES), 0)
    query_at = lax.broadcasted_iota(jnp.int32, (LTXT, LANES), 1) % LTXT
    return jnp.logical_and(key_at <= query_at, seg_col == seg_row)


def key_block(mode, ref, r, picks):
    if mode == "image":
        return ref[...]
    if mode == "text":
        return ref[pl.ds(pl.multiple_of(r * LTXT, LTXT), LTXT), :]
    return ref[picks[r]]


def attend_kernel(mode, rows, scale, *refs):
    if mode == "cross":
        picks, q_ref, k_ref, v_ref, o_ref, l_ref = refs
    elif mode == "text":
        picks = None
        q_ref, k_ref, v_ref, segc_ref, segr_ref, o_ref, l_ref = refs
    else:
        picks = None
        q_ref, k_ref, v_ref, o_ref, l_ref = refs
    low = low_half()

    def step(r, carry):
        at = pl.ds(pl.multiple_of(r * LTXT, LTXT), LTXT)
        queries = (stack_heads(q_ref[at, :], low) * scale).astype(BF16)
        keys = key_block(mode, k_ref, r, picks)
        vals = key_block(mode, v_ref, r, picks)
        scores = dot_rows(keys, queries)
        if mode == "text":
            scores = jnp.where(causal_mask(segc_ref[at, :], segr_ref[pl.ds(r, 1), :]), scores, NEG)
        top = jnp.max(scores, axis=0, keepdims=True)
        grown = jnp.exp(scores - top)
        total = jnp.sum(grown, axis=0, keepdims=True)
        weights = (grown * (1.0 / total)).astype(BF16)
        mixed = dot_first(weights, vals)
        o_ref[at, :] = merge_heads(mixed, low).astype(BF16)
        l_ref[0, pl.ds(r, 1), :] = top + jnp.log(total)
        return carry

    lax.fori_loop(0, rows, step, 0, unroll=3)


def attend_back_kernel(mode, rows, scale, pairs, *refs):
    if mode == "cross":
        picks, q_ref, k_ref, v_ref, g_ref, l_ref, dq_ref, dk_ref, dv_ref, dk_acc, dv_acc = refs
    elif mode == "text":
        picks = None
        q_ref, k_ref, v_ref, g_ref, l_ref, segc_ref, segr_ref, d_ref, dk_acc, dv_acc = refs
    else:
        picks = None
        q_ref, k_ref, v_ref, g_ref, l_ref, d_ref, dk_acc, dv_acc = refs
    low = low_half()
    pair = pl.program_id(0)
    if mode != "text":
        dk_acc[...] = jnp.zeros_like(dk_acc)
        dv_acc[...] = jnp.zeros_like(dv_acc)

    def lanes(part):
        return pl.ds(pl.multiple_of((part * pairs + pair) * LANES, LANES), LANES)

    def step(r, carry):
        at = pl.ds(pl.multiple_of(r * LTXT, LTXT), LTXT)
        queries = (stack_heads(q_ref[at, :], low) * scale).astype(BF16)
        grads = stack_heads(g_ref[at, :], low).astype(BF16)
        keys = key_block(mode, k_ref, r, picks)
        vals = key_block(mode, v_ref, r, picks)
        scores = dot_rows(keys, queries)
        if mode == "text":
            scores = jnp.where(causal_mask(segc_ref[at, :], segr_ref[pl.ds(r, 1), :]), scores, NEG)
        weights = jnp.exp(scores - l_ref[0, pl.ds(r, 1), :])
        grad_w = dot_rows(vals, grads)
        row_dot = jnp.sum(weights * grad_w, axis=0, keepdims=True)
        grad_s = (weights * (grad_w - row_dot)).astype(BF16)
        grad_q = merge_heads(dot_first(grad_s, keys), low) * scale
        grad_k = dot_plain(grad_s, queries)
        grad_v = dot_plain(weights.astype(BF16), grads)
        if mode == "cross":
            dq_ref[at, :] = grad_q.astype(BF16)
            dk_acc[picks[r]] += grad_k
            dv_acc[picks[r]] += grad_v
        elif mode == "text":
            d_ref[at, lanes(0)] = grad_q.astype(BF16)
            d_ref[at, lanes(1)] = grad_k.astype(BF16)
            d_ref[at, lanes(2)] = grad_v.astype(BF16)
        else:
            d_ref[at, lanes(0)] = grad_q.astype(BF16)
            dk_acc[...] += grad_k
            dv_acc[...] += grad_v
        return carry

    lax.fori_loop(0, rows, step, 0)
    if mode == "cross":
        dk_ref[...] = dk_acc[...].astype(BF16)
        dv_ref[...] = dv_acc[...].astype(BF16)
    elif mode == "image":
        d_ref[:, lanes(1)] = dk_acc[...].astype(BF16)
        d_ref[:, lanes(2)] = dv_acc[...].astype(BF16)


def column(part, pairs, rows):
    return pl.BlockSpec((rows, LANES), lambda i, *_: (0, part * pairs + i))


def whole(shape):
    return pl.BlockSpec(shape, lambda i, *_: (0,) * len(shape))


def tops_spec():
    return pl.BlockSpec((1, 16, LANES), lambda i, *_: (i, 0, 0))


def self_cost(tokens, heads, products, mode):
    keys = PATCH if mode != "text" else LTXT
    return pl.CostEstimate(
        flops=2 * products * 2 * tokens * keys * HDIM * heads,
        bytes_accessed=8 * tokens * heads * HDIM,
        transcendentals=tokens * keys * heads,
    )


def kernel_params():
    return pltpu.CompilerParams(vmem_limit_bytes=VMEM_LIMIT)


def self_attend(mode, packed, seg_col, seg_row, scale):
    tokens = packed.shape[0]
    pairs = packed.shape[1] // (3 * LANES)
    rows = tokens // LTXT
    specs = [column(part, pairs, tokens) for part in range(3)]
    extra = ()
    if mode == "text":
        specs += [whole(seg_col.shape), whole(seg_row.shape)]
        extra = (seg_col, seg_row)
    return pl.pallas_call(
        functools.partial(attend_kernel, mode, rows, scale),
        grid=(pairs,),
        in_specs=specs,
        out_specs=[column(0, pairs, tokens), tops_spec()],
        out_shape=[
            jax.ShapeDtypeStruct((tokens, pairs * LANES), BF16),
            jax.ShapeDtypeStruct((pairs, 16, LANES), F32),
        ],
        compiler_params=kernel_params(),
        cost_estimate=self_cost(tokens, 2 * pairs, 2, mode),
        name="attend_" + mode,
    )(packed, packed, packed, *extra)


def self_attend_back(mode, packed, grads, tops, seg_col, seg_row, scale):
    tokens = packed.shape[0]
    pairs = packed.shape[1] // (3 * LANES)
    rows = tokens // LTXT
    specs = [column(part, pairs, tokens) for part in range(3)] + [column(0, pairs, tokens), tops_spec()]
    extra = ()
    if mode == "text":
        specs += [whole(seg_col.shape), whole(seg_row.shape)]
        extra = (seg_col, seg_row)
    return pl.pallas_call(
        functools.partial(attend_back_kernel, mode, rows, scale, pairs),
        grid=(pairs,),
        in_specs=specs,
        out_specs=whole(packed.shape),
        out_shape=jax.ShapeDtypeStruct(packed.shape, BF16),
        scratch_shapes=[pltpu.VMEM((tokens, LANES), F32), pltpu.VMEM((tokens, LANES), F32)],
        compiler_params=kernel_params(),
        cost_estimate=self_cost(tokens, 2 * pairs, 5, mode),
        name="attend_back_" + mode,
    )(packed, packed, packed, grads, tops, *extra)


def image_block(images, keys):
    return pl.BlockSpec((images, keys, LANES), lambda i, *_: (0, 0, i))


def cross_attend(queries, keys, vals, picks, scale):
    tokens, wide = queries.shape
    pairs = wide // LANES
    images, key_rows, _ = keys.shape
    grid = pltpu.PrefetchScalarGridSpec(
        num_scalar_prefetch=1,
        grid=(pairs,),
        in_specs=[column(0, pairs, tokens), image_block(images, key_rows), image_block(images, key_rows)],
        out_specs=[column(0, pairs, tokens), tops_spec()],
    )
    return pl.pallas_call(
        functools.partial(attend_kernel, "cross", tokens // LTXT, scale),
        grid_spec=grid,
        out_shape=[
            jax.ShapeDtypeStruct((tokens, wide), BF16),
            jax.ShapeDtypeStruct((pairs, 16, LANES), F32),
        ],
        compiler_params=kernel_params(),
        cost_estimate=self_cost(tokens, 2 * pairs, 2, "cross"),
        name="attend_cross",
    )(picks, queries, keys, vals)


def cross_attend_back(queries, keys, vals, grads, tops, picks, scale):
    tokens, wide = queries.shape
    pairs = wide // LANES
    images, key_rows, _ = keys.shape
    grid = pltpu.PrefetchScalarGridSpec(
        num_scalar_prefetch=1,
        grid=(pairs,),
        in_specs=[
            column(0, pairs, tokens),
            image_block(images, key_rows),
            image_block(images, key_rows),
            column(0, pairs, tokens),
            tops_spec(),
        ],
        out_specs=[column(0, pairs, tokens), image_block(images, key_rows), image_block(images, key_rows)],
        scratch_shapes=[pltpu.VMEM((images, key_rows, LANES), F32)] * 2,
    )
    return pl.pallas_call(
        functools.partial(attend_back_kernel, "cross", tokens // LTXT, scale, pairs),
        grid_spec=grid,
        out_shape=[
            jax.ShapeDtypeStruct((tokens, wide), BF16),
            jax.ShapeDtypeStruct(keys.shape, BF16),
            jax.ShapeDtypeStruct(keys.shape, BF16),
        ],
        compiler_params=kernel_params(),
        cost_estimate=self_cost(tokens, 2 * pairs, 5, "cross"),
        name="attend_back_cross",
    )(picks, queries, keys, vals, grads, tops)


def spots():
    tower = lax.axis_index("tower")
    dp = lax.axis_index("dp")
    z = lax.axis_index("mp")
    core = lax.rem(dp, 2)
    line = dp // 2
    return tower, dp, z, core, line, dp + 2 - 4 * line, dp + 1 - 2 * core


def greet(target):
    pl.semaphore_signal(pltpu.get_barrier_semaphore(), inc=1, device_id=target, device_id_type=MESH)


def weight_steps(pieces, srcs, outs, stages, sems):
    send_sem, recv_sem, local_sem, twin_send, twin_recv = sems
    tower, dp, z, core, line, other, partner = spots()
    place = z + core * (3 - 2 * z)
    ahead = z + 1 - 2 * core
    behind = z - 1 + 2 * core
    slot_of = (core, 1 - core)
    holder = place <= 1
    far_src = [p[0] for p in pieces if p[5]]

    def spot(piece, slot, half):
        which, first, start, size, _, _ = piece
        part = size // 2
        return outs[which].at[pl.ds(first, srcs[which].shape[0]), slot, pl.ds(start + half * part, part), :]

    def own(piece):
        which, first, start, size, _, far = piece
        part = size // 2
        if far:
            return spot(piece, lax.rem(z, 2), line)
        return srcs[which].at[:, pl.ds(start + line * part, part), :]

    def move(k, source, slot, half, kind, arrive, target):
        return pltpu.make_async_remote_copy(
            src_ref=source,
            dst_ref=spot(pieces[k], slot, half),
            send_sem=send_sem.at[k, kind],
            recv_sem=recv_sem.at[k, arrive],
            device_id=target,
            device_id_type=MESH,
        )

    def twin_copy():
        which = far_src[0]
        return pltpu.make_async_remote_copy(
            src_ref=srcs[which],
            dst_ref=outs[which].at[pl.ds(0, srcs[which].shape[0]), lax.rem(z, 2)],
            send_sem=twin_send,
            recv_sem=twin_recv,
            device_id={"tower": 1 - tower},
            device_id_type=MESH,
        )

    def local_in(i):
        return pltpu.make_async_copy(srcs[i], stages[i], local_sem.at[i, 0])

    def local_out(i):
        first = outs[i].shape[0] - srcs[i].shape[0]
        return pltpu.make_async_copy(
            stages[i], outs[i].at[pl.ds(first, srcs[i].shape[0]), lax.rem(z, 2)], local_sem.at[i, 1]
        )

    def gate(piece, cond):
        return cond if piece[4] is None else jnp.logical_and(cond, tower == piece[4])

    def send_own(k):
        piece = pieces[k]

        @pl.when(gate(piece, place == 0))
        def _():
            move(k, own(piece), slot_of[0], line, 0, 0, {"mp": ahead}).start()

        @pl.when(gate(piece, place == 1))
        def _():
            move(k, own(piece), slot_of[1], line, 1, 1, {"mp": ahead}).start()
            move(k, own(piece), slot_of[1], line, 2, 1, {"mp": behind}).start()

    def begin():
        if far_src:

            @pl.when(jnp.logical_and(holder, tower == 0))
            def _():
                twin_copy().start()

        for k, piece in enumerate(pieces):
            if not piece[5]:
                send_own(k)

    def begin_local():
        for i in range(len(srcs)):
            flag = next(p[4] for p in pieces if p[0] == i)
            keep = holder if flag is None else jnp.logical_and(holder, tower == flag)

            @pl.when(keep)
            def _(i=i):
                local_in(i).start()

        for i in range(len(srcs)):
            flag = next(p[4] for p in pieces if p[0] == i)
            keep = holder if flag is None else jnp.logical_and(holder, tower == flag)

            @pl.when(keep)
            def _(i=i):
                local_in(i).wait()
                local_out(i).start()

    def pass_on(k):
        piece = pieces[k]
        if piece[5]:

            @pl.when(jnp.logical_and(holder, tower == 1))
            def _():
                twin_copy().wait_recv()

            send_own(k)

        @pl.when(gate(piece, place >= 1))
        def _():
            here = spot(piece, slot_of[0], line)
            move(k, here, slot_of[0], line, 0, 0, {"mp": z}).wait_recv()
            move(k, here, slot_of[0], line, 3, 2, {"dp": other}).start()

        @pl.when(gate(piece, jnp.logical_and(place >= 1, place <= 2)))
        def _():
            here = spot(piece, slot_of[0], line)
            move(k, here, slot_of[0], line, 0, 0, {"mp": ahead}).start()

        @pl.when(gate(piece, place != 1))
        def _():
            here = spot(piece, slot_of[1], line)
            move(k, here, slot_of[1], line, 1, 1, {"mp": z}).wait_recv()
            move(k, here, slot_of[1], line, 4, 3, {"dp": other}).start()

        @pl.when(gate(piece, place == 2))
        def _():
            here = spot(piece, slot_of[1], line)
            move(k, here, slot_of[1], line, 1, 1, {"mp": ahead}).start()

    def arrived(k):
        piece = pieces[k]

        @pl.when(gate(piece, place >= 1))
        def _():
            move(k, spot(piece, slot_of[0], 1 - line), slot_of[0], 1 - line, 3, 2, {"dp": dp}).wait_recv()

        @pl.when(gate(piece, place != 1))
        def _():
            move(k, spot(piece, slot_of[1], 1 - line), slot_of[1], 1 - line, 4, 3, {"dp": dp}).wait_recv()

    def sent(k):
        piece = pieces[k]

        @pl.when(gate(piece, place <= 2))
        def _():
            move(k, spot(piece, slot_of[0], line), slot_of[0], line, 0, 0, {"mp": z}).wait_send()

        @pl.when(gate(piece, jnp.logical_and(place >= 1, place <= 2)))
        def _():
            move(k, spot(piece, slot_of[1], line), slot_of[1], line, 1, 1, {"mp": z}).wait_send()

        @pl.when(gate(piece, place == 1))
        def _():
            move(k, spot(piece, slot_of[1], line), slot_of[1], line, 2, 1, {"mp": z}).wait_send()

        @pl.when(gate(piece, place >= 1))
        def _():
            move(k, spot(piece, slot_of[0], line), slot_of[0], line, 3, 2, {"dp": dp}).wait_send()

        @pl.when(gate(piece, place != 1))
        def _():
            move(k, spot(piece, slot_of[1], line), slot_of[1], line, 4, 3, {"dp": dp}).wait_send()

    def end_local():
        for i in range(len(srcs)):
            flag = next(p[4] for p in pieces if p[0] == i)
            keep = holder if flag is None else jnp.logical_and(holder, tower == flag)

            @pl.when(keep)
            def _(i=i):
                local_out(i).wait()

        if far_src:

            @pl.when(jnp.logical_and(holder, tower == 0))
            def _():
                twin_copy().wait_send()

    return begin, begin_local, pass_on, arrived, sent, end_local


def token_steps(blocks, outs, stage, sems):
    send_sem, recv_sem, local_sem = sems
    tower, dp, z, core, line, other, partner = spots()
    stays = z == 3 * core
    size = blocks[0].shape[0]

    def rows(which_core):
        return pl.ds(pl.multiple_of(which_core * size, 16), size)

    def away(i):
        target = {"dp": 2 * line + lax.rem(z, 2), "mp": 2 * core + z // 2}
        return pltpu.make_async_remote_copy(
            src_ref=blocks[i],
            dst_ref=outs[i].at[rows(lax.rem(z, 2)), :],
            send_sem=send_sem.at[i, 0],
            recv_sem=recv_sem.at[i, 0],
            device_id=target,
            device_id_type=MESH,
        )

    def across(i, which_core):
        return pltpu.make_async_remote_copy(
            src_ref=outs[i].at[rows(which_core), :],
            dst_ref=outs[i].at[rows(which_core), :],
            send_sem=send_sem.at[i, 1],
            recv_sem=recv_sem.at[i, 1],
            device_id={"dp": partner},
            device_id_type=MESH,
        )

    def begin(i):
        @pl.when(jnp.logical_not(stays))
        def _():
            away(i).start()

        @pl.when(stays)
        def _():
            first = pltpu.make_async_copy(blocks[i], stage.at[i], local_sem.at[i, 0])
            first.start()
            first.wait()
            second = pltpu.make_async_copy(stage.at[i], outs[i].at[rows(core), :], local_sem.at[i, 1])
            second.start()
            second.wait()
            across(i, core).start()

    def relay(i):
        @pl.when(jnp.logical_not(stays))
        def _():
            away(i).wait_recv()
            across(i, core).start()

    def finish(i):
        across(i, 1 - core).wait_recv()
        across(i, core).wait_send()

        @pl.when(jnp.logical_not(stays))
        def _():
            away(i).wait_send()

    return begin, relay, finish


def gather_kernel(pieces, n_src, *refs):
    it = iter(refs)
    srcs = [next(it) for _ in range(n_src)]
    blocks = [next(it) for _ in range(2)]
    notes = next(it)
    outs = [next(it) for _ in range(n_src)]
    tokens = [next(it) for _ in range(2)]
    notes_out = next(it)
    stages = [next(it) for _ in range(n_src)]
    weight_sems = [next(it) for _ in range(5)]
    token_stage = next(it)
    token_sems = [next(it) for _ in range(3)]
    note_sem = next(it)
    tower, dp, z, core, line, other, partner = spots()
    stays = z == 3 * core

    @pl.when(z > 0)
    def _():
        greet({"mp": z - 1})

    @pl.when(z < 3)
    def _():
        greet({"mp": z + 1})

    greet({"dp": other})
    greet({"tower": 1 - tower})
    greet({"dp": partner})

    @pl.when(jnp.logical_not(stays))
    def _():
        greet({"dp": 2 * line + lax.rem(z, 2), "mp": 2 * core + z // 2})
        greet({"dp": 2 * line + z // 2, "mp": 2 * lax.rem(z, 2) + core})

    at_end = jnp.logical_or(z == 0, z == 3)

    @pl.when(stays)
    def _():
        pl.semaphore_wait(pltpu.get_barrier_semaphore(), 4)

    @pl.when(jnp.logical_and(at_end, jnp.logical_not(stays)))
    def _():
        pl.semaphore_wait(pltpu.get_barrier_semaphore(), 6)

    @pl.when(jnp.logical_not(at_end))
    def _():
        pl.semaphore_wait(pltpu.get_barrier_semaphore(), 7)

    begin, begin_local, pass_on, arrived, sent, end_local = weight_steps(pieces, srcs, outs, stages, weight_sems)
    token_begin, token_relay, token_finish = token_steps(blocks, tokens, token_stage, token_sems)
    note_copy = pltpu.make_async_remote_copy(
        src_ref=notes,
        dst_ref=notes_out,
        send_sem=note_sem.at[0],
        recv_sem=note_sem.at[1],
        device_id={"dp": partner},
        device_id_type=MESH,
    )
    note_copy.start()
    token_begin(0)
    begin()
    token_begin(1)
    begin_local()
    token_relay(0)
    for k in range(len(pieces)):
        pass_on(k)
        if k == 1:
            token_relay(1)
    for k in range(len(pieces)):
        arrived(k)
        sent(k)
    end_local()
    token_finish(0)
    token_finish(1)
    note_copy.wait()


def later_kernel(pieces, n_src, only, *refs):
    srcs = refs[:n_src]
    outs = refs[2 * n_src : 3 * n_src]
    stages = refs[3 * n_src : 4 * n_src]
    weight_sems = refs[4 * n_src :]

    @pl.when(lax.axis_index("tower") == only)
    def _():
        tower, dp, z, core, line, other, partner = spots()

        @pl.when(z > 0)
        def _():
            greet({"mp": z - 1})

        @pl.when(z < 3)
        def _():
            greet({"mp": z + 1})

        greet({"dp": other})

        @pl.when(jnp.logical_or(z == 0, z == 3))
        def _():
            pl.semaphore_wait(pltpu.get_barrier_semaphore(), 2)

        @pl.when(jnp.logical_and(z > 0, z < 3))
        def _():
            pl.semaphore_wait(pltpu.get_barrier_semaphore(), 3)

        begin, begin_local, pass_on, arrived, sent, end_local = weight_steps(
            pieces, srcs, outs, stages, weight_sems
        )
        begin()
        begin_local()
        for k in range(len(pieces)):
            pass_on(k)
        for k in range(len(pieces)):
            arrived(k)
            sent(k)
        end_local()


def weight_scratch(n, shards):
    return [pltpu.VMEM(s.shape, BF16) for s in shards] + [
        pltpu.SemaphoreType.DMA((n, 5)),
        pltpu.SemaphoreType.DMA((n, 4)),
        pltpu.SemaphoreType.DMA((len(shards), 2)),
        pltpu.SemaphoreType.DMA,
        pltpu.SemaphoreType.DMA,
    ]


def row_cuts(i, shard, flag):
    rows = shard.shape[1]
    cut = rows if rows <= 192 else rows // 2
    return [(i, 0, at, cut, flag, False) for at in range(0, rows, cut)]


def gather_weights(shards, blocks, notes):
    qkv, out, cross, ffn_in, ffn_out = shards
    n_src = len(shards)
    pieces = row_cuts(0, qkv, None) + row_cuts(1, out, None)
    pieces += [(2, cross.shape[0], 0, cross.shape[1], 1, False), (2, 0, 0, cross.shape[1], 1, True)]
    pieces += row_cuts(3, ffn_in, 0) + row_cuts(4, ffn_out, 0)
    outs = [
        jax.ShapeDtypeStruct(((2 if i == 2 else 1) * s.shape[0], 2) + s.shape[1:], BF16) for i, s in enumerate(shards)
    ]
    outs += [jax.ShapeDtypeStruct((2 * b.shape[0], b.shape[1]), b.dtype) for b in blocks]
    outs += [jax.ShapeDtypeStruct(notes.shape, notes.dtype)]
    any_spec = pl.BlockSpec(memory_space=pltpu.HBM)
    return pl.pallas_call(
        functools.partial(gather_kernel, tuple(pieces), n_src),
        in_specs=[any_spec] * (n_src + 3),
        out_specs=[any_spec] * (n_src + 3),
        out_shape=outs,
        scratch_shapes=weight_scratch(len(pieces), shards)
        + [
            pltpu.VMEM((2,) + blocks[0].shape, BF16),
            pltpu.SemaphoreType.DMA((2, 2)),
            pltpu.SemaphoreType.DMA((2, 2)),
            pltpu.SemaphoreType.DMA((2, 2)),
            pltpu.SemaphoreType.DMA((2,)),
        ],
        compiler_params=pltpu.CompilerParams(
            collective_id=0, has_side_effects=True, vmem_limit_bytes=VMEM_LIMIT
        ),
        name="gather_weights",
    )(*shards, *blocks, notes)


def gather_later(shards, filled):
    n_src = len(shards)
    pieces = []
    for i, s in enumerate(shards):
        pieces += row_cuts(i, s, None)
    any_spec = pl.BlockSpec(memory_space=pltpu.HBM)
    return pl.pallas_call(
        functools.partial(later_kernel, tuple(pieces), n_src, 1),
        in_specs=[any_spec] * (2 * n_src),
        out_specs=[any_spec] * n_src,
        out_shape=[jax.ShapeDtypeStruct(f.shape, f.dtype) for f in filled],
        input_output_aliases={n_src + i: i for i in range(n_src)},
        scratch_shapes=weight_scratch(len(pieces), shards),
        compiler_params=pltpu.CompilerParams(
            collective_id=3, has_side_effects=True, vmem_limit_bytes=VMEM_LIMIT
        ),
        name="gather_later",
    )(*shards, *filled)


TILE = 32
WINDOW = 2


def reduce_kernel(pieces, flags, n_src, with_smalls, only, *refs):
    if only is None:
        reduce_steps(pieces, flags, n_src, with_smalls, refs)
    else:

        @pl.when(lax.axis_index("tower") == only)
        def _():
            reduce_steps(pieces, flags, n_src, with_smalls, refs)


def reduce_steps(pieces, flags, n_src, with_smalls, refs):
    it = iter(refs)
    srcs = [next(it) for _ in range(n_src)]
    small_in = next(it) if with_smalls else None
    outs = [next(it) for _ in range(n_src)]
    small_out = next(it) if with_smalls else None
    mine = [next(it) for _ in range(n_src)]
    near = [next(it) for _ in range(n_src)]
    far = [next(it) for _ in range(n_src)]
    if with_smalls:
        small_near, small_all = next(it), next(it)
        small_sem = next(it)
    local_sem, y_send, y_recv, z_send, z_recv, c_send, c_recv = it
    tower = lax.axis_index("tower")
    dp = lax.axis_index("dp")
    z = lax.axis_index("mp")
    core = lax.rem(dp, 2)
    line = dp // 2
    other = dp + 2 - 4 * line
    partner = dp + 1 - 2 * core
    holder = z // 2 == core
    slot = lax.rem(z, 2)
    half = srcs[0].shape[3] // 2

    barrier = pltpu.get_barrier_semaphore()
    pl.semaphore_signal(barrier, inc=1, device_id={"dp": other}, device_id_type=MESH)
    pl.semaphore_signal(barrier, inc=1, device_id={"dp": partner}, device_id_type=MESH)
    for away in range(1, 4):
        pl.semaphore_signal(barrier, inc=1, device_id={"mp": lax.rem(z + away, 4)}, device_id_type=MESH)
    pl.semaphore_wait(barrier, 5)

    def guarded(k, run, cond=None):
        flag = flags[pieces[k][0]]
        if flag is not None:
            here = tower == flag
            cond = here if cond is None else jnp.logical_and(cond, here)
        if cond is None:
            run()
        else:
            pl.when(cond)(run)

    def cut(k):
        _, first, count, start, size = pieces[k]
        return (pl.ds(first, count), pl.ds(start, size))

    def to_line(k):
        which = pieces[k][0]
        span, rows = cut(k)
        return pltpu.make_async_remote_copy(
            src_ref=srcs[which].at[span, :, rows, pl.ds(pl.multiple_of((1 - line) * half, LANES), half)],
            dst_ref=near[which].at[span, :, rows, :],
            send_sem=y_send.at[k],
            recv_sem=y_recv.at[k],
            device_id={"dp": other},
            device_id_type=MESH,
        )

    def to_mine(k):
        which = pieces[k][0]
        span, rows = cut(k)
        return pltpu.make_async_copy(
            srcs[which].at[span, :, rows, pl.ds(pl.multiple_of(line * half, LANES), half)],
            mine[which].at[span, :, rows, :],
            local_sem.at[k],
        )

    def to_chip(k, shard, seat):
        which = pieces[k][0]
        span, rows = cut(k)
        return pltpu.make_async_remote_copy(
            src_ref=mine[which].at[span, shard, rows, :],
            dst_ref=far[which].at[seat, span, rows, :],
            send_sem=z_send.at[k, shard],
            recv_sem=z_recv.at[k, seat],
            device_id={"mp": 2 * core + shard},
            device_id_type=MESH,
        )

    def to_core(k):
        which = pieces[k][0]
        span, rows = cut(k)
        return pltpu.make_async_remote_copy(
            src_ref=outs[which].at[span, rows, :],
            dst_ref=outs[which].at[span, rows, :],
            send_sem=c_send.at[k],
            recv_sem=c_recv.at[k],
            device_id={"dp": partner},
            device_id_type=MESH,
        )

    def seat_of(shard):
        return lax.rem(z - (2 * core + shard) + 4, 4) - 1

    towers = [0, 1] if any(f is not None for f in flags) else [None]
    lists = []
    for t in towers:
        lists.append([k for k in range(len(pieces)) if t is None or flags[pieces[k][0]] in (None, t)])

    def start_line(t, place):
        chosen = lists[towers.index(t)]
        if place >= len(chosen):
            return
        k = chosen[place]

        def run():
            to_line(k).start()

        if t is None:
            run()
        else:
            pl.when(tower == t)(run)

    for t in towers:
        for place in range(WINDOW):
            start_line(t, place)
    for k in range(len(pieces)):
        guarded(k, lambda k=k: to_mine(k).start())

    if with_smalls:
        small_line = pltpu.make_async_remote_copy(
            src_ref=small_in,
            dst_ref=small_near,
            send_sem=small_sem.at[0],
            recv_sem=small_sem.at[1],
            device_id={"dp": other},
            device_id_type=MESH,
        )
        small_line.start()

        def small_pair(sender, away):
            return pltpu.make_async_remote_copy(
                src_ref=small_all.at[sender],
                dst_ref=small_all.at[sender],
                send_sem=small_sem.at[1 + away],
                recv_sem=small_sem.at[4 + away],
                device_id={"mp": lax.rem(z + away, 4)},
                device_id_type=MESH,
            )

        def small_move(away):
            return small_pair(z, away)

        def small_got(away):
            return small_pair(lax.rem(z + 4 - away, 4), away)

        def small_core(which):
            return pltpu.make_async_remote_copy(
                src_ref=small_out.at[which],
                dst_ref=small_out.at[which],
                send_sem=small_sem.at[8],
                recv_sem=small_sem.at[9],
                device_id={"dp": partner},
                device_id_type=MESH,
            )

        small_line.wait()
        small_all[z] = small_in[...] + small_near[...]

    for k, piece in enumerate(pieces):
        which, first, count, start, size = piece

        def add_near(k=k, which=which, first=first, count=count, start=start, size=size):
            to_mine(k).wait()
            to_line(k).wait_recv()
            to_line(k).wait_send()
            for t, chosen in zip(towers, lists):
                if k in chosen:
                    start_line(t, chosen.index(k) + WINDOW)

            @pl.loop(0, size // TILE)
            def _(i):
                rows = pl.ds(pl.multiple_of(start + i * TILE, TILE), TILE)
                for a in range(first, first + count):
                    for b in range(2):
                        total = mine[which][a, b, rows, :].astype(F32) + near[which][a, b, rows, :].astype(F32)
                        mine[which][a, b, rows, :] = total.astype(BF16)

            for shard in range(2):

                @pl.when(z != 2 * core + shard)
                def _(shard=shard):
                    to_chip(k, shard, seat_of(shard)).start()

        guarded(k, add_near)
        if with_smalls and k == 0:
            for away in range(1, 4):
                small_move(away).start()

    for k, piece in enumerate(pieces):
        which, first, count, start, size = piece

        def add_far(k=k, which=which, first=first, count=count, start=start, size=size):
            for seat in range(3):
                to_chip(k, 0, seat).wait_recv()

            @pl.loop(0, size // TILE)
            def _(i):
                rows = pl.ds(pl.multiple_of(start + i * TILE, TILE), TILE)
                for a in range(first, first + count):
                    total = mine[which][a, slot, rows, :].astype(F32)
                    for seat in range(3):
                        total = total + far[which][seat, a, rows, :].astype(F32)
                    outs[which][a, rows, :] = total.astype(BF16)

            to_core(k).start()

        guarded(k, add_far, holder)

    if with_smalls:
        for away in range(1, 4):
            small_got(away).wait_recv()
        small_out[core] = ((small_all[0] + small_all[1]) + small_all[2]) + small_all[3]
        small_core(core).start()

    for k, piece in enumerate(pieces):

        def ended(k=k):
            for shard in range(2):

                @pl.when(z != 2 * core + shard)
                def _(shard=shard):
                    to_chip(k, shard, 0).wait_send()

            @pl.when(holder)
            def _():
                to_core(k).wait_send()

            @pl.when(jnp.logical_not(holder))
            def _():
                to_core(k).wait_recv()

        guarded(k, ended)

    if with_smalls:
        for away in range(1, 4):
            small_move(away).wait_send()
        small_core(core).wait_send()
        small_core(1 - core).wait_recv()


def reduce_grads(grads, flags, smalls, only, collective_id):
    n_src = len(grads)
    pieces = []
    for i, g in enumerate(grads):
        rows = g.shape[2]
        cut = rows if rows <= 192 else rows // 4
        pieces += [
            (i, first, 1, at, cut) for first in range(g.shape[0]) for at in range(0, rows, cut)
        ]
    n = len(pieces)
    half = grads[0].shape[3] // 2
    any_spec = pl.BlockSpec(memory_space=pl.ANY)
    vmem_spec = pl.BlockSpec(memory_space=pltpu.VMEM)
    in_specs = [any_spec] * n_src
    out_shape = [jax.ShapeDtypeStruct((g.shape[0], g.shape[2], half), BF16) for g in grads]
    out_specs = [vmem_spec] * n_src
    args = list(grads)
    with_smalls = smalls is not None
    scratch = (
        [pltpu.VMEM(g.shape[:3] + (half,), BF16) for g in grads] * 2
        + [pltpu.VMEM((3, g.shape[0], g.shape[2], half), BF16) for g in grads]
    )
    if with_smalls:
        in_specs.append(vmem_spec)
        out_specs.append(vmem_spec)
        out_shape.append(jax.ShapeDtypeStruct((2,) + smalls.shape, F32))
        args.append(smalls)
        scratch += [
            pltpu.VMEM(smalls.shape, F32),
            pltpu.VMEM((4,) + smalls.shape, F32),
            pltpu.SemaphoreType.DMA((10,)),
        ]
    scratch += [
        pltpu.SemaphoreType.DMA((n,)),
        pltpu.SemaphoreType.DMA((n,)),
        pltpu.SemaphoreType.DMA((n,)),
        pltpu.SemaphoreType.DMA((n, 2)),
        pltpu.SemaphoreType.DMA((n, 3)),
        pltpu.SemaphoreType.DMA((n,)),
        pltpu.SemaphoreType.DMA((n,)),
    ]
    return pl.pallas_call(
        functools.partial(reduce_kernel, tuple(pieces), tuple(flags), n_src, with_smalls, only),
        in_specs=in_specs,
        out_specs=out_specs,
        out_shape=out_shape,
        scratch_shapes=scratch,
        compiler_params=pltpu.CompilerParams(
            collective_id=collective_id, has_side_effects=True, vmem_limit_bytes=VMEM_LIMIT
        ),
        name="reduce_grads_%d" % collective_id,
    )(*args)


def gather_plain(shards):
    core = lax.rem(lax.axis_index("dp"), 2)
    outs = []
    for i, s in enumerate(shards):
        if i == 2:
            s = jnp.concatenate([lax.ppermute(s, "tower", [(0, 1)]), s], axis=0)
        full = lax.all_gather(s, "mp", axis=1, tiled=False)
        outs.append(lax.dynamic_slice_in_dim(full, 2 * core, 2, 1))
    return outs


def reduce_plain(grads, smalls):
    dp = lax.axis_index("dp")
    core = lax.rem(dp, 2)
    outs = []
    for g in grads:
        n, _, rows, wide = g.shape
        full = jnp.zeros((n, 4, rows, wide), BF16)
        full = lax.dynamic_update_slice(full, g, (0, 2 * core, 0, 0))
        part = lax.psum_scatter(full, "mp", scatter_dimension=1, tiled=False)
        part = lax.psum_scatter(part, "dp", scatter_dimension=2, tiled=True)
        outs.append(part)
    if smalls is None:
        return outs
    both = jnp.zeros((2,) + smalls.shape, F32)
    both = lax.dynamic_update_slice(both, smalls[None], (core, 0, 0))
    return outs + [lax.psum(both, ("dp", "mp"))]


def body(
    tower_in,
    out_cot,
    segment_ids,
    row_image,
    attn_qkv,
    attn_out,
    mlp_in,
    mlp_out,
    cross_proj,
    qv_bias,
    out_bias,
    mlp_bias_in,
    mlp_bias_out,
    norm_gain,
    norm_bias,
):
    lines = lax.axis_size("dp") // 2
    depth = lax.axis_size("mp")
    devices = lax.axis_size("dp")
    is_enc = lax.axis_index("tower") == 0
    dp = lax.axis_index("dp")
    z = lax.axis_index("mp")
    core = lax.rem(dp, 2)
    side = lax.rem(z, 2)
    group = z // 2
    direct = lines == 2
    assert depth == 4
    quarter = tower_in.shape[1]
    tokens = 2 * quarter
    assert tokens == PATCH
    width = tower_in.shape[2]
    head_cols = 2 * attn_qkv.shape[3]
    hidden = 2 * mlp_in.shape[2]
    scale_qk = HDIM ** (-0.5)

    out_moves, back_moves = [], []
    for d in range(devices):
        for place in range(depth):
            here = d * depth + place
            there = (d - d % 2 + place % 2) * depth + 2 * (d % 2) + place // 2
            out_moves.append((here, there))
            back_moves.append((there, here))

    def swap_cores(x):
        return lax.ppermute(x, "dp", [(i, i ^ 1) for i in range(devices)])

    def both_cores(own):
        other = swap_cores(own)
        return jnp.where(core == 0, jnp.concatenate([own, other], -2), jnp.concatenate([other, own], -2))

    def own_rows(full):
        return lax.dynamic_slice_in_dim(full, core * quarter, quarter, full.ndim - 2)

    def lowered(part):
        return lax.reduce_precision(part, 8, 7).astype(BF16)

    def add_lowered(low):
        return low.astype(F32) + swap_cores(low).astype(F32)

    def add_cores(part):
        return add_lowered(lowered(part))

    def only_image(run, *operands):
        def idle(*inputs):
            return jax.tree.map(lambda x: jnp.zeros(x.shape, x.dtype), jax.eval_shape(run, *inputs))

        return lax.cond(is_enc, run, idle, *operands)

    shards = [
        jnp.swapaxes(attn_qkv[0], 1, 2),
        attn_out,
        jnp.swapaxes(cross_proj[0], 1, 2),
        mlp_in,
        mlp_out,
    ]
    notes = jnp.concatenate([segment_ids, row_image[:, None]], axis=1)
    if direct:
        *gathered, stream_low, cot_low, other_notes = gather_weights(shards, [tower_in[0], out_cot[0]], notes)
    else:
        gathered = gather_plain(shards)
        stream_low = both_cores(lax.ppermute(tower_in[0], ("dp", "mp"), out_moves))
        cot_low = both_cores(lax.ppermute(out_cot[0], ("dp", "mp"), out_moves))
        other_notes = swap_cores(notes)
    w_qkv = gathered[0].reshape(3 * head_cols, width)
    w_out = gathered[1].reshape(head_cols, width)
    w_cross = gathered[2].reshape(4, head_cols, width)
    bias_qv = lax.dynamic_slice_in_dim(qv_bias[0], core * head_cols, head_cols, 1)
    bias_packed = jnp.concatenate([bias_qv[0], jnp.zeros_like(bias_qv[0]), bias_qv[1]])
    bias_in = lax.dynamic_slice_in_dim(mlp_bias_in[0], core * hidden, hidden, 0)
    gains = norm_gain[0]
    shifts = norm_bias[0]
    stream = stream_low.astype(F32)
    rows = segment_ids.shape[0] // 2
    chosen = jnp.where(core == group, notes, other_notes)
    chosen = lax.dynamic_slice_in_dim(chosen, rows * side, rows, 0)
    segs = chosen[:, :LTXT]
    picks = chosen[:, LTXT]
    seg_row = jnp.pad(jnp.concatenate([segs, segs], axis=1), ((0, 16 - rows), (0, 0)))
    seg_col = jnp.broadcast_to(segs.reshape(rows * LTXT, 1), (rows * LTXT, LANES))

    act_one = norm_rows(stream, gains[0], shifts[0]).astype(BF16)
    packed = (dot_rows(act_one, w_qkv) + bias_packed).astype(BF16)
    mixed, tops = lax.cond(
        is_enc,
        lambda p: tuple(self_attend("image", p, seg_col, seg_row, scale_qk)),
        lambda p: tuple(self_attend("text", p, seg_col, seg_row, scale_qk)),
        packed,
    )
    stream_one = stream + add_cores(dot_plain(mixed, w_out)) + out_bias[0]

    filled = gathered[3:]
    if direct:
        *filled, stream_one = lax.optimization_barrier((*filled, stream_one))
        filled = gather_later(shards[3:], filled)
    w_in = filled[0][0]
    w_mlp = filled[1].reshape(hidden, width)

    def feed_forward(values):
        act = norm_rows(values, gains[1], shifts[1]).astype(BF16)
        pre = jnp.concatenate([dot_plain(act, w_in[0]), dot_plain(act, w_in[1])], axis=1) + bias_in
        hid = gelu_tanh(pre).astype(BF16)
        return (act, pre, hid, lowered(dot_plain(hid, w_mlp)))

    act_enc, pre_enc, hid_enc, part_enc = only_image(feed_forward, stream_one)
    out_enc = stream_one + add_lowered(part_enc) + mlp_bias_out[0]
    base_three = jnp.where(is_enc, out_enc, stream_one)
    act_three = norm_rows(base_three, gains[2], shifts[2]).astype(BF16)

    near_half = lax.ppermute(own_rows(act_three), "tower", [(0, 1)])
    far_half = lax.ppermute(near_half, "mp", [(i, i ^ 1) for i in range(depth)])
    halves = jnp.where(side == 0, jnp.stack([near_half, far_half]), jnp.stack([far_half, near_half]))
    images = both_cores(halves)

    cross_q = dot_rows(act_three, w_cross[2]).astype(BF16)
    flat_images = images.reshape(2 * tokens, width)
    cross_k = dot_rows(flat_images, w_cross[0]).astype(BF16).reshape(2, tokens, head_cols)
    cross_v = dot_rows(flat_images, w_cross[1]).astype(BF16).reshape(2, tokens, head_cols)
    cross_mix, cross_tops = cross_attend(cross_q, cross_k, cross_v, picks, scale_qk)
    stream_two = stream_one + add_cores(dot_plain(cross_mix, w_cross[3]))

    act_dec, pre_dec, hid_dec, part_dec = feed_forward(stream_two)
    out_dec = stream_two + add_lowered(part_dec) + mlp_bias_out[0]
    tower_out = own_rows(jnp.where(is_enc, out_enc, out_dec).astype(BF16))
    tower_out = lax.ppermute(tower_out, ("dp", "mp"), back_moves)

    def feed_back(grad_low, pre):
        grad_hid = dot_rows(grad_low, w_mlp)
        _, pullback = jax.vjp(gelu_tanh, pre)
        grad_pre = pullback(grad_hid)[0].astype(BF16)
        cols = hidden // 2
        part = dot_rows(grad_pre[:, :cols], w_in[0]) + dot_rows(grad_pre[:, cols:], w_in[1])
        return (grad_pre, lowered(part))

    def feed_grads(grad_low, act, grad_pre, hid):
        g_in = dot_first(grad_pre, act).astype(BF16)
        g_mlp = dot_first(hid, grad_low).astype(BF16)
        return (
            g_in.reshape(1, 2, hidden // 2, width),
            g_mlp.reshape(1, 2, hidden // 2, width),
        )

    cot = cot_low.astype(F32)
    grad_pre_dec, back_in = feed_back(cot_low, pre_dec)
    back_a, gain_a, shift_a = norm_back(stream_two, gains[1], add_lowered(back_in))
    grad_two = cot + back_a
    grad_two_low = grad_two.astype(BF16)

    grad_mix = dot_rows(grad_two_low, w_cross[3]).astype(BF16)
    grad_q, grad_k, grad_v = cross_attend_back(
        cross_q, cross_k, cross_v, grad_mix, cross_tops, picks, scale_qk
    )
    flat_k = grad_k.reshape(2 * tokens, head_cols)
    flat_v = grad_v.reshape(2 * tokens, head_cols)
    part_images = dot_plain(flat_k, w_cross[0]) + dot_plain(flat_v, w_cross[1])
    part_low = part_images.astype(BF16).reshape(2, 2, quarter, width)
    give = lax.dynamic_index_in_dim(part_low, 1 - core, 1, keepdims=False)
    keep = lax.dynamic_index_in_dim(part_low, core, 1, keepdims=False)
    pair_sum = (keep.astype(F32) + swap_cores(give).astype(F32)).astype(BF16)
    give = lax.dynamic_index_in_dim(pair_sum, 1 - side, 0, keepdims=False)
    keep = lax.dynamic_index_in_dim(pair_sum, side, 0, keepdims=False)
    got = lax.ppermute(give, "mp", [(i, i ^ 1) for i in range(depth)])
    image_sum = (keep.astype(F32) + got.astype(F32)).astype(BF16)
    image_half = lax.ppermute(image_sum, "tower", [(1, 0)])
    later = lax.optimization_barrier(
        (cot_low, act_dec, grad_pre_dec, hid_dec, flat_k, flat_v, grad_q, cross_mix, image_sum)
    )
    g_in_dec, g_mlp_dec = feed_grads(later[0], later[1], later[2], later[3])
    g_cross = jnp.concatenate(
        [
            dot_first(later[4], flat_images).astype(BF16),
            dot_first(later[5], flat_images).astype(BF16),
            dot_first(later[6], act_three).astype(BF16),
            dot_first(later[7], grad_two_low).astype(BF16),
        ],
        axis=0,
    ).reshape(4, 2, head_cols // 2, width)
    text_grads = [g_in_dec, g_mlp_dec, g_cross]
    if direct:
        *text_grads, image_half = lax.optimization_barrier((*text_grads, image_half))
        text_sums = reduce_grads(text_grads, [None] * 3, None, 1, 1)
        image_half, *text_sums = lax.optimization_barrier((image_half, *text_sums))
    else:
        text_sums = reduce_plain(text_grads, None)
    image_back = both_cores(image_half).astype(F32)
    query_back = add_cores(dot_plain(grad_q, w_cross[2]))

    back_three, gain_three, shift_three = norm_back(
        base_three, gains[2], jnp.where(is_enc, image_back, query_back)
    )
    grad_enc = cot + back_three
    grad_enc_low = grad_enc.astype(BF16)

    def image_back_run(grad_low, pre, act, hid):
        grad_pre, part = feed_back(grad_low, pre)
        return (grad_pre, part) + feed_grads(grad_low, act, grad_pre, hid)

    grad_pre_enc, back_in, g_in, g_mlp = only_image(image_back_run, grad_enc_low, pre_enc, act_enc, hid_enc)
    back_b, gain_b, shift_b = norm_back(stream_one, gains[1], add_lowered(back_in))
    grad_one = jnp.where(is_enc, grad_enc + back_b, grad_two + back_three)
    grad_one_low = grad_one.astype(BF16)

    feed_low = jnp.where(is_enc, grad_enc_low, cot_low)
    feed_pre = jnp.where(is_enc, grad_pre_enc, grad_pre_dec)

    g_out = dot_first(mixed, grad_one_low).astype(BF16).reshape(1, 2, head_cols // 2, width)
    grad_mixed = dot_rows(grad_one_low, w_out).astype(BF16)
    grad_packed = lax.cond(
        is_enc,
        lambda p, g, t: self_attend_back("image", p, g, t, seg_col, seg_row, scale_qk),
        lambda p, g, t: self_attend_back("text", p, g, t, seg_col, seg_row, scale_qk),
        packed,
        grad_mixed,
        tops,
    )
    g_qkv = dot_first(grad_packed, act_one).astype(BF16).reshape(3, 2, head_cols // 2, width)
    back_in = add_cores(dot_plain(grad_packed, w_qkv))
    back_one, gain_one, shift_one = norm_back(stream, gains[0], back_in)
    grad_in = own_rows((grad_one + back_one).astype(BF16))
    grad_in = lax.ppermute(grad_in, ("dp", "mp"), back_moves)

    packed_sum = jnp.sum(grad_packed, axis=0, dtype=F32)
    shared = [
        jnp.sum(grad_one_low, axis=0, dtype=F32),
        jnp.sum(feed_low, axis=0, dtype=F32),
        gain_one,
        jnp.where(is_enc, gain_b, gain_a),
        gain_three,
        shift_one,
        jnp.where(is_enc, shift_b, shift_a),
        shift_three,
    ]
    by_core = [
        packed_sum[:head_cols],
        packed_sum[2 * head_cols :],
        jnp.sum(feed_pre, axis=0, dtype=F32),
    ]
    smalls = jnp.concatenate(shared + by_core)
    used = smalls.shape[0]
    lines_of = -(-used // (8 * LANES)) * 8
    smalls = jnp.pad(smalls, (0, lines_of * LANES - used)).reshape(lines_of, LANES)

    grads = [g_in, g_mlp, g_out, g_qkv]
    if direct:
        *sums, total = reduce_grads(grads, [0, 0, None, None], smalls, None, 2)

        def own_cols(x):
            cut = x.shape[2] // 2
            return jnp.where(core == 0, x[:, :, :cut], x[:, :, cut:])

        sums = [own_cols(x) for x in sums]
        text_sums = [own_cols(x) for x in text_sums]
    else:
        *sums, total = reduce_plain(grads, smalls)
    s_in, s_mlp, s_out, s_qkv = sums
    s_in = jnp.where(is_enc, s_in, text_sums[0])
    s_mlp = jnp.where(is_enc, s_mlp, text_sums[1])
    s_cross = text_sums[2]
    s_cross, s_qkv = lax.optimization_barrier((s_cross, s_qkv))
    from_text = lax.ppermute(s_cross[:2], "tower", [(1, 0)])
    s_cross = jnp.where(is_enc, from_text, s_cross[2:])

    def turned(x):
        return jnp.swapaxes(x, 1, 2).astype(F32)

    cross_pair = jnp.stack(
        [
            s_cross[0].T,
            s_cross[1].T,
        ]
    ).astype(F32)
    total = total.reshape(2, lines_of * LANES)
    first = total[0]
    pieces = [first[i * width : (i + 1) * width] for i in range(8)]
    at = 8 * width
    parts = total[:, at:]
    qv_total = jnp.stack(
        [
            parts[:, :head_cols].reshape(-1),
            parts[:, head_cols : 2 * head_cols].reshape(-1),
        ]
    )
    in_total = parts[:, 2 * head_cols : 2 * head_cols + hidden].reshape(-1)
    return (
        tower_out[None],
        grad_in[None],
        turned(s_qkv)[None],
        s_out.astype(F32),
        turned(s_in),
        s_mlp.astype(F32),
        cross_pair[None],
        qv_total[None],
        pieces[0][None],
        in_total[None],
        pieces[1][None],
        jnp.stack(pieces[2:5])[None],
        jnp.stack(pieces[5:8])[None],
    )


def solution(mesh):
    return jax.shard_map(
        body,
        mesh=mesh,
        in_specs=(
            P("tower", ("dp", "mp"), None),
            P("tower", ("dp", "mp"), None),
            P("dp", None),
            P("dp"),
            P("tower", None, None, "mp"),
            P("tower", "mp", None),
            P("tower", None, "mp"),
            P("tower", "mp", None),
            P("tower", None, None, "mp"),
            P("tower", None, None),
            P("tower", None),
            P("tower", None),
            P("tower", None),
            P("tower", None, None),
            P("tower", None, None),
        ),
        out_specs=(
            P("tower", ("dp", "mp"), None),
            P("tower", ("dp", "mp"), None),
            P("tower", None, "dp", "mp"),
            P("tower", "mp", "dp"),
            P("tower", "dp", "mp"),
            P("tower", "mp", "dp"),
            P("tower", None, "dp", "mp"),
            P("tower", None, None),
            P("tower", None),
            P("tower", None),
            P("tower", None),
            P("tower", None, None),
            P("tower", None, None),
        ),
        check_vma=False,
    )
```

```python
import functools
from typing import Any, NamedTuple

import jax
import jax.numpy as jnp
from jax import lax
from jax.experimental import pallas as pl
from jax.experimental.pallas import tpu as pltpu
from jax.sharding import PartitionSpec as P

TOWER = "tower"
DP = "dp"
MP = "mp"
HDIM = 64
PATCH = 576
LTXT = 64
EPS = 1e-06
NEG = -1e30
LANES = 128
MESH = pl.DeviceIdType.MESH
F32 = jnp.float32
BF16 = jnp.bfloat16
VMEM_LIMIT = 60 * 1024 * 1024
TAIL_LIMIT = 67043328


def norm_parts(values):
    center = values - jnp.mean(values, axis=-1, keepdims=True)
    spread = jnp.mean(center * center, axis=-1, keepdims=True)
    scale = lax.rsqrt(spread + EPS)
    return (center * scale, scale)


def norm_rows(values, gain_vec, shift_vec):
    unit, _ = norm_parts(values)
    return unit * gain_vec + shift_vec


def norm_back(values, gain_vec, grad_normed):
    unit, scale = norm_parts(values)
    inner = grad_normed * gain_vec
    mean_one = jnp.mean(inner, axis=-1, keepdims=True)
    mean_two = jnp.mean(inner * unit, axis=-1, keepdims=True)
    back = (inner - mean_one - unit * mean_two) * scale
    return (back, jnp.sum(grad_normed * unit, axis=0), jnp.sum(grad_normed, axis=0))


def gelu_tanh(values):
    return jax.nn.gelu(values, approximate=True)


def dot_rows(left, right):
    return lax.dot_general(left, right, (((1,), (1,)), ((), ())), preferred_element_type=F32)


def dot_first(left, right):
    return lax.dot_general(left, right, (((0,), (0,)), ((), ())), preferred_element_type=F32)


def dot_plain(left, right):
    return lax.dot_general(left, right, (((1,), (0,)), ((), ())), preferred_element_type=F32)


def spots():
    tower = lax.axis_index(TOWER)
    dp = lax.axis_index(DP)
    z = lax.axis_index(MP)
    core = lax.rem(dp, 2)
    line = dp // 2
    return tower, dp, z, core, line, dp + 2 - 4 * line, dp + 1 - 2 * core


def greet(target):
    pl.semaphore_signal(pltpu.get_barrier_semaphore(), inc=1, device_id=target, device_id_type=MESH)


def weight_steps(pieces, srcs, outs, stages, sems):
    send_sem, recv_sem, local_sem, twin_send, twin_recv = sems
    tower, dp, z, core, line, other, partner = spots()
    place = z + core * (3 - 2 * z)
    ahead = z + 1 - 2 * core
    behind = z - 1 + 2 * core
    slot_of = (core, 1 - core)
    holder = place <= 1
    far_src = [k for k, p in enumerate(pieces) if p[7]]

    def spot(piece, slot, half):
        which, first, _, count, start, size, _, _ = piece
        part = size // 2
        return outs[which].at[pl.ds(first, count), slot, pl.ds(start + half * part, part), :]

    def own(piece):
        which, _, first, count, start, size, _, far = piece
        part = size // 2
        if far:
            return spot(piece, lax.rem(z, 2), line)
        return srcs[which].at[pl.ds(first, count), pl.ds(start + line * part, part), :]

    def move(k, source, slot, half, kind, arrive, target):
        return pltpu.make_async_remote_copy(
            src_ref=source,
            dst_ref=spot(pieces[k], slot, half),
            send_sem=send_sem.at[k, kind],
            recv_sem=recv_sem.at[k, arrive],
            device_id=target,
            device_id_type=MESH,
        )

    def twin_copy():
        which = pieces[far_src[0]][0]
        return pltpu.make_async_remote_copy(
            src_ref=srcs[which],
            dst_ref=outs[which].at[pl.ds(0, srcs[which].shape[0]), lax.rem(z, 2)],
            send_sem=twin_send,
            recv_sem=twin_recv,
            device_id={TOWER: 1 - tower},
            device_id_type=MESH,
        )

    def local_in(i):
        return pltpu.make_async_copy(srcs[i], stages[i], local_sem.at[i, 0])

    def local_out(i):
        first = outs[i].shape[0] - srcs[i].shape[0]
        return pltpu.make_async_copy(
            stages[i], outs[i].at[pl.ds(first, srcs[i].shape[0]), lax.rem(z, 2)], local_sem.at[i, 1]
        )

    def gate(piece, cond):
        return cond if piece[6] is None else jnp.logical_and(cond, tower == piece[6])

    def send_own(k):
        piece = pieces[k]

        @pl.when(gate(piece, place == 0))
        def _():
            move(k, own(piece), slot_of[0], line, 0, 0, {MP: ahead}).start()

        @pl.when(gate(piece, place == 1))
        def _():
            move(k, own(piece), slot_of[1], line, 1, 1, {MP: ahead}).start()
            move(k, own(piece), slot_of[1], line, 2, 1, {MP: behind}).start()

    orders = {t: [k for k, p in enumerate(pieces) if p[6] in (None, t)] for t in (0, 1)}

    def launch(t, place):
        if place >= len(orders[t]):
            return
        k = orders[t][place]

        @pl.when(jnp.logical_and(holder, tower == t))
        def _():
            if far_src and k == far_src[0]:
                twin_copy().wait_recv()
            send_own(k)

    def own_sent(k):
        piece = pieces[k]

        @pl.when(gate(piece, place == 0))
        def _():
            move(k, own(piece), slot_of[0], line, 0, 0, {MP: z}).wait_send()

        @pl.when(gate(piece, place == 1))
        def _():
            move(k, own(piece), slot_of[1], line, 1, 1, {MP: z}).wait_send()
            move(k, own(piece), slot_of[1], line, 2, 1, {MP: z}).wait_send()

    def begin():
        if far_src:

            @pl.when(jnp.logical_and(holder, tower == 0))
            def _():
                twin_copy().start()

        for t in (0, 1):
            for start in range(WINDOW):
                launch(t, start)

    def keeps(i):
        flags = {p[6] for p in pieces if p[0] == i}
        flag = None if len(flags) > 1 else flags.pop()
        return holder if flag is None else jnp.logical_and(holder, tower == flag)

    def begin_local():
        for i in range(len(srcs)):

            @pl.when(keeps(i))
            def _(i=i):
                local_in(i).start()

        for i in range(len(srcs)):

            @pl.when(keeps(i))
            def _(i=i):
                local_in(i).wait()
                local_out(i).start()

    def pass_on(k):
        piece = pieces[k]

        @pl.when(gate(piece, place >= 1))
        def _():
            here = spot(piece, slot_of[0], line)
            move(k, here, slot_of[0], line, 0, 0, {MP: z}).wait_recv()
            move(k, here, slot_of[0], line, 3, 2, {DP: other}).start()

        @pl.when(gate(piece, jnp.logical_and(place >= 1, place <= 2)))
        def _():
            here = spot(piece, slot_of[0], line)
            move(k, here, slot_of[0], line, 0, 0, {MP: ahead}).start()

        @pl.when(gate(piece, place != 1))
        def _():
            here = spot(piece, slot_of[1], line)
            move(k, here, slot_of[1], line, 1, 1, {MP: z}).wait_recv()
            move(k, here, slot_of[1], line, 4, 3, {DP: other}).start()

        @pl.when(gate(piece, place == 2))
        def _():
            here = spot(piece, slot_of[1], line)
            move(k, here, slot_of[1], line, 1, 1, {MP: ahead}).start()

        own_sent(k)
        for t in (0, 1):
            if k in orders[t]:
                launch(t, orders[t].index(k) + WINDOW)

    def arrived(k):
        piece = pieces[k]

        @pl.when(gate(piece, place >= 1))
        def _():
            move(k, spot(piece, slot_of[0], 1 - line), slot_of[0], 1 - line, 3, 2, {DP: dp}).wait_recv()

        @pl.when(gate(piece, place != 1))
        def _():
            move(k, spot(piece, slot_of[1], 1 - line), slot_of[1], 1 - line, 4, 3, {DP: dp}).wait_recv()

    def sent(k):
        piece = pieces[k]

        @pl.when(gate(piece, jnp.logical_or(place == 1, place == 2)))
        def _():
            move(k, spot(piece, slot_of[0], line), slot_of[0], line, 0, 0, {MP: z}).wait_send()

        @pl.when(gate(piece, place == 2))
        def _():
            move(k, spot(piece, slot_of[1], line), slot_of[1], line, 1, 1, {MP: z}).wait_send()

        @pl.when(gate(piece, place >= 1))
        def _():
            move(k, spot(piece, slot_of[0], line), slot_of[0], line, 3, 2, {DP: dp}).wait_send()

        @pl.when(gate(piece, place != 1))
        def _():
            move(k, spot(piece, slot_of[1], line), slot_of[1], line, 4, 3, {DP: dp}).wait_send()

    def end_local(i):
        @pl.when(keeps(i))
        def _():
            local_out(i).wait()

    def end_twin():
        @pl.when(jnp.logical_and(holder, tower == 0))
        def _():
            twin_copy().wait_send()

    return begin, begin_local, pass_on, arrived, sent, end_local, end_twin


def token_steps(blocks, outs, stage, sems):
    send_sem, recv_sem, local_sem = sems
    tower, dp, z, core, line, other, partner = spots()
    stays = z == 3 * core
    size = blocks[0].shape[0]

    def rows(which_core):
        return pl.ds(pl.multiple_of(which_core * size, 16), size)

    def away(i):
        target = {DP: 2 * line + lax.rem(z, 2), MP: 2 * core + z // 2}
        return pltpu.make_async_remote_copy(
            src_ref=blocks[i],
            dst_ref=outs[i].at[rows(lax.rem(z, 2)), :],
            send_sem=send_sem.at[i, 0],
            recv_sem=recv_sem.at[i, 0],
            device_id=target,
            device_id_type=MESH,
        )

    def across(i, which_core):
        return pltpu.make_async_remote_copy(
            src_ref=outs[i].at[rows(which_core), :],
            dst_ref=outs[i].at[rows(which_core), :],
            send_sem=send_sem.at[i, 1],
            recv_sem=recv_sem.at[i, 1],
            device_id={DP: partner},
            device_id_type=MESH,
        )

    def begin(i):
        @pl.when(jnp.logical_not(stays))
        def _():
            away(i).start()

        @pl.when(stays)
        def _():
            first = pltpu.make_async_copy(blocks[i], stage.at[i], local_sem.at[i, 0])
            first.start()
            first.wait()
            second = pltpu.make_async_copy(stage.at[i], outs[i].at[rows(core), :], local_sem.at[i, 1])
            second.start()
            second.wait()
            across(i, core).start()

    def relay(i):
        @pl.when(jnp.logical_not(stays))
        def _():
            away(i).wait_recv()
            across(i, core).start()

    def finish(i):
        across(i, 1 - core).wait_recv()
        across(i, core).wait_send()

        @pl.when(jnp.logical_not(stays))
        def _():
            away(i).wait_send()

    return begin, relay, finish


TILE = 32
WINDOW = 2


def barrier_all(peers, options):
    for cond, target in peers:
        if cond is None:
            greet(target)
        else:
            pl.when(cond)(functools.partial(greet, target))
    for cond, count in options:

        @pl.when(cond)
        def _(count=count):
            pl.semaphore_wait(pltpu.get_barrier_semaphore(), count)


def fold_rows(tile):
    return jnp.sum(tile.reshape(tile.shape[0] // 8, 8, tile.shape[1]), axis=0)


def row_tiles(total, run, carry):
    tile = 64 if total % 192 == 0 else 32
    turns = total // tile

    def step(i, kept):
        return run(pl.ds(pl.multiple_of(i * tile, tile), tile), kept)

    return lax.fori_loop(0, turns, step, carry, unroll=3 if turns % 3 == 0 else 1)


def norm_back_tile(values, gain, grads):
    unit, scale = norm_parts(values)
    inner = grads * gain
    mean_one = jnp.mean(inner, axis=-1, keepdims=True)
    mean_two = jnp.mean(inner * unit, axis=-1, keepdims=True)
    return ((inner - mean_one - unit * mean_two) * scale, fold_rows(grads * unit), fold_rows(grads))


def gelu_both(v):
    rate = 0.7978845608028654
    square = v * v
    bend = jnp.tanh(rate * (v + 0.044715 * (square * v)))
    lifted = 0.5 * (1.0 + bend)
    slope = lifted + 0.5 * v * (1.0 - bend * bend) * (rate * (1.0 + 3.0 * 0.044715 * square))
    return (v * lifted, slope)


def low_lanes_of(count):
    return lax.broadcasted_iota(jnp.int32, (count, LANES), 1) < HDIM


def stack_all(block, low):
    wide = block.astype(F32)
    return jnp.concatenate([jnp.where(low, wide, 0.0), jnp.where(low, 0.0, wide)], axis=0)


def merge_all(both, low):
    count = both.shape[0] // 2
    return jnp.where(low, both[:count], both[count:])


def lane_block(index):
    return pl.ds(pl.multiple_of(index * LANES, LANES), LANES)


def scores_of(keys, queries, mask):
    scores = dot_rows(keys, queries)
    if mask is None:
        return scores
    block = mask[...]
    return scores + jnp.concatenate([block, block], axis=1)


def forward_heads(queries, keys, vals, mask, low):
    scores = scores_of(keys, queries, mask)
    top = jnp.max(scores, axis=0, keepdims=True)
    grown = jnp.exp(scores - top)
    total = jnp.sum(grown, axis=0, keepdims=True)
    weights = (grown * (1.0 / total)).astype(BF16)
    return (merge_all(dot_first(weights, vals), low), top + jnp.log(total))


def backward_heads(queries, keys, vals, grads, tops, mask, low, scale):
    weights = jnp.exp(scores_of(keys, queries, mask) - tops)
    grad_w = dot_rows(vals, grads)
    row_dot = jnp.sum(weights * grad_w, axis=0, keepdims=True)
    grad_s = (weights * (grad_w - row_dot)).astype(BF16)
    grad_q = merge_all(dot_first(keys, grad_s).T, low) * scale
    return (grad_q, dot_plain(grad_s, queries), dot_plain(weights.astype(BF16), grads))


def fill_mask(mask, col, row, is_dec):
    count = mask.shape[0]

    def tile(rows, kept):
        shape = (rows.size, count)
        key_at = lax.broadcasted_iota(jnp.int32, shape, 0) + rows.start
        query_at = lax.broadcasted_iota(jnp.int32, shape, 1)
        allowed = jnp.logical_and(key_at <= query_at, col[rows, 0:1] == row[0:1, :])
        mask[rows, :] = jnp.where(jnp.logical_or(allowed, jnp.logical_not(is_dec)), 0.0, NEG)
        return kept

    row_tiles(count, tile, 0)


def self_forward(packed, mask, out, tops, pairs, scale):
    low = low_lanes_of(packed.shape[0])

    @pl.loop(0, pairs)
    def _(pair):
        queries = (stack_all(packed[:, lane_block(pair)], low) * scale).astype(BF16)
        mixed, top = forward_heads(
            queries, packed[:, lane_block(pairs + pair)], packed[:, lane_block(2 * pairs + pair)], mask, low
        )
        out[:, lane_block(pair)] = mixed.astype(BF16)
        tops[pair, 0:1, :] = top


def self_backward(packed, grads, tops, mask, out, pairs, scale):
    low = low_lanes_of(packed.shape[0])

    @pl.loop(0, pairs)
    def _(pair):
        queries = (stack_all(packed[:, lane_block(pair)], low) * scale).astype(BF16)
        head_grads = stack_all(grads[:, lane_block(pair)], low).astype(BF16)
        grad_q, grad_k, grad_v = backward_heads(
            queries,
            packed[:, lane_block(pairs + pair)],
            packed[:, lane_block(2 * pairs + pair)],
            head_grads,
            tops[pair, 0:1, :],
            mask,
            low,
            scale,
        )
        out[:, lane_block(pair)] = grad_q.astype(BF16)
        out[:, lane_block(pairs + pair)] = grad_k.astype(BF16)
        out[:, lane_block(2 * pairs + pair)] = grad_v.astype(BF16)


def cross_forward(query, keys, vals, picks, out, tops, pairs, scale):
    low = low_lanes_of(query.shape[0])

    @pl.loop(0, pairs)
    def _(pair):
        cols = lane_block(pair)
        queries = (stack_all(query[:, cols], low) * scale).astype(BF16)

        @pl.loop(0, 2)
        def _(image):
            mixed, top = forward_heads(queries, keys[image, :, cols], vals[image, :, cols], None, low)
            kept = jnp.where(picks[...] == image, mixed, out[:, cols].astype(F32))
            out[:, cols] = kept.astype(BF16)
            tops[image, pair, 0:1, :] = top


def cross_backward(query, keys, vals, grads, picks, tops, dq, dk, dv, sum_q, pairs, scale):
    low = low_lanes_of(query.shape[0])

    @pl.loop(0, pairs)
    def _(pair):
        cols = lane_block(pair)
        queries = (stack_all(query[:, cols], low) * scale).astype(BF16)
        sum_q[...] = jnp.zeros_like(sum_q)

        @pl.loop(0, 2)
        def _(image):
            own = jnp.where(picks[...] == image, grads[:, cols].astype(F32), 0.0)
            grad_q, grad_k, grad_v = backward_heads(
                queries,
                keys[image, :, cols],
                vals[image, :, cols],
                stack_all(own, low).astype(BF16),
                tops[image, pair, 0:1, :],
                None,
                low,
                scale,
            )
            sum_q[...] += grad_q
            dk[image, :, cols] = grad_k.astype(BF16)
            dv[image, :, cols] = grad_v.astype(BF16)

        dq[:, cols] = sum_q[...].astype(BF16)


class Reducer:
    def __init__(self, pieces, grads, near, far, outs, sems, window):
        self.pieces, self.grads, self.near, self.far, self.outs = pieces, grads, near, far, outs
        self.window = window
        self.y_send, self.y_recv, self.z_send, self.z_recv, self.c_send, self.c_recv = sems
        self.tower, self.dp, self.z, self.core, self.line, self.other, self.partner = spots()
        self.place = self.z + self.core * (3 - 2 * self.z)
        self.holder = self.place <= 1
        self.slot = lax.rem(self.z, 2)
        self.half = grads[0].shape[3] // 2
        self.done = {t: [0, 0, 0, 0] for t in pieces}
        self.ready = {t: 0 for t in pieces}

    def lanes(self, line):
        return pl.ds(pl.multiple_of(line * self.half, LANES), self.half)

    def to_line(self, t, k):
        which, a, start, size = self.pieces[t][k]
        rows = pl.ds(start, size)
        return pltpu.make_async_remote_copy(
            src_ref=self.grads[which].at[a, :, rows, self.lanes(1 - self.line)],
            dst_ref=self.near[which].at[a, :, rows, :],
            send_sem=self.y_send.at[k],
            recv_sem=self.y_recv.at[k],
            device_id={DP: self.other},
            device_id_type=MESH,
        )

    def send(self, source, target, k, sent, got, where):
        return pltpu.make_async_remote_copy(
            src_ref=source,
            dst_ref=target,
            send_sem=self.z_send.at[k, sent],
            recv_sem=self.z_recv.at[k, got],
            device_id={MP: where},
            device_id_type=MESH,
        )

    def inward(self, t, k):
        which, a, start, size = self.pieces[t][k]
        rows = pl.ds(start, size)
        return self.send(self.near[which].at[a, :, rows, :], self.far[which].at[:, a, rows, :], k, 0, 0, 2 - self.core)

    def beside(self, t, k):
        which, a, start, size = self.pieces[t][k]
        rows = pl.ds(start, size)
        where = 4 * self.core + 1 - self.z
        return self.send(self.near[which].at[a, 1 - self.slot, rows, :], self.far[which].at[0, a, rows, :], k, 0, 0, where)

    def onward(self, t, k, shard):
        which, a, start, size = self.pieces[t][k]
        rows = pl.ds(start, size)
        where = 2 * self.core + shard
        return self.send(self.near[which].at[a, shard, rows, :], self.far[which].at[1, a, rows, :], k, shard, 1, where)

    def to_core(self, t, k):
        which, a, start, size = self.pieces[t][k]
        here = self.outs[which].at[a, pl.ds(start, size), :]
        return pltpu.make_async_remote_copy(
            src_ref=here,
            dst_ref=here,
            send_sem=self.c_send.at[k],
            recv_sem=self.c_recv.at[k],
            device_id={DP: self.partner},
            device_id_type=MESH,
        )

    def launch(self, t):
        state = self.done[t]
        while state[0] < self.ready[t] and state[0] - state[1] < self.window:
            self.to_line(t, state[0]).start()
            state[0] += 1

    def allow(self, t, count):
        self.ready[t] = count
        self.launch(t)

    def add_near(self, t):
        k = self.done[t][1]
        which, a, start, size = self.pieces[t][k]
        self.to_line(t, k).wait_send()
        self.to_line(t, k).wait_recv()
        self.done[t][1] += 1
        self.launch(t)
        grads, near = self.grads[which], self.near[which]

        @pl.loop(0, size // TILE)
        def _(i):
            rows = pl.ds(pl.multiple_of(start + i * TILE, TILE), TILE)
            for b in range(2):
                total = grads[a, b, rows, self.lanes(self.line)].astype(F32) + near[a, b, rows, :].astype(F32)
                near[a, b, rows, :] = total.astype(BF16)

        pl.when(self.place == 3)(self.inward(t, k).start)
        pl.when(self.holder)(self.beside(t, k).start)

    def add_mid(self, t):
        k = self.done[t][2]
        self.done[t][2] += 1
        which, a, start, size = self.pieces[t][k]
        near, far = self.near[which], self.far[which]

        @pl.when(self.place == 2)
        def _():
            self.inward(t, k).wait_recv()

            @pl.loop(0, size // TILE)
            def _(i):
                rows = pl.ds(pl.multiple_of(start + i * TILE, TILE), TILE)
                for b in range(2):
                    total = near[a, b, rows, :].astype(F32) + far[b, a, rows, :].astype(F32)
                    near[a, b, rows, :] = total.astype(BF16)

            for shard in range(2):
                self.onward(t, k, shard).start()

    def add_far(self, t):
        k = self.done[t][3]
        self.done[t][3] += 1
        which, a, start, size = self.pieces[t][k]
        near, far, out = self.near[which], self.far[which], self.outs[which]

        @pl.when(self.holder)
        def _():
            self.beside(t, k).wait_recv()
            self.onward(t, k, 0).wait_recv()

            @pl.loop(0, size // TILE)
            def _(i):
                rows = pl.ds(pl.multiple_of(start + i * TILE, TILE), TILE)
                total = near[a, self.slot, rows, :].astype(F32)
                for seat in range(2):
                    total = total + far[seat, a, rows, :].astype(F32)
                out[a, rows, :] = total.astype(BF16)

            self.to_core(t, k).start()

    def step(self, t, count=1):
        for _ in range(count):
            state = self.done[t]
            if state[1] < state[0]:
                self.add_near(t)
                if state[2] + 1 < state[1]:
                    self.add_mid(t)

    def drain(self, t):
        total = len(self.pieces[t])
        state = self.done[t]
        while state[3] < total:
            if state[1] < total:
                self.add_near(t)
            if state[2] + 1 < state[1] or state[1] == total > state[2]:
                self.add_mid(t)
            if state[3] + 2 < state[2] or state[2] == total:
                self.add_far(t)

    def close(self, t):
        for k in range(len(self.pieces[t])):
            pl.when(self.place == 3)(self.inward(t, k).wait_send)

            @pl.when(self.place == 2)
            def _(k=k):
                for shard in range(2):
                    self.onward(t, k, shard).wait_send()

            @pl.when(self.holder)
            def _(k=k):
                self.beside(t, k).wait_send()
                self.to_core(t, k).wait_send()

            @pl.when(jnp.logical_not(self.holder))
            def _(k=k):
                self.to_core(t, k).wait_recv()


class Tail(NamedTuple):
    d_three: Any
    base: Any
    upstream: Any
    gains: Any
    smalls: Any
    w_mlp: Any
    pre: Any
    hid: Any
    act: Any
    w_in: Any
    x1: Any
    w_out: Any
    mixed: Any
    packed: Any
    tops: Any
    seg_col: Any
    seg_row: Any
    a_one: Any
    w_qkv: Any
    x0: Any


IMAGE_ONLY = Tail._fields[5:11]


def tail_kernel(pieces, n_loads, pairs, scale, *refs):
    it = iter(refs)
    hbm = Tail(*[next(it) for _ in Tail._fields])
    cross_in = next(it)
    outs = [next(it) for _ in range(5)]
    small_out, grad_out, from_text = next(it), next(it), next(it)
    vm = Tail(*[next(it) for _ in Tail._fields])
    grads = [next(it) for _ in range(5)]
    near = [next(it) for _ in range(5)]
    far = [next(it) for _ in range(5)]
    g_f32, g_low, grad_hid, grad_pre, d_packed, mix_grad = (next(it) for _ in range(6))
    part_send, part_recv, mask, smalls, small_near, small_all, own_grad = (next(it) for _ in range(7))
    load_sem, red_sems, part_sem, small_sem, move_sem, twin_sem = next(it), [next(it) for _ in range(6)], next(it), next(it), next(it), next(it)
    tower, dp, z, core, line, other, partner = spots()
    is_enc = tower == 0
    is_dec = tower == 1
    stays = z == 3 * core
    tokens, width = g_f32.shape
    rows_txt = tokens // LTXT
    quarter = tokens // 2
    heads = mix_grad.shape[1]

    home = {DP: 2 * line + z // 2, MP: 2 * lax.rem(z, 2) + core}
    guest = {DP: 2 * line + lax.rem(z, 2), MP: 2 * core + z // 2}
    moved = jnp.logical_not(stays)
    peers = [(None, {DP: other}), (None, {DP: partner}), (is_enc, {TOWER: 1 - tower})]
    peers += [(None, {MP: lax.rem(z + away, 4)}) for away in range(1, 4)]
    peers += [(moved, home), (moved, guest)]
    barrier_all(
        peers,
        [
            (jnp.logical_and(is_enc, stays), 5),
            (jnp.logical_and(is_enc, moved), 7),
            (jnp.logical_and(is_dec, stays), 6),
            (jnp.logical_and(is_dec, moved), 8),
        ],
    )

    def load(i):
        return pltpu.make_async_copy(hbm[i], vm[i], load_sem.at[i])

    def on_side(i, run):
        if Tail._fields[i] in IMAGE_ONLY:
            pl.when(is_enc)(run)
        else:
            run()

    pl.when(is_dec)(lambda: pltpu.make_async_copy(cross_in, grads[4], load_sem.at[len(hbm)]).start())
    for i in range(len(hbm)):
        on_side(i, load(i).start)

    def need(*wanted):
        for i, ref in enumerate(vm):
            if any(ref is one for one in wanted):
                on_side(i, load(i).wait)

    red = Reducer(pieces, grads, near, far, outs, red_sems, 4)

    def twin_copy():
        return pltpu.make_async_remote_copy(
            src_ref=outs[4].at[pl.ds(0, 2)],
            dst_ref=from_text,
            send_sem=twin_sem.at[0],
            recv_sem=twin_sem.at[1],
            device_id={TOWER: 1 - tower},
            device_id_type=MESH,
        )

    cross_load = pltpu.make_async_copy(cross_in, grads[4], load_sem.at[len(hbm)])

    @pl.when(is_dec)
    def _():
        cross_load.wait()
        red.allow(1, 4)

    def home_move(source, target, k):
        return pltpu.make_async_remote_copy(
            src_ref=source,
            dst_ref=target,
            send_sem=move_sem.at[k, 0],
            recv_sem=move_sem.at[k, 1],
            device_id=home,
            device_id_type=MESH,
        )

    def part_copy(k):
        return pltpu.make_async_remote_copy(
            src_ref=part_send.at[k],
            dst_ref=part_recv.at[k],
            send_sem=part_sem.at[k, 0],
            recv_sem=part_sem.at[k, 1],
            device_id={DP: partner},
            device_id_type=MESH,
        )

    zero = jnp.zeros((8, width), F32)
    need(vm.d_three, vm.base, vm.upstream, vm.gains, vm.smalls)
    smalls[...] = vm.smalls[...]

    def put(row, value):
        smalls[pl.ds(row, 1), :] = jnp.sum(value, axis=0, keepdims=True)

    def third(rows, kept):
        back, dg, db = norm_back_tile(vm.base[rows, :], vm.gains[2:3, :], vm.d_three[rows, :])
        total = vm.upstream[rows, :] + back
        g_f32[rows, :] = total
        low = total.astype(BF16)
        g_low[rows, :] = low
        return (kept[0] + dg, kept[1] + db, kept[2] + fold_rows(low.astype(F32)))

    dg, db, bias = row_tiles(tokens, third, (zero, zero, zero))
    put(4, dg)
    put(7, db)

    @pl.when(is_enc)
    def _():
        put(1, bias)
        need(vm.w_mlp, vm.pre)

        for b in range(2):
            cols = pl.ds(b * width, width)
            grad_hid[...] = dot_rows(g_low[...], vm.w_mlp[pl.ds(b * width, width), :])

            def bend(rows, kept):
                low = (grad_hid[rows, :] * gelu_both(vm.pre[rows, cols])[1]).astype(BF16)
                grad_pre[b, rows, :] = low
                return kept + fold_rows(low.astype(F32))

            put(9 + b, row_tiles(tokens, bend, zero))
        need(vm.hid, vm.act, vm.w_in)
        grad_hid[...] = dot_rows(grad_pre[0], vm.w_in[0]) + dot_rows(grad_pre[1], vm.w_in[1])

        def lower(rows, kept):
            part_send[0, rows, :] = grad_hid[rows, :].astype(BF16)
            return kept

        row_tiles(tokens, lower, 0)
        part_copy(0).start()
        for b in range(2):
            grads[0][0, b] = dot_first(grad_pre[b], vm.act[...]).astype(BF16)
        red.allow(0, 4)
        for b in range(2):
            grads[1][0, b] = dot_first(vm.hid[:, pl.ds(b * width, width)], g_low[...]).astype(BF16)
        red.allow(0, 8)
        need(vm.x1)
        part_copy(0).wait()

        def second(rows, kept):
            grad = part_send[0, rows, :].astype(F32) + part_recv[0, rows, :].astype(F32)
            back, dg, db = norm_back_tile(vm.x1[rows, :], vm.gains[1:2, :], grad)
            total = g_f32[rows, :] + back
            g_f32[rows, :] = total
            low = total.astype(BF16)
            g_low[rows, :] = low
            return (kept[0] + dg, kept[1] + db, kept[2] + fold_rows(low.astype(F32)))

        dg, db, bias_two = row_tiles(tokens, second, (zero, zero, zero))
        put(3, dg)
        put(6, db)
        put(0, bias_two)
        red.step(0)

    @pl.when(is_dec)
    def _():
        put(0, bias)
        red.step(1)

    need(vm.w_out, vm.mixed, vm.packed, vm.tops, vm.seg_col, vm.seg_row)
    mix_grad[...] = dot_rows(g_low[...], vm.w_out[...]).astype(BF16)
    grads[2][0] = dot_first(vm.mixed[...], g_low[...]).astype(BF16).reshape(grads[2].shape[1:])

    fill_mask(mask, vm.seg_col, vm.seg_row, is_dec)
    self_backward(vm.packed, mix_grad, vm.tops, mask, d_packed, pairs, scale)

    @pl.when(is_enc)
    def _():
        red.step(0)

    @pl.when(is_dec)
    def _():
        red.step(1, 2)

    need(vm.a_one, vm.w_qkv, vm.x0)
    grad_hid[...] = dot_plain(d_packed[...], vm.w_qkv[...])

    def lower_two(rows, kept):
        part_send[1, rows, :] = grad_hid[rows, :].astype(BF16)
        return (
            kept[0] + fold_rows(d_packed[rows, pl.ds(0, heads)].astype(F32)),
            kept[1] + fold_rows(d_packed[rows, pl.ds(2 * heads, heads)].astype(F32)),
        )

    small_zero = jnp.zeros((8, heads), F32)
    q_sum, v_sum = row_tiles(tokens, lower_two, (small_zero, small_zero))
    part_copy(1).start()
    smalls[8:9, :] = jnp.concatenate(
        [jnp.sum(q_sum, axis=0, keepdims=True), jnp.sum(v_sum, axis=0, keepdims=True)], axis=1
    )
    for a in range(3):
        made = dot_first(d_packed[:, pl.ds(a * heads, heads)], vm.a_one[...]).astype(BF16)
        grads[3][a] = made.reshape(grads[3].shape[1:])

    @pl.when(is_enc)
    def _():
        red.allow(0, len(pieces[0]))
        red.step(0)

    @pl.when(is_dec)
    def _():
        red.allow(1, len(pieces[1]))
        red.step(1)

    part_copy(1).wait()

    def first(rows, kept):
        grad = part_send[1, rows, :].astype(F32) + part_recv[1, rows, :].astype(F32)
        back, dg, db = norm_back_tile(vm.x0[rows, :].astype(F32), vm.gains[0:1, :], grad)
        part_send[1, rows, :] = (g_f32[rows, :] + back).astype(BF16)
        return (kept[0] + dg, kept[1] + db)

    dg, db = row_tiles(tokens, first, (zero, zero))
    put(2, dg)
    put(5, db)
    mine = pl.ds(pl.multiple_of(core * quarter, TILE), quarter)

    def own_copy(rows, kept):
        shifted = pl.ds(pl.multiple_of(core * quarter + rows.start, 32), rows.size)
        own_grad[rows, :] = part_send[1, shifted, :]
        return kept

    row_tiles(quarter, own_copy, 0)

    small_line = pltpu.make_async_remote_copy(
        src_ref=smalls,
        dst_ref=small_near,
        send_sem=small_sem.at[0],
        recv_sem=small_sem.at[1],
        device_id={DP: other},
        device_id_type=MESH,
    )
    small_line.start()

    @pl.when(moved)
    def _():
        home_move(own_grad, grad_out, 1).start()

    @pl.when(stays)
    def _():
        pltpu.make_async_copy(own_grad, grad_out, move_sem.at[1, 0]).start()

    @pl.when(is_enc)
    def _():
        red.step(0)

    @pl.when(is_dec)
    def _():
        red.step(1)

    def small_pair(sender, away):
        return pltpu.make_async_remote_copy(
            src_ref=small_all.at[sender],
            dst_ref=small_all.at[sender],
            send_sem=small_sem.at[1 + away],
            recv_sem=small_sem.at[4 + away],
            device_id={MP: lax.rem(z + away, 4)},
            device_id_type=MESH,
        )

    def small_core(which):
        return pltpu.make_async_remote_copy(
            src_ref=small_out.at[which],
            dst_ref=small_out.at[which],
            send_sem=small_sem.at[8],
            recv_sem=small_sem.at[9],
            device_id={DP: partner},
            device_id_type=MESH,
        )

    small_line.wait()
    small_all[z] = smalls[...] + small_near[...]

    @pl.when(is_enc)
    def _():
        red.step(0)

    @pl.when(is_dec)
    def _():
        red.step(1)

    for away in range(1, 4):
        small_pair(z, away).start()

    @pl.when(is_dec)
    def _():
        red.drain(1)
        red.close(1)
        twin_copy().start()

    @pl.when(is_enc)
    def _():
        red.drain(0)
        red.close(0)

    for away in range(1, 4):
        small_pair(lax.rem(z + 4 - away, 4), away).wait_recv()
    small_out[core] = ((small_all[0] + small_all[1]) + small_all[2]) + small_all[3]
    small_core(core).start()
    for away in range(1, 4):
        small_pair(z, away).wait_send()

    @pl.when(moved)
    def _():
        home_move(own_grad, grad_out, 1).wait()

    @pl.when(stays)
    def _():
        pltpu.make_async_copy(own_grad, grad_out, move_sem.at[1, 0]).wait()

    pl.when(is_dec)(twin_copy().wait_send)
    pl.when(is_enc)(twin_copy().wait_recv)
    small_core(core).wait_send()
    small_core(1 - core).wait_recv()


def tail(values, cross_grad, scale):
    tokens, width = values.base.shape
    heads = values.mixed.shape[1]
    pairs = heads // LANES
    hidden = values.pre.shape[1]
    quarter = tokens // 2
    half = width // 2
    grad_shapes = [
        (1, 2, hidden // 2, width),
        (1, 2, hidden // 2, width),
        (1, 2, heads // 2, width),
        (3, 2, heads // 2, width),
        cross_grad.shape,
    ]

    def cuts(i):
        n, _, rows, _ = grad_shapes[i]
        cut = rows if rows <= 192 else rows // 4
        return [(i, a, at, cut) for a in range(n) for at in range(0, rows, cut)]

    enc = cuts(0) + cuts(1) + cuts(2) + cuts(3)
    dec = cuts(4) + cuts(2) + cuts(3)
    most = max(len(enc), len(dec))
    hbm = pl.BlockSpec(memory_space=pltpu.HBM)
    vmem = pl.BlockSpec(memory_space=pltpu.VMEM)
    n_in = len(values)
    scratch = [pltpu.VMEM(x.shape, x.dtype) for x in values]
    scratch += [pltpu.VMEM(g, BF16) for g in grad_shapes]
    scratch += [pltpu.VMEM(g[:3] + (half,), BF16) for g in grad_shapes]
    scratch += [pltpu.VMEM((2, g[0], g[2], half), BF16) for g in grad_shapes]
    scratch += [
        pltpu.VMEM((tokens, width), F32),
        pltpu.VMEM((tokens, width), BF16),
        pltpu.VMEM((tokens, width), F32),
        pltpu.VMEM((2, tokens, hidden // 2), BF16),
        pltpu.VMEM((tokens, 3 * heads), BF16),
        pltpu.VMEM((tokens, heads), BF16),
        pltpu.VMEM((2, tokens, width), BF16),
        pltpu.VMEM((2, tokens, width), BF16),
        pltpu.VMEM((tokens, tokens), F32),
        pltpu.VMEM(values.smalls.shape, F32),
        pltpu.VMEM(values.smalls.shape, F32),
        pltpu.VMEM((4,) + values.smalls.shape, F32),
        pltpu.VMEM((quarter, width), BF16),
    ]
    dma = pltpu.SemaphoreType.DMA
    scratch += [dma((n_in + 1,)), dma((most,)), dma((most,)), dma((most, 2)), dma((most, 2)), dma((most,)), dma((most,))]
    scratch += [dma((2, 2)), dma((10,)), dma((2, 2)), dma((2,))]
    out_shape = [jax.ShapeDtypeStruct((g[0], g[2], half), BF16) for g in grad_shapes]
    out_shape += [
        jax.ShapeDtypeStruct((2,) + values.smalls.shape, F32),
        jax.ShapeDtypeStruct((quarter, width), BF16),
        jax.ShapeDtypeStruct((2, heads // 2, half), BF16),
    ]
    return pl.pallas_call(
        functools.partial(tail_kernel, {0: tuple(enc), 1: tuple(dec)}, n_in, pairs, scale),
        in_specs=[hbm] * (n_in + 1),
        out_specs=[vmem] * 6 + [hbm] * 2,
        out_shape=out_shape,
        scratch_shapes=scratch,
        compiler_params=pltpu.CompilerParams(
            collective_id=1, has_side_effects=True, vmem_limit_bytes=TAIL_LIMIT
        ),
        name="tail",
    )(*values, cross_grad)


class Head(NamedTuple):
    packed: Any
    mixed: Any
    tops: Any
    a_one: Any
    x1: Any
    base: Any
    act_three: Any
    act: Any
    pre: Any
    hid: Any
    query: Any


def head_kernel(pieces, pairs, scale, *refs):
    it = iter(refs)
    srcs = [next(it) for _ in range(5)]
    blocks = [next(it)]
    seg_ref, image_ref = next(it), next(it)
    gains, shifts, out_b, ffn_out_b, ffn_in_b, qv_b = (next(it) for _ in range(6))
    outs = [next(it) for _ in range(5)]
    tokens = [next(it)]
    seg_out = [next(it) for _ in range(3)]
    hbm = Head(*[next(it) for _ in Head._fields])
    stages = [next(it) for _ in range(5)]
    weight_sems = [next(it) for _ in range(5)]
    token_stage = next(it)
    token_sems = [next(it) for _ in range(3)]
    w_qkv, w_out, w_q, w_in, w_mlp = (next(it) for _ in range(5))
    vm = Head(*[next(it) for _ in Head._fields])
    part_send, part_recv, raw, mask = next(it), next(it), next(it), next(it)
    seg_sem, load_sem, store_sem, part_sem = (next(it) for _ in range(4))
    tower, dp, z, core, line, other, partner = spots()
    is_enc = tower == 0
    is_dec = tower == 1
    stays = z == 3 * core
    moved = jnp.logical_not(stays)
    count, width = vm.x1.shape
    rows_txt = count // LTXT
    heads = vm.mixed.shape[1]
    at_end = jnp.logical_or(z == 0, z == 3)

    peers = [(z > 0, {MP: z - 1}), (z < 3, {MP: z + 1})]
    peers += [(None, {DP: other}), (None, {TOWER: 1 - tower}), (None, {DP: partner})]
    peers += [
        (moved, {DP: 2 * line + lax.rem(z, 2), MP: 2 * core + z // 2}),
        (moved, {DP: 2 * line + z // 2, MP: 2 * lax.rem(z, 2) + core}),
    ]
    barrier_all(
        peers,
        [(stays, 4), (jnp.logical_and(at_end, moved), 6), (jnp.logical_not(at_end), 7)],
    )

    begin, begin_local, pass_on, arrived, sent, end_local, end_twin = weight_steps(
        pieces, srcs, outs, stages, weight_sems
    )
    token_begin, token_relay, token_finish = token_steps(blocks, tokens, token_stage, token_sems)
    token_begin(0)
    begin()

    has_notes = core == z // 2

    def note_send(i):
        return pltpu.make_async_remote_copy(
            src_ref=seg_out[i],
            dst_ref=seg_out[i],
            send_sem=seg_sem.at[i, 0],
            recv_sem=seg_sem.at[i, 1],
            device_id={DP: partner},
            device_id_type=MESH,
        )

    @pl.when(has_notes)
    def _():
        rows = seg_ref.shape[0] // 2
        side = lax.rem(z, 2)
        segs = jnp.where(side == 0, seg_ref[0:rows, :], seg_ref[rows : 2 * rows, :])
        marks = segs + LTXT * lax.broadcasted_iota(jnp.int32, segs.shape, 0)
        tall = jnp.concatenate([marks.astype(F32), jnp.zeros((16 - rows, LTXT), F32)], axis=0).T
        seg_out[1][...] = jnp.zeros_like(seg_out[1])
        for r in range(rows):
            at = pl.ds(r * LTXT, LTXT)
            seg_out[0][at, :] = jnp.broadcast_to(tall[:, r : r + 1], (LTXT, LANES)).astype(jnp.int32)
            seg_out[1][0:1, at] = marks[r : r + 1, :]
            seg_out[2][at, :] = jnp.full((LTXT, LANES), image_ref[side * rows + r], jnp.int32)
        for i in range(3):
            note_send(i).start()

    begin_local()
    token_relay(0)

    def load(i, target, source):
        return pltpu.make_async_copy(source, target, load_sem.at[i])

    def store(ref):
        i = [x is ref for x in vm].index(True)
        return pltpu.make_async_copy(vm[i], hbm[i], store_sem.at[i])

    def part_copy(k):
        return pltpu.make_async_remote_copy(
            src_ref=part_send.at[k],
            dst_ref=part_recv.at[k],
            send_sem=part_sem.at[k, 0],
            recv_sem=part_sem.at[k, 1],
            device_id={DP: partner},
            device_id_type=MESH,
        )

    def normed(source, target, which):
        gain, shift = gains[which : which + 1, :], shifts[which : which + 1, :]

        def tile(rows, kept):
            unit, _ = norm_parts(source[rows, :].astype(F32))
            target[rows, :] = (unit * gain + shift).astype(BF16)
            return kept

        row_tiles(count, tile, 0)

    def chosen(which, flag, far=False):
        return [k for k, p in enumerate(pieces) if p[0] == which and p[6] == flag and p[7] == far]

    enc_in, enc_mlp, dec_in = chosen(3, 0), chosen(4, 0), chosen(3, 1)
    k_qkv, k_out, k_own, k_far = chosen(0, None), chosen(1, None), chosen(2, 1), chosen(2, 1, True)
    waiting = {0: enc_in + enc_mlp, 1: k_own + k_far + dec_in}

    def relay(enc=0, dec=0):
        for t, count in ((0, enc), (1, dec)):
            for k in waiting[t][:count]:
                pass_on(k)
            waiting[t] = waiting[t][count:]

    token_finish(0)
    normed(tokens[0], vm.a_one, 0)
    store(vm.a_one).start()
    for k in k_qkv + k_out:
        pass_on(k)
    for k in k_qkv:
        arrived(k)
    end_local(0)
    load(0, w_qkv, outs[0]).start()
    load(0, w_qkv, outs[0]).wait()
    for part in range(3):
        cols = pl.ds(part * heads, heads)
        own = pl.ds(pl.multiple_of(core * heads, LANES), heads)
        bias = 0.0 if part == 1 else qv_b[part // 2 : part // 2 + 1, own]
        made = dot_rows(vm.a_one[...], w_qkv[part].reshape(heads, width)) + bias
        vm.packed[:, cols] = made.astype(BF16)
    store(vm.packed).start()

    @pl.when(has_notes)
    def _():
        for i in range(3):
            note_send(i).wait_send()

    @pl.when(jnp.logical_not(has_notes))
    def _():
        for i in range(3):
            note_send(i).wait_recv()

    relay(1, 1)
    fill_mask(mask, seg_out[0], seg_out[1], is_dec)
    self_forward(vm.packed, mask, vm.mixed, vm.tops, pairs, scale)
    store(vm.mixed).start()
    store(vm.tops).start()
    for k in k_out:
        arrived(k)
    end_local(1)
    load(1, w_out, outs[1]).start()
    relay(1, 1)
    load(1, w_out, outs[1]).wait()
    part_send[0] = dot_plain(vm.mixed[...], w_out[0].reshape(heads, width)).astype(BF16)
    part_copy(0).start()
    relay(1, 1)
    part_copy(0).wait()

    def add_one(rows, kept):
        total = part_send[0, rows, :].astype(F32) + part_recv[0, rows, :].astype(F32)
        vm.x1[rows, :] = tokens[0][rows, :].astype(F32) + total + out_b[...]
        return kept

    row_tiles(count, add_one, 0)
    store(vm.x1).start()

    @pl.when(is_enc)
    def _():
        relay(1)
        normed(vm.x1, vm.act, 1)
        store(vm.act).start()
        relay(1)
        for k in enc_in:
            arrived(k)
        end_local(3)
        load(3, w_in, outs[3]).start()
        load(3, w_in, outs[3]).wait()
        for b in range(2):
            cols = pl.ds(b * width, width)
            raw[...] = dot_plain(vm.act[...], w_in[0, b])

            def bend(rows, kept):
                pre = raw[rows, :] + ffn_in_b[0:1, pl.ds(pl.multiple_of((2 * core + b) * width, LANES), width)]
                vm.pre[rows, cols] = pre
                vm.hid[rows, cols] = gelu_tanh(pre).astype(BF16)
                return kept

            row_tiles(count, bend, 0)
            relay(1)
        store(vm.pre).start()
        store(vm.hid).start()
        relay(len(waiting[0]))
        for k in enc_mlp:
            arrived(k)
        end_local(4)
        load(4, w_mlp, outs[4]).start()
        load(4, w_mlp, outs[4]).wait()
        part_send[1] = dot_plain(vm.hid[...], w_mlp[0].reshape(2 * width, width)).astype(BF16)
        part_copy(1).start()
        part_copy(1).wait()

        def add_two(rows, kept):
            total = part_send[1, rows, :].astype(F32) + part_recv[1, rows, :].astype(F32)
            vm.base[rows, :] = vm.x1[rows, :] + total + ffn_out_b[...]
            return kept

        row_tiles(count, add_two, 0)

    @pl.when(is_dec)
    def _():
        def same(rows, kept):
            vm.base[rows, :] = vm.x1[rows, :]
            return kept

        row_tiles(count, same, 0)

    store(vm.base).start()
    normed(vm.base, vm.act_three, 2)
    store(vm.act_three).start()

    @pl.when(is_dec)
    def _():
        relay(0, 2)
        for k in k_own:
            arrived(k)
        end_local(2)
        load(2, w_q, outs[2].at[2]).start()
        load(2, w_q, outs[2].at[2]).wait()
        vm.query[...] = dot_rows(vm.act_three[...], w_q[...].reshape(heads, width)).astype(BF16)
        store(vm.query).start()
        relay(0, len(waiting[1]))
        for k in k_far + dec_in:
            arrived(k)
        end_local(3)

    for k in range(len(pieces)):
        sent(k)
    end_twin()
    for ref in vm:
        if ref is vm.act or ref is vm.pre or ref is vm.hid:
            pl.when(is_enc)(store(ref).wait)
        elif ref is vm.query:
            pl.when(is_dec)(store(ref).wait)
        else:
            store(ref).wait()


def head(shards, blocks, segment_ids, row_image, vecs, scale):
    qkv, out, cross, ffn_in, ffn_out = shards
    heads = 2 * out.shape[1]
    width = out.shape[2]
    pairs = heads // LANES
    count = 2 * blocks[0].shape[0]
    hidden = 2 * ffn_in.shape[2]

    def cuts(i, flag):
        blocks_of, rows, _ = shards[i].shape
        cut = rows if rows <= 192 else rows // 4
        return [(i, a, a, 1, at, cut, flag, False) for a in range(blocks_of) for at in range(0, rows, cut)]

    pieces = cuts(0, None) + cuts(1, None)
    rows = cross.shape[1]
    pieces += [(2, 2 + a, a, 1, 0, rows, 1, False) for a in range(2)] + [(2, a, a, 1, 0, rows, 1, True) for a in range(2)]
    pieces += cuts(3, 0) + cuts(4, 0) + cuts(3, 1)
    n = len(pieces)
    hbm = pl.BlockSpec(memory_space=pltpu.HBM)
    vmem = pl.BlockSpec(memory_space=pltpu.VMEM)
    struct = jax.ShapeDtypeStruct
    made = Head(
        packed=struct((count, 3 * heads), BF16),
        mixed=struct((count, heads), BF16),
        tops=struct((pairs, 8, 2 * count), F32),
        a_one=struct((count, width), BF16),
        x1=struct((count, width), F32),
        base=struct((count, width), F32),
        act_three=struct((count, width), BF16),
        act=struct((count, width), BF16),
        pre=struct((count, hidden), F32),
        hid=struct((count, hidden), BF16),
        query=struct((count, heads), BF16),
    )
    out_shape = [
        jax.ShapeDtypeStruct(((2 if i == 2 else 1) * x.shape[0], 2) + x.shape[1:], BF16) for i, x in enumerate(shards)
    ]
    out_shape += [jax.ShapeDtypeStruct((count, width), BF16)]
    out_shape += [struct((count, LANES), jnp.int32), struct((8, count), jnp.int32), struct((count, LANES), jnp.int32)]
    out_shape += list(made)
    dma = pltpu.SemaphoreType.DMA
    scratch = [pltpu.VMEM(x.shape, BF16) for x in shards]
    scratch += [dma((n, 5)), dma((n, 4)), dma((5, 2)), dma, dma]
    scratch += [pltpu.VMEM((1,) + blocks[0].shape, BF16), dma((1, 2)), dma((1, 2)), dma((1, 2))]
    scratch += [
        pltpu.VMEM((3, 2) + qkv.shape[1:], BF16),
        pltpu.VMEM((1, 2) + out.shape[1:], BF16),
        pltpu.VMEM((2,) + cross.shape[1:], BF16),
        pltpu.VMEM((1, 2) + ffn_in.shape[1:], BF16),
        pltpu.VMEM((1, 2) + ffn_out.shape[1:], BF16),
    ]
    scratch += [pltpu.VMEM(x.shape, x.dtype) for x in made]
    scratch += [
        pltpu.VMEM((2, count, width), BF16),
        pltpu.VMEM((2, count, width), BF16),
        pltpu.VMEM((count, width), F32),
        pltpu.VMEM((count, count), F32),
        dma((3, 2)),
        dma((5,)),
        dma((len(made),)),
        dma((2, 2)),
    ]
    results = pl.pallas_call(
        functools.partial(head_kernel, tuple(pieces), pairs, scale),
        in_specs=[hbm] * 6 + [vmem, pl.BlockSpec(memory_space=pltpu.SMEM)] + [vmem] * 6,
        out_specs=[hbm] * 5 + [vmem] + [vmem] * 3 + [hbm] * len(made),
        out_shape=out_shape,
        scratch_shapes=scratch,
        compiler_params=pltpu.CompilerParams(
            collective_id=0, has_side_effects=True, vmem_limit_bytes=VMEM_LIMIT
        ),
        name="head",
    )(*shards, *blocks, segment_ids, row_image, *vecs)
    return results[:5], results[5], results[6:9], Head(*results[9:])


CHUNKS = 3


def mid_kernel(pieces, red_pieces, pairs, scale, *refs):
    it = iter(refs)
    act_three, x1, query_in, w_cross_in, w_in_in, ffn_shard, cot_block, base = (next(it) for _ in range(8))
    gains, shifts, out_b, ffn_out_b, ffn_in_b, qv_b, picks = (next(it) for _ in range(7))
    d_three, upstream, smalls, tower_out, cross_out = (next(it) for _ in range(5))
    outs = [next(it) for _ in range(2)]
    stages = [next(it)]
    weight_sems = [next(it) for _ in range(5)]
    token_stage = next(it)
    token_sems = [next(it) for _ in range(3)]
    images, keys, vals, w_cross, w_in, w_mlp = (next(it) for _ in range(6))
    act_txt, query, mixed, tops, y1, y2, act, pre, hid = (next(it) for _ in range(9))
    raw, grad_pre, g_low, mix_grad, dq, dk, dv, sum_q = (next(it) for _ in range(8))
    cot, part_send, part_recv, halves, half_near, sums, image_grad, own_rows = (next(it) for _ in range(8))
    grads = [next(it) for _ in range(3)]
    near = [next(it) for _ in range(2)]
    far = [next(it) for _ in range(2)]
    red_sems = [next(it) for _ in range(6)]
    load_sem, store_sem, part_sem, twin_sem, side_sem, core_sem, half_sem, sum_sem, back_sem, give_sem, home_sem = it
    tower, dp, z, core, line, other, partner = spots()
    is_enc = tower == 0
    is_dec = tower == 1
    stays = z == 3 * core
    moved = jnp.logical_not(stays)
    side = lax.rem(z, 2)
    across_chip = z + 1 - 2 * side
    count, width = y1.shape
    quarter = count // 2
    chunk = quarter // CHUNKS
    heads = mixed.shape[1]

    home = {DP: 2 * line + z // 2, MP: 2 * lax.rem(z, 2) + core}
    guest = {DP: 2 * line + lax.rem(z, 2), MP: 2 * core + z // 2}
    peers = [(None, {DP: other}), (None, {DP: partner}), (None, {TOWER: 1 - tower})]
    peers += [(None, {MP: lax.rem(z + away, 4)}) for away in range(1, 4)]
    peers += [(moved, home), (moved, guest)]
    barrier_all(peers, [(stays, 6), (moved, 8)])

    def remote(source, target, sends, recvs, where):
        return pltpu.make_async_remote_copy(
            src_ref=source,
            dst_ref=target,
            send_sem=sends,
            recv_sem=recvs,
            device_id=where,
            device_id_type=MESH,
        )

    def span(which_core, i):
        return pl.ds(pl.multiple_of(which_core * quarter + i * chunk, TILE), chunk)

    def twin_copy(i):
        rows = span(core, i)
        return remote(
            act_three.at[rows, :], images.at[side, rows, :], twin_sem.at[i, 0], twin_sem.at[i, 1], {TOWER: 1 - tower}
        )

    def side_copy(i, image):
        here = images.at[image, span(core, i), :]
        return remote(here, here, side_sem.at[i, 0], side_sem.at[i, 1], {MP: across_chip})

    def core_copy(i, image, which_core, far_image):
        here = images.at[image, span(which_core, i), :]
        return remote(here, here, core_sem.at[far_image, i, 0], core_sem.at[far_image, i, 1], {DP: partner})

    @pl.when(is_enc)
    def _():
        for i in range(CHUNKS):
            twin_copy(i).start()

    token_begin, token_relay, token_finish = token_steps([cot_block], [cot], token_stage, token_sems)
    token_begin(0)
    begin, begin_local, pass_on, arrived, sent, end_local, _ = weight_steps(
        pieces, [ffn_shard], [w_mlp], stages, weight_sems
    )
    begin()

    def load(i, source, target):
        return pltpu.make_async_copy(source, target, load_sem.at[i])

    text_loads = [
        load(0, w_cross_in, w_cross),
        load(1, query_in, query),
        load(2, x1, y1),
        load(3, w_in_in, w_in),
        load(4, act_three, act_txt),
    ]

    def part_copy(k):
        return remote(
            part_send.at[k % 3], part_recv.at[k % 3], part_sem.at[k, 0], part_sem.at[k, 1], {DP: partner}
        )

    def home_move():
        return remote(own_rows, tower_out, home_sem.at[0], home_sem.at[1], home)

    def home_stay():
        return pltpu.make_async_copy(own_rows, tower_out, home_sem.at[0])

    def go_home():
        pl.when(moved)(home_move().start)
        pl.when(stays)(home_stay().start)

    def back_copy(i):
        rows = pl.ds(i * chunk, chunk)
        return remote(
            sums.at[1, rows, :], image_grad.at[span(core, i), :], back_sem.at[i, 0], back_sem.at[i, 1], {TOWER: 1 - tower}
        )

    def back_core(i, which_core):
        here = image_grad.at[span(which_core, i), :]
        return remote(here, here, give_sem.at[i, 0], give_sem.at[i, 1], {DP: partner})

    store_grad = pltpu.make_async_copy(y2, upstream, store_sem.at[0])
    store_three = pltpu.make_async_copy(raw, d_three, store_sem.at[1])
    zero = jnp.zeros((8, width), F32)
    red = Reducer({1: red_pieces}, grads, near, far, outs, red_sems, 4)

    @pl.when(is_enc)
    def _():
        smalls[...] = jnp.zeros_like(smalls)
        mine = pl.ds(pl.multiple_of(core * quarter, TILE), quarter)
        take = load(2, base.at[mine, :], y1.at[pl.ds(0, quarter), :])
        take.start()
        take.wait()

        def lower(rows, kept):
            own_rows[rows, :] = y1[rows, :].astype(BF16)
            return kept

        row_tiles(quarter, lower, 0)
        go_home()
        token_relay(0)
        token_finish(0)

        def lift(rows, kept):
            y2[rows, :] = cot[rows, :].astype(F32)
            return kept

        row_tiles(count, lift, 0)
        store_grad.start()
        for i in range(CHUNKS):
            back_copy(i).wait_recv()
            back_core(i, core).start()
        for i in range(CHUNKS):
            back_core(i, 1 - core).wait_recv()

        def lift_three(rows, kept):
            raw[rows, :] = image_grad[rows, :].astype(F32)
            return kept

        row_tiles(count, lift_three, 0)
        store_three.start()
        for i in range(CHUNKS):
            twin_copy(i).wait_send()
            back_core(i, core).wait_send()

    @pl.when(is_dec)
    def _():
        for one in text_loads:
            one.start()
        begin_local()
        smalls[...] = jnp.zeros_like(smalls)

        def put(row, value):
            smalls[pl.ds(row, 1), :] = jnp.sum(value, axis=0, keepdims=True)

        for i in range(CHUNKS):
            twin_copy(i).wait_recv()
            side_copy(i, side).start()
            core_copy(i, side, core, 0).start()
        for i in range(CHUNKS):
            core_copy(i, side, 1 - core, 0).wait_recv()
        for one in text_loads[:2]:
            one.wait()

        def project(image):
            for part, target in ((0, keys), (1, vals)):
                target[image] = dot_rows(images[image], w_cross[part].reshape(heads, width)).astype(BF16)

        project(side)
        pass_on(0)
        pass_on(1)
        for i in range(CHUNKS):
            side_copy(i, 1 - side).wait_recv()
            core_copy(i, 1 - side, core, 1).start()
        token_relay(0)
        for i in range(CHUNKS):
            core_copy(i, 1 - side, 1 - core, 1).wait_recv()
        project(1 - side)

        mixed[...] = jnp.zeros_like(mixed)
        cross_forward(query, keys, vals, picks, mixed, tops, pairs, scale)
        pass_on(2)
        pass_on(3)
        part_send[0] = dot_plain(mixed[...], w_cross[3].reshape(heads, width)).astype(BF16)
        part_copy(0).start()
        for one in text_loads[2:]:
            one.wait()
        gain, shift = gains[1:2, :], shifts[1:2, :]
        part_copy(0).wait()

        def add_cross(rows, kept):
            total = part_send[0, rows, :].astype(F32) + part_recv[0, rows, :].astype(F32)
            value = y1[rows, :] + total
            y2[rows, :] = value
            unit, _ = norm_parts(value)
            act[rows, :] = (unit * gain + shift).astype(BF16)
            return kept

        row_tiles(count, add_cross, 0)
        token_finish(0)
        for k in range(len(pieces)):
            arrived(k)
        end_local(0)

        for b in range(2):
            cols = pl.ds(b * width, width)
            pre[...] = dot_plain(act[...], w_in[0, b])
            raw[...] = dot_rows(cot[...], w_mlp[0, b])

            def bend(rows, kept):
                value = pre[rows, :] + ffn_in_b[0:1, pl.ds(pl.multiple_of((2 * core + b) * width, LANES), width)]
                lifted, slope = gelu_both(value)
                hid[rows, cols] = lifted.astype(BF16)
                low = (raw[rows, :] * slope).astype(BF16)
                grad_pre[b, rows, :] = low
                return kept + fold_rows(low.astype(F32))

            put(9 + b, row_tiles(count, bend, zero))
        part_send[2] = (dot_rows(grad_pre[0], w_in[0, 0]) + dot_rows(grad_pre[1], w_in[0, 1])).astype(BF16)
        part_copy(2).start()
        for b in range(2):
            grads[0][0, b] = dot_first(grad_pre[b], act[...]).astype(BF16)
        red.allow(1, 4)
        part_copy(2).wait()

        def second(rows, kept):
            low_cot = cot[rows, :].astype(F32)
            grad = part_send[2, rows, :].astype(F32) + part_recv[2, rows, :].astype(F32)
            back, dg, db = norm_back_tile(y2[rows, :], gain, grad)
            total = low_cot + back
            raw[rows, :] = total
            g_low[rows, :] = total.astype(BF16)
            return (kept[0] + dg, kept[1] + db, kept[2] + fold_rows(low_cot))

        dg, db, cot_sum = row_tiles(count, second, (zero, zero, zero))
        put(3, dg)
        put(6, db)
        put(1, cot_sum)

        mix_grad[...] = dot_rows(g_low[...], w_cross[3].reshape(heads, width)).astype(BF16)
        cross_backward(query, keys, vals, mix_grad, picks, tops, dq, dk, dv, sum_q, pairs, scale)

        def half_copy(image, far_image):
            return remote(
                halves.at[image, pl.ds(pl.multiple_of((1 - core) * quarter, TILE), quarter), :],
                half_near.at[far_image],
                half_sem.at[far_image, 0],
                half_sem.at[far_image, 1],
                {DP: partner},
            )

        def give(image, far_image):
            made = dot_plain(dk[image], w_cross[0].reshape(heads, width))
            made = made + dot_plain(dv[image], w_cross[1].reshape(heads, width))
            halves[image] = made.astype(BF16)
            half_copy(image, far_image).start()

        def sum_copy(i):
            rows = pl.ds(i * chunk, chunk)
            return remote(
                sums.at[0, rows, :], sums.at[2, rows, :], sum_sem.at[i, 0], sum_sem.at[i, 1], {MP: across_chip}
            )

        give(1 - side, 1)
        give(side, 0)
        half_copy(1 - side, 1).wait_recv()
        for i in range(CHUNKS):

            def add_far(rows, kept):
                at = pl.ds(pl.multiple_of(i * chunk + rows.start, 32), rows.size)
                own = pl.ds(pl.multiple_of(core * quarter + i * chunk + rows.start, 32), rows.size)
                total = halves[1 - side, own, :].astype(F32) + half_near[1, at, :].astype(F32)
                sums[0, at, :] = total.astype(BF16)
                return kept

            row_tiles(chunk, add_far, 0)
            sum_copy(i).start()
        for b in range(2):
            grads[1][0, b] = dot_first(hid[:, pl.ds(b * width, width)], cot[...]).astype(BF16)
        half_copy(side, 0).wait_recv()
        for i in range(CHUNKS):
            sum_copy(i).wait_recv()

            def add_own(rows, kept):
                at = pl.ds(pl.multiple_of(i * chunk + rows.start, 32), rows.size)
                own = pl.ds(pl.multiple_of(core * quarter + i * chunk + rows.start, 32), rows.size)
                total = halves[side, own, :].astype(F32) + half_near[0, at, :].astype(F32)
                sums[1, at, :] = (total + sums[2, at, :].astype(F32)).astype(BF16)
                return kept

            row_tiles(chunk, add_own, 0)
            back_copy(i).start()

        part_send[0] = dot_plain(dq[...], w_cross[2].reshape(heads, width)).astype(BF16)
        part_copy(3).start()
        red.allow(1, 8)
        red.step(1, 3)

        def keep_two(rows, kept):
            y1[rows, :] = raw[rows, :]
            return kept

        row_tiles(count, keep_two, 0)
        pltpu.make_async_copy(y1, upstream, store_sem.at[0]).start()
        part_copy(3).wait()

        def lift_query(rows, kept):
            raw[rows, :] = part_send[0, rows, :].astype(F32) + part_recv[0, rows, :].astype(F32)
            return kept

        row_tiles(count, lift_query, 0)
        store_three.start()
        part_send[1] = (
            dot_plain(hid[:, pl.ds(0, width)], w_mlp[0, 0]) + dot_plain(hid[:, pl.ds(width, width)], w_mlp[0, 1])
        ).astype(BF16)
        part_copy(1).start()
        red.step(1)
        for which, source in ((0, dk), (1, dv)):
            made = dot_first(source[0], images[0]) + dot_first(source[1], images[1])
            grads[2][which] = made.astype(BF16).reshape(grads[2].shape[1:])
        red.step(1)
        grads[2][2] = dot_first(dq[...], act_txt[...]).astype(BF16).reshape(grads[2].shape[1:])
        grads[2][3] = dot_first(mixed[...], g_low[...]).astype(BF16).reshape(grads[2].shape[1:])
        store_cross = pltpu.make_async_copy(grads[2], cross_out, store_sem.at[2])
        store_cross.start()
        part_copy(1).wait()

        def add_last(rows, kept):
            own = pl.ds(pl.multiple_of(core * quarter + rows.start, 32), rows.size)
            total = part_send[1, own, :].astype(F32) + part_recv[1, own, :].astype(F32)
            own_rows[rows, :] = (y2[own, :] + total + ffn_out_b[...]).astype(BF16)
            return kept

        row_tiles(quarter, add_last, 0)
        go_home()
        red.drain(1)
        red.close(1)
        store_cross.wait()
        for i in range(CHUNKS):
            side_copy(i, side).wait_send()
            core_copy(i, side, core, 0).wait_send()
            core_copy(i, 1 - side, core, 1).wait_send()
            sum_copy(i).wait_send()
            back_copy(i).wait_send()
        half_copy(1 - side, 1).wait_send()
        half_copy(side, 0).wait_send()
        for k in range(len(pieces)):
            sent(k)

    pl.when(moved)(home_move().wait)
    pl.when(stays)(home_stay().wait)
    store_grad.wait()
    store_three.wait()


def middle(values, w_cross, w_in, ffn_shard, cot_block, vecs, picks, scale):
    count, width = values.base.shape
    heads = values.mixed.shape[1]
    pairs = heads // LANES
    hidden = values.hid.shape[1]
    quarter = count // 2
    half = width // 2
    chunk = quarter // CHUNKS
    assert chunk * CHUNKS == quarter
    shapes = [(1, 2, hidden // 2, width), (1, 2, hidden // 2, width), (4, 2, heads // 2, width)]
    rows = ffn_shard.shape[1]
    pieces = [(0, 0, 0, 1, at, rows // 4, 1, False) for at in range(0, rows, rows // 4)]
    red_pieces = []
    for i, g in enumerate(shapes[:2]):
        cut = g[2] if g[2] <= 192 else g[2] // 4
        red_pieces += [(i, a, at, cut) for a in range(g[0]) for at in range(0, g[2], cut)]
    n, m = len(pieces), len(red_pieces)
    hbm = pl.BlockSpec(memory_space=pltpu.HBM)
    vmem = pl.BlockSpec(memory_space=pltpu.VMEM)
    dma = pltpu.SemaphoreType.DMA
    low, wide = (count, width), (count, heads)
    scratch = [pltpu.VMEM(ffn_shard.shape, BF16), dma((n, 5)), dma((n, 4)), dma((1, 2)), dma, dma]
    scratch += [pltpu.VMEM((1,) + cot_block.shape, BF16), dma((1, 2)), dma((1, 2)), dma((1, 2))]
    scratch += [
        pltpu.VMEM((2,) + low, BF16),
        pltpu.VMEM((2,) + wide, BF16),
        pltpu.VMEM((2,) + wide, BF16),
        pltpu.VMEM((4, 2, heads // 2, width), BF16),
        pltpu.VMEM((1, 2, width, hidden // 2), BF16),
        pltpu.VMEM((1, 2, hidden // 2, width), BF16),
        pltpu.VMEM(low, BF16),
        pltpu.VMEM(wide, BF16),
        pltpu.VMEM(wide, BF16),
        pltpu.VMEM((2, pairs, 8, 2 * count), F32),
        pltpu.VMEM(low, F32),
        pltpu.VMEM(low, F32),
        pltpu.VMEM(low, BF16),
        pltpu.VMEM(low, F32),
        pltpu.VMEM((count, hidden), BF16),
        pltpu.VMEM(low, F32),
        pltpu.VMEM((2, count, hidden // 2), BF16),
        pltpu.VMEM(low, BF16),
        pltpu.VMEM(wide, BF16),
        pltpu.VMEM(wide, BF16),
        pltpu.VMEM((2,) + wide, BF16),
        pltpu.VMEM((2,) + wide, BF16),
        pltpu.VMEM((count, LANES), F32),
        pltpu.VMEM(low, BF16),
        pltpu.VMEM((3,) + low, BF16),
        pltpu.VMEM((3,) + low, BF16),
        pltpu.VMEM((2,) + low, BF16),
        pltpu.VMEM((2, quarter, width), BF16),
        pltpu.VMEM((3, quarter, width), BF16),
        pltpu.VMEM(low, BF16),
        pltpu.VMEM((quarter, width), BF16),
    ]
    scratch += [pltpu.VMEM(g, BF16) for g in shapes]
    scratch += [pltpu.VMEM(g[:3] + (half,), BF16) for g in shapes[:2]]
    scratch += [pltpu.VMEM((2, g[0], g[2], half), BF16) for g in shapes[:2]]
    scratch += [dma((m,)), dma((m,)), dma((m, 2)), dma((m, 2)), dma((m,)), dma((m,))]
    scratch += [
        dma((5,)),
        dma((3,)),
        dma((4, 2)),
        dma((CHUNKS, 2)),
        dma((CHUNKS, 2)),
        dma((2, CHUNKS, 2)),
        dma((2, 2)),
        dma((CHUNKS, 2)),
        dma((CHUNKS, 2)),
        dma((CHUNKS, 2)),
        dma((2,)),
    ]
    out_shape = [
        jax.ShapeDtypeStruct(low, F32),
        jax.ShapeDtypeStruct(low, F32),
        jax.ShapeDtypeStruct((16, width), F32),
        jax.ShapeDtypeStruct((quarter, width), BF16),
        jax.ShapeDtypeStruct(shapes[2], BF16),
    ]
    out_shape += [jax.ShapeDtypeStruct((g[0], g[2], half), BF16) for g in shapes[:2]]
    args = [values.act_three, values.x1, values.query, w_cross, w_in]
    return pl.pallas_call(
        functools.partial(mid_kernel, tuple(pieces), tuple(red_pieces), pairs, scale),
        in_specs=[hbm] * 8 + [vmem] * 7,
        out_specs=[hbm, hbm, vmem, hbm, hbm] + [vmem] * 2,
        out_shape=out_shape,
        scratch_shapes=scratch,
        compiler_params=pltpu.CompilerParams(
            collective_id=2, has_side_effects=True, vmem_limit_bytes=TAIL_LIMIT
        ),
        name="middle",
    )(*args, ffn_shard, cot_block, values.base, *vecs, picks)


def finish_kernel(*refs):
    it = iter(refs)
    s_in, s_mlp, s_out, s_qkv, t_in, t_mlp, t_cross, from_text, total = (next(it) for _ in range(9))
    rows_in = [next(it) for _ in range(2)]
    rows_out = [next(it) for _ in range(2)]
    o_qkv, o_out, o_in, o_mlp, o_cross, o_qv, o_outb, o_inb, o_mlpb, o_gain, o_shift = (next(it) for _ in range(11))
    held = [next(it) for _ in range(2)]
    b_in, b_mlp, b_out, b_qkv, b_cross, sem = it
    tower, dp, z, core, line, other, partner = spots()

    def bring(i, image_src, text_src, target):
        @pl.when(tower == 0)
        def _():
            pltpu.make_async_copy(image_src, target, sem.at[i]).start()

        @pl.when(tower == 1)
        def _():
            pltpu.make_async_copy(text_src, target, sem.at[i]).start()

    bring(0, s_in, t_in, b_in)
    bring(1, s_mlp, t_mlp, b_mlp)
    bring(2, s_out, s_out, b_out)
    bring(3, s_qkv, s_qkv, b_qkv)
    bring(4, from_text, t_cross.at[pl.ds(2, 2)], b_cross)
    for i in range(2):
        pltpu.make_async_copy(rows_in[i], held[i], sem.at[5 + i]).start()

    width = total.shape[2]
    heads = width // 2
    first = total[0]
    o_outb[...] = first[0:1, :]
    o_mlpb[...] = first[1:2, :]
    o_gain[0] = first[2:5, :]
    o_shift[0] = first[5:8, :]
    for side in range(2):
        lanes = slice(side * heads, (side + 1) * heads)
        o_qv[0, 0:1, lanes] = total[side, 8:9, :heads]
        o_qv[0, 1:2, lanes] = total[side, 8:9, heads:]
        for b in range(2):
            at = (2 * side + b) * width
            o_inb[0:1, at : at + width] = total[side, 9 + b : 10 + b, :]

    def mine(block):
        cut = block.shape[1] // 2
        wide = block.astype(F32)
        return jnp.where(core == 0, wide[:, :cut], wide[:, cut:])

    for i in range(2):
        pltpu.make_async_copy(rows_in[i], held[i], sem.at[5 + i]).wait()
        pltpu.make_async_copy(held[i], rows_out[i].at[0], sem.at[7 + i]).start()
    pltpu.make_async_copy(s_in, b_in, sem.at[0]).wait()
    part = b_in.shape[1] // 2
    for i in range(2):
        o_in[0, :, i * part : (i + 1) * part] = mine(b_in[0, i * part : (i + 1) * part, :]).T
    pltpu.make_async_copy(s_mlp, b_mlp, sem.at[1]).wait()
    o_mlp[0] = mine(b_mlp[0])
    pltpu.make_async_copy(s_out, b_out, sem.at[2]).wait()
    o_out[0] = mine(b_out[0])
    pltpu.make_async_copy(s_qkv, b_qkv, sem.at[3]).wait()
    for a in range(3):
        o_qkv[0, a] = mine(b_qkv[a]).T
    pltpu.make_async_copy(from_text, b_cross, sem.at[4]).wait()
    for a in range(2):
        o_cross[0, a] = mine(b_cross[a]).T
    for i in range(2):
        pltpu.make_async_copy(held[i], rows_out[i].at[0], sem.at[7 + i]).wait()


def finish(sums, text, total, token_rows):
    s_in, s_mlp, s_out, s_qkv = sums
    t_in, t_mlp, t_cross, from_text = text
    hbm = pl.BlockSpec(memory_space=pltpu.HBM)
    vmem = pl.BlockSpec(memory_space=pltpu.VMEM)
    struct = jax.ShapeDtypeStruct
    width = total.shape[2]
    ffn, half = s_in.shape[1:]
    cut = half // 2
    cols = s_out.shape[1]
    out_shape = [struct((1,) + x.shape, BF16) for x in token_rows]
    out_shape += [
        struct((1, 3, cut, cols), F32),
        struct((1, cols, cut), F32),
        struct((1, cut, ffn), F32),
        struct((1, ffn, cut), F32),
        struct((1, 2, cut, cols), F32),
        struct((1, 2, width), F32),
        struct((1, width), F32),
        struct((1, 4 * width), F32),
        struct((1, width), F32),
        struct((1, 3, width), F32),
        struct((1, 3, width), F32),
    ]
    scratch = [pltpu.VMEM(x.shape, BF16) for x in token_rows]
    scratch += [pltpu.VMEM(x.shape, BF16) for x in (s_in, s_mlp, s_out, s_qkv, from_text)]
    scratch += [pltpu.SemaphoreType.DMA((9,))]
    return pl.pallas_call(
        finish_kernel,
        in_specs=[hbm] * 8 + [vmem] + [hbm] * 2,
        out_specs=[hbm] * 2 + [vmem] * 11,
        out_shape=out_shape,
        scratch_shapes=scratch,
        compiler_params=pltpu.CompilerParams(vmem_limit_bytes=VMEM_LIMIT),
        name="finish",
    )(s_in, s_mlp, s_out, s_qkv, t_in, t_mlp, t_cross, from_text, total, *token_rows)


def split_heads(flat):
    return jnp.swapaxes(flat.reshape(flat.shape[0], -1, HDIM), 0, 1)


def join_heads(split):
    return jnp.swapaxes(split, 0, 1).reshape(split.shape[1], -1)


def batch_dot(left, right, left_dim, right_dim):
    return lax.dot_general(left, right, (((left_dim,), (right_dim,)), ((0,), (0,))), preferred_element_type=F32)


def attend_plain(queries, keys, vals, allowed, scale):
    queries, keys, vals = (split_heads(x) for x in (queries, keys, vals))
    scores = jnp.where(allowed, batch_dot(queries, keys, 2, 2) * scale, NEG)
    top = jnp.max(scores, axis=-1, keepdims=True)
    tops = top + jnp.log(jnp.sum(jnp.exp(scores - top), axis=-1, keepdims=True))
    weights = jnp.exp(scores - tops).astype(BF16)
    return (join_heads(batch_dot(weights, vals, 2, 1)).astype(BF16), tops)


def attend_back_plain(queries, keys, vals, grads, tops, allowed, scale):
    queries, keys, vals, grads = (split_heads(x) for x in (queries, keys, vals, grads))
    scores = jnp.where(allowed, batch_dot(queries, keys, 2, 2) * scale, NEG)
    weights = jnp.exp(scores - tops)
    grad_w = batch_dot(grads, vals, 2, 2)
    grad_s = (weights * (grad_w - jnp.sum(weights * grad_w, axis=-1, keepdims=True))).astype(BF16)
    return (
        join_heads(batch_dot(grad_s, keys, 2, 1) * scale).astype(BF16),
        join_heads(batch_dot(grad_s, queries, 1, 1) * scale).astype(BF16),
        join_heads(batch_dot(weights.astype(BF16), grads, 1, 1)).astype(BF16),
    )


def gather_plain(shards):
    core = lax.rem(lax.axis_index(DP), 2)
    outs = []
    for i, s in enumerate(shards):
        if i == 2:
            s = jnp.concatenate([lax.ppermute(s, TOWER, [(0, 1)]), s], axis=0)
        full = lax.all_gather(s, MP, axis=1, tiled=False)
        outs.append(lax.dynamic_slice_in_dim(full, 2 * core, 2, 1))
    return outs


def reduce_plain(grads, smalls):
    dp = lax.axis_index(DP)
    core = lax.rem(dp, 2)
    outs = []
    for g in grads:
        n, _, rows, wide = g.shape
        full = jnp.zeros((n, 4, rows, wide), BF16)
        full = lax.dynamic_update_slice(full, g, (0, 2 * core, 0, 0))
        part = lax.psum_scatter(full, MP, scatter_dimension=1, tiled=False)
        part = lax.psum_scatter(part, DP, scatter_dimension=2, tiled=True)
        outs.append(part)
    if smalls is None:
        return outs
    both = jnp.zeros((2,) + smalls.shape, F32)
    both = lax.dynamic_update_slice(both, smalls[None], (core, 0, 0))
    return outs + [lax.psum(both, (DP, MP))]


def body(
    tower_in,
    out_cot,
    segment_ids,
    row_image,
    attn_qkv,
    attn_out,
    mlp_in,
    mlp_out,
    cross_proj,
    qv_bias,
    out_bias,
    mlp_bias_in,
    mlp_bias_out,
    norm_gain,
    norm_bias,
):
    lines = lax.axis_size(DP) // 2
    depth = lax.axis_size(MP)
    devices = lax.axis_size(DP)
    is_enc = lax.axis_index(TOWER) == 0
    dp = lax.axis_index(DP)
    z = lax.axis_index(MP)
    core = lax.rem(dp, 2)
    side = lax.rem(z, 2)
    group = z // 2
    direct = lines == 2
    assert depth == 4
    quarter = tower_in.shape[1]
    tokens = 2 * quarter
    assert tokens == PATCH
    width = tower_in.shape[2]
    head_cols = 2 * attn_qkv.shape[3]
    hidden = 2 * mlp_in.shape[2]
    scale_qk = HDIM ** (-0.5)

    out_moves, back_moves = [], []
    for d in range(devices):
        for place in range(depth):
            here = d * depth + place
            there = (d - d % 2 + place % 2) * depth + 2 * (d % 2) + place // 2
            out_moves.append((here, there))
            back_moves.append((there, here))

    def swap_cores(x):
        return lax.ppermute(x, DP, [(i, i ^ 1) for i in range(devices)])

    def both_cores(own):
        other = swap_cores(own)
        return jnp.where(core == 0, jnp.concatenate([own, other], -2), jnp.concatenate([other, own], -2))

    def own_rows(full):
        return lax.dynamic_slice_in_dim(full, core * quarter, quarter, full.ndim - 2)

    def lowered(part):
        return lax.reduce_precision(part, 8, 7).astype(BF16)

    def add_lowered(low):
        return low.astype(F32) + swap_cores(low).astype(F32)

    def add_cores(part):
        return add_lowered(lowered(part))

    def only_image(run, *operands):
        def idle(*inputs):
            return jax.tree.map(lambda x: jnp.zeros(x.shape, x.dtype), jax.eval_shape(run, *inputs))

        return lax.cond(is_enc, run, idle, *operands)

    shards = [
        jnp.swapaxes(attn_qkv[0], 1, 2),
        attn_out,
        jnp.swapaxes(cross_proj[0], 1, 2),
        mlp_in,
        mlp_out,
    ]
    rows = segment_ids.shape[0] // 2

    bias_qv = lax.dynamic_slice_in_dim(qv_bias[0], core * head_cols, head_cols, 1)
    bias_packed = jnp.concatenate([bias_qv[0], jnp.zeros_like(bias_qv[0]), bias_qv[1]])
    bias_in = lax.dynamic_slice_in_dim(mlp_bias_in[0], core * hidden, hidden, 0)
    gains = norm_gain[0]
    shifts = norm_bias[0]

    def feed_forward(values):
        act = norm_rows(values, gains[1], shifts[1]).astype(BF16)
        pre = jnp.concatenate([dot_plain(act, w_in[0]), dot_plain(act, w_in[1])], axis=1) + bias_in
        hid = gelu_tanh(pre).astype(BF16)
        return (act, pre, hid, lowered(dot_plain(hid, w_mlp)))

    if direct:
        vecs = (gains, shifts, out_bias, mlp_bias_out, mlp_bias_in, qv_bias[0])
        gathered, stream_low, notes, first = head(
            shards, [tower_in[0]], segment_ids, row_image, vecs, scale_qk
        )
        seg_col, seg_row, picks = notes
    else:
        gathered = gather_plain(shards)
        stream_low = both_cores(lax.ppermute(tower_in[0], (DP, MP), out_moves))
        cot_low = both_cores(lax.ppermute(out_cot[0], (DP, MP), out_moves))
        segs = jnp.where(core == group, segment_ids, swap_cores(segment_ids))
        segs = lax.dynamic_slice_in_dim(segs, rows * side, rows, 0)
        marks = (segs + LTXT * jnp.arange(rows, dtype=jnp.int32)[:, None]).reshape(tokens)
        images_of = jnp.where(core == group, row_image, swap_cores(row_image))
        images_of = jnp.repeat(lax.dynamic_slice_in_dim(images_of, rows * side, rows, 0), LTXT)
        places = jnp.arange(tokens)
        allowed = (places[None, :] <= places[:, None]) & (marks[None, :] == marks[:, None])
        allowed = jnp.logical_or(allowed, is_enc)
        sees = images_of[:, None] == jnp.arange(2 * tokens)[None, :] // tokens
    w_qkv = gathered[0].reshape(3 * head_cols, width)
    w_out = gathered[1].reshape(head_cols, width)
    w_cross = gathered[2].reshape(4, head_cols, width)
    w_in = gathered[3][0]
    w_mlp = gathered[4].reshape(hidden, width)
    stream = stream_low.astype(F32)

    if not direct:
        act_one = norm_rows(stream, gains[0], shifts[0]).astype(BF16)
        packed = (dot_rows(act_one, w_qkv) + bias_packed).astype(BF16)
        parts = [packed[:, i * head_cols : (i + 1) * head_cols] for i in range(3)]
        mixed, tops = attend_plain(*parts, allowed, scale_qk)
        stream_one = stream + add_cores(dot_plain(mixed, w_out)) + out_bias[0]
        act_enc, pre_enc, hid_enc, part_enc = feed_forward(stream_one)
        out_enc = stream_one + add_lowered(part_enc) + mlp_bias_out[0]
        base_three = jnp.where(is_enc, out_enc, stream_one)
        act_three = norm_rows(base_three, gains[2], shifts[2]).astype(BF16)
        cross_q = dot_rows(act_three, w_cross[2]).astype(BF16)

    if direct:
        back_in_three, upstream, smalls, tower_out, g_cross, t_in, t_mlp = middle(
            first, gathered[2], gathered[3], mlp_out, out_cot[0], vecs, picks, scale_qk
        )
        values = Tail(
            d_three=back_in_three,
            base=first.base,
            upstream=upstream,
            gains=gains,
            smalls=smalls,
            w_mlp=w_mlp,
            pre=first.pre,
            hid=first.hid,
            act=first.act,
            w_in=w_in,
            x1=first.x1,
            w_out=w_out,
            mixed=first.mixed,
            packed=first.packed,
            tops=first.tops,
            seg_col=seg_col,
            seg_row=seg_row,
            a_one=first.a_one,
            w_qkv=w_qkv,
            x0=stream_low,
        )
        *sums, t_cross, total, grad_in, from_text = tail(values, g_cross, scale_qk)
        return finish(sums, [t_in, t_mlp, t_cross, from_text], total, [tower_out, grad_in])
    else:
        near_half = lax.ppermute(own_rows(act_three), TOWER, [(0, 1)])
        far_half = lax.ppermute(near_half, MP, [(i, i ^ 1) for i in range(depth)])
        halves = jnp.where(side == 0, jnp.stack([near_half, far_half]), jnp.stack([far_half, near_half]))
        images = both_cores(halves)

        flat_images = images.reshape(2 * tokens, width)
        cross_k = dot_rows(flat_images, w_cross[0]).astype(BF16)
        cross_v = dot_rows(flat_images, w_cross[1]).astype(BF16)
        cross_mix, cross_tops = attend_plain(cross_q, cross_k, cross_v, sees, scale_qk)
        stream_two = stream_one + add_cores(dot_plain(cross_mix, w_cross[3]))

        act_dec, pre_dec, hid_dec, part_dec = feed_forward(stream_two)
        out_dec = stream_two + add_lowered(part_dec) + mlp_bias_out[0]
        tower_rows = own_rows(jnp.where(is_enc, base_three, out_dec).astype(BF16))

        def feed_back(grad_low, pre):
            grad_hid = dot_rows(grad_low, w_mlp)
            _, pullback = jax.vjp(gelu_tanh, pre)
            grad_pre = pullback(grad_hid)[0].astype(BF16)
            cols = hidden // 2
            part = dot_rows(grad_pre[:, :cols], w_in[0]) + dot_rows(grad_pre[:, cols:], w_in[1])
            return (grad_pre, lowered(part))

        def feed_grads(grad_low, act, grad_pre, hid):
            g_in = dot_first(grad_pre, act).astype(BF16)
            g_mlp = dot_first(hid, grad_low).astype(BF16)
            return (
                g_in.reshape(1, 2, hidden // 2, width),
                g_mlp.reshape(1, 2, hidden // 2, width),
            )

        cot = cot_low.astype(F32)
        grad_pre_dec, back_in = feed_back(cot_low, pre_dec)
        back_a, gain_a, shift_a = norm_back(stream_two, gains[1], add_lowered(back_in))
        grad_two = cot + back_a
        grad_two_low = grad_two.astype(BF16)

        grad_mix = dot_rows(grad_two_low, w_cross[3]).astype(BF16)
        grad_q, flat_k, flat_v = attend_back_plain(
            cross_q, cross_k, cross_v, grad_mix, cross_tops, sees, scale_qk
        )
        part_images = dot_plain(flat_k, w_cross[0]) + dot_plain(flat_v, w_cross[1])
        part_low = part_images.astype(BF16).reshape(2, 2, quarter, width)
        give = lax.dynamic_index_in_dim(part_low, 1 - core, 1, keepdims=False)
        keep = lax.dynamic_index_in_dim(part_low, core, 1, keepdims=False)
        pair_sum = (keep.astype(F32) + swap_cores(give).astype(F32)).astype(BF16)
        give = lax.dynamic_index_in_dim(pair_sum, 1 - side, 0, keepdims=False)
        keep = lax.dynamic_index_in_dim(pair_sum, side, 0, keepdims=False)
        got = lax.ppermute(give, MP, [(i, i ^ 1) for i in range(depth)])
        image_sum = (keep.astype(F32) + got.astype(F32)).astype(BF16)
        image_half = lax.ppermute(image_sum, TOWER, [(1, 0)])
        later = lax.optimization_barrier(
            (cot_low, act_dec, grad_pre_dec, hid_dec, flat_k, flat_v, grad_q, cross_mix, image_sum)
        )
        g_in_dec, g_mlp_dec = feed_grads(later[0], later[1], later[2], later[3])
        g_cross = jnp.concatenate(
            [
                dot_first(later[4], flat_images).astype(BF16),
                dot_first(later[5], flat_images).astype(BF16),
                dot_first(later[6], act_three).astype(BF16),
                dot_first(later[7], grad_two_low).astype(BF16),
            ],
            axis=0,
        ).reshape(4, 2, head_cols // 2, width)
        image_back = both_cores(image_half).astype(F32)
        query_back = add_cores(dot_plain(grad_q, w_cross[2]))
        back_in_three = jnp.where(is_enc, image_back, query_back)
        text_smalls = (
            jnp.zeros((16, width), F32)
            .at[1]
            .set(jnp.sum(cot_low, axis=0, dtype=F32))
            .at[3]
            .set(gain_a)
            .at[6]
            .set(shift_a)
            .at[9:11]
            .set(jnp.sum(grad_pre_dec, axis=0, dtype=F32).reshape(2, width))
        )
        smalls = jnp.where(is_enc, 0.0, text_smalls)
        tower_out = lax.ppermute(tower_rows, (DP, MP), back_moves)
        back_three, gain_three, shift_three = norm_back(
            base_three, gains[2], back_in_three
        )
        grad_enc = cot + back_three
        grad_enc_low = grad_enc.astype(BF16)

        grad_pre_enc, back_in = feed_back(grad_enc_low, pre_enc)
        g_in, g_mlp = feed_grads(grad_enc_low, act_enc, grad_pre_enc, hid_enc)
        back_b, gain_b, shift_b = norm_back(stream_one, gains[1], add_lowered(back_in))
        grad_one = jnp.where(is_enc, grad_enc + back_b, grad_two + back_three)
        grad_one_low = grad_one.astype(BF16)

        g_out = dot_first(mixed, grad_one_low).astype(BF16).reshape(1, 2, head_cols // 2, width)
        grad_mixed = dot_rows(grad_one_low, w_out).astype(BF16)
        grad_packed = jnp.concatenate(
            attend_back_plain(*parts, grad_mixed, tops, allowed, scale_qk), axis=1
        )
        g_qkv = dot_first(grad_packed, act_one).astype(BF16).reshape(3, 2, head_cols // 2, width)
        back_in = add_cores(dot_plain(grad_packed, w_qkv))
        back_one, gain_one, shift_one = norm_back(stream, gains[0], back_in)
        grad_in = own_rows((grad_one + back_one).astype(BF16))
        grad_in = lax.ppermute(grad_in, (DP, MP), back_moves)

        grad_pre_sum = jnp.sum(grad_pre_enc, axis=0, dtype=F32).reshape(2, width)
        packed_sum = jnp.sum(grad_packed, axis=0, dtype=F32)
        smalls = jnp.concatenate(
            [
                jnp.sum(grad_one_low, axis=0, dtype=F32)[None],
                jnp.where(is_enc, jnp.sum(grad_enc_low, axis=0, dtype=F32), smalls[1])[None],
                gain_one[None],
                jnp.where(is_enc, gain_b, smalls[3])[None],
                gain_three[None],
                shift_one[None],
                jnp.where(is_enc, shift_b, smalls[6])[None],
                shift_three[None],
                jnp.concatenate([packed_sum[:head_cols], packed_sum[2 * head_cols :]])[None],
                jnp.where(is_enc, grad_pre_sum, smalls[9:11]),
                smalls[11:],
            ]
        )
        g_in = jnp.where(is_enc, g_in, g_in_dec)
        g_mlp = jnp.where(is_enc, g_mlp, g_mlp_dec)
        s_in, s_mlp, s_out, s_qkv, s_cross, total = reduce_plain([g_in, g_mlp, g_out, g_qkv, g_cross], smalls)
        s_cross = jnp.where(is_enc, lax.ppermute(s_cross[:2], TOWER, [(1, 0)]), s_cross[2:])

    def turned(x):
        return jnp.swapaxes(x, 1, 2).astype(F32)

    cross_pair = jnp.stack(
        [
            s_cross[0].T,
            s_cross[1].T,
        ]
    ).astype(F32)
    first = total[0]
    qv_total = jnp.stack(
        [
            total[:, 8, :head_cols].reshape(-1),
            total[:, 8, head_cols:].reshape(-1),
        ]
    )
    in_total = total[:, 9:11].reshape(-1)
    return (
        tower_out[None],
        grad_in[None],
        turned(s_qkv)[None],
        s_out.astype(F32),
        turned(s_in),
        s_mlp.astype(F32),
        cross_pair[None],
        qv_total[None],
        first[0:1],
        in_total[None],
        first[1:2],
        first[2:5][None],
        first[5:8][None],
    )


def solution(mesh):
    return jax.shard_map(
        body,
        mesh=mesh,
        in_specs=(
            P(TOWER, (DP, MP), None),
            P(TOWER, (DP, MP), None),
            P(DP, None),
            P(DP),
            P(TOWER, None, None, MP),
            P(TOWER, MP, None),
            P(TOWER, None, MP),
            P(TOWER, MP, None),
            P(TOWER, None, None, MP),
            P(TOWER, None, None),
            P(TOWER, None),
            P(TOWER, None),
            P(TOWER, None),
            P(TOWER, None, None),
            P(TOWER, None, None),
        ),
        out_specs=(
            P(TOWER, (DP, MP), None),
            P(TOWER, (DP, MP), None),
            P(TOWER, None, DP, MP),
            P(TOWER, MP, DP),
            P(TOWER, DP, MP),
            P(TOWER, MP, DP),
            P(TOWER, None, DP, MP),
            P(TOWER, None, None),
            P(TOWER, None),
            P(TOWER, None),
            P(TOWER, None),
            P(TOWER, None, None),
            P(TOWER, None, None),
        ),
        check_vma=False,
    )
```

```python
import functools
from typing import Any, NamedTuple

import jax
import jax.numpy as jnp
from jax import lax
from jax.experimental import pallas as pl
from jax.experimental.pallas import tpu as pltpu
from jax.sharding import PartitionSpec as P

TOWER = "tower"
DP = "dp"
MP = "mp"
HDIM = 64
PATCH = 576
LTXT = 64
EPS = 1e-06
NEG = -1e30
LANES = 128
MESH = pl.DeviceIdType.MESH
F32 = jnp.float32
BF16 = jnp.bfloat16
VMEM_LIMIT = 60 * 1024 * 1024
TAIL_LIMIT = 67043328


def norm_parts(values):
    center = values - jnp.mean(values, axis=-1, keepdims=True)
    spread = jnp.mean(center * center, axis=-1, keepdims=True)
    scale = lax.rsqrt(spread + EPS)
    return (center * scale, scale)


def norm_rows(values, gain_vec, shift_vec):
    unit, _ = norm_parts(values)
    return unit * gain_vec + shift_vec


def norm_back(values, gain_vec, grad_normed):
    unit, scale = norm_parts(values)
    inner = grad_normed * gain_vec
    mean_one = jnp.mean(inner, axis=-1, keepdims=True)
    mean_two = jnp.mean(inner * unit, axis=-1, keepdims=True)
    back = (inner - mean_one - unit * mean_two) * scale
    return (back, jnp.sum(grad_normed * unit, axis=0), jnp.sum(grad_normed, axis=0))


def gelu_tanh(values):
    return jax.nn.gelu(values, approximate=True)


def dot_rows(left, right):
    return lax.dot_general(left, right, (((1,), (1,)), ((), ())), preferred_element_type=F32)


def dot_first(left, right):
    return lax.dot_general(left, right, (((0,), (0,)), ((), ())), preferred_element_type=F32)


def dot_plain(left, right):
    return lax.dot_general(left, right, (((1,), (0,)), ((), ())), preferred_element_type=F32)


def spots():
    tower = lax.axis_index(TOWER)
    dp = lax.axis_index(DP)
    z = lax.axis_index(MP)
    core = lax.rem(dp, 2)
    line = dp // 2
    return tower, dp, z, core, line, dp + 2 - 4 * line, dp + 1 - 2 * core


def greet(target):
    pl.semaphore_signal(pltpu.get_barrier_semaphore(), inc=1, device_id=target, device_id_type=MESH)


def weight_steps(pieces, srcs, outs, stages, sems):
    send_sem, recv_sem, local_sem, twin_send, twin_recv = sems
    tower, dp, z, core, line, other, partner = spots()
    place = z + core * (3 - 2 * z)
    ahead = z + 1 - 2 * core
    behind = z - 1 + 2 * core
    slot_of = (core, 1 - core)
    holder = place <= 1
    far_src = [k for k, p in enumerate(pieces) if p[7]]

    def spot(piece, slot, half):
        which, first, _, count, start, size, _, _ = piece
        part = size // 2
        return outs[which].at[pl.ds(first, count), slot, pl.ds(start + half * part, part), :]

    def own(piece):
        which, _, first, count, start, size, _, far = piece
        part = size // 2
        if far:
            return spot(piece, lax.rem(z, 2), line)
        return srcs[which].at[pl.ds(first, count), pl.ds(start + line * part, part), :]

    def move(k, source, slot, half, kind, arrive, target):
        return pltpu.make_async_remote_copy(
            src_ref=source,
            dst_ref=spot(pieces[k], slot, half),
            send_sem=send_sem.at[k, kind],
            recv_sem=recv_sem.at[k, arrive],
            device_id=target,
            device_id_type=MESH,
        )

    def twin_copy():
        which = pieces[far_src[0]][0]
        return pltpu.make_async_remote_copy(
            src_ref=srcs[which],
            dst_ref=outs[which].at[pl.ds(0, srcs[which].shape[0]), lax.rem(z, 2)],
            send_sem=twin_send,
            recv_sem=twin_recv,
            device_id={TOWER: 1 - tower},
            device_id_type=MESH,
        )

    def local_in(i):
        return pltpu.make_async_copy(srcs[i], stages[i], local_sem.at[i, 0])

    def local_out(i):
        first = outs[i].shape[0] - srcs[i].shape[0]
        return pltpu.make_async_copy(
            stages[i], outs[i].at[pl.ds(first, srcs[i].shape[0]), lax.rem(z, 2)], local_sem.at[i, 1]
        )

    def gate(piece, cond):
        return cond if piece[6] is None else jnp.logical_and(cond, tower == piece[6])

    def send_own(k):
        piece = pieces[k]

        @pl.when(gate(piece, place == 0))
        def _():
            move(k, own(piece), slot_of[0], line, 0, 0, {MP: ahead}).start()

        @pl.when(gate(piece, place == 1))
        def _():
            move(k, own(piece), slot_of[1], line, 1, 1, {MP: ahead}).start()
            move(k, own(piece), slot_of[1], line, 2, 1, {MP: behind}).start()

    orders = {t: [k for k, p in enumerate(pieces) if p[6] in (None, t)] for t in (0, 1)}

    def launch(t, place):
        if place >= len(orders[t]):
            return
        k = orders[t][place]

        @pl.when(jnp.logical_and(holder, tower == t))
        def _():
            if far_src and k == far_src[0]:
                twin_copy().wait_recv()
            send_own(k)

    def own_sent(k):
        piece = pieces[k]

        @pl.when(gate(piece, place == 0))
        def _():
            move(k, own(piece), slot_of[0], line, 0, 0, {MP: z}).wait_send()

        @pl.when(gate(piece, place == 1))
        def _():
            move(k, own(piece), slot_of[1], line, 1, 1, {MP: z}).wait_send()
            move(k, own(piece), slot_of[1], line, 2, 1, {MP: z}).wait_send()

    def begin():
        if far_src:

            @pl.when(jnp.logical_and(holder, tower == 0))
            def _():
                twin_copy().start()

        for t in (0, 1):
            for start in range(WINDOW):
                launch(t, start)

    def keeps(i):
        flags = {p[6] for p in pieces if p[0] == i}
        flag = None if len(flags) > 1 else flags.pop()
        return holder if flag is None else jnp.logical_and(holder, tower == flag)

    def begin_local():
        for i in range(len(srcs)):

            @pl.when(keeps(i))
            def _(i=i):
                local_in(i).start()

        for i in range(len(srcs)):

            @pl.when(keeps(i))
            def _(i=i):
                local_in(i).wait()
                local_out(i).start()

    def pass_on(k):
        piece = pieces[k]

        @pl.when(gate(piece, place >= 1))
        def _():
            here = spot(piece, slot_of[0], line)
            move(k, here, slot_of[0], line, 0, 0, {MP: z}).wait_recv()
            move(k, here, slot_of[0], line, 3, 2, {DP: other}).start()

        @pl.when(gate(piece, jnp.logical_and(place >= 1, place <= 2)))
        def _():
            here = spot(piece, slot_of[0], line)
            move(k, here, slot_of[0], line, 0, 0, {MP: ahead}).start()

        @pl.when(gate(piece, place != 1))
        def _():
            here = spot(piece, slot_of[1], line)
            move(k, here, slot_of[1], line, 1, 1, {MP: z}).wait_recv()
            move(k, here, slot_of[1], line, 4, 3, {DP: other}).start()

        @pl.when(gate(piece, place == 2))
        def _():
            here = spot(piece, slot_of[1], line)
            move(k, here, slot_of[1], line, 1, 1, {MP: ahead}).start()

        own_sent(k)
        for t in (0, 1):
            if k in orders[t]:
                launch(t, orders[t].index(k) + WINDOW)

    def arrived(k):
        piece = pieces[k]

        @pl.when(gate(piece, place >= 1))
        def _():
            move(k, spot(piece, slot_of[0], 1 - line), slot_of[0], 1 - line, 3, 2, {DP: dp}).wait_recv()

        @pl.when(gate(piece, place != 1))
        def _():
            move(k, spot(piece, slot_of[1], 1 - line), slot_of[1], 1 - line, 4, 3, {DP: dp}).wait_recv()

    def sent(k):
        piece = pieces[k]

        @pl.when(gate(piece, jnp.logical_or(place == 1, place == 2)))
        def _():
            move(k, spot(piece, slot_of[0], line), slot_of[0], line, 0, 0, {MP: z}).wait_send()

        @pl.when(gate(piece, place == 2))
        def _():
            move(k, spot(piece, slot_of[1], line), slot_of[1], line, 1, 1, {MP: z}).wait_send()

        @pl.when(gate(piece, place >= 1))
        def _():
            move(k, spot(piece, slot_of[0], line), slot_of[0], line, 3, 2, {DP: dp}).wait_send()

        @pl.when(gate(piece, place != 1))
        def _():
            move(k, spot(piece, slot_of[1], line), slot_of[1], line, 4, 3, {DP: dp}).wait_send()

    def end_local(i):
        @pl.when(keeps(i))
        def _():
            local_out(i).wait()

    def end_twin():
        @pl.when(jnp.logical_and(holder, tower == 0))
        def _():
            twin_copy().wait_send()

    return begin, begin_local, pass_on, arrived, sent, end_local, end_twin


def token_steps(blocks, outs, stage, sems):
    send_sem, recv_sem, local_sem = sems
    tower, dp, z, core, line, other, partner = spots()
    stays = z == 3 * core
    size = blocks[0].shape[0]

    def rows(which_core):
        return pl.ds(pl.multiple_of(which_core * size, 16), size)

    def away(i):
        target = {DP: 2 * line + lax.rem(z, 2), MP: 2 * core + z // 2}
        return pltpu.make_async_remote_copy(
            src_ref=blocks[i],
            dst_ref=outs[i].at[rows(lax.rem(z, 2)), :],
            send_sem=send_sem.at[i, 0],
            recv_sem=recv_sem.at[i, 0],
            device_id=target,
            device_id_type=MESH,
        )

    def across(i, which_core):
        return pltpu.make_async_remote_copy(
            src_ref=outs[i].at[rows(which_core), :],
            dst_ref=outs[i].at[rows(which_core), :],
            send_sem=send_sem.at[i, 1],
            recv_sem=recv_sem.at[i, 1],
            device_id={DP: partner},
            device_id_type=MESH,
        )

    def begin(i):
        @pl.when(jnp.logical_not(stays))
        def _():
            away(i).start()

        @pl.when(stays)
        def _():
            first = pltpu.make_async_copy(blocks[i], stage.at[i], local_sem.at[i, 0])
            first.start()
            first.wait()
            second = pltpu.make_async_copy(stage.at[i], outs[i].at[rows(core), :], local_sem.at[i, 1])
            second.start()
            second.wait()
            across(i, core).start()

    def relay(i):
        @pl.when(jnp.logical_not(stays))
        def _():
            away(i).wait_recv()
            across(i, core).start()

    def finish(i):
        across(i, 1 - core).wait_recv()
        across(i, core).wait_send()

        @pl.when(jnp.logical_not(stays))
        def _():
            away(i).wait_send()

    return begin, relay, finish


TILE = 32
LAG = 1
WINDOW = 2


def barrier_all(peers, options):
    for cond, target in peers:
        if cond is None:
            greet(target)
        else:
            pl.when(cond)(functools.partial(greet, target))
    for cond, count in options:

        @pl.when(cond)
        def _(count=count):
            pl.semaphore_wait(pltpu.get_barrier_semaphore(), count)


def fold_rows(tile):
    return jnp.sum(tile.reshape(tile.shape[0] // 8, 8, tile.shape[1]), axis=0)


def row_tiles(total, run, carry, first=0, unroll=1):
    tile = next(t for t, by in ((64, 192), (96, 96), (48, 48), (32, 32)) if total % by == 0)
    turns = total // tile

    def step(i, kept):
        return run(pl.ds(pl.multiple_of(first + i * tile, 16), tile), kept)

    return lax.fori_loop(0, turns, step, carry, unroll=unroll)


def norm_back_tile(values, gain, grads):
    unit, scale = norm_parts(values)
    inner = grads * gain
    mean_one = jnp.mean(inner, axis=-1, keepdims=True)
    mean_two = jnp.mean(inner * unit, axis=-1, keepdims=True)
    return ((inner - mean_one - unit * mean_two) * scale, fold_rows(grads * unit), fold_rows(grads))


def gelu_both(v):
    rate = 0.7978845608028654
    square = v * v
    bend = jnp.tanh(rate * (v + 0.044715 * (square * v)))
    lifted = 0.5 * (1.0 + bend)
    slope = lifted + 0.5 * v * (1.0 - bend * bend) * (rate * (1.0 + 3.0 * 0.044715 * square))
    return (v * lifted, slope)


def low_lanes_of(count):
    return lax.broadcasted_iota(jnp.int32, (count, LANES), 1) < HDIM


def stack_all(block, low):
    wide = block.astype(F32)
    return jnp.concatenate([jnp.where(low, wide, 0.0), jnp.where(low, 0.0, wide)], axis=0)


def merge_all(both, low):
    count = both.shape[0] // 2
    return jnp.where(low, both[:count], both[count:])


def lane_block(index):
    return pl.ds(pl.multiple_of(index * LANES, LANES), LANES)


def scores_of(keys, queries, mask):
    scores = dot_rows(keys, queries)
    if mask is None:
        return scores
    block = mask[...]
    return scores + jnp.concatenate([block, block], axis=1)


def forward_heads(queries, keys, vals, mask, low):
    scores = scores_of(keys, queries, mask)
    top = jnp.max(scores, axis=0, keepdims=True)
    grown = jnp.exp(scores - top)
    total = jnp.sum(grown, axis=0, keepdims=True)
    weights = (grown * (1.0 / total)).astype(BF16)
    return (merge_all(dot_first(weights, vals), low), top + jnp.log(total))


def backward_heads(queries, keys, vals, grads, tops, mask, low, scale):
    weights = jnp.exp(scores_of(keys, queries, mask) - tops)
    grad_w = dot_rows(vals, grads)
    row_dot = jnp.sum(weights * grad_w, axis=0, keepdims=True)
    grad_s = (weights * (grad_w - row_dot)).astype(BF16)
    grad_q = merge_all(dot_first(keys, grad_s).T, low) * scale
    return (grad_q, dot_plain(grad_s, queries), dot_plain(weights.astype(BF16), grads))


def fill_mask(mask, col, row, is_dec):
    count = mask.shape[0]

    def tile(rows, kept):
        shape = (rows.size, count)
        key_at = lax.broadcasted_iota(jnp.int32, shape, 0) + rows.start
        query_at = lax.broadcasted_iota(jnp.int32, shape, 1)
        allowed = jnp.logical_and(key_at <= query_at, col[rows, 0:1] == row[0:1, :])
        mask[rows, :] = jnp.where(jnp.logical_or(allowed, jnp.logical_not(is_dec)), 0.0, NEG)
        return kept

    row_tiles(count, tile, 0)


def self_forward(packed, mask, out, tops, pairs, scale):
    low = low_lanes_of(packed.shape[0])

    @pl.loop(0, pairs)
    def _(pair):
        queries = (stack_all(packed[:, lane_block(pair)], low) * scale).astype(BF16)
        mixed, top = forward_heads(
            queries, packed[:, lane_block(pairs + pair)], packed[:, lane_block(2 * pairs + pair)], mask, low
        )
        out[:, lane_block(pair)] = mixed.astype(BF16)
        tops[pair, 0:1, :] = top


def self_backward(packed, grads, tops, mask, out, pairs, scale, between):
    low = low_lanes_of(packed.shape[0])

    @pl.loop(0, pairs)
    def _(pair):
        queries = (stack_all(packed[:, lane_block(pair)], low) * scale).astype(BF16)
        head_grads = stack_all(grads[:, lane_block(pair)], low).astype(BF16)
        grad_q, grad_k, grad_v = backward_heads(
            queries,
            packed[:, lane_block(pairs + pair)],
            packed[:, lane_block(2 * pairs + pair)],
            head_grads,
            tops[pair, 0:1, :],
            mask,
            low,
            scale,
        )
        out[:, lane_block(pair)] = grad_q.astype(BF16)
        out[:, lane_block(pairs + pair)] = grad_k.astype(BF16)
        out[:, lane_block(2 * pairs + pair)] = grad_v.astype(BF16)
        pl.when(pair == 1)(between)


def cross_forward(image, query, keys, vals, picks, out, tops, pairs, scale):
    low = low_lanes_of(query.shape[0])

    @pl.loop(0, pairs)
    def _(pair):
        cols = lane_block(pair)
        queries = (stack_all(query[:, cols], low) * scale).astype(BF16)
        mixed, top = forward_heads(queries, keys[image, :, cols], vals[image, :, cols], None, low)
        kept = jnp.where(picks[...] == image, mixed, out[:, cols].astype(F32))
        out[:, cols] = kept.astype(BF16)
        tops[image, pair, 0:1, :] = top


def cross_backward(query, keys, vals, grads, picks, tops, dq, dk, dv, sum_q, pairs, scale):
    low = low_lanes_of(query.shape[0])

    @pl.loop(0, pairs)
    def _(pair):
        cols = lane_block(pair)
        queries = (stack_all(query[:, cols], low) * scale).astype(BF16)
        sum_q[...] = jnp.zeros_like(sum_q)

        @pl.loop(0, 2)
        def _(image):
            own = jnp.where(picks[...] == image, grads[:, cols].astype(F32), 0.0)
            grad_q, grad_k, grad_v = backward_heads(
                queries,
                keys[image, :, cols],
                vals[image, :, cols],
                stack_all(own, low).astype(BF16),
                tops[image, pair, 0:1, :],
                None,
                low,
                scale,
            )
            sum_q[...] += grad_q
            dk[image, :, cols] = grad_k.astype(BF16)
            dv[image, :, cols] = grad_v.astype(BF16)

        dq[:, cols] = sum_q[...].astype(BF16)


class Reducer:
    def __init__(self, grads, near, far, outs, sems, window, first, last):
        self.grads, self.near, self.far, self.outs = grads, near, far, outs
        self.y_send, self.y_recv, self.z_send, self.z_recv, self.c_send, self.c_recv = sems
        self.tower, self.dp, self.z, self.core, self.line, self.other, self.partner = spots()
        self.place = self.z + self.core * (3 - 2 * self.z)
        self.holder = self.place <= 1
        self.slot = lax.rem(self.z, 2)
        self.half = grads.shape[3] // 2
        self.rows = grads.shape[2]
        self.window, self.first, self.last = window, first, last

    def lanes(self, line):
        return pl.ds(pl.multiple_of(line * self.half, LANES), self.half)

    def to_line(self, k):
        return pltpu.make_async_remote_copy(
            src_ref=self.grads.at[k, :, :, self.lanes(1 - self.line)],
            dst_ref=self.near.at[k],
            send_sem=self.y_send.at[k],
            recv_sem=self.y_recv.at[k],
            device_id={DP: self.other},
            device_id_type=MESH,
        )

    def send(self, source, target, k, sent, got, where):
        return pltpu.make_async_remote_copy(
            src_ref=source,
            dst_ref=target,
            send_sem=self.z_send.at[k, sent],
            recv_sem=self.z_recv.at[k, got],
            device_id={MP: where},
            device_id_type=MESH,
        )

    def inward(self, k):
        return self.send(self.near.at[k], self.far.at[k], k, 0, 0, 2 - self.core)

    def beside(self, k):
        return self.send(self.near.at[k, 1 - self.slot], self.far.at[k, 0], k, 0, 0, 4 * self.core + 1 - self.z)

    def onward(self, k, shard):
        return self.send(self.near.at[k, shard], self.far.at[k, 1], k, shard, 1, 2 * self.core + shard)

    def to_core(self, k):
        return pltpu.make_async_remote_copy(
            src_ref=self.outs.at[k],
            dst_ref=self.outs.at[k],
            send_sem=self.c_send.at[k],
            recv_sem=self.c_recv.at[k],
            device_id={DP: self.partner},
            device_id_type=MESH,
        )

    def launch(self, k):
        self.to_line(k).start()

    def tiles(self, run):
        @pl.loop(0, self.rows // TILE)
        def _(i):
            run(pl.ds(pl.multiple_of(i * TILE, TILE), TILE))

    def add_near(self, k, more=True):
        self.to_line(k).wait_send()
        self.to_line(k).wait_recv()
        if more:
            pl.when(k + self.window < self.last)(lambda: self.launch(k + self.window))

        def run(rows):
            for b in range(2):
                total = self.grads[k, b, rows, self.lanes(self.line)].astype(F32) + self.near[k, b, rows, :].astype(F32)
                self.near[k, b, rows, :] = total.astype(BF16)

        self.tiles(run)
        pl.when(self.place == 3)(self.inward(k).start)
        pl.when(self.holder)(self.beside(k).start)

    def add_mid(self, k):
        @pl.when(self.place == 2)
        def _():
            self.inward(k).wait_recv()

            def run(rows):
                for b in range(2):
                    total = self.near[k, b, rows, :].astype(F32) + self.far[k, b, rows, :].astype(F32)
                    self.near[k, b, rows, :] = total.astype(BF16)

            self.tiles(run)
            for shard in range(2):
                self.onward(k, shard).start()

    def add_far(self, k):
        @pl.when(self.holder)
        def _():
            self.beside(k).wait_recv()
            self.onward(k, 0).wait_recv()

            def run(rows):
                total = self.near[k, self.slot, rows, :].astype(F32)
                for seat in range(2):
                    total = total + self.far[k, seat, rows, :].astype(F32)
                self.outs[k, rows, :] = total.astype(BF16)

            self.tiles(run)
            self.to_core(k).start()

    def step(self, k):
        self.add_near(k)
        pl.when(k - LAG >= self.first)(lambda: self.add_mid(k - LAG))

    def drain(self, begin):
        @pl.loop(begin, self.last + 2 * LAG)
        def _(i):
            pl.when(i < self.last)(lambda: self.add_near(i))
            j = i - LAG
            pl.when(jnp.logical_and(j >= self.first, j < self.last))(lambda: self.add_mid(j))
            n = j - LAG
            pl.when(jnp.logical_and(n >= begin - 2 * LAG, n >= self.first))(lambda: self.add_far(n))

    def far_before(self, begin):
        @pl.loop(self.first, jnp.maximum(self.first, begin - 2 * LAG))
        def _(k):
            self.add_far(k)

    def close(self):
        @pl.loop(self.first, self.last)
        def _(k):
            pl.when(self.place == 3)(self.inward(k).wait_send)

            @pl.when(self.place == 2)
            def _():
                for shard in range(2):
                    self.onward(k, shard).wait_send()

            @pl.when(self.holder)
            def _():
                self.beside(k).wait_send()
                self.to_core(k).wait_send()

            @pl.when(jnp.logical_not(self.holder))
            def _():
                self.to_core(k).wait_recv()


class Tail(NamedTuple):
    d_three: Any
    base: Any
    upstream: Any
    gains: Any
    smalls: Any
    hid: Any
    w_mlp: Any
    pre: Any
    act: Any
    w_in: Any
    x1: Any
    w_out: Any
    mixed: Any
    packed: Any
    tops: Any
    seg_col: Any
    seg_row: Any
    a_one: Any
    w_qkv: Any
    x0: Any


IMAGE_ONLY = Tail._fields[5:11]


def tail_kernel(pairs, scale, *refs):
    it = iter(refs)
    hbm = Tail(*[next(it) for _ in Tail._fields])
    cross_in = next(it)
    outs = next(it)
    small_out, grad_out, from_text = next(it), next(it), next(it)
    vm = Tail(*[next(it) for _ in Tail._fields])
    grads, near, far = next(it), next(it), next(it)
    g_f32, g_low, grad_hid, grad_pre, d_packed, mix_grad = (next(it) for _ in range(6))
    part_send, part_recv, mask, smalls, small_near, small_all, own_grad = (next(it) for _ in range(7))
    load_sem, red_sems, part_sem, small_sem, move_sem, twin_sem = next(it), [next(it) for _ in range(6)], next(it), next(it), next(it), next(it)
    tower, dp, z, core, line, other, partner = spots()
    is_enc = tower == 0
    is_dec = tower == 1
    stays = z == 3 * core
    tokens, width = g_f32.shape
    rows_txt = tokens // LTXT
    quarter = tokens // 2
    heads = mix_grad.shape[1]
    rows_of = grads.shape[2]
    ffn_blocks = width // rows_of

    home = {DP: 2 * line + z // 2, MP: 2 * lax.rem(z, 2) + core}
    guest = {DP: 2 * line + lax.rem(z, 2), MP: 2 * core + z // 2}
    moved = jnp.logical_not(stays)
    peers = [(None, {DP: other}), (None, {DP: partner}), (is_enc, {TOWER: 1 - tower})]
    peers += [(None, {MP: lax.rem(z + away, 4)}) for away in range(1, 4)]
    peers += [(moved, home), (moved, guest)]
    barrier_all(
        peers,
        [
            (jnp.logical_and(is_enc, stays), 5),
            (jnp.logical_and(is_enc, moved), 7),
            (jnp.logical_and(is_dec, stays), 6),
            (jnp.logical_and(is_dec, moved), 8),
        ],
    )

    def load(i):
        return pltpu.make_async_copy(hbm[i], vm[i], load_sem.at[i])

    def on_side(i, run):
        if Tail._fields[i] in IMAGE_ONLY:
            pl.when(is_enc)(run)
        else:
            run()

    pl.when(is_dec)(lambda: pltpu.make_async_copy(cross_in, grads.at[pl.ds(ffn_blocks, ffn_blocks)], load_sem.at[len(hbm)]).start())
    for i in range(len(hbm)):
        on_side(i, load(i).start)

    def need(*wanted):
        for i, ref in enumerate(vm):
            if any(ref is one for one in wanted):
                on_side(i, load(i).wait)

    first_block = ffn_blocks * tower
    blocks = grads.shape[0]
    red = Reducer(grads, near, far, outs, red_sems, 2, first_block, blocks)

    def twin_copy():
        return pltpu.make_async_remote_copy(
            src_ref=outs.at[pl.ds(ffn_blocks, 2)],
            dst_ref=from_text,
            send_sem=twin_sem.at[0],
            recv_sem=twin_sem.at[1],
            device_id={TOWER: 1 - tower},
            device_id_type=MESH,
        )

    cross_load = pltpu.make_async_copy(cross_in, grads.at[pl.ds(ffn_blocks, ffn_blocks)], load_sem.at[len(hbm)])

    @pl.when(is_dec)
    def _():
        cross_load.wait()
        red.launch(ffn_blocks)

    def home_move(source, target, k):
        return pltpu.make_async_remote_copy(
            src_ref=source,
            dst_ref=target,
            send_sem=move_sem.at[k, 0],
            recv_sem=move_sem.at[k, 1],
            device_id=home,
            device_id_type=MESH,
        )

    def part_copy(k):
        return pltpu.make_async_remote_copy(
            src_ref=part_send.at[k],
            dst_ref=part_recv.at[k],
            send_sem=part_sem.at[k, 0],
            recv_sem=part_sem.at[k, 1],
            device_id={DP: partner},
            device_id_type=MESH,
        )

    zero = jnp.zeros((8, width), F32)
    need(vm.d_three, vm.base, vm.upstream, vm.gains, vm.smalls)
    smalls[...] = vm.smalls[...]

    def put(row, value):
        smalls[pl.ds(row, 1), :] = jnp.sum(value, axis=0, keepdims=True)

    def third(rows, kept):
        back, dg, db = norm_back_tile(vm.base[rows, :], vm.gains[2], vm.d_three[rows, :])
        total = vm.upstream[rows, :] + back
        g_f32[rows, :] = total
        low = total.astype(BF16)
        g_low[rows, :] = low
        return (kept[0] + dg, kept[1] + db, kept[2] + fold_rows(low.astype(F32)))

    dg, db, bias = row_tiles(tokens, third, (zero, zero, zero), 0, 3)
    put(4, dg)
    put(7, db)

    @pl.when(is_enc)
    def _():
        put(1, bias)
        need(vm.hid)

        @pl.loop(0, 2)
        def _(b):
            made = dot_first(vm.hid[:, pl.ds(pl.multiple_of(b * width, LANES), width)], g_low[...]).astype(BF16)
            grads[0:ffn_blocks, b] = made.reshape(ffn_blocks, rows_of, width)

        red.launch(0)
        need(vm.w_mlp, vm.pre)

        @pl.loop(0, 2)
        def _(b):
            cols = pl.ds(pl.multiple_of(b * width, LANES), width)
            grad_hid[...] = dot_rows(g_low[...], vm.w_mlp[cols, :])

            def bend(rows, kept):
                low = (grad_hid[rows, :] * gelu_both(vm.pre[rows, cols])[1]).astype(BF16)
                grad_pre[b, rows, :] = low
                return kept + fold_rows(low.astype(F32))

            put(9 + b, row_tiles(tokens, bend, zero))

        red.launch(1)
        need(vm.act, vm.w_in)

        @pl.loop(0, 2)
        def _(b):
            made = dot_first(grad_pre[b], vm.act[...]).astype(BF16)
            grads[ffn_blocks : 2 * ffn_blocks, b] = made.reshape(ffn_blocks, rows_of, width)

        red.step(0)
        grad_hid[...] = jnp.zeros_like(grad_hid)

        @pl.loop(0, 2)
        def _(b):
            grad_hid[...] += dot_rows(grad_pre[b], vm.w_in[b])

        def lower(rows, kept):
            part_send[0, rows, :] = grad_hid[rows, :].astype(BF16)
            return kept

        row_tiles(tokens, lower, 0)
        part_copy(0).start()
        need(vm.x1)
        part_copy(0).wait()

        def second(rows, kept):
            grad = part_send[0, rows, :].astype(F32) + part_recv[0, rows, :].astype(F32)
            back, dg, db = norm_back_tile(vm.x1[rows, :], vm.gains[1], grad)
            total = g_f32[rows, :] + back
            g_f32[rows, :] = total
            low = total.astype(BF16)
            g_low[rows, :] = low
            return (kept[0] + dg, kept[1] + db, kept[2] + fold_rows(low.astype(F32)))

        dg, db, bias_two = row_tiles(tokens, second, (zero, zero, zero), 0, 3)
        put(3, dg)
        put(6, db)
        put(0, bias_two)
        red.step(1)

    @pl.when(is_dec)
    def _():
        put(0, bias)
        red.launch(ffn_blocks + 1)

    need(vm.w_out, vm.mixed, vm.packed, vm.tops, vm.seg_col, vm.seg_row)
    mix_grad[...] = dot_rows(g_low[...], vm.w_out[...]).astype(BF16)
    grads[2 * ffn_blocks] = dot_first(vm.mixed[...], g_low[...]).astype(BF16).reshape(grads.shape[1:])
    now = 2 + (ffn_blocks - 2) * tower

    fill_mask(mask, vm.seg_col, vm.seg_row, is_dec)
    red.step(now)
    self_backward(vm.packed, mix_grad, vm.tops, mask, d_packed, pairs, scale, lambda: red.step(now + 1))
    red.step(now + 2)


    need(vm.a_one, vm.w_qkv, vm.x0)
    grad_hid[...] = jnp.zeros_like(grad_hid)

    @pl.loop(0, 3)
    def _(a):
        cols = pl.ds(pl.multiple_of(a * heads, LANES), heads)
        made = dot_first(d_packed[:, cols], vm.a_one[...]).astype(BF16)
        grads[2 * ffn_blocks + 1 + a] = made.reshape(grads.shape[1:])
        grad_hid[...] += dot_plain(d_packed[:, cols], vm.w_qkv[cols, :])

    red.step(now + 3)


    def lower_two(rows, kept):
        part_send[1, rows, :] = grad_hid[rows, :].astype(BF16)
        return (
            kept[0] + fold_rows(d_packed[rows, pl.ds(0, heads)].astype(F32)),
            kept[1] + fold_rows(d_packed[rows, pl.ds(2 * heads, heads)].astype(F32)),
        )

    small_zero = jnp.zeros((8, heads), F32)
    q_sum, v_sum = row_tiles(tokens, lower_two, (small_zero, small_zero))
    part_copy(1).start()
    smalls[8:9, :] = jnp.concatenate(
        [jnp.sum(q_sum, axis=0, keepdims=True), jnp.sum(v_sum, axis=0, keepdims=True)], axis=1
    )
    part_copy(1).wait()

    def first(rows, kept):
        grad = part_send[1, rows, :].astype(F32) + part_recv[1, rows, :].astype(F32)
        back, dg, db = norm_back_tile(vm.x0[rows, :].astype(F32), vm.gains[0], grad)
        part_send[1, rows, :] = (g_f32[rows, :] + back).astype(BF16)
        return (kept[0] + dg, kept[1] + db)

    dg, db = row_tiles(tokens, first, (zero, zero), 0, 3)
    put(2, dg)
    put(5, db)
    mine = pl.ds(pl.multiple_of(core * quarter, TILE), quarter)

    def own_copy(rows, kept):
        shifted = pl.ds(pl.multiple_of(core * quarter + rows.start, 32), rows.size)
        own_grad[rows, :] = part_send[1, shifted, :]
        return kept

    row_tiles(quarter, own_copy, 0)
    red.step(now + 4)

    small_line = pltpu.make_async_remote_copy(
        src_ref=smalls,
        dst_ref=small_near,
        send_sem=small_sem.at[0],
        recv_sem=small_sem.at[1],
        device_id={DP: other},
        device_id_type=MESH,
    )
    small_line.start()

    @pl.when(moved)
    def _():
        home_move(own_grad, grad_out, 1).start()

    @pl.when(stays)
    def _():
        pltpu.make_async_copy(own_grad, grad_out, move_sem.at[1, 0]).start()


    def small_pair(sender, away):
        return pltpu.make_async_remote_copy(
            src_ref=small_all.at[sender],
            dst_ref=small_all.at[sender],
            send_sem=small_sem.at[1 + away],
            recv_sem=small_sem.at[4 + away],
            device_id={MP: lax.rem(z + away, 4)},
            device_id_type=MESH,
        )

    def small_core(which):
        return pltpu.make_async_remote_copy(
            src_ref=small_out.at[which],
            dst_ref=small_out.at[which],
            send_sem=small_sem.at[8],
            recv_sem=small_sem.at[9],
            device_id={DP: partner},
            device_id_type=MESH,
        )

    small_line.wait()
    small_all[z] = smalls[...] + small_near[...]


    for away in range(1, 4):
        small_pair(z, away).start()

    red.far_before(now + 5)
    red.drain(now + 5)
    red.close()
    pl.when(is_dec)(twin_copy().start)

    for away in range(1, 4):
        small_pair(lax.rem(z + 4 - away, 4), away).wait_recv()
    small_out[core] = ((small_all[0] + small_all[1]) + small_all[2]) + small_all[3]
    small_core(core).start()
    for away in range(1, 4):
        small_pair(z, away).wait_send()

    @pl.when(moved)
    def _():
        home_move(own_grad, grad_out, 1).wait()

    @pl.when(stays)
    def _():
        pltpu.make_async_copy(own_grad, grad_out, move_sem.at[1, 0]).wait()

    pl.when(is_dec)(twin_copy().wait_send)
    pl.when(is_enc)(twin_copy().wait_recv)
    small_core(core).wait_send()
    small_core(1 - core).wait_recv()


def tail(values, cross_grad, scale):
    tokens, width = values.base.shape
    heads = values.mixed.shape[1]
    pairs = heads // LANES
    hidden = values.pre.shape[1]
    quarter = tokens // 2
    half = width // 2
    rows_of = heads // 2
    blocks = 2 * (width // rows_of) + 4
    assert hidden == 2 * width and cross_grad.shape[0] == width // rows_of
    hbm = pl.BlockSpec(memory_space=pltpu.HBM)
    vmem = pl.BlockSpec(memory_space=pltpu.VMEM)
    n_in = len(values)
    scratch = [pltpu.VMEM(x.shape, x.dtype) for x in values]
    scratch += [pltpu.VMEM((blocks, 2, rows_of, width), BF16)]
    scratch += [pltpu.VMEM((blocks, 2, rows_of, half), BF16)] * 2
    scratch += [
        pltpu.VMEM((tokens, width), F32),
        pltpu.VMEM((tokens, width), BF16),
        pltpu.VMEM((tokens, width), F32),
        pltpu.VMEM((2, tokens, hidden // 2), BF16),
        pltpu.VMEM((tokens, 3 * heads), BF16),
        pltpu.VMEM((tokens, heads), BF16),
        pltpu.VMEM((2, tokens, width), BF16),
        pltpu.VMEM((2, tokens, width), BF16),
        pltpu.VMEM((tokens, tokens), F32),
        pltpu.VMEM(values.smalls.shape, F32),
        pltpu.VMEM(values.smalls.shape, F32),
        pltpu.VMEM((4,) + values.smalls.shape, F32),
        pltpu.VMEM((quarter, width), BF16),
    ]
    dma = pltpu.SemaphoreType.DMA
    scratch += [dma((n_in + 1,)), dma((blocks,)), dma((blocks,)), dma((blocks, 2)), dma((blocks, 2)), dma((blocks,)), dma((blocks,))]
    scratch += [dma((2, 2)), dma((10,)), dma((2, 2)), dma((2,))]
    out_shape = [jax.ShapeDtypeStruct((blocks, rows_of, half), BF16)]
    out_shape += [
        jax.ShapeDtypeStruct((2,) + values.smalls.shape, F32),
        jax.ShapeDtypeStruct((quarter, width), BF16),
        jax.ShapeDtypeStruct((2, heads // 2, half), BF16),
    ]
    return pl.pallas_call(
        functools.partial(tail_kernel, pairs, scale),
        in_specs=[hbm] * (n_in + 1),
        out_specs=[vmem] * 2 + [hbm] * 2,
        out_shape=out_shape,
        scratch_shapes=scratch,
        compiler_params=pltpu.CompilerParams(
            collective_id=1, has_side_effects=True, vmem_limit_bytes=TAIL_LIMIT
        ),
        name="tail",
    )(*values, cross_grad)


class Head(NamedTuple):
    packed: Any
    mixed: Any
    tops: Any
    a_one: Any
    x1: Any
    base: Any
    act_three: Any
    act: Any
    pre: Any
    hid: Any
    query: Any


def head_kernel(pieces, pairs, scale, *refs):
    it = iter(refs)
    srcs = [next(it) for _ in range(5)]
    blocks = [next(it)]
    seg_ref, image_ref = next(it), next(it)
    gains, shifts, out_b, ffn_out_b, ffn_in_b, qv_b = (next(it) for _ in range(6))
    outs = [next(it) for _ in range(5)]
    tokens = [next(it)]
    seg_out = [next(it) for _ in range(3)]
    hbm = Head(*[next(it) for _ in Head._fields])
    stages = [next(it) for _ in range(5)]
    weight_sems = [next(it) for _ in range(5)]
    token_stage = next(it)
    token_sems = [next(it) for _ in range(3)]
    w_qkv, w_out, w_q, w_in, w_mlp = (next(it) for _ in range(5))
    vm = Head(*[next(it) for _ in Head._fields])
    part_send, part_recv, raw, mask = next(it), next(it), next(it), next(it)
    seg_sem, load_sem, store_sem, part_sem = (next(it) for _ in range(4))
    tower, dp, z, core, line, other, partner = spots()
    is_enc = tower == 0
    is_dec = tower == 1
    stays = z == 3 * core
    moved = jnp.logical_not(stays)
    count, width = vm.x1.shape
    rows_txt = count // LTXT
    heads = vm.mixed.shape[1]
    at_end = jnp.logical_or(z == 0, z == 3)

    peers = [(z > 0, {MP: z - 1}), (z < 3, {MP: z + 1})]
    peers += [(None, {DP: other}), (None, {TOWER: 1 - tower}), (None, {DP: partner})]
    peers += [
        (moved, {DP: 2 * line + lax.rem(z, 2), MP: 2 * core + z // 2}),
        (moved, {DP: 2 * line + z // 2, MP: 2 * lax.rem(z, 2) + core}),
    ]
    barrier_all(
        peers,
        [(stays, 4), (jnp.logical_and(at_end, moved), 6), (jnp.logical_not(at_end), 7)],
    )

    begin, begin_local, pass_on, arrived, sent, end_local, end_twin = weight_steps(
        pieces, srcs, outs, stages, weight_sems
    )
    token_begin, token_relay, token_finish = token_steps(blocks, tokens, token_stage, token_sems)
    token_begin(0)
    begin()

    has_notes = core == z // 2

    def note_send(i):
        return pltpu.make_async_remote_copy(
            src_ref=seg_out[i],
            dst_ref=seg_out[i],
            send_sem=seg_sem.at[i, 0],
            recv_sem=seg_sem.at[i, 1],
            device_id={DP: partner},
            device_id_type=MESH,
        )

    @pl.when(has_notes)
    def _():
        rows = seg_ref.shape[0] // 2
        side = lax.rem(z, 2)
        segs = jnp.where(side == 0, seg_ref[0:rows, :], seg_ref[rows : 2 * rows, :])
        marks = segs + LTXT * lax.broadcasted_iota(jnp.int32, segs.shape, 0)
        tall = jnp.concatenate([marks.astype(F32), jnp.zeros((16 - rows, LTXT), F32)], axis=0).T
        seg_out[1][...] = jnp.zeros_like(seg_out[1])
        for r in range(rows):
            at = pl.ds(r * LTXT, LTXT)
            seg_out[0][at, :] = jnp.broadcast_to(tall[:, r : r + 1], (LTXT, LANES)).astype(jnp.int32)
            seg_out[1][0:1, at] = marks[r : r + 1, :]
            seg_out[2][at, :] = jnp.full((LTXT, LANES), image_ref[side * rows + r], jnp.int32)
        for i in range(3):
            note_send(i).start()

    begin_local()
    token_relay(0)

    def load(i, target, source):
        return pltpu.make_async_copy(source, target, load_sem.at[i])

    def store(ref):
        i = [x is ref for x in vm].index(True)
        return pltpu.make_async_copy(vm[i], hbm[i], store_sem.at[i])

    def part_copy(k):
        return pltpu.make_async_remote_copy(
            src_ref=part_send.at[k],
            dst_ref=part_recv.at[k],
            send_sem=part_sem.at[k, 0],
            recv_sem=part_sem.at[k, 1],
            device_id={DP: partner},
            device_id_type=MESH,
        )

    def normed(source, target, which):
        gain, shift = gains[which], shifts[which]

        def tile(rows, kept):
            unit, _ = norm_parts(source[rows, :].astype(F32))
            target[rows, :] = (unit * gain + shift).astype(BF16)
            return kept

        row_tiles(count, tile, 0, 0, 3)

    def chosen(which, flag, far=False):
        return [k for k, p in enumerate(pieces) if p[0] == which and p[6] == flag and p[7] == far]

    enc_in, enc_mlp, dec_in = chosen(3, 0), chosen(4, 0), chosen(3, 1) + chosen(4, 1)
    k_qkv, k_out, k_own, k_far = chosen(0, None), chosen(1, None), chosen(2, 1), chosen(2, 1, True)
    waiting = {0: enc_in + enc_mlp, 1: k_own + k_far + dec_in}

    def relay(enc=0, dec=0):
        for t, count in ((0, enc), (1, dec)):
            for k in waiting[t][:count]:
                pass_on(k)
            waiting[t] = waiting[t][count:]

    token_finish(0)
    normed(tokens[0], vm.a_one, 0)
    store(vm.a_one).start()
    for k in k_qkv + k_out:
        pass_on(k)
    for k in k_qkv:
        arrived(k)
    end_local(0)
    load(0, w_qkv, outs[0]).start()
    load(0, w_qkv, outs[0]).wait()

    @pl.loop(0, 3)
    def _(part):
        cols = pl.ds(pl.multiple_of(part * heads, LANES), heads)
        own = pl.ds(pl.multiple_of(core * heads, LANES), heads)
        bias = jnp.where(part == 1, 0.0, qv_b[pl.ds(part // 2, 1), own])
        made = dot_rows(vm.a_one[...], w_qkv[part].reshape(heads, width)) + bias
        vm.packed[:, cols] = made.astype(BF16)

    store(vm.packed).start()

    @pl.when(has_notes)
    def _():
        for i in range(3):
            note_send(i).wait_send()

    @pl.when(jnp.logical_not(has_notes))
    def _():
        for i in range(3):
            note_send(i).wait_recv()

    relay(1, 1)
    fill_mask(mask, seg_out[0], seg_out[1], is_dec)
    self_forward(vm.packed, mask, vm.mixed, vm.tops, pairs, scale)
    store(vm.mixed).start()
    store(vm.tops).start()
    for k in k_out:
        arrived(k)
    end_local(1)
    load(1, w_out, outs[1]).start()
    relay(1, 1)
    load(1, w_out, outs[1]).wait()
    part_send[0] = dot_plain(vm.mixed[...], w_out[0].reshape(heads, width)).astype(BF16)
    part_copy(0).start()
    relay(1, 1)
    part_copy(0).wait()

    def add_one(rows, kept):
        total = part_send[0, rows, :].astype(F32) + part_recv[0, rows, :].astype(F32)
        vm.x1[rows, :] = tokens[0][rows, :].astype(F32) + total + out_b[...]
        return kept

    row_tiles(count, add_one, 0)
    store(vm.x1).start()

    @pl.when(is_enc)
    def _():
        relay(1)
        normed(vm.x1, vm.act, 1)
        store(vm.act).start()
        relay(1)
        for k in enc_in:
            arrived(k)
        end_local(3)
        load(3, w_in, outs[3]).start()
        load(3, w_in, outs[3]).wait()
        relay(1)

        @pl.loop(0, 2)
        def _(b):
            cols = pl.ds(pl.multiple_of(b * width, LANES), width)
            raw[...] = dot_plain(vm.act[...], w_in[0, b])
            bias = ffn_in_b[0:1, pl.ds(pl.multiple_of((2 * core + b) * width, LANES), width)]

            def bend(rows, kept):
                pre = raw[rows, :] + bias
                vm.pre[rows, cols] = pre
                vm.hid[rows, cols] = gelu_tanh(pre).astype(BF16)
                return kept

            row_tiles(count, bend, 0)

        relay(1)
        store(vm.pre).start()
        store(vm.hid).start()
        relay(len(waiting[0]))
        for k in enc_mlp:
            arrived(k)
        end_local(4)
        load(4, w_mlp, outs[4]).start()
        load(4, w_mlp, outs[4]).wait()
        part_send[1] = dot_plain(vm.hid[...], w_mlp[0].reshape(2 * width, width)).astype(BF16)
        part_copy(1).start()
        part_copy(1).wait()

        def add_two(rows, kept):
            total = part_send[1, rows, :].astype(F32) + part_recv[1, rows, :].astype(F32)
            vm.base[rows, :] = vm.x1[rows, :] + total + ffn_out_b[...]
            return kept

        row_tiles(count, add_two, 0)

    @pl.when(is_dec)
    def _():
        def same(rows, kept):
            vm.base[rows, :] = vm.x1[rows, :]
            return kept

        row_tiles(count, same, 0)

    store(vm.base).start()
    normed(vm.base, vm.act_three, 2)
    store(vm.act_three).start()

    @pl.when(is_dec)
    def _():
        relay(0, 2)
        for k in k_own:
            arrived(k)
        end_local(2)
        load(2, w_q, outs[2].at[2]).start()
        load(2, w_q, outs[2].at[2]).wait()
        vm.query[...] = dot_rows(vm.act_three[...], w_q[...].reshape(heads, width)).astype(BF16)
        store(vm.query).start()
        relay(0, len(waiting[1]))
        for k in k_far + dec_in:
            arrived(k)
        end_local(3)
        end_local(4)

    for k in range(len(pieces)):
        sent(k)
    end_twin()
    for ref in vm:
        if ref is vm.act or ref is vm.pre or ref is vm.hid:
            pl.when(is_enc)(store(ref).wait)
        elif ref is vm.query:
            pl.when(is_dec)(store(ref).wait)
        else:
            store(ref).wait()


def head(shards, blocks, segment_ids, row_image, vecs, scale):
    qkv, out, cross, ffn_in, ffn_out = shards
    heads = 2 * out.shape[1]
    width = out.shape[2]
    pairs = heads // LANES
    count = 2 * blocks[0].shape[0]
    hidden = 2 * ffn_in.shape[2]

    def cuts(i, flag):
        blocks_of, rows, _ = shards[i].shape
        cut = rows if rows <= 192 else rows // 4
        return [(i, a, a, 1, at, cut, flag, False) for a in range(blocks_of) for at in range(0, rows, cut)]

    pieces = cuts(0, None) + cuts(1, None)
    rows = cross.shape[1]
    pieces += [(2, 2 + a, a, 1, 0, rows, 1, False) for a in range(2)] + [(2, a, a, 1, 0, rows, 1, True) for a in range(2)]
    pieces += cuts(3, 0) + cuts(4, 0) + cuts(3, 1) + cuts(4, 1)[:2]
    n = len(pieces)
    hbm = pl.BlockSpec(memory_space=pltpu.HBM)
    vmem = pl.BlockSpec(memory_space=pltpu.VMEM)
    struct = jax.ShapeDtypeStruct
    made = Head(
        packed=struct((count, 3 * heads), BF16),
        mixed=struct((count, heads), BF16),
        tops=struct((pairs, 8, 2 * count), F32),
        a_one=struct((count, width), BF16),
        x1=struct((count, width), F32),
        base=struct((count, width), F32),
        act_three=struct((count, width), BF16),
        act=struct((count, width), BF16),
        pre=struct((count, hidden), F32),
        hid=struct((count, hidden), BF16),
        query=struct((count, heads), BF16),
    )
    out_shape = [
        jax.ShapeDtypeStruct(((2 if i == 2 else 1) * x.shape[0], 2) + x.shape[1:], BF16) for i, x in enumerate(shards)
    ]
    out_shape += [jax.ShapeDtypeStruct((count, width), BF16)]
    out_shape += [struct((count, LANES), jnp.int32), struct((8, count), jnp.int32), struct((count, LANES), jnp.int32)]
    out_shape += list(made)
    dma = pltpu.SemaphoreType.DMA
    scratch = [pltpu.VMEM(x.shape, BF16) for x in shards]
    scratch += [dma((n, 5)), dma((n, 4)), dma((5, 2)), dma, dma]
    scratch += [pltpu.VMEM((1,) + blocks[0].shape, BF16), dma((1, 2)), dma((1, 2)), dma((1, 2))]
    scratch += [
        pltpu.VMEM((3, 2) + qkv.shape[1:], BF16),
        pltpu.VMEM((1, 2) + out.shape[1:], BF16),
        pltpu.VMEM((2,) + cross.shape[1:], BF16),
        pltpu.VMEM((1, 2) + ffn_in.shape[1:], BF16),
        pltpu.VMEM((1, 2) + ffn_out.shape[1:], BF16),
    ]
    scratch += [pltpu.VMEM(x.shape, x.dtype) for x in made]
    scratch += [
        pltpu.VMEM((2, count, width), BF16),
        pltpu.VMEM((2, count, width), BF16),
        pltpu.VMEM((count, width), F32),
        pltpu.VMEM((count, count), F32),
        dma((3, 2)),
        dma((5,)),
        dma((len(made),)),
        dma((2, 2)),
    ]
    results = pl.pallas_call(
        functools.partial(head_kernel, tuple(pieces), pairs, scale),
        in_specs=[hbm] * 6 + [vmem, pl.BlockSpec(memory_space=pltpu.SMEM)] + [vmem] * 6,
        out_specs=[hbm] * 5 + [vmem] + [vmem] * 3 + [hbm] * len(made),
        out_shape=out_shape,
        scratch_shapes=scratch,
        compiler_params=pltpu.CompilerParams(
            collective_id=0, has_side_effects=True, vmem_limit_bytes=VMEM_LIMIT
        ),
        name="head",
    )(*shards, *blocks, segment_ids, row_image, *vecs)
    return results[:5], results[5], results[6:9], Head(*results[9:])


CHUNKS = 6


def mid_kernel(pieces, pairs, scale, *refs):
    it = iter(refs)
    act_three, x1, query_in, w_cross_in, w_in_in, w_mlp_in, ffn_shard, cot_block, base = (next(it) for _ in range(9))
    gains, shifts, out_b, ffn_out_b, ffn_in_b, qv_b, picks = (next(it) for _ in range(7))
    d_three, upstream, smalls, tower_out, cross_out = (next(it) for _ in range(5))
    outs = next(it)
    stages = [next(it)]
    weight_sems = [next(it) for _ in range(5)]
    token_stage = next(it)
    token_sems = [next(it) for _ in range(3)]
    images, kv, w_cross, w_in, w_mlp = (next(it) for _ in range(5))
    act_txt, query, mixed, tops, y1, y2, act, pre, hid = (next(it) for _ in range(9))
    grad_hid, raw, grad_pre, g_low, mix_grad, dq, dkv, sum_q = (next(it) for _ in range(8))
    keys, vals, dk, dv = kv.at[0], kv.at[1], dkv.at[0], dkv.at[1]
    cot, part_send, part_recv, halves, half_near, sums, image_grad, own_rows = (next(it) for _ in range(8))
    grads, cross_grad, near, far = (next(it) for _ in range(4))
    red_sems = [next(it) for _ in range(6)]
    load_sem, store_sem, part_sem, twin_sem, side_sem, core_sem, half_sem, sum_sem, back_sem, give_sem, home_sem = it
    tower, dp, z, core, line, other, partner = spots()
    is_enc = tower == 0
    is_dec = tower == 1
    stays = z == 3 * core
    moved = jnp.logical_not(stays)
    side = lax.rem(z, 2)
    across_chip = z + 1 - 2 * side
    count, width = y1.shape
    quarter = count // 2
    chunk = quarter // CHUNKS
    heads = mixed.shape[1]

    home = {DP: 2 * line + z // 2, MP: 2 * lax.rem(z, 2) + core}
    guest = {DP: 2 * line + lax.rem(z, 2), MP: 2 * core + z // 2}
    peers = [(None, {DP: other}), (None, {DP: partner}), (None, {TOWER: 1 - tower})]
    peers += [(None, {MP: lax.rem(z + away, 4)}) for away in range(1, 4)]
    peers += [(moved, home), (moved, guest)]
    barrier_all(peers, [(stays, 6), (moved, 8)])

    def remote(source, target, sends, recvs, where):
        return pltpu.make_async_remote_copy(
            src_ref=source,
            dst_ref=target,
            send_sem=sends,
            recv_sem=recvs,
            device_id=where,
            device_id_type=MESH,
        )

    def span(which_core, i):
        return pl.ds(pl.multiple_of(which_core * quarter + i * chunk, 16), chunk)

    def twin_copy(i):
        rows = span(core, i)
        return remote(
            act_three.at[rows, :], images.at[side, rows, :], twin_sem.at[i, 0], twin_sem.at[i, 1], {TOWER: 1 - tower}
        )

    def side_copy(i, image):
        here = images.at[image, span(core, i), :]
        return remote(here, here, side_sem.at[i, 0], side_sem.at[i, 1], {MP: across_chip})

    def core_copy(i, image, which_core, far_image):
        here = images.at[image, span(which_core, i), :]
        return remote(here, here, core_sem.at[far_image, i, 0], core_sem.at[far_image, i, 1], {DP: partner})

    @pl.when(is_enc)
    def _():
        for i in range(CHUNKS):
            twin_copy(i).start()

    token_begin, token_relay, token_finish = token_steps([cot_block], [cot], token_stage, token_sems)
    pl.when(is_enc)(functools.partial(token_begin, 0))
    begin, begin_local, pass_on, arrived, sent, end_local, _ = weight_steps(
        pieces, [ffn_shard], [w_mlp], stages, weight_sems
    )

    def load(i, source, target):
        return pltpu.make_async_copy(source, target, load_sem.at[i])

    held = pl.ds(0, ffn_shard.shape[1] // 2)
    early = [load(5, w_mlp_in.at[:, :, held, :], w_mlp.at[:, :, held, :])]
    text_loads = [
        load(0, w_cross_in, w_cross),
        load(1, query_in, query),
        load(2, x1, y1),
        load(3, w_in_in, w_in),
        load(4, act_three, act_txt),
    ]

    def part_copy(k, h):
        rows = pl.ds(h * quarter, quarter)
        return remote(
            part_send.at[k % 3, rows, :],
            part_recv.at[k % 3, rows, :],
            part_sem.at[k, h, 0],
            part_sem.at[k, h, 1],
            {DP: partner},
        )

    def home_move():
        return remote(own_rows, tower_out, home_sem.at[0], home_sem.at[1], home)

    def home_stay():
        return pltpu.make_async_copy(own_rows, tower_out, home_sem.at[0])

    def go_home():
        pl.when(moved)(home_move().start)
        pl.when(stays)(home_stay().start)

    def back_copy(i):
        rows = pl.ds(i * chunk, chunk)
        return remote(
            sums.at[1, rows, :], image_grad.at[span(core, i), :], back_sem.at[i, 0], back_sem.at[i, 1], {TOWER: 1 - tower}
        )

    def back_core(i, which_core):
        here = image_grad.at[span(which_core, i), :]
        return remote(here, here, give_sem.at[i, 0], give_sem.at[i, 1], {DP: partner})

    store_grad = pltpu.make_async_copy(y2, upstream, store_sem.at[0])
    store_three = pltpu.make_async_copy(raw, d_three, store_sem.at[1])
    zero = jnp.zeros((8, width), F32)
    blocks, rows_of = grads.shape[0], grads.shape[2]
    red = Reducer(grads, near, far, outs, red_sems, 4, 0, blocks)

    @pl.when(is_enc)
    def _():
        smalls[...] = jnp.zeros_like(smalls)
        mine = pl.ds(pl.multiple_of(core * quarter, TILE), quarter)
        take = load(2, base.at[mine, :], y1.at[pl.ds(0, quarter), :])
        take.start()
        take.wait()

        def lower(rows, kept):
            own_rows[rows, :] = y1[rows, :].astype(BF16)
            return kept

        row_tiles(quarter, lower, 0)
        go_home()
        token_relay(0)
        token_finish(0)

        def lift(rows, kept):
            y2[rows, :] = cot[rows, :].astype(F32)
            return kept

        row_tiles(count, lift, 0)
        store_grad.start()
        for i in range(CHUNKS):
            back_copy(i).wait_recv()
            back_core(i, core).start()
        for i in range(CHUNKS):
            back_core(i, 1 - core).wait_recv()

        def lift_three(rows, kept):
            raw[rows, :] = image_grad[rows, :].astype(F32)
            return kept

        row_tiles(count, lift_three, 0)
        store_three.start()
        for i in range(CHUNKS):
            twin_copy(i).wait_send()
            back_core(i, core).wait_send()

    @pl.when(is_dec)
    def _():
        for one in early + text_loads:
            one.start()
        for one in early:
            one.wait()
        begin_local()
        smalls[...] = jnp.zeros_like(smalls)

        def put(row, value):
            smalls[pl.ds(row, 1), :] = jnp.sum(value, axis=0, keepdims=True)

        for i in range(CHUNKS):
            twin_copy(i).wait_recv()
            side_copy(i, side).start()
            core_copy(i, side, core, 0).start()
        begin()
        for one in text_loads[:2]:
            one.wait()
        mixed[...] = jnp.zeros_like(mixed)
        for i in range(CHUNKS):
            core_copy(i, side, 1 - core, 0).wait_recv()

        @pl.loop(0, 2)
        def _(turn):
            image = side + turn * (1 - 2 * side)

            @pl.when(turn == 1)
            def _():
                for i in range(CHUNKS):
                    side_copy(i, 1 - side).wait_recv()
                    core_copy(i, 1 - side, core, 1).start()
                token_begin(0)
                for i in range(CHUNKS):
                    core_copy(i, 1 - side, 1 - core, 1).wait_recv()

            @pl.loop(0, 2)
            def _(part):
                kv[part, image] = dot_rows(images[image], w_cross[part].reshape(heads, width)).astype(BF16)

            cross_forward(image, query, keys, vals, picks, mixed, tops, pairs, scale)

        for k in range(len(pieces)):
            pass_on(k)
        token_relay(0)

        def half_part(k, made):
            for h in range(2):
                part_send[k % 3, pl.ds(h * quarter, quarter), :] = made(pl.ds(h * quarter, quarter)).astype(BF16)
                part_copy(k, h).start()

        def add_halves(k, run, carry):
            for h in range(2):
                part_copy(k, h).wait()
                carry = row_tiles(quarter, run, carry, h * quarter)
            return carry

        half_part(0, lambda rows: dot_plain(mixed[rows, :], w_cross[3].reshape(heads, width)))
        for one in text_loads[2:]:
            one.wait()
        gain, shift = gains[1], shifts[1]

        def add_cross(rows, kept):
            total = part_send[0, rows, :].astype(F32) + part_recv[0, rows, :].astype(F32)
            value = y1[rows, :] + total
            y2[rows, :] = value
            unit, _ = norm_parts(value)
            act[rows, :] = (unit * gain + shift).astype(BF16)
            return kept

        token_finish(0)
        for k in range(len(pieces)):
            arrived(k)
        end_local(0)

        @pl.loop(0, 2)
        def _(b):
            grad_hid[b] = dot_rows(cot[...], w_mlp[0, b])

        add_halves(0, add_cross, 0)

        @pl.loop(0, 2)
        def _(b):
            cols = pl.ds(pl.multiple_of(b * width, LANES), width)
            pre[...] = dot_plain(act[...], w_in[0, b])
            bias = ffn_in_b[0:1, pl.ds(pl.multiple_of((2 * core + b) * width, LANES), width)]

            def bend(rows, kept):
                lifted, slope = gelu_both(pre[rows, :] + bias)
                hid[rows, cols] = lifted.astype(BF16)
                low = (grad_hid[b, rows, :] * slope).astype(BF16)
                grad_pre[b, rows, :] = low
                return kept + fold_rows(low.astype(F32))

            put(9 + b, row_tiles(count, bend, zero))

        half_part(2, lambda rows: dot_rows(grad_pre[0, rows, :], w_in[0, 0]) + dot_rows(grad_pre[1, rows, :], w_in[0, 1]))

        @pl.loop(0, 2)
        def _(b):
            made = dot_first(grad_pre[b], act[...]).astype(BF16)
            grads[0 : blocks // 2, b] = made.reshape(blocks // 2, rows_of, width)

        red.launch(0)
        red.launch(1)

        def second(rows, kept):
            low_cot = cot[rows, :].astype(F32)
            grad = part_send[2, rows, :].astype(F32) + part_recv[2, rows, :].astype(F32)
            back, dg, db = norm_back_tile(y2[rows, :], gain, grad)
            total = low_cot + back
            raw[rows, :] = total
            g_low[rows, :] = total.astype(BF16)
            return (kept[0] + dg, kept[1] + db, kept[2] + fold_rows(low_cot))

        dg, db, cot_sum = add_halves(2, second, (zero, zero, zero))
        put(3, dg)
        put(6, db)
        put(1, cot_sum)

        mix_grad[...] = dot_rows(g_low[...], w_cross[3].reshape(heads, width)).astype(BF16)
        cross_backward(query, keys, vals, mix_grad, picks, tops, dq, dk, dv, sum_q, pairs, scale)

        def half_copy(image, far_image):
            return remote(
                halves.at[image, pl.ds(pl.multiple_of((1 - core) * quarter, TILE), quarter), :],
                half_near.at[far_image],
                half_sem.at[far_image, 0],
                half_sem.at[far_image, 1],
                {DP: partner},
            )

        @pl.loop(0, 2)
        def _(i):
            image = side + (1 - i) * (1 - 2 * side)
            made = dot_plain(dkv[0, image], w_cross[0].reshape(heads, width))
            made = made + dot_plain(dkv[1, image], w_cross[1].reshape(heads, width))
            halves[image] = made.astype(BF16)
            half_copy(image, 1 - i).start()

        for k in range(2):
            red.add_near(k, False)
            red.launch(k + 2)

        def sum_copy(i):
            rows = pl.ds(i * chunk, chunk)
            return remote(
                sums.at[0, rows, :], sums.at[2, rows, :], sum_sem.at[i, 0], sum_sem.at[i, 1], {MP: across_chip}
            )

        half_copy(1 - side, 1).wait_recv()
        for i in range(CHUNKS):

            def add_far(rows, kept):
                at = pl.ds(pl.multiple_of(i * chunk + rows.start, 16), rows.size)
                own = pl.ds(pl.multiple_of(core * quarter + i * chunk + rows.start, 16), rows.size)
                total = halves[1 - side, own, :].astype(F32) + half_near[1, at, :].astype(F32)
                sums[0, at, :] = total.astype(BF16)
                return kept

            row_tiles(chunk, add_far, 0)
            sum_copy(i).start()
        @pl.loop(0, 2)
        def _(b):
            cols = pl.ds(pl.multiple_of(b * width, LANES), width)
            made = dot_first(hid[:, cols], cot[...]).astype(BF16)
            grads[blocks // 2 : blocks, b] = made.reshape(blocks // 2, rows_of, width)

        red.launch(4)
        red.launch(5)
        half_copy(side, 0).wait_recv()
        for i in range(CHUNKS):
            sum_copy(i).wait_recv()

            def add_own(rows, kept):
                at = pl.ds(pl.multiple_of(i * chunk + rows.start, 16), rows.size)
                own = pl.ds(pl.multiple_of(core * quarter + i * chunk + rows.start, 16), rows.size)
                total = halves[side, own, :].astype(F32) + half_near[0, at, :].astype(F32)
                sums[1, at, :] = (total + sums[2, at, :].astype(F32)).astype(BF16)
                return kept

            row_tiles(chunk, add_own, 0)
            back_copy(i).start()

        half_part(3, lambda rows: dot_plain(dq[rows, :], w_cross[2].reshape(heads, width)))
        red.add_mid(0)
        red.step(2)

        def keep_two(rows, kept):
            y1[rows, :] = raw[rows, :]
            return kept

        row_tiles(count, keep_two, 0)
        pltpu.make_async_copy(y1, upstream, store_sem.at[0]).start()

        def lift_query(rows, kept):
            raw[rows, :] = part_send[0, rows, :].astype(F32) + part_recv[0, rows, :].astype(F32)
            return kept

        add_halves(3, lift_query, 0)
        store_three.start()
        pre[...] = jnp.zeros_like(pre)

        @pl.loop(0, 2)
        def _(b):
            pre[...] += dot_plain(hid[:, pl.ds(pl.multiple_of(b * width, LANES), width)], w_mlp[0, b])

        for h in range(2):
            rows = pl.ds(h * quarter, quarter)
            part_send[1, rows, :] = pre[rows, :].astype(BF16)
            part_copy(1, h).start()
        red.step(3)

        @pl.loop(0, 2)
        def _(which):
            made = dot_first(dkv[which, 0], images[0]) + dot_first(dkv[which, 1], images[1])
            cross_grad[which] = made.astype(BF16).reshape(cross_grad.shape[1:])

        red.step(4)
        cross_grad[2] = dot_first(dq[...], act_txt[...]).astype(BF16).reshape(cross_grad.shape[1:])
        cross_grad[3] = dot_first(mixed[...], g_low[...]).astype(BF16).reshape(cross_grad.shape[1:])
        store_cross = pltpu.make_async_copy(cross_grad, cross_out, store_sem.at[2])
        store_cross.start()
        for h in range(2):
            part_copy(1, h).wait()

        def add_last(rows, kept):
            own = pl.ds(pl.multiple_of(core * quarter + rows.start, 32), rows.size)
            total = part_send[1, own, :].astype(F32) + part_recv[1, own, :].astype(F32)
            own_rows[rows, :] = (y2[own, :] + total + ffn_out_b[...]).astype(BF16)
            return kept

        row_tiles(quarter, add_last, 0)
        go_home()
        red.far_before(5)
        red.drain(5)
        red.close()
        store_cross.wait()
        for i in range(CHUNKS):
            side_copy(i, side).wait_send()
            core_copy(i, side, core, 0).wait_send()
            core_copy(i, 1 - side, core, 1).wait_send()
            sum_copy(i).wait_send()
            back_copy(i).wait_send()
        half_copy(1 - side, 1).wait_send()
        half_copy(side, 0).wait_send()
        for k in range(len(pieces)):
            sent(k)

    pl.when(moved)(home_move().wait)
    pl.when(stays)(home_stay().wait)
    store_grad.wait()
    store_three.wait()


def middle(values, w_cross, w_in, w_mlp, ffn_shard, cot_block, vecs, picks, scale):
    count, width = values.base.shape
    heads = values.mixed.shape[1]
    pairs = heads // LANES
    hidden = values.hid.shape[1]
    quarter = count // 2
    half = width // 2
    chunk = quarter // CHUNKS
    assert chunk * CHUNKS == quarter
    rows_of = heads // 2
    blocks = 2 * (width // rows_of)
    assert hidden == 2 * width
    cross_shape = (4, 2, rows_of, width)
    rows = ffn_shard.shape[1]
    pieces = [(0, 0, 0, 1, at, rows // 4, 1, False) for at in range(rows // 2, rows, rows // 4)]
    n = len(pieces)
    hbm = pl.BlockSpec(memory_space=pltpu.HBM)
    vmem = pl.BlockSpec(memory_space=pltpu.VMEM)
    dma = pltpu.SemaphoreType.DMA
    low, wide = (count, width), (count, heads)
    scratch = [pltpu.VMEM(ffn_shard.shape, BF16), dma((n, 5)), dma((n, 4)), dma((1, 2)), dma, dma]
    scratch += [pltpu.VMEM((1,) + cot_block.shape, BF16), dma((1, 2)), dma((1, 2)), dma((1, 2))]
    scratch += [
        pltpu.VMEM((2,) + low, BF16),
        pltpu.VMEM((2, 2) + wide, BF16),
        pltpu.VMEM((4, 2, heads // 2, width), BF16),
        pltpu.VMEM((1, 2, width, hidden // 2), BF16),
        pltpu.VMEM((1, 2, hidden // 2, width), BF16),
        pltpu.VMEM(low, BF16),
        pltpu.VMEM(wide, BF16),
        pltpu.VMEM(wide, BF16),
        pltpu.VMEM((2, pairs, 8, 2 * count), F32),
        pltpu.VMEM(low, F32),
        pltpu.VMEM(low, F32),
        pltpu.VMEM(low, BF16),
        pltpu.VMEM(low, F32),
        pltpu.VMEM((count, hidden), BF16),
        pltpu.VMEM((2,) + low, F32),
        pltpu.VMEM(low, F32),
        pltpu.VMEM((2, count, hidden // 2), BF16),
        pltpu.VMEM(low, BF16),
        pltpu.VMEM(wide, BF16),
        pltpu.VMEM(wide, BF16),
        pltpu.VMEM((2, 2) + wide, BF16),
        pltpu.VMEM((count, LANES), F32),
        pltpu.VMEM(low, BF16),
        pltpu.VMEM((3,) + low, BF16),
        pltpu.VMEM((3,) + low, BF16),
        pltpu.VMEM((2,) + low, BF16),
        pltpu.VMEM((2, quarter, width), BF16),
        pltpu.VMEM((3, quarter, width), BF16),
        pltpu.VMEM(low, BF16),
        pltpu.VMEM((quarter, width), BF16),
    ]
    scratch += [pltpu.VMEM((blocks, 2, rows_of, width), BF16), pltpu.VMEM(cross_shape, BF16)]
    scratch += [pltpu.VMEM((blocks, 2, rows_of, half), BF16)] * 2
    scratch += [dma((blocks,)), dma((blocks,)), dma((blocks, 2)), dma((blocks, 2)), dma((blocks,)), dma((blocks,))]
    scratch += [
        dma((6,)),
        dma((3,)),
        dma((4, 2, 2)),
        dma((CHUNKS, 2)),
        dma((CHUNKS, 2)),
        dma((2, CHUNKS, 2)),
        dma((2, 2)),
        dma((CHUNKS, 2)),
        dma((CHUNKS, 2)),
        dma((CHUNKS, 2)),
        dma((2,)),
    ]
    out_shape = [
        jax.ShapeDtypeStruct(low, F32),
        jax.ShapeDtypeStruct(low, F32),
        jax.ShapeDtypeStruct((16, width), F32),
        jax.ShapeDtypeStruct((quarter, width), BF16),
        jax.ShapeDtypeStruct(cross_shape, BF16),
        jax.ShapeDtypeStruct((blocks, rows_of, half), BF16),
    ]
    args = [values.act_three, values.x1, values.query, w_cross, w_in, w_mlp]
    return pl.pallas_call(
        functools.partial(mid_kernel, tuple(pieces), pairs, scale),
        in_specs=[hbm] * 9 + [vmem] * 7,
        out_specs=[hbm, hbm, vmem, hbm, hbm, vmem],
        out_shape=out_shape,
        scratch_shapes=scratch,
        compiler_params=pltpu.CompilerParams(
            collective_id=2, has_side_effects=True, vmem_limit_bytes=TAIL_LIMIT
        ),
        name="middle",
    )(*args, ffn_shard, cot_block, values.base, *vecs, picks)


def finish_kernel(*refs):
    it = iter(refs)
    late, early, from_text, total = (next(it) for _ in range(4))
    rows_in = [next(it) for _ in range(2)]
    rows_out = [next(it) for _ in range(2)]
    o_qkv, o_out, o_in, o_mlp, o_cross, o_qv, o_outb, o_inb, o_mlpb, o_gain, o_shift = (next(it) for _ in range(11))
    held = [next(it) for _ in range(2)]
    b_in, b_mlp, b_out, b_qkv, b_cross, sem = it
    tower, dp, z, core, line, other, partner = spots()

    def bring(i, image_src, text_src, target):
        @pl.when(tower == 0)
        def _():
            pltpu.make_async_copy(image_src, target, sem.at[i]).start()

        @pl.when(tower == 1)
        def _():
            pltpu.make_async_copy(text_src, target, sem.at[i]).start()

    n = b_in.shape[0]
    bring(0, late.at[pl.ds(n, n)], early.at[pl.ds(0, n)], b_in)
    bring(1, late.at[pl.ds(0, n)], early.at[pl.ds(n, n)], b_mlp)
    bring(2, late.at[2 * n], late.at[2 * n], b_out)
    bring(3, late.at[pl.ds(2 * n + 1, 3)], late.at[pl.ds(2 * n + 1, 3)], b_qkv)
    bring(4, from_text, late.at[pl.ds(n + 2, 2)], b_cross)
    for i in range(2):
        pltpu.make_async_copy(rows_in[i], held[i], sem.at[5 + i]).start()

    width = total.shape[2]
    heads = width // 2
    first = total[0]
    o_outb[...] = first[0:1, :]
    o_mlpb[...] = first[1:2, :]
    for i in range(3):
        o_gain[i] = first[2 + i : 3 + i, :]
        o_shift[i] = first[5 + i : 6 + i, :]
    for side in range(2):
        lanes = slice(side * heads, (side + 1) * heads)
        o_qv[0, 0:1, lanes] = total[side, 8:9, :heads]
        o_qv[0, 1:2, lanes] = total[side, 8:9, heads:]
        for b in range(2):
            at = (2 * side + b) * width
            o_inb[0:1, at : at + width] = total[side, 9 + b : 10 + b, :]

    def mine(block):
        cut = block.shape[1] // 2
        wide = block.astype(F32)
        return jnp.where(core == 0, wide[:, :cut], wide[:, cut:])

    for i in range(2):
        pltpu.make_async_copy(rows_in[i], held[i], sem.at[5 + i]).wait()
        pltpu.make_async_copy(held[i], rows_out[i].at[0], sem.at[7 + i]).start()
    half = b_in.shape[2]
    cols = b_in.shape[1]
    pltpu.make_async_copy(late.at[pl.ds(0, n)], b_in, sem.at[0]).wait()
    for i in range(n // 2):
        pair = b_in[2 * i : 2 * i + 2].reshape(2 * cols, half)
        o_in[0, :, 2 * i * cols : 2 * (i + 1) * cols] = mine(pair).T
    pltpu.make_async_copy(late.at[pl.ds(0, n)], b_mlp, sem.at[1]).wait()
    for i in range(n // 2):
        pair = b_mlp[2 * i : 2 * i + 2].reshape(2 * cols, half)
        o_mlp[0, :, 2 * i * cols : 2 * (i + 1) * cols] = mine(pair).T
    pltpu.make_async_copy(late.at[0], b_out, sem.at[2]).wait()
    o_out[0] = mine(b_out[...])
    pltpu.make_async_copy(late.at[pl.ds(0, 3)], b_qkv, sem.at[3]).wait()
    for a in range(3):
        o_qkv[0, a] = mine(b_qkv[a]).T
    pltpu.make_async_copy(late.at[pl.ds(0, 2)], b_cross, sem.at[4]).wait()
    for a in range(2):
        o_cross[0, a] = mine(b_cross[a]).T
    for i in range(2):
        pltpu.make_async_copy(held[i], rows_out[i].at[0], sem.at[7 + i]).wait()


def finish(late, early, from_text, total, token_rows):
    hbm = pl.BlockSpec(memory_space=pltpu.HBM)
    vmem = pl.BlockSpec(memory_space=pltpu.VMEM)
    struct = jax.ShapeDtypeStruct
    width = total.shape[2]
    blocks, cols, half = early.shape
    n = blocks // 2
    ffn, cut = n * cols, half // 2
    out_shape = [struct((1,) + x.shape, BF16) for x in token_rows]
    out_shape += [
        struct((1, 3, cut, cols), F32),
        struct((1, cols, cut), F32),
        struct((1, cut, ffn), F32),
        struct((1, cut, ffn), F32),
        struct((1, 2, cut, cols), F32),
        struct((1, 2, width), F32),
        struct((1, width), F32),
        struct((1, 4 * width), F32),
        struct((1, width), F32),
        struct((3, 1, width), F32),
        struct((3, 1, width), F32),
    ]
    scratch = [pltpu.VMEM(x.shape, BF16) for x in token_rows]
    scratch += [pltpu.VMEM(x + (cols, half), BF16) for x in ((n,), (n,), (), (3,), (2,))]
    scratch += [pltpu.SemaphoreType.DMA((9,))]
    results = pl.pallas_call(
        finish_kernel,
        in_specs=[hbm] * 3 + [vmem] + [hbm] * 2,
        out_specs=[hbm] * 2 + [vmem] * 11,
        out_shape=out_shape,
        scratch_shapes=scratch,
        compiler_params=pltpu.CompilerParams(vmem_limit_bytes=VMEM_LIMIT),
        name="finish",
    )(late, early, from_text, total, *token_rows)
    turned = {5: (1, 2), 11: (0, 1), 12: (0, 1)}
    return tuple(jnp.swapaxes(x, *turned[i]) if i in turned else x for i, x in enumerate(results))


def split_heads(flat):
    return jnp.swapaxes(flat.reshape(flat.shape[0], -1, HDIM), 0, 1)


def join_heads(split):
    return jnp.swapaxes(split, 0, 1).reshape(split.shape[1], -1)


def batch_dot(left, right, left_dim, right_dim):
    return lax.dot_general(left, right, (((left_dim,), (right_dim,)), ((0,), (0,))), preferred_element_type=F32)


def attend_plain(queries, keys, vals, allowed, scale):
    queries, keys, vals = (split_heads(x) for x in (queries, keys, vals))
    scores = jnp.where(allowed, batch_dot(queries, keys, 2, 2) * scale, NEG)
    top = jnp.max(scores, axis=-1, keepdims=True)
    tops = top + jnp.log(jnp.sum(jnp.exp(scores - top), axis=-1, keepdims=True))
    weights = jnp.exp(scores - tops).astype(BF16)
    return (join_heads(batch_dot(weights, vals, 2, 1)).astype(BF16), tops)


def attend_back_plain(queries, keys, vals, grads, tops, allowed, scale):
    queries, keys, vals, grads = (split_heads(x) for x in (queries, keys, vals, grads))
    scores = jnp.where(allowed, batch_dot(queries, keys, 2, 2) * scale, NEG)
    weights = jnp.exp(scores - tops)
    grad_w = batch_dot(grads, vals, 2, 2)
    grad_s = (weights * (grad_w - jnp.sum(weights * grad_w, axis=-1, keepdims=True))).astype(BF16)
    return (
        join_heads(batch_dot(grad_s, keys, 2, 1) * scale).astype(BF16),
        join_heads(batch_dot(grad_s, queries, 1, 1) * scale).astype(BF16),
        join_heads(batch_dot(weights.astype(BF16), grads, 1, 1)).astype(BF16),
    )


def gather_plain(shards):
    core = lax.rem(lax.axis_index(DP), 2)
    outs = []
    for i, s in enumerate(shards):
        if i == 2:
            s = jnp.concatenate([lax.ppermute(s, TOWER, [(0, 1)]), s], axis=0)
        full = lax.all_gather(s, MP, axis=1, tiled=False)
        outs.append(lax.dynamic_slice_in_dim(full, 2 * core, 2, 1))
    return outs


def reduce_plain(grads, smalls):
    dp = lax.axis_index(DP)
    core = lax.rem(dp, 2)
    outs = []
    for g in grads:
        n, _, rows, wide = g.shape
        full = jnp.zeros((n, 4, rows, wide), BF16)
        full = lax.dynamic_update_slice(full, g, (0, 2 * core, 0, 0))
        part = lax.psum_scatter(full, MP, scatter_dimension=1, tiled=False)
        part = lax.psum_scatter(part, DP, scatter_dimension=2, tiled=True)
        outs.append(part)
    if smalls is None:
        return outs
    both = jnp.zeros((2,) + smalls.shape, F32)
    both = lax.dynamic_update_slice(both, smalls[None], (core, 0, 0))
    return outs + [lax.psum(both, (DP, MP))]


def body(
    tower_in,
    out_cot,
    segment_ids,
    row_image,
    attn_qkv,
    attn_out,
    mlp_in,
    mlp_out,
    cross_proj,
    qv_bias,
    out_bias,
    mlp_bias_in,
    mlp_bias_out,
    norm_gain,
    norm_bias,
):
    lines = lax.axis_size(DP) // 2
    depth = lax.axis_size(MP)
    devices = lax.axis_size(DP)
    is_enc = lax.axis_index(TOWER) == 0
    dp = lax.axis_index(DP)
    z = lax.axis_index(MP)
    core = lax.rem(dp, 2)
    side = lax.rem(z, 2)
    group = z // 2
    direct = lines == 2
    assert depth == 4
    quarter = tower_in.shape[1]
    tokens = 2 * quarter
    assert tokens == PATCH
    width = tower_in.shape[2]
    head_cols = 2 * attn_qkv.shape[3]
    hidden = 2 * mlp_in.shape[2]
    scale_qk = HDIM ** (-0.5)

    out_moves, back_moves = [], []
    for d in range(devices):
        for place in range(depth):
            here = d * depth + place
            there = (d - d % 2 + place % 2) * depth + 2 * (d % 2) + place // 2
            out_moves.append((here, there))
            back_moves.append((there, here))

    def swap_cores(x):
        return lax.ppermute(x, DP, [(i, i ^ 1) for i in range(devices)])

    def both_cores(own):
        other = swap_cores(own)
        return jnp.where(core == 0, jnp.concatenate([own, other], -2), jnp.concatenate([other, own], -2))

    def own_rows(full):
        return lax.dynamic_slice_in_dim(full, core * quarter, quarter, full.ndim - 2)

    def lowered(part):
        return lax.reduce_precision(part, 8, 7).astype(BF16)

    def add_lowered(low):
        return low.astype(F32) + swap_cores(low).astype(F32)

    def add_cores(part):
        return add_lowered(lowered(part))

    def only_image(run, *operands):
        def idle(*inputs):
            return jax.tree.map(lambda x: jnp.zeros(x.shape, x.dtype), jax.eval_shape(run, *inputs))

        return lax.cond(is_enc, run, idle, *operands)

    shards = [
        jnp.swapaxes(attn_qkv[0], 1, 2),
        attn_out,
        jnp.swapaxes(cross_proj[0], 1, 2),
        mlp_in,
        mlp_out,
    ]
    rows = segment_ids.shape[0] // 2

    bias_qv = lax.dynamic_slice_in_dim(qv_bias[0], core * head_cols, head_cols, 1)
    bias_packed = jnp.concatenate([bias_qv[0], jnp.zeros_like(bias_qv[0]), bias_qv[1]])
    bias_in = lax.dynamic_slice_in_dim(mlp_bias_in[0], core * hidden, hidden, 0)
    gains = norm_gain[0]
    shifts = norm_bias[0]

    def feed_forward(values):
        act = norm_rows(values, gains[1], shifts[1]).astype(BF16)
        pre = jnp.concatenate([dot_plain(act, w_in[0]), dot_plain(act, w_in[1])], axis=1) + bias_in
        hid = gelu_tanh(pre).astype(BF16)
        return (act, pre, hid, lowered(dot_plain(hid, w_mlp)))

    if direct:
        tall_gains, tall_shifts = (jnp.swapaxes(x, 0, 1) for x in (norm_gain, norm_bias))
        vecs = (tall_gains, tall_shifts, out_bias, mlp_bias_out, mlp_bias_in, qv_bias[0])
        gathered, stream_low, notes, first = head(
            shards, [tower_in[0]], segment_ids, row_image, vecs, scale_qk
        )
        seg_col, seg_row, picks = notes
    else:
        gathered = gather_plain(shards)
        stream_low = both_cores(lax.ppermute(tower_in[0], (DP, MP), out_moves))
        cot_low = both_cores(lax.ppermute(out_cot[0], (DP, MP), out_moves))
        segs = jnp.where(core == group, segment_ids, swap_cores(segment_ids))
        segs = lax.dynamic_slice_in_dim(segs, rows * side, rows, 0)
        marks = (segs + LTXT * jnp.arange(rows, dtype=jnp.int32)[:, None]).reshape(tokens)
        images_of = jnp.where(core == group, row_image, swap_cores(row_image))
        images_of = jnp.repeat(lax.dynamic_slice_in_dim(images_of, rows * side, rows, 0), LTXT)
        places = jnp.arange(tokens)
        allowed = (places[None, :] <= places[:, None]) & (marks[None, :] == marks[:, None])
        allowed = jnp.logical_or(allowed, is_enc)
        sees = images_of[:, None] == jnp.arange(2 * tokens)[None, :] // tokens
    w_qkv = gathered[0].reshape(3 * head_cols, width)
    w_out = gathered[1].reshape(head_cols, width)
    w_cross = gathered[2].reshape(4, head_cols, width)
    w_in = gathered[3][0]
    w_mlp = gathered[4].reshape(hidden, width)
    stream = stream_low.astype(F32)

    if not direct:
        act_one = norm_rows(stream, gains[0], shifts[0]).astype(BF16)
        packed = (dot_rows(act_one, w_qkv) + bias_packed).astype(BF16)
        parts = [packed[:, i * head_cols : (i + 1) * head_cols] for i in range(3)]
        mixed, tops = attend_plain(*parts, allowed, scale_qk)
        stream_one = stream + add_cores(dot_plain(mixed, w_out)) + out_bias[0]
        act_enc, pre_enc, hid_enc, part_enc = feed_forward(stream_one)
        out_enc = stream_one + add_lowered(part_enc) + mlp_bias_out[0]
        base_three = jnp.where(is_enc, out_enc, stream_one)
        act_three = norm_rows(base_three, gains[2], shifts[2]).astype(BF16)
        cross_q = dot_rows(act_three, w_cross[2]).astype(BF16)

    if direct:
        back_in_three, upstream, smalls, tower_out, g_cross, early = middle(
            first, gathered[2], gathered[3], gathered[4], mlp_out, out_cot[0], vecs, picks, scale_qk
        )
        values = Tail(
            d_three=back_in_three,
            base=first.base,
            upstream=upstream,
            gains=tall_gains,
            smalls=smalls,
            w_mlp=w_mlp,
            pre=first.pre,
            hid=first.hid,
            act=first.act,
            w_in=w_in,
            x1=first.x1,
            w_out=w_out,
            mixed=first.mixed,
            packed=first.packed,
            tops=first.tops,
            seg_col=seg_col,
            seg_row=seg_row,
            a_one=first.a_one,
            w_qkv=w_qkv,
            x0=stream_low,
        )
        late, total, grad_in, from_text = tail(values, g_cross, scale_qk)
        return finish(late, early, from_text, total, [tower_out, grad_in])
    else:
        near_half = lax.ppermute(own_rows(act_three), TOWER, [(0, 1)])
        far_half = lax.ppermute(near_half, MP, [(i, i ^ 1) for i in range(depth)])
        halves = jnp.where(side == 0, jnp.stack([near_half, far_half]), jnp.stack([far_half, near_half]))
        images = both_cores(halves)

        flat_images = images.reshape(2 * tokens, width)
        cross_k = dot_rows(flat_images, w_cross[0]).astype(BF16)
        cross_v = dot_rows(flat_images, w_cross[1]).astype(BF16)
        cross_mix, cross_tops = attend_plain(cross_q, cross_k, cross_v, sees, scale_qk)
        stream_two = stream_one + add_cores(dot_plain(cross_mix, w_cross[3]))

        act_dec, pre_dec, hid_dec, part_dec = feed_forward(stream_two)
        out_dec = stream_two + add_lowered(part_dec) + mlp_bias_out[0]
        tower_rows = own_rows(jnp.where(is_enc, base_three, out_dec).astype(BF16))

        def feed_back(grad_low, pre):
            grad_hid = dot_rows(grad_low, w_mlp)
            _, pullback = jax.vjp(gelu_tanh, pre)
            grad_pre = pullback(grad_hid)[0].astype(BF16)
            cols = hidden // 2
            part = dot_rows(grad_pre[:, :cols], w_in[0]) + dot_rows(grad_pre[:, cols:], w_in[1])
            return (grad_pre, lowered(part))

        def feed_grads(grad_low, act, grad_pre, hid):
            g_in = dot_first(grad_pre, act).astype(BF16)
            g_mlp = dot_first(hid, grad_low).astype(BF16)
            return (
                g_in.reshape(1, 2, hidden // 2, width),
                g_mlp.reshape(1, 2, hidden // 2, width),
            )

        cot = cot_low.astype(F32)
        grad_pre_dec, back_in = feed_back(cot_low, pre_dec)
        back_a, gain_a, shift_a = norm_back(stream_two, gains[1], add_lowered(back_in))
        grad_two = cot + back_a
        grad_two_low = grad_two.astype(BF16)

        grad_mix = dot_rows(grad_two_low, w_cross[3]).astype(BF16)
        grad_q, flat_k, flat_v = attend_back_plain(
            cross_q, cross_k, cross_v, grad_mix, cross_tops, sees, scale_qk
        )
        part_images = dot_plain(flat_k, w_cross[0]) + dot_plain(flat_v, w_cross[1])
        part_low = part_images.astype(BF16).reshape(2, 2, quarter, width)
        give = lax.dynamic_index_in_dim(part_low, 1 - core, 1, keepdims=False)
        keep = lax.dynamic_index_in_dim(part_low, core, 1, keepdims=False)
        pair_sum = (keep.astype(F32) + swap_cores(give).astype(F32)).astype(BF16)
        give = lax.dynamic_index_in_dim(pair_sum, 1 - side, 0, keepdims=False)
        keep = lax.dynamic_index_in_dim(pair_sum, side, 0, keepdims=False)
        got = lax.ppermute(give, MP, [(i, i ^ 1) for i in range(depth)])
        image_sum = (keep.astype(F32) + got.astype(F32)).astype(BF16)
        image_half = lax.ppermute(image_sum, TOWER, [(1, 0)])
        later = lax.optimization_barrier(
            (cot_low, act_dec, grad_pre_dec, hid_dec, flat_k, flat_v, grad_q, cross_mix, image_sum)
        )
        g_in_dec, g_mlp_dec = feed_grads(later[0], later[1], later[2], later[3])
        g_cross = jnp.concatenate(
            [
                dot_first(later[4], flat_images).astype(BF16),
                dot_first(later[5], flat_images).astype(BF16),
                dot_first(later[6], act_three).astype(BF16),
                dot_first(later[7], grad_two_low).astype(BF16),
            ],
            axis=0,
        ).reshape(4, 2, head_cols // 2, width)
        image_back = both_cores(image_half).astype(F32)
        query_back = add_cores(dot_plain(grad_q, w_cross[2]))
        back_in_three = jnp.where(is_enc, image_back, query_back)
        text_smalls = (
            jnp.zeros((16, width), F32)
            .at[1]
            .set(jnp.sum(cot_low, axis=0, dtype=F32))
            .at[3]
            .set(gain_a)
            .at[6]
            .set(shift_a)
            .at[9:11]
            .set(jnp.sum(grad_pre_dec, axis=0, dtype=F32).reshape(2, width))
        )
        smalls = jnp.where(is_enc, 0.0, text_smalls)
        tower_out = lax.ppermute(tower_rows, (DP, MP), back_moves)
        back_three, gain_three, shift_three = norm_back(
            base_three, gains[2], back_in_three
        )
        grad_enc = cot + back_three
        grad_enc_low = grad_enc.astype(BF16)

        grad_pre_enc, back_in = feed_back(grad_enc_low, pre_enc)
        g_in, g_mlp = feed_grads(grad_enc_low, act_enc, grad_pre_enc, hid_enc)
        back_b, gain_b, shift_b = norm_back(stream_one, gains[1], add_lowered(back_in))
        grad_one = jnp.where(is_enc, grad_enc + back_b, grad_two + back_three)
        grad_one_low = grad_one.astype(BF16)

        g_out = dot_first(mixed, grad_one_low).astype(BF16).reshape(1, 2, head_cols // 2, width)
        grad_mixed = dot_rows(grad_one_low, w_out).astype(BF16)
        grad_packed = jnp.concatenate(
            attend_back_plain(*parts, grad_mixed, tops, allowed, scale_qk), axis=1
        )
        g_qkv = dot_first(grad_packed, act_one).astype(BF16).reshape(3, 2, head_cols // 2, width)
        back_in = add_cores(dot_plain(grad_packed, w_qkv))
        back_one, gain_one, shift_one = norm_back(stream, gains[0], back_in)
        grad_in = own_rows((grad_one + back_one).astype(BF16))
        grad_in = lax.ppermute(grad_in, (DP, MP), back_moves)

        grad_pre_sum = jnp.sum(grad_pre_enc, axis=0, dtype=F32).reshape(2, width)
        packed_sum = jnp.sum(grad_packed, axis=0, dtype=F32)
        smalls = jnp.concatenate(
            [
                jnp.sum(grad_one_low, axis=0, dtype=F32)[None],
                jnp.where(is_enc, jnp.sum(grad_enc_low, axis=0, dtype=F32), smalls[1])[None],
                gain_one[None],
                jnp.where(is_enc, gain_b, smalls[3])[None],
                gain_three[None],
                shift_one[None],
                jnp.where(is_enc, shift_b, smalls[6])[None],
                shift_three[None],
                jnp.concatenate([packed_sum[:head_cols], packed_sum[2 * head_cols :]])[None],
                jnp.where(is_enc, grad_pre_sum, smalls[9:11]),
                smalls[11:],
            ]
        )
        g_in = jnp.where(is_enc, g_in, g_in_dec)
        g_mlp = jnp.where(is_enc, g_mlp, g_mlp_dec)
        s_in, s_mlp, s_out, s_qkv, s_cross, total = reduce_plain([g_in, g_mlp, g_out, g_qkv, g_cross], smalls)
        s_cross = jnp.where(is_enc, lax.ppermute(s_cross[:2], TOWER, [(1, 0)]), s_cross[2:])

    def turned(x):
        return jnp.swapaxes(x, 1, 2).astype(F32)

    cross_pair = jnp.stack(
        [
            s_cross[0].T,
            s_cross[1].T,
        ]
    ).astype(F32)
    first = total[0]
    qv_total = jnp.stack(
        [
            total[:, 8, :head_cols].reshape(-1),
            total[:, 8, head_cols:].reshape(-1),
        ]
    )
    in_total = total[:, 9:11].reshape(-1)
    return (
        tower_out[None],
        grad_in[None],
        turned(s_qkv)[None],
        s_out.astype(F32),
        turned(s_in),
        s_mlp.astype(F32),
        cross_pair[None],
        qv_total[None],
        first[0:1],
        in_total[None],
        first[1:2],
        first[2:5][None],
        first[5:8][None],
    )


def solution(mesh):
    return jax.shard_map(
        body,
        mesh=mesh,
        in_specs=(
            P(TOWER, (DP, MP), None),
            P(TOWER, (DP, MP), None),
            P(DP, None),
            P(DP),
            P(TOWER, None, None, MP),
            P(TOWER, MP, None),
            P(TOWER, None, MP),
            P(TOWER, MP, None),
            P(TOWER, None, None, MP),
            P(TOWER, None, None),
            P(TOWER, None),
            P(TOWER, None),
            P(TOWER, None),
            P(TOWER, None, None),
            P(TOWER, None, None),
        ),
        out_specs=(
            P(TOWER, (DP, MP), None),
            P(TOWER, (DP, MP), None),
            P(TOWER, None, DP, MP),
            P(TOWER, MP, DP),
            P(TOWER, DP, MP),
            P(TOWER, MP, DP),
            P(TOWER, None, DP, MP),
            P(TOWER, None, None),
            P(TOWER, None),
            P(TOWER, None),
            P(TOWER, None),
            P(TOWER, None, None),
            P(TOWER, None, None),
        ),
        check_vma=False,
    )
```

```python
import functools
from typing import Any, NamedTuple

import jax
import jax.numpy as jnp
from jax import lax
from jax.experimental import pallas as pl
from jax.experimental.pallas import tpu as pltpu
from jax.sharding import PartitionSpec as P

TOWER = "tower"
DP = "dp"
MP = "mp"
HDIM = 64
PATCH = 576
LTXT = 64
EPS = 1e-06
NEG = -1e30
LANES = 128
MESH = pl.DeviceIdType.MESH
F32 = jnp.float32
BF16 = jnp.bfloat16
VMEM_LIMIT = 60 * 1024 * 1024
TAIL_LIMIT = 67043328


def norm_parts(values):
    center = values - jnp.mean(values, axis=-1, keepdims=True)
    spread = jnp.mean(center * center, axis=-1, keepdims=True)
    scale = lax.rsqrt(spread + EPS)
    return (center * scale, scale)


def norm_rows(values, gain_vec, shift_vec):
    unit, _ = norm_parts(values)
    return unit * gain_vec + shift_vec


def norm_back(values, gain_vec, grad_normed):
    unit, scale = norm_parts(values)
    inner = grad_normed * gain_vec
    mean_one = jnp.mean(inner, axis=-1, keepdims=True)
    mean_two = jnp.mean(inner * unit, axis=-1, keepdims=True)
    back = (inner - mean_one - unit * mean_two) * scale
    return (back, jnp.sum(grad_normed * unit, axis=0), jnp.sum(grad_normed, axis=0))


def gelu_tanh(values):
    return jax.nn.gelu(values, approximate=True)


def dot_rows(left, right):
    return lax.dot_general(left, right, (((1,), (1,)), ((), ())), preferred_element_type=F32)


def dot_first(left, right):
    return lax.dot_general(left, right, (((0,), (0,)), ((), ())), preferred_element_type=F32)


def dot_plain(left, right):
    return lax.dot_general(left, right, (((1,), (0,)), ((), ())), preferred_element_type=F32)


def spots():
    tower = lax.axis_index(TOWER)
    dp = lax.axis_index(DP)
    z = lax.axis_index(MP)
    core = lax.rem(dp, 2)
    line = dp // 2
    return tower, dp, z, core, line, dp + 2 - 4 * line, dp + 1 - 2 * core


def greet(target):
    pl.semaphore_signal(pltpu.get_barrier_semaphore(), inc=1, device_id=target, device_id_type=MESH)


def weight_steps(pieces, srcs, outs, stages, sems):
    send_sem, recv_sem, local_sem, twin_send, twin_recv = sems
    tower, dp, z, core, line, other, partner = spots()
    place = z + core * (3 - 2 * z)
    ahead = z + 1 - 2 * core
    behind = z - 1 + 2 * core
    slot_of = (core, 1 - core)
    holder = place <= 1
    far_src = [k for k, p in enumerate(pieces) if p[7]]

    def spot(piece, slot, half):
        which, first, _, count, start, size, _, _ = piece
        part = size // 2
        return outs[which].at[pl.ds(first, count), slot, pl.ds(start + half * part, part), :]

    def own(piece):
        which, _, first, count, start, size, _, far = piece
        part = size // 2
        if far:
            return spot(piece, lax.rem(z, 2), line)
        return srcs[which].at[pl.ds(first, count), pl.ds(start + line * part, part), :]

    def move(k, source, slot, half, kind, arrive, target):
        return pltpu.make_async_remote_copy(
            src_ref=source,
            dst_ref=spot(pieces[k], slot, half),
            send_sem=send_sem.at[k, kind],
            recv_sem=recv_sem.at[k, arrive],
            device_id=target,
            device_id_type=MESH,
        )

    def twin_copy():
        which = pieces[far_src[0]][0]
        return pltpu.make_async_remote_copy(
            src_ref=srcs[which],
            dst_ref=outs[which].at[pl.ds(0, srcs[which].shape[0]), lax.rem(z, 2)],
            send_sem=twin_send,
            recv_sem=twin_recv,
            device_id={TOWER: 1 - tower},
            device_id_type=MESH,
        )

    def local_in(i):
        return pltpu.make_async_copy(srcs[i], stages[i], local_sem.at[i, 0])

    def local_out(i):
        first = outs[i].shape[0] - srcs[i].shape[0]
        return pltpu.make_async_copy(
            stages[i], outs[i].at[pl.ds(first, srcs[i].shape[0]), lax.rem(z, 2)], local_sem.at[i, 1]
        )

    def gate(piece, cond):
        return cond if piece[6] is None else jnp.logical_and(cond, tower == piece[6])

    def send_own(k):
        piece = pieces[k]

        @pl.when(gate(piece, place == 0))
        def _():
            move(k, own(piece), slot_of[0], line, 0, 0, {MP: ahead}).start()

        @pl.when(gate(piece, place == 1))
        def _():
            move(k, own(piece), slot_of[1], line, 1, 1, {MP: ahead}).start()
            move(k, own(piece), slot_of[1], line, 2, 1, {MP: behind}).start()

    orders = {t: [k for k, p in enumerate(pieces) if p[6] in (None, t)] for t in (0, 1)}

    def launch(t, place):
        if place >= len(orders[t]):
            return
        k = orders[t][place]

        @pl.when(jnp.logical_and(holder, tower == t))
        def _():
            if far_src and k == far_src[0]:
                twin_copy().wait_recv()
            send_own(k)

    def own_sent(k):
        piece = pieces[k]

        @pl.when(gate(piece, place == 0))
        def _():
            move(k, own(piece), slot_of[0], line, 0, 0, {MP: z}).wait_send()

        @pl.when(gate(piece, place == 1))
        def _():
            move(k, own(piece), slot_of[1], line, 1, 1, {MP: z}).wait_send()
            move(k, own(piece), slot_of[1], line, 2, 1, {MP: z}).wait_send()

    def begin():
        if far_src:

            @pl.when(jnp.logical_and(holder, tower == 0))
            def _():
                twin_copy().start()

        for t in (0, 1):
            for start in range(WINDOW):
                launch(t, start)

    def keeps(i):
        flags = {p[6] for p in pieces if p[0] == i}
        flag = None if len(flags) > 1 else flags.pop()
        return holder if flag is None else jnp.logical_and(holder, tower == flag)

    def begin_local():
        for i in range(len(srcs)):

            @pl.when(keeps(i))
            def _(i=i):
                local_in(i).start()

        for i in range(len(srcs)):

            @pl.when(keeps(i))
            def _(i=i):
                local_in(i).wait()
                local_out(i).start()

    def pass_on(k):
        piece = pieces[k]

        @pl.when(gate(piece, place >= 1))
        def _():
            here = spot(piece, slot_of[0], line)
            move(k, here, slot_of[0], line, 0, 0, {MP: z}).wait_recv()
            move(k, here, slot_of[0], line, 3, 2, {DP: other}).start()

        @pl.when(gate(piece, jnp.logical_and(place >= 1, place <= 2)))
        def _():
            here = spot(piece, slot_of[0], line)
            move(k, here, slot_of[0], line, 0, 0, {MP: ahead}).start()

        @pl.when(gate(piece, place != 1))
        def _():
            here = spot(piece, slot_of[1], line)
            move(k, here, slot_of[1], line, 1, 1, {MP: z}).wait_recv()
            move(k, here, slot_of[1], line, 4, 3, {DP: other}).start()

        @pl.when(gate(piece, place == 2))
        def _():
            here = spot(piece, slot_of[1], line)
            move(k, here, slot_of[1], line, 1, 1, {MP: ahead}).start()

        own_sent(k)
        for t in (0, 1):
            if k in orders[t]:
                launch(t, orders[t].index(k) + WINDOW)

    def arrived(k):
        piece = pieces[k]

        @pl.when(gate(piece, place >= 1))
        def _():
            move(k, spot(piece, slot_of[0], 1 - line), slot_of[0], 1 - line, 3, 2, {DP: dp}).wait_recv()

        @pl.when(gate(piece, place != 1))
        def _():
            move(k, spot(piece, slot_of[1], 1 - line), slot_of[1], 1 - line, 4, 3, {DP: dp}).wait_recv()

    def sent(k):
        piece = pieces[k]

        @pl.when(gate(piece, jnp.logical_or(place == 1, place == 2)))
        def _():
            move(k, spot(piece, slot_of[0], line), slot_of[0], line, 0, 0, {MP: z}).wait_send()

        @pl.when(gate(piece, place == 2))
        def _():
            move(k, spot(piece, slot_of[1], line), slot_of[1], line, 1, 1, {MP: z}).wait_send()

        @pl.when(gate(piece, place >= 1))
        def _():
            move(k, spot(piece, slot_of[0], line), slot_of[0], line, 3, 2, {DP: dp}).wait_send()

        @pl.when(gate(piece, place != 1))
        def _():
            move(k, spot(piece, slot_of[1], line), slot_of[1], line, 4, 3, {DP: dp}).wait_send()

    def end_local(i):
        @pl.when(keeps(i))
        def _():
            local_out(i).wait()

    def end_twin():
        @pl.when(jnp.logical_and(holder, tower == 0))
        def _():
            twin_copy().wait_send()

    return begin, begin_local, pass_on, arrived, sent, end_local, end_twin


def token_steps(blocks, outs, stage, sems):
    send_sem, recv_sem, local_sem = sems
    tower, dp, z, core, line, other, partner = spots()
    stays = z == 3 * core
    size = blocks[0].shape[0]

    def rows(which_core):
        return pl.ds(pl.multiple_of(which_core * size, 16), size)

    def away(i):
        target = {DP: 2 * line + lax.rem(z, 2), MP: 2 * core + z // 2}
        return pltpu.make_async_remote_copy(
            src_ref=blocks[i],
            dst_ref=outs[i].at[rows(lax.rem(z, 2)), :],
            send_sem=send_sem.at[i, 0],
            recv_sem=recv_sem.at[i, 0],
            device_id=target,
            device_id_type=MESH,
        )

    def across(i, which_core):
        return pltpu.make_async_remote_copy(
            src_ref=outs[i].at[rows(which_core), :],
            dst_ref=outs[i].at[rows(which_core), :],
            send_sem=send_sem.at[i, 1],
            recv_sem=recv_sem.at[i, 1],
            device_id={DP: partner},
            device_id_type=MESH,
        )

    def begin(i):
        @pl.when(jnp.logical_not(stays))
        def _():
            away(i).start()

        @pl.when(stays)
        def _():
            first = pltpu.make_async_copy(blocks[i], stage.at[i], local_sem.at[i, 0])
            first.start()
            first.wait()
            second = pltpu.make_async_copy(stage.at[i], outs[i].at[rows(core), :], local_sem.at[i, 1])
            second.start()
            second.wait()
            across(i, core).start()

    def relay(i):
        @pl.when(jnp.logical_not(stays))
        def _():
            away(i).wait_recv()
            across(i, core).start()

    def finish(i):
        across(i, 1 - core).wait_recv()
        across(i, core).wait_send()

        @pl.when(jnp.logical_not(stays))
        def _():
            away(i).wait_send()

    return begin, relay, finish


TILE = 32
LAG = 1
WINDOW = 2


def barrier_all(peers, options):
    for cond, target in peers:
        if cond is None:
            greet(target)
        else:
            pl.when(cond)(functools.partial(greet, target))
    for cond, count in options:

        @pl.when(cond)
        def _(count=count):
            pl.semaphore_wait(pltpu.get_barrier_semaphore(), count)


def fold_rows(tile):
    return jnp.sum(tile.reshape(tile.shape[0] // 8, 8, tile.shape[1]), axis=0)


def row_tiles(total, run, carry, first=0, unroll=1):
    tile = next(t for t, by in ((64, 192), (96, 96), (48, 48), (32, 32)) if total % by == 0)
    turns = total // tile

    def step(i, kept):
        return run(pl.ds(pl.multiple_of(first + i * tile, 16), tile), kept)

    return lax.fori_loop(0, turns, step, carry, unroll=unroll)


def norm_back_tile(values, gain, grads):
    unit, scale = norm_parts(values)
    inner = grads * gain
    mean_one = jnp.mean(inner, axis=-1, keepdims=True)
    mean_two = jnp.mean(inner * unit, axis=-1, keepdims=True)
    return ((inner - mean_one - unit * mean_two) * scale, fold_rows(grads * unit), fold_rows(grads))


def gelu_both(v):
    rate = 0.7978845608028654
    square = v * v
    bend = jnp.tanh(rate * (v + 0.044715 * (square * v)))
    lifted = 0.5 * (1.0 + bend)
    slope = lifted + 0.5 * v * (1.0 - bend * bend) * (rate * (1.0 + 3.0 * 0.044715 * square))
    return (v * lifted, slope)


def low_lanes_of(count):
    return lax.broadcasted_iota(jnp.int32, (count, LANES), 1) < HDIM


def stack_all(block, low):
    wide = block.astype(F32)
    return jnp.concatenate([jnp.where(low, wide, 0.0), jnp.where(low, 0.0, wide)], axis=0)


def merge_all(both, low):
    count = both.shape[0] // 2
    return jnp.where(low, both[:count], both[count:])


def lane_block(index):
    return pl.ds(pl.multiple_of(index * LANES, LANES), LANES)


def scores_of(keys, queries, mask):
    scores = dot_rows(keys, queries)
    if mask is None:
        return scores
    block = mask[...]
    return scores + jnp.concatenate([block, block], axis=1)


def forward_heads(queries, keys, vals, mask, low):
    scores = scores_of(keys, queries, mask)
    top = jnp.max(scores, axis=0, keepdims=True)
    grown = jnp.exp(scores - top)
    total = jnp.sum(grown, axis=0, keepdims=True)
    weights = (grown * (1.0 / total)).astype(BF16)
    return (merge_all(dot_first(weights, vals), low), top + jnp.log(total))


def backward_heads(queries, keys, vals, grads, tops, mask, low, scale):
    weights = jnp.exp(scores_of(keys, queries, mask) - tops)
    grad_w = dot_rows(vals, grads)
    row_dot = jnp.sum(weights * grad_w, axis=0, keepdims=True)
    grad_s = (weights * (grad_w - row_dot)).astype(BF16)
    grad_q = merge_all(dot_first(keys, grad_s).T, low) * scale
    return (grad_q, dot_plain(grad_s, queries), dot_plain(weights.astype(BF16), grads))


def fill_mask(mask, col, row, is_dec):
    count = mask.shape[0]

    def tile(rows, kept):
        shape = (rows.size, count)
        key_at = lax.broadcasted_iota(jnp.int32, shape, 0) + rows.start
        query_at = lax.broadcasted_iota(jnp.int32, shape, 1)
        allowed = jnp.logical_and(key_at <= query_at, col[rows, 0:1] == row[0:1, :])
        mask[rows, :] = jnp.where(jnp.logical_or(allowed, jnp.logical_not(is_dec)), 0.0, NEG)
        return kept

    row_tiles(count, tile, 0)


def self_forward(packed, mask, out, tops, pairs, scale):
    low = low_lanes_of(packed.shape[0])

    @pl.loop(0, pairs)
    def _(pair):
        queries = (stack_all(packed[:, lane_block(pair)], low) * scale).astype(BF16)
        mixed, top = forward_heads(
            queries, packed[:, lane_block(pairs + pair)], packed[:, lane_block(2 * pairs + pair)], mask, low
        )
        out[:, lane_block(pair)] = mixed.astype(BF16)
        tops[pair, 0:1, :] = top


def self_backward(packed, grads, tops, mask, out, pairs, scale, between):
    low = low_lanes_of(packed.shape[0])

    @pl.loop(0, pairs)
    def _(pair):
        queries = (stack_all(packed[:, lane_block(pair)], low) * scale).astype(BF16)
        head_grads = stack_all(grads[:, lane_block(pair)], low).astype(BF16)
        grad_q, grad_k, grad_v = backward_heads(
            queries,
            packed[:, lane_block(pairs + pair)],
            packed[:, lane_block(2 * pairs + pair)],
            head_grads,
            tops[pair, 0:1, :],
            mask,
            low,
            scale,
        )
        out[:, lane_block(pair)] = grad_q.astype(BF16)
        out[:, lane_block(pairs + pair)] = grad_k.astype(BF16)
        out[:, lane_block(2 * pairs + pair)] = grad_v.astype(BF16)
        pl.when(pair == 1)(between)


def cross_forward(image, query, keys, vals, picks, out, tops, pairs, scale):
    low = low_lanes_of(query.shape[0])

    @pl.loop(0, pairs)
    def _(pair):
        cols = lane_block(pair)
        queries = (stack_all(query[:, cols], low) * scale).astype(BF16)
        mixed, top = forward_heads(queries, keys[image, :, cols], vals[image, :, cols], None, low)
        kept = jnp.where(picks[...] == image, mixed, out[:, cols].astype(F32))
        out[:, cols] = kept.astype(BF16)
        tops[image, pair, 0:1, :] = top


def cross_backward(query, keys, vals, grads, picks, tops, dq, dk, dv, sum_q, pairs, scale):
    low = low_lanes_of(query.shape[0])

    @pl.loop(0, pairs)
    def _(pair):
        cols = lane_block(pair)
        queries = (stack_all(query[:, cols], low) * scale).astype(BF16)
        sum_q[...] = jnp.zeros_like(sum_q)

        @pl.loop(0, 2)
        def _(image):
            own = jnp.where(picks[...] == image, grads[:, cols].astype(F32), 0.0)
            grad_q, grad_k, grad_v = backward_heads(
                queries,
                keys[image, :, cols],
                vals[image, :, cols],
                stack_all(own, low).astype(BF16),
                tops[image, pair, 0:1, :],
                None,
                low,
                scale,
            )
            sum_q[...] += grad_q
            dk[image, :, cols] = grad_k.astype(BF16)
            dv[image, :, cols] = grad_v.astype(BF16)

        dq[:, cols] = sum_q[...].astype(BF16)


class Reducer:
    def __init__(self, grads, near, far, outs, sems, window, first, last, near_last):
        self.grads, self.near, self.far, self.outs = grads, near, far, outs
        self.y_send, self.y_recv, self.z_send, self.z_recv, self.c_send, self.c_recv = sems
        self.tower, self.dp, self.z, self.core, self.line, self.other, self.partner = spots()
        self.place = self.z + self.core * (3 - 2 * self.z)
        self.holder = self.place <= 1
        self.slot = lax.rem(self.z, 2)
        self.half = grads.shape[3] // 2
        self.rows = grads.shape[2]
        self.window, self.first, self.last, self.near_last = window, first, last, near_last

    def lanes(self, line):
        return pl.ds(pl.multiple_of(line * self.half, LANES), self.half)

    def to_line(self, k):
        return pltpu.make_async_remote_copy(
            src_ref=self.grads.at[k, :, :, self.lanes(1 - self.line)],
            dst_ref=self.near.at[k],
            send_sem=self.y_send.at[k],
            recv_sem=self.y_recv.at[k],
            device_id={DP: self.other},
            device_id_type=MESH,
        )

    def send(self, source, target, k, sent, got, where):
        return pltpu.make_async_remote_copy(
            src_ref=source,
            dst_ref=target,
            send_sem=self.z_send.at[k, sent],
            recv_sem=self.z_recv.at[k, got],
            device_id={MP: where},
            device_id_type=MESH,
        )

    def inward(self, k):
        return self.send(self.near.at[k], self.far.at[k], k, 0, 0, 2 - self.core)

    def beside(self, k):
        return self.send(self.near.at[k, 1 - self.slot], self.far.at[k, 0], k, 0, 0, 4 * self.core + 1 - self.z)

    def onward(self, k, shard):
        return self.send(self.near.at[k, shard], self.far.at[k, 1], k, shard, 1, 2 * self.core + shard)

    def to_core(self, k):
        return pltpu.make_async_remote_copy(
            src_ref=self.outs.at[k],
            dst_ref=self.outs.at[k],
            send_sem=self.c_send.at[k],
            recv_sem=self.c_recv.at[k],
            device_id={DP: self.partner},
            device_id_type=MESH,
        )

    def launch(self, k):
        self.to_line(k).start()

    def tiles(self, run):
        @pl.loop(0, self.rows // TILE)
        def _(i):
            run(pl.ds(pl.multiple_of(i * TILE, TILE), TILE))

    def add_near(self, k, more=True):
        self.to_line(k).wait_send()
        self.to_line(k).wait_recv()
        if more:
            pl.when(k + self.window < self.near_last)(lambda: self.launch(k + self.window))

        def run(rows):
            for b in range(2):
                total = self.grads[k, b, rows, self.lanes(self.line)].astype(F32) + self.near[k, b, rows, :].astype(F32)
                self.near[k, b, rows, :] = total.astype(BF16)

        self.tiles(run)
        if more:
            pl.when(k < self.last)(lambda: self.hop(k))

    def hop(self, k):
        pl.when(self.place == 3)(self.inward(k).start)
        pl.when(self.holder)(self.beside(k).start)

    def add_mid(self, k):
        @pl.when(self.place == 2)
        def _():
            self.inward(k).wait_recv()

            def run(rows):
                for b in range(2):
                    total = self.near[k, b, rows, :].astype(F32) + self.far[k, b, rows, :].astype(F32)
                    self.near[k, b, rows, :] = total.astype(BF16)

            self.tiles(run)
            for shard in range(2):
                self.onward(k, shard).start()

    def add_far(self, k):
        @pl.when(self.holder)
        def _():
            self.beside(k).wait_recv()
            self.onward(k, 0).wait_recv()

            def run(rows):
                total = self.near[k, self.slot, rows, :].astype(F32)
                for seat in range(2):
                    total = total + self.far[k, seat, rows, :].astype(F32)
                self.outs[k, rows, :] = total.astype(BF16)

            self.tiles(run)
            self.to_core(k).start()

    def step(self, k, mid=1):
        self.add_near(k)
        if mid:
            pl.when(k - LAG >= self.first)(lambda: self.add_mid(k - LAG))

    def drain(self, begin):
        @pl.loop(begin, max(self.near_last, self.last + 2 * LAG))
        def _(i):
            pl.when(i < self.near_last)(lambda: self.add_near(i))
            j = i - LAG
            pl.when(jnp.logical_and(j >= self.first, j < self.last))(lambda: self.add_mid(j))
            n = j - LAG
            pl.when(jnp.logical_and(n < self.last, n >= self.first))(lambda: self.add_far(n))

    def far_before(self, begin):
        @pl.loop(self.first, jnp.maximum(self.first, begin - 2 * LAG))
        def _(k):
            self.add_far(k)

    def close(self):
        @pl.loop(self.first, self.last)
        def _(k):
            pl.when(self.place == 3)(self.inward(k).wait_send)

            @pl.when(self.place == 2)
            def _():
                for shard in range(2):
                    self.onward(k, shard).wait_send()

            @pl.when(self.holder)
            def _():
                self.beside(k).wait_send()
                self.to_core(k).wait_send()

            @pl.when(jnp.logical_not(self.holder))
            def _():
                self.to_core(k).wait_recv()


class Tail(NamedTuple):
    d_three: Any
    base: Any
    upstream: Any
    gains: Any
    smalls: Any
    hid: Any
    w_mlp: Any
    pre: Any
    act: Any
    w_in: Any
    x1: Any
    w_out: Any
    mixed: Any
    packed: Any
    tops: Any
    seg_col: Any
    seg_row: Any
    a_one: Any
    w_qkv: Any
    x0: Any


IMAGE_ONLY = Tail._fields[5:11]


def tail_kernel(pairs, scale, *refs):
    it = iter(refs)
    hbm = Tail(*[next(it) for _ in Tail._fields])
    cross_in, tower_rows = next(it), next(it)
    outs = next(it)
    small_out, grad_out, from_text, tower_out = next(it), next(it), next(it), next(it)
    vm = Tail(*[next(it) for _ in Tail._fields])
    grads, near, far = next(it), next(it), next(it)
    g_f32, g_low, grad_hid, grad_pre, d_packed, mix_grad = (next(it) for _ in range(6))
    part_send, part_recv, mask, smalls, small_near, small_all, own_grad = (next(it) for _ in range(7))
    load_sem, red_sems, part_sem, small_sem, move_sem, twin_sem = next(it), [next(it) for _ in range(6)], next(it), next(it), next(it), next(it)
    tower, dp, z, core, line, other, partner = spots()
    is_enc = tower == 0
    is_dec = tower == 1
    stays = z == 3 * core
    tokens, width = g_f32.shape
    rows_txt = tokens // LTXT
    quarter = tokens // 2
    heads = mix_grad.shape[1]
    rows_of = grads.shape[2]
    ffn_blocks = width // rows_of
    text_first = 2 * ffn_blocks - 2

    home = {DP: 2 * line + z // 2, MP: 2 * lax.rem(z, 2) + core}
    guest = {DP: 2 * line + lax.rem(z, 2), MP: 2 * core + z // 2}
    moved = jnp.logical_not(stays)
    peers = [(None, {DP: other}), (None, {DP: partner}), (is_enc, {TOWER: 1 - tower})]
    peers += [(None, {MP: lax.rem(z + away, 4)}) for away in range(1, 4)]
    peers += [(moved, home), (moved, guest)]
    barrier_all(
        peers,
        [
            (jnp.logical_and(is_enc, stays), 5),
            (jnp.logical_and(is_enc, moved), 7),
            (jnp.logical_and(is_dec, stays), 6),
            (jnp.logical_and(is_dec, moved), 8),
        ],
    )

    def load(i):
        return pltpu.make_async_copy(hbm[i], vm[i], load_sem.at[i])

    def on_side(i, run):
        if Tail._fields[i] in IMAGE_ONLY:
            pl.when(is_enc)(run)
        else:
            run()

    pl.when(is_dec)(lambda: pltpu.make_async_copy(cross_in, near.at[pl.ds(text_first, 2)], load_sem.at[len(hbm)]).start())
    for i in range(len(hbm)):
        on_side(i, load(i).start)

    def need(*wanted):
        for i, ref in enumerate(vm):
            if any(ref is one for one in wanted):
                on_side(i, load(i).wait)

    first_block = text_first * tower
    blocks = grads.shape[0]
    red = Reducer(grads, near, far, outs, red_sems, 2 + tower, first_block, blocks, blocks)

    def twin_copy():
        return pltpu.make_async_remote_copy(
            src_ref=outs.at[pl.ds(text_first, 2)],
            dst_ref=from_text,
            send_sem=twin_sem.at[0],
            recv_sem=twin_sem.at[1],
            device_id={TOWER: 1 - tower},
            device_id_type=MESH,
        )

    cross_load = pltpu.make_async_copy(cross_in, near.at[pl.ds(text_first, 2)], load_sem.at[len(hbm)])

    @pl.when(is_dec)
    def _():
        cross_load.wait()
        red.hop(text_first)
        red.hop(text_first + 1)

    def home_move(source, target, k):
        return pltpu.make_async_remote_copy(
            src_ref=source,
            dst_ref=target,
            send_sem=move_sem.at[k, 0],
            recv_sem=move_sem.at[k, 1],
            device_id=home,
            device_id_type=MESH,
        )

    @pl.when(moved)
    def _():
        home_move(tower_rows, tower_out, 0).start()

    @pl.when(stays)
    def _():
        pltpu.make_async_copy(tower_rows, own_grad, move_sem.at[0, 0]).start()
        pltpu.make_async_copy(tower_rows, own_grad, move_sem.at[0, 0]).wait()
        pltpu.make_async_copy(own_grad, tower_out, move_sem.at[0, 1]).start()
        pltpu.make_async_copy(own_grad, tower_out, move_sem.at[0, 1]).wait()

    def part_copy(k):
        return pltpu.make_async_remote_copy(
            src_ref=part_send.at[k],
            dst_ref=part_recv.at[k],
            send_sem=part_sem.at[k, 0],
            recv_sem=part_sem.at[k, 1],
            device_id={DP: partner},
            device_id_type=MESH,
        )

    zero = jnp.zeros((8, width), F32)
    need(vm.d_three, vm.base, vm.upstream, vm.gains, vm.smalls)
    smalls[...] = vm.smalls[...]

    def put(row, value):
        smalls[pl.ds(row, 1), :] = jnp.sum(value, axis=0, keepdims=True)

    def third(rows, kept):
        back, dg, db = norm_back_tile(vm.base[rows, :], vm.gains[2], vm.d_three[rows, :])
        total = vm.upstream[rows, :] + back
        g_f32[rows, :] = total
        low = total.astype(BF16)
        g_low[rows, :] = low
        return (kept[0] + dg, kept[1] + db, kept[2] + fold_rows(low.astype(F32)))

    dg, db, bias = row_tiles(tokens, third, (zero, zero, zero), 0, 3)
    put(4, dg)
    put(7, db)

    @pl.when(is_enc)
    def _():
        put(1, bias)
        need(vm.hid)

        @pl.loop(0, 2)
        def _(b):
            made = dot_first(vm.hid[:, pl.ds(pl.multiple_of(b * width, LANES), width)], g_low[...]).astype(BF16)
            grads[0:ffn_blocks, b] = made.reshape(ffn_blocks, rows_of, width)

        red.launch(0)
        need(vm.w_mlp, vm.pre)

        @pl.loop(0, 2)
        def _(b):
            cols = pl.ds(pl.multiple_of(b * width, LANES), width)
            grad_hid[...] = dot_rows(g_low[...], vm.w_mlp[cols, :])

            def bend(rows, kept):
                low = (grad_hid[rows, :] * gelu_both(vm.pre[rows, cols])[1]).astype(BF16)
                grad_pre[b, rows, :] = low
                return kept + fold_rows(low.astype(F32))

            put(9 + b, row_tiles(tokens, bend, zero))

        red.launch(1)
        need(vm.act, vm.w_in)

        @pl.loop(0, 2)
        def _(b):
            made = dot_first(grad_pre[b], vm.act[...]).astype(BF16)
            grads[ffn_blocks : 2 * ffn_blocks, b] = made.reshape(ffn_blocks, rows_of, width)

        red.step(0)
        grad_hid[...] = jnp.zeros_like(grad_hid)

        @pl.loop(0, 2)
        def _(b):
            grad_hid[...] += dot_rows(grad_pre[b], vm.w_in[b])

        def lower(rows, kept):
            part_send[0, rows, :] = grad_hid[rows, :].astype(BF16)
            return kept

        row_tiles(tokens, lower, 0)
        part_copy(0).start()
        need(vm.x1)
        part_copy(0).wait()

        def second(rows, kept):
            grad = part_send[0, rows, :].astype(F32) + part_recv[0, rows, :].astype(F32)
            back, dg, db = norm_back_tile(vm.x1[rows, :], vm.gains[1], grad)
            total = g_f32[rows, :] + back
            g_f32[rows, :] = total
            low = total.astype(BF16)
            g_low[rows, :] = low
            return (kept[0] + dg, kept[1] + db, kept[2] + fold_rows(low.astype(F32)))

        dg, db, bias_two = row_tiles(tokens, second, (zero, zero, zero), 0, 3)
        put(3, dg)
        put(6, db)
        put(0, bias_two)
        red.step(1)

    @pl.when(is_dec)
    def _():
        put(0, bias)

    need(vm.w_out, vm.mixed, vm.packed, vm.tops, vm.seg_col, vm.seg_row)
    mix_grad[...] = dot_rows(g_low[...], vm.w_out[...]).astype(BF16)
    grads[2 * ffn_blocks] = dot_first(vm.mixed[...], g_low[...]).astype(BF16).reshape(grads.shape[1:])

    fill_mask(mask, vm.seg_col, vm.seg_row, is_dec)

    @pl.when(is_enc)
    def _():
        red.step(2)

    @pl.when(is_dec)
    def _():
        red.launch(2 * ffn_blocks)

    def between():
        @pl.when(is_enc)
        def _():
            red.step(3)

    self_backward(vm.packed, mix_grad, vm.tops, mask, d_packed, pairs, scale, between)


    @pl.when(is_enc)
    def _():
        red.step(4)

    @pl.when(is_dec)
    def _():
        red.add_mid(text_first)

    now = 5 + (2 * ffn_blocks - 5) * tower


    need(vm.a_one, vm.w_qkv, vm.x0)

    @pl.loop(0, 3)
    def _(a):
        cols = pl.ds(pl.multiple_of(a * heads, LANES), heads)
        made = dot_first(d_packed[:, cols], vm.a_one[...]).astype(BF16)
        grads[2 * ffn_blocks + 1 + a] = made.reshape(grads.shape[1:])


    @pl.when(is_dec)
    def _():
        red.launch(2 * ffn_blocks + 1)
        red.launch(2 * ffn_blocks + 2)

    red.step(now)
    grad_hid[...] = jnp.zeros_like(grad_hid)

    @pl.loop(0, 3)
    def _(a):
        cols = pl.ds(pl.multiple_of(a * heads, LANES), heads)
        grad_hid[...] += dot_plain(d_packed[:, cols], vm.w_qkv[cols, :])


    def lower_two(rows, kept):
        part_send[1, rows, :] = grad_hid[rows, :].astype(BF16)
        return (
            kept[0] + fold_rows(d_packed[rows, pl.ds(0, heads)].astype(F32)),
            kept[1] + fold_rows(d_packed[rows, pl.ds(2 * heads, heads)].astype(F32)),
        )

    small_zero = jnp.zeros((8, heads), F32)
    q_sum, v_sum = row_tiles(tokens, lower_two, (small_zero, small_zero))
    part_copy(1).start()
    pl.when(is_enc)(lambda: red.step(now + 1))
    smalls[8:9, :] = jnp.concatenate(
        [jnp.sum(q_sum, axis=0, keepdims=True), jnp.sum(v_sum, axis=0, keepdims=True)], axis=1
    )
    part_copy(1).wait()

    def first(rows, kept):
        grad = part_send[1, rows, :].astype(F32) + part_recv[1, rows, :].astype(F32)
        back, dg, db = norm_back_tile(vm.x0[rows, :].astype(F32), vm.gains[0], grad)
        part_send[1, rows, :] = (g_f32[rows, :] + back).astype(BF16)
        return (kept[0] + dg, kept[1] + db)

    dg, db = row_tiles(tokens, first, (zero, zero), 0, 3)
    put(2, dg)
    put(5, db)
    mine = pl.ds(pl.multiple_of(core * quarter, TILE), quarter)

    def own_copy(rows, kept):
        shifted = pl.ds(pl.multiple_of(core * quarter + rows.start, 32), rows.size)
        own_grad[rows, :] = part_send[1, shifted, :]
        return kept

    row_tiles(quarter, own_copy, 0)

    small_line = pltpu.make_async_remote_copy(
        src_ref=smalls,
        dst_ref=small_near,
        send_sem=small_sem.at[0],
        recv_sem=small_sem.at[1],
        device_id={DP: other},
        device_id_type=MESH,
    )
    small_line.start()

    @pl.when(moved)
    def _():
        home_move(own_grad, grad_out, 1).start()

    @pl.when(stays)
    def _():
        pltpu.make_async_copy(own_grad, grad_out, move_sem.at[1, 0]).start()


    def small_pair(sender, away):
        return pltpu.make_async_remote_copy(
            src_ref=small_all.at[sender],
            dst_ref=small_all.at[sender],
            send_sem=small_sem.at[1 + away],
            recv_sem=small_sem.at[4 + away],
            device_id={MP: lax.rem(z + away, 4)},
            device_id_type=MESH,
        )

    def small_core(which):
        return pltpu.make_async_remote_copy(
            src_ref=small_out.at[which],
            dst_ref=small_out.at[which],
            send_sem=small_sem.at[8],
            recv_sem=small_sem.at[9],
            device_id={DP: partner},
            device_id_type=MESH,
        )

    small_line.wait()
    small_all[z] = smalls[...] + small_near[...]


    for away in range(1, 4):
        small_pair(z, away).start()

    for away in range(1, 4):
        small_pair(lax.rem(z + 4 - away, 4), away).wait_recv()
    small_out[core] = ((small_all[0] + small_all[1]) + small_all[2]) + small_all[3]
    small_core(core).start()
    red.far_before(now + 2 - tower)
    red.drain(now + 2 - tower)
    red.close()
    pl.when(is_dec)(twin_copy().start)

    for away in range(1, 4):
        small_pair(z, away).wait_send()

    @pl.when(moved)
    def _():
        home_move(tower_rows, tower_out, 0).wait()
        home_move(own_grad, grad_out, 1).wait()

    @pl.when(stays)
    def _():
        pltpu.make_async_copy(own_grad, grad_out, move_sem.at[1, 0]).wait()

    pl.when(is_dec)(twin_copy().wait_send)
    pl.when(is_enc)(twin_copy().wait_recv)
    small_core(core).wait_send()
    small_core(1 - core).wait_recv()


def tail(values, cross_grad, tower_rows, scale):
    tokens, width = values.base.shape
    heads = values.mixed.shape[1]
    pairs = heads // LANES
    hidden = values.pre.shape[1]
    quarter = tokens // 2
    half = width // 2
    rows_of = heads // 2
    blocks = 2 * (width // rows_of) + 4
    assert hidden == 2 * width and cross_grad.shape[0] == 2
    hbm = pl.BlockSpec(memory_space=pltpu.HBM)
    vmem = pl.BlockSpec(memory_space=pltpu.VMEM)
    n_in = len(values)
    scratch = [pltpu.VMEM(x.shape, x.dtype) for x in values]
    scratch += [pltpu.VMEM((blocks, 2, rows_of, width), BF16)]
    scratch += [pltpu.VMEM((blocks, 2, rows_of, half), BF16)] * 2
    scratch += [
        pltpu.VMEM((tokens, width), F32),
        pltpu.VMEM((tokens, width), BF16),
        pltpu.VMEM((tokens, width), F32),
        pltpu.VMEM((2, tokens, hidden // 2), BF16),
        pltpu.VMEM((tokens, 3 * heads), BF16),
        pltpu.VMEM((tokens, heads), BF16),
        pltpu.VMEM((2, tokens, width), BF16),
        pltpu.VMEM((2, tokens, width), BF16),
        pltpu.VMEM((tokens, tokens), F32),
        pltpu.VMEM(values.smalls.shape, F32),
        pltpu.VMEM(values.smalls.shape, F32),
        pltpu.VMEM((4,) + values.smalls.shape, F32),
        pltpu.VMEM((quarter, width), BF16),
    ]
    dma = pltpu.SemaphoreType.DMA
    scratch += [dma((n_in + 1,)), dma((blocks,)), dma((blocks,)), dma((blocks, 2)), dma((blocks, 2)), dma((blocks,)), dma((blocks,))]
    scratch += [dma((2, 2)), dma((10,)), dma((2, 2)), dma((2,))]
    out_shape = [jax.ShapeDtypeStruct((blocks, rows_of, half), BF16)]
    out_shape += [
        jax.ShapeDtypeStruct((2,) + values.smalls.shape, F32),
        jax.ShapeDtypeStruct((quarter, width), BF16),
        jax.ShapeDtypeStruct((2, heads // 2, half), BF16),
        jax.ShapeDtypeStruct((quarter, width), BF16),
    ]
    return pl.pallas_call(
        functools.partial(tail_kernel, pairs, scale),
        in_specs=[hbm] * (n_in + 2),
        out_specs=[vmem] * 2 + [hbm] * 3,
        out_shape=out_shape,
        scratch_shapes=scratch,
        compiler_params=pltpu.CompilerParams(
            collective_id=1, has_side_effects=True, vmem_limit_bytes=TAIL_LIMIT
        ),
        name="tail",
    )(*values, cross_grad, tower_rows)


class Head(NamedTuple):
    packed: Any
    mixed: Any
    tops: Any
    a_one: Any
    x1: Any
    base: Any
    act_three: Any
    act: Any
    pre: Any
    hid: Any
    query: Any


def head_kernel(pieces, pairs, scale, *refs):
    it = iter(refs)
    srcs = [next(it) for _ in range(5)]
    blocks = [next(it)]
    seg_ref, image_ref = next(it), next(it)
    gains, shifts, out_b, ffn_out_b, ffn_in_b, qv_b = (next(it) for _ in range(6))
    outs = [next(it) for _ in range(5)]
    tokens = [next(it)]
    seg_out = [next(it) for _ in range(3)]
    hbm = Head(*[next(it) for _ in Head._fields])
    stages = [next(it) for _ in range(5)]
    weight_sems = [next(it) for _ in range(5)]
    token_stage = next(it)
    token_sems = [next(it) for _ in range(3)]
    w_qkv, w_out, w_q, w_in, w_mlp = (next(it) for _ in range(5))
    vm = Head(*[next(it) for _ in Head._fields])
    part_send, part_recv, raw, mask = next(it), next(it), next(it), next(it)
    seg_sem, load_sem, store_sem, part_sem = (next(it) for _ in range(4))
    tower, dp, z, core, line, other, partner = spots()
    is_enc = tower == 0
    is_dec = tower == 1
    stays = z == 3 * core
    moved = jnp.logical_not(stays)
    count, width = vm.x1.shape
    rows_txt = count // LTXT
    heads = vm.mixed.shape[1]
    at_end = jnp.logical_or(z == 0, z == 3)

    peers = [(z > 0, {MP: z - 1}), (z < 3, {MP: z + 1})]
    peers += [(None, {DP: other}), (None, {TOWER: 1 - tower}), (None, {DP: partner})]
    peers += [
        (moved, {DP: 2 * line + lax.rem(z, 2), MP: 2 * core + z // 2}),
        (moved, {DP: 2 * line + z // 2, MP: 2 * lax.rem(z, 2) + core}),
    ]
    barrier_all(
        peers,
        [(stays, 4), (jnp.logical_and(at_end, moved), 6), (jnp.logical_not(at_end), 7)],
    )

    begin, begin_local, pass_on, arrived, sent, end_local, end_twin = weight_steps(
        pieces, srcs, outs, stages, weight_sems
    )
    token_begin, token_relay, token_finish = token_steps(blocks, tokens, token_stage, token_sems)
    token_begin(0)
    begin()

    has_notes = core == z // 2

    def note_send(i):
        return pltpu.make_async_remote_copy(
            src_ref=seg_out[i],
            dst_ref=seg_out[i],
            send_sem=seg_sem.at[i, 0],
            recv_sem=seg_sem.at[i, 1],
            device_id={DP: partner},
            device_id_type=MESH,
        )

    @pl.when(has_notes)
    def _():
        rows = seg_ref.shape[0] // 2
        side = lax.rem(z, 2)
        segs = jnp.where(side == 0, seg_ref[0:rows, :], seg_ref[rows : 2 * rows, :])
        marks = segs + LTXT * lax.broadcasted_iota(jnp.int32, segs.shape, 0)
        tall = jnp.concatenate([marks.astype(F32), jnp.zeros((16 - rows, LTXT), F32)], axis=0).T
        seg_out[1][...] = jnp.zeros_like(seg_out[1])
        for r in range(rows):
            at = pl.ds(r * LTXT, LTXT)
            seg_out[0][at, :] = jnp.broadcast_to(tall[:, r : r + 1], (LTXT, LANES)).astype(jnp.int32)
            seg_out[1][0:1, at] = marks[r : r + 1, :]
            seg_out[2][at, :] = jnp.full((LTXT, LANES), image_ref[side * rows + r], jnp.int32)
        for i in range(3):
            note_send(i).start()

    begin_local()
    token_relay(0)

    def load(i, target, source):
        return pltpu.make_async_copy(source, target, load_sem.at[i])

    def store(ref):
        i = [x is ref for x in vm].index(True)
        return pltpu.make_async_copy(vm[i], hbm[i], store_sem.at[i])

    def part_copy(k):
        return pltpu.make_async_remote_copy(
            src_ref=part_send.at[k],
            dst_ref=part_recv.at[k],
            send_sem=part_sem.at[k, 0],
            recv_sem=part_sem.at[k, 1],
            device_id={DP: partner},
            device_id_type=MESH,
        )

    def normed(source, target, which):
        gain, shift = gains[which], shifts[which]

        def tile(rows, kept):
            unit, _ = norm_parts(source[rows, :].astype(F32))
            target[rows, :] = (unit * gain + shift).astype(BF16)
            return kept

        row_tiles(count, tile, 0, 0, 3)

    def chosen(which, flag, far=False):
        return [k for k, p in enumerate(pieces) if p[0] == which and p[6] == flag and p[7] == far]

    enc_in, enc_mlp, dec_in = chosen(3, 0), chosen(4, 0), chosen(3, 1) + chosen(4, 1)
    k_qkv, k_out, k_own, k_far = chosen(0, None), chosen(1, None), chosen(2, 1), chosen(2, 1, True)
    waiting = {0: enc_in + enc_mlp, 1: k_own + k_far + dec_in}

    def relay(enc=0, dec=0):
        for t, count in ((0, enc), (1, dec)):
            for k in waiting[t][:count]:
                pass_on(k)
            waiting[t] = waiting[t][count:]

    token_finish(0)
    normed(tokens[0], vm.a_one, 0)
    store(vm.a_one).start()
    for k in k_qkv + k_out:
        pass_on(k)
    for k in k_qkv:
        arrived(k)
    end_local(0)
    load(0, w_qkv, outs[0]).start()
    load(0, w_qkv, outs[0]).wait()

    @pl.loop(0, 3)
    def _(part):
        cols = pl.ds(pl.multiple_of(part * heads, LANES), heads)
        own = pl.ds(pl.multiple_of(core * heads, LANES), heads)
        bias = jnp.where(part == 1, 0.0, qv_b[pl.ds(part // 2, 1), own])
        made = dot_rows(vm.a_one[...], w_qkv[part].reshape(heads, width)) + bias
        vm.packed[:, cols] = made.astype(BF16)

    store(vm.packed).start()

    @pl.when(has_notes)
    def _():
        for i in range(3):
            note_send(i).wait_send()

    @pl.when(jnp.logical_not(has_notes))
    def _():
        for i in range(3):
            note_send(i).wait_recv()

    relay(1, 1)
    fill_mask(mask, seg_out[0], seg_out[1], is_dec)
    self_forward(vm.packed, mask, vm.mixed, vm.tops, pairs, scale)
    store(vm.mixed).start()
    store(vm.tops).start()
    for k in k_out:
        arrived(k)
    end_local(1)
    load(1, w_out, outs[1]).start()
    relay(1, 1)
    load(1, w_out, outs[1]).wait()
    part_send[0] = dot_plain(vm.mixed[...], w_out[0].reshape(heads, width)).astype(BF16)
    part_copy(0).start()
    relay(1, 1)
    part_copy(0).wait()

    def add_one(rows, kept):
        total = part_send[0, rows, :].astype(F32) + part_recv[0, rows, :].astype(F32)
        vm.x1[rows, :] = tokens[0][rows, :].astype(F32) + total + out_b[...]
        return kept

    row_tiles(count, add_one, 0)
    store(vm.x1).start()

    @pl.when(is_enc)
    def _():
        relay(1)
        normed(vm.x1, vm.act, 1)
        store(vm.act).start()
        relay(1)
        for k in enc_in:
            arrived(k)
        end_local(3)
        load(3, w_in, outs[3]).start()
        load(3, w_in, outs[3]).wait()
        relay(1)

        @pl.loop(0, 2)
        def _(b):
            cols = pl.ds(pl.multiple_of(b * width, LANES), width)
            raw[...] = dot_plain(vm.act[...], w_in[0, b])
            bias = ffn_in_b[0:1, pl.ds(pl.multiple_of((2 * core + b) * width, LANES), width)]

            def bend(rows, kept):
                pre = raw[rows, :] + bias
                vm.pre[rows, cols] = pre
                vm.hid[rows, cols] = gelu_tanh(pre).astype(BF16)
                return kept

            row_tiles(count, bend, 0)

        relay(1)
        store(vm.pre).start()
        store(vm.hid).start()
        relay(len(waiting[0]))
        for k in enc_mlp:
            arrived(k)
        end_local(4)
        load(4, w_mlp, outs[4]).start()
        load(4, w_mlp, outs[4]).wait()
        part_send[1] = dot_plain(vm.hid[...], w_mlp[0].reshape(2 * width, width)).astype(BF16)
        part_copy(1).start()
        part_copy(1).wait()

        def add_two(rows, kept):
            total = part_send[1, rows, :].astype(F32) + part_recv[1, rows, :].astype(F32)
            vm.base[rows, :] = vm.x1[rows, :] + total + ffn_out_b[...]
            return kept

        row_tiles(count, add_two, 0)

    @pl.when(is_dec)
    def _():
        def same(rows, kept):
            vm.base[rows, :] = vm.x1[rows, :]
            return kept

        row_tiles(count, same, 0)

    store(vm.base).start()
    normed(vm.base, vm.act_three, 2)
    store(vm.act_three).start()

    @pl.when(is_dec)
    def _():
        relay(0, 2)
        for k in k_own:
            arrived(k)
        end_local(2)
        load(2, w_q, outs[2].at[2]).start()
        load(2, w_q, outs[2].at[2]).wait()
        vm.query[...] = dot_rows(vm.act_three[...], w_q[...].reshape(heads, width)).astype(BF16)
        store(vm.query).start()
        relay(0, len(waiting[1]))
        for k in k_far + dec_in:
            arrived(k)
        end_local(3)
        end_local(4)

    for k in range(len(pieces)):
        sent(k)
    end_twin()
    for ref in vm:
        if ref is vm.act or ref is vm.pre or ref is vm.hid:
            pl.when(is_enc)(store(ref).wait)
        elif ref is vm.query:
            pl.when(is_dec)(store(ref).wait)
        else:
            store(ref).wait()


def head(shards, blocks, segment_ids, row_image, vecs, scale):
    qkv, out, cross, ffn_in, ffn_out = shards
    heads = 2 * out.shape[1]
    width = out.shape[2]
    pairs = heads // LANES
    count = 2 * blocks[0].shape[0]
    hidden = 2 * ffn_in.shape[2]

    def cuts(i, flag):
        blocks_of, rows, _ = shards[i].shape
        cut = rows if rows <= 192 else rows // 4
        return [(i, a, a, 1, at, cut, flag, False) for a in range(blocks_of) for at in range(0, rows, cut)]

    pieces = cuts(0, None) + cuts(1, None)
    rows = cross.shape[1]
    pieces += [(2, 2 + a, a, 1, 0, rows, 1, False) for a in range(2)] + [(2, a, a, 1, 0, rows, 1, True) for a in range(2)]
    pieces += cuts(3, 0) + cuts(4, 0) + cuts(3, 1) + cuts(4, 1)[:2]
    n = len(pieces)
    hbm = pl.BlockSpec(memory_space=pltpu.HBM)
    vmem = pl.BlockSpec(memory_space=pltpu.VMEM)
    struct = jax.ShapeDtypeStruct
    made = Head(
        packed=struct((count, 3 * heads), BF16),
        mixed=struct((count, heads), BF16),
        tops=struct((pairs, 8, 2 * count), F32),
        a_one=struct((count, width), BF16),
        x1=struct((count, width), F32),
        base=struct((count, width), F32),
        act_three=struct((count, width), BF16),
        act=struct((count, width), BF16),
        pre=struct((count, hidden), F32),
        hid=struct((count, hidden), BF16),
        query=struct((count, heads), BF16),
    )
    out_shape = [
        jax.ShapeDtypeStruct(((2 if i == 2 else 1) * x.shape[0], 2) + x.shape[1:], BF16) for i, x in enumerate(shards)
    ]
    out_shape += [jax.ShapeDtypeStruct((count, width), BF16)]
    out_shape += [struct((count, LANES), jnp.int32), struct((8, count), jnp.int32), struct((count, LANES), jnp.int32)]
    out_shape += list(made)
    dma = pltpu.SemaphoreType.DMA
    scratch = [pltpu.VMEM(x.shape, BF16) for x in shards]
    scratch += [dma((n, 5)), dma((n, 4)), dma((5, 2)), dma, dma]
    scratch += [pltpu.VMEM((1,) + blocks[0].shape, BF16), dma((1, 2)), dma((1, 2)), dma((1, 2))]
    scratch += [
        pltpu.VMEM((3, 2) + qkv.shape[1:], BF16),
        pltpu.VMEM((1, 2) + out.shape[1:], BF16),
        pltpu.VMEM((2,) + cross.shape[1:], BF16),
        pltpu.VMEM((1, 2) + ffn_in.shape[1:], BF16),
        pltpu.VMEM((1, 2) + ffn_out.shape[1:], BF16),
    ]
    scratch += [pltpu.VMEM(x.shape, x.dtype) for x in made]
    scratch += [
        pltpu.VMEM((2, count, width), BF16),
        pltpu.VMEM((2, count, width), BF16),
        pltpu.VMEM((count, width), F32),
        pltpu.VMEM((count, count), F32),
        dma((3, 2)),
        dma((5,)),
        dma((len(made),)),
        dma((2, 2)),
    ]
    results = pl.pallas_call(
        functools.partial(head_kernel, tuple(pieces), pairs, scale),
        in_specs=[hbm] * 6 + [vmem, pl.BlockSpec(memory_space=pltpu.SMEM)] + [vmem] * 6,
        out_specs=[hbm] * 5 + [vmem] + [vmem] * 3 + [hbm] * len(made),
        out_shape=out_shape,
        scratch_shapes=scratch,
        compiler_params=pltpu.CompilerParams(
            collective_id=0, has_side_effects=True, vmem_limit_bytes=VMEM_LIMIT
        ),
        name="head",
    )(*shards, *blocks, segment_ids, row_image, *vecs)
    return results[:5], results[5], results[6:9], Head(*results[9:])


CHUNKS = 6


def mid_kernel(pieces, pairs, scale, *refs):
    it = iter(refs)
    act_three, x1, query_in, w_cross_in, w_in_in, w_mlp_in, ffn_shard, cot_block, base = (next(it) for _ in range(9))
    gains, shifts, out_b, ffn_out_b, ffn_in_b, qv_b, picks = (next(it) for _ in range(7))
    d_three, upstream, smalls, tower_out, cross_out = (next(it) for _ in range(5))
    outs = next(it)
    stages = [next(it)]
    weight_sems = [next(it) for _ in range(5)]
    token_stage = next(it)
    token_sems = [next(it) for _ in range(3)]
    images, kv, w_cross, w_in, w_mlp = (next(it) for _ in range(5))
    act_txt, query, mixed, tops, y1, y2, act, pre, hid = (next(it) for _ in range(9))
    grad_hid, raw, grad_pre, g_low, mix_grad, dq, dkv, sum_q = (next(it) for _ in range(8))
    keys, vals, dk, dv = kv.at[0], kv.at[1], dkv.at[0], dkv.at[1]
    cot, part_send, part_recv, halves, half_near, sums, image_grad, own_rows = (next(it) for _ in range(8))
    grads, near, far = (next(it) for _ in range(3))
    red_sems = [next(it) for _ in range(6)]
    load_sem, store_sem, part_sem, twin_sem, side_sem, core_sem, half_sem, sum_sem, back_sem, give_sem, home_sem = it
    tower, dp, z, core, line, other, partner = spots()
    is_enc = tower == 0
    is_dec = tower == 1
    stays = z == 3 * core
    moved = jnp.logical_not(stays)
    side = lax.rem(z, 2)
    across_chip = z + 1 - 2 * side
    count, width = y1.shape
    quarter = count // 2
    chunk = quarter // CHUNKS
    heads = mixed.shape[1]

    home = {DP: 2 * line + z // 2, MP: 2 * lax.rem(z, 2) + core}
    guest = {DP: 2 * line + lax.rem(z, 2), MP: 2 * core + z // 2}
    peers = [(None, {DP: other}), (None, {DP: partner}), (None, {TOWER: 1 - tower})]
    peers += [(None, {MP: lax.rem(z + away, 4)}) for away in range(1, 4)]
    peers += [(moved, home), (moved, guest)]
    barrier_all(peers, [(stays, 6), (moved, 8)])

    def remote(source, target, sends, recvs, where):
        return pltpu.make_async_remote_copy(
            src_ref=source,
            dst_ref=target,
            send_sem=sends,
            recv_sem=recvs,
            device_id=where,
            device_id_type=MESH,
        )

    def span(which_core, i):
        return pl.ds(pl.multiple_of(which_core * quarter + i * chunk, 16), chunk)

    def twin_copy(i):
        rows = span(core, i)
        return remote(
            act_three.at[rows, :], images.at[side, rows, :], twin_sem.at[i, 0], twin_sem.at[i, 1], {TOWER: 1 - tower}
        )

    def side_copy(i, image):
        here = images.at[image, span(core, i), :]
        return remote(here, here, side_sem.at[i, 0], side_sem.at[i, 1], {MP: across_chip})

    def core_copy(i, image, which_core, far_image):
        here = images.at[image, span(which_core, i), :]
        return remote(here, here, core_sem.at[far_image, i, 0], core_sem.at[far_image, i, 1], {DP: partner})

    @pl.when(is_enc)
    def _():
        for i in range(CHUNKS):
            twin_copy(i).start()

    token_begin, token_relay, token_finish = token_steps([cot_block], [cot], token_stage, token_sems)
    pl.when(is_enc)(functools.partial(token_begin, 0))
    begin, begin_local, pass_on, arrived, sent, end_local, _ = weight_steps(
        pieces, [ffn_shard], [w_mlp], stages, weight_sems
    )

    def load(i, source, target):
        return pltpu.make_async_copy(source, target, load_sem.at[i])

    held = pl.ds(0, ffn_shard.shape[1] // 2)
    early = [load(5, w_mlp_in.at[:, :, held, :], w_mlp.at[:, :, held, :])]
    text_loads = [
        load(0, w_cross_in, w_cross),
        load(1, query_in, query),
        load(2, x1, y1),
        load(3, w_in_in, w_in),
        load(4, act_three, act_txt),
    ]

    def part_copy(k, h):
        rows = pl.ds(h * quarter, quarter)
        return remote(
            part_send.at[k % 3, rows, :],
            part_recv.at[k % 3, rows, :],
            part_sem.at[k, h, 0],
            part_sem.at[k, h, 1],
            {DP: partner},
        )

    rows_copy = pltpu.make_async_copy(own_rows, tower_out, home_sem.at[0])

    def back_copy(i):
        rows = pl.ds(i * chunk, chunk)
        return remote(
            sums.at[1, rows, :], image_grad.at[span(core, i), :], back_sem.at[i, 0], back_sem.at[i, 1], {TOWER: 1 - tower}
        )

    def back_core(i, which_core):
        here = image_grad.at[span(which_core, i), :]
        return remote(here, here, give_sem.at[i, 0], give_sem.at[i, 1], {DP: partner})

    store_grad = pltpu.make_async_copy(y2, upstream, store_sem.at[0])
    store_three = pltpu.make_async_copy(raw, d_three, store_sem.at[1])
    zero = jnp.zeros((8, width), F32)
    blocks, rows_of = outs.shape[0], outs.shape[1]
    ffn_blocks = width // rows_of
    red = Reducer(grads, near, far, outs, red_sems, 4, 0, blocks, blocks + 2)

    @pl.when(is_enc)
    def _():
        smalls[...] = jnp.zeros_like(smalls)
        mine = pl.ds(pl.multiple_of(core * quarter, TILE), quarter)
        take = load(2, base.at[mine, :], y1.at[pl.ds(0, quarter), :])
        take.start()
        take.wait()

        def lower(rows, kept):
            own_rows[rows, :] = y1[rows, :].astype(BF16)
            return kept

        row_tiles(quarter, lower, 0)
        rows_copy.start()
        token_relay(0)
        token_finish(0)

        def lift(rows, kept):
            y2[rows, :] = cot[rows, :].astype(F32)
            return kept

        row_tiles(count, lift, 0)
        store_grad.start()
        for i in range(CHUNKS):
            back_copy(i).wait_recv()
            back_core(i, core).start()
        for i in range(CHUNKS):
            back_core(i, 1 - core).wait_recv()

        def lift_three(rows, kept):
            raw[rows, :] = image_grad[rows, :].astype(F32)
            return kept

        row_tiles(count, lift_three, 0)
        store_three.start()
        for i in range(CHUNKS):
            twin_copy(i).wait_send()
            back_core(i, core).wait_send()

    @pl.when(is_dec)
    def _():
        for one in early + text_loads:
            one.start()
        for one in early:
            one.wait()
        begin_local()
        smalls[...] = jnp.zeros_like(smalls)

        def put(row, value):
            smalls[pl.ds(row, 1), :] = jnp.sum(value, axis=0, keepdims=True)

        for i in range(CHUNKS):
            twin_copy(i).wait_recv()
            side_copy(i, side).start()
            core_copy(i, side, core, 0).start()
        begin()
        for one in text_loads[:2]:
            one.wait()
        mixed[...] = jnp.zeros_like(mixed)
        for i in range(CHUNKS):
            core_copy(i, side, 1 - core, 0).wait_recv()

        @pl.loop(0, 2)
        def _(turn):
            image = side + turn * (1 - 2 * side)

            @pl.when(turn == 1)
            def _():
                for i in range(CHUNKS):
                    side_copy(i, 1 - side).wait_recv()
                    core_copy(i, 1 - side, core, 1).start()
                token_begin(0)
                for i in range(CHUNKS):
                    core_copy(i, 1 - side, 1 - core, 1).wait_recv()

            @pl.loop(0, 2)
            def _(part):
                kv[part, image] = dot_rows(images[image], w_cross[part].reshape(heads, width)).astype(BF16)

            cross_forward(image, query, keys, vals, picks, mixed, tops, pairs, scale)

        for k in range(len(pieces)):
            pass_on(k)
        token_relay(0)

        def half_part(k, made):
            for h in range(2):
                part_send[k % 3, pl.ds(h * quarter, quarter), :] = made(pl.ds(h * quarter, quarter)).astype(BF16)
                part_copy(k, h).start()

        def add_halves(k, run, carry):
            for h in range(2):
                part_copy(k, h).wait()
                carry = row_tiles(quarter, run, carry, h * quarter)
            return carry

        half_part(0, lambda rows: dot_plain(mixed[rows, :], w_cross[3].reshape(heads, width)))
        for one in text_loads[2:]:
            one.wait()
        gain, shift = gains[1], shifts[1]

        def add_cross(rows, kept):
            total = part_send[0, rows, :].astype(F32) + part_recv[0, rows, :].astype(F32)
            value = y1[rows, :] + total
            y2[rows, :] = value
            unit, _ = norm_parts(value)
            act[rows, :] = (unit * gain + shift).astype(BF16)
            return kept

        token_finish(0)
        for k in range(len(pieces)):
            arrived(k)
        end_local(0)

        @pl.loop(0, 2)
        def _(b):
            grad_hid[b] = dot_rows(cot[...], w_mlp[0, b])

        add_halves(0, add_cross, 0)

        @pl.loop(0, 2)
        def _(b):
            cols = pl.ds(pl.multiple_of(b * width, LANES), width)
            pre[...] = dot_plain(act[...], w_in[0, b])
            bias = ffn_in_b[0:1, pl.ds(pl.multiple_of((2 * core + b) * width, LANES), width)]

            def bend(rows, kept):
                lifted, slope = gelu_both(pre[rows, :] + bias)
                hid[rows, cols] = lifted.astype(BF16)
                low = (grad_hid[b, rows, :] * slope).astype(BF16)
                grad_pre[b, rows, :] = low
                return kept + fold_rows(low.astype(F32))

            put(9 + b, row_tiles(count, bend, zero))

        half_part(2, lambda rows: dot_rows(grad_pre[0, rows, :], w_in[0, 0]) + dot_rows(grad_pre[1, rows, :], w_in[0, 1]))

        @pl.loop(0, 2)
        def _(b):
            made = dot_first(grad_pre[b], act[...]).astype(BF16)
            grads[0:ffn_blocks, b] = made.reshape(ffn_blocks, rows_of, width)

        red.launch(0)
        red.launch(1)

        def second(rows, kept):
            low_cot = cot[rows, :].astype(F32)
            grad = part_send[2, rows, :].astype(F32) + part_recv[2, rows, :].astype(F32)
            back, dg, db = norm_back_tile(y2[rows, :], gain, grad)
            total = low_cot + back
            raw[rows, :] = total
            g_low[rows, :] = total.astype(BF16)
            return (kept[0] + dg, kept[1] + db, kept[2] + fold_rows(low_cot))

        dg, db, cot_sum = add_halves(2, second, (zero, zero, zero))
        put(3, dg)
        put(6, db)
        put(1, cot_sum)

        mix_grad[...] = dot_rows(g_low[...], w_cross[3].reshape(heads, width)).astype(BF16)
        cross_backward(query, keys, vals, mix_grad, picks, tops, dq, dk, dv, sum_q, pairs, scale)

        def half_copy(image, far_image):
            return remote(
                halves.at[image, pl.ds(pl.multiple_of((1 - core) * quarter, TILE), quarter), :],
                half_near.at[far_image],
                half_sem.at[far_image, 0],
                half_sem.at[far_image, 1],
                {DP: partner},
            )

        @pl.loop(0, 2)
        def _(i):
            image = side + (1 - i) * (1 - 2 * side)
            made = dot_plain(dkv[0, image], w_cross[0].reshape(heads, width))
            made = made + dot_plain(dkv[1, image], w_cross[1].reshape(heads, width))
            halves[image] = made.astype(BF16)
            half_copy(image, 1 - i).start()

        for k in range(2):
            red.add_near(k, False)
            red.launch(k + 2)

        def sum_copy(i):
            rows = pl.ds(i * chunk, chunk)
            return remote(
                sums.at[0, rows, :], sums.at[2, rows, :], sum_sem.at[i, 0], sum_sem.at[i, 1], {MP: across_chip}
            )

        half_copy(1 - side, 1).wait_recv()
        for i in range(CHUNKS):

            def add_far(rows, kept):
                at = pl.ds(pl.multiple_of(i * chunk + rows.start, 16), rows.size)
                own = pl.ds(pl.multiple_of(core * quarter + i * chunk + rows.start, 16), rows.size)
                total = halves[1 - side, own, :].astype(F32) + half_near[1, at, :].astype(F32)
                sums[0, at, :] = total.astype(BF16)
                return kept

            row_tiles(chunk, add_far, 0)
            sum_copy(i).start()
        @pl.loop(0, 2)
        def _(b):
            cols = pl.ds(pl.multiple_of(b * width, LANES), width)
            made = dot_first(hid[:, cols], cot[...]).astype(BF16)
            grads[ffn_blocks : 2 * ffn_blocks, b] = made.reshape(ffn_blocks, rows_of, width)

        red.launch(4)
        red.launch(5)
        half_copy(side, 0).wait_recv()
        for i in range(CHUNKS):
            sum_copy(i).wait_recv()

            def add_own(rows, kept):
                at = pl.ds(pl.multiple_of(i * chunk + rows.start, 16), rows.size)
                own = pl.ds(pl.multiple_of(core * quarter + i * chunk + rows.start, 16), rows.size)
                total = halves[side, own, :].astype(F32) + half_near[0, at, :].astype(F32)
                sums[1, at, :] = (total + sums[2, at, :].astype(F32)).astype(BF16)
                return kept

            row_tiles(chunk, add_own, 0)
            back_copy(i).start()

        half_part(3, lambda rows: dot_plain(dq[rows, :], w_cross[2].reshape(heads, width)))
        red.hop(0)
        red.hop(1)
        red.step(2, 0)

        def keep_two(rows, kept):
            y1[rows, :] = raw[rows, :]
            return kept

        row_tiles(count, keep_two, 0)
        pltpu.make_async_copy(y1, upstream, store_sem.at[0]).start()

        def lift_query(rows, kept):
            raw[rows, :] = part_send[0, rows, :].astype(F32) + part_recv[0, rows, :].astype(F32)
            return kept

        add_halves(3, lift_query, 0)
        store_three.start()
        pre[...] = jnp.zeros_like(pre)

        @pl.loop(0, 2)
        def _(b):
            pre[...] += dot_plain(hid[:, pl.ds(pl.multiple_of(b * width, LANES), width)], w_mlp[0, b])

        for h in range(2):
            rows = pl.ds(h * quarter, quarter)
            part_send[1, rows, :] = pre[rows, :].astype(BF16)
            part_copy(1, h).start()
        red.add_mid(0)
        red.step(3, 0)
        red.add_mid(1)
        grads[2 * ffn_blocks] = dot_first(dq[...], act_txt[...]).astype(BF16).reshape(grads.shape[1:])
        grads[2 * ffn_blocks + 1] = dot_first(mixed[...], g_low[...]).astype(BF16).reshape(grads.shape[1:])
        red.add_mid(2)
        red.step(4)

        @pl.loop(0, 2)
        def _(which):
            made = dot_first(dkv[which, 0], images[0]) + dot_first(dkv[which, 1], images[1])
            grads[blocks + which] = made.astype(BF16).reshape(grads.shape[1:])

        red.step(5)
        for h in range(2):
            part_copy(1, h).wait()

        def add_last(rows, kept):
            own = pl.ds(pl.multiple_of(core * quarter + rows.start, 32), rows.size)
            total = part_send[1, own, :].astype(F32) + part_recv[1, own, :].astype(F32)
            own_rows[rows, :] = (y2[own, :] + total + ffn_out_b[...]).astype(BF16)
            return kept

        row_tiles(quarter, add_last, 0)
        rows_copy.start()
        red.far_before(6)
        red.drain(6)
        store_cross = pltpu.make_async_copy(near.at[pl.ds(blocks, 2)], cross_out, store_sem.at[2])
        store_cross.start()
        red.close()
        store_cross.wait()
        for i in range(CHUNKS):
            side_copy(i, side).wait_send()
            core_copy(i, side, core, 0).wait_send()
            core_copy(i, 1 - side, core, 1).wait_send()
            sum_copy(i).wait_send()
            back_copy(i).wait_send()
        half_copy(1 - side, 1).wait_send()
        half_copy(side, 0).wait_send()
        for k in range(len(pieces)):
            sent(k)

    rows_copy.wait()
    store_grad.wait()
    store_three.wait()


def middle(values, w_cross, w_in, w_mlp, ffn_shard, cot_block, vecs, picks, scale):
    count, width = values.base.shape
    heads = values.mixed.shape[1]
    pairs = heads // LANES
    hidden = values.hid.shape[1]
    quarter = count // 2
    half = width // 2
    chunk = quarter // CHUNKS
    assert chunk * CHUNKS == quarter
    rows_of = heads // 2
    blocks = 2 * (width // rows_of) + 2
    assert hidden == 2 * width
    cross_shape = (2, 2, rows_of, half)
    rows = ffn_shard.shape[1]
    pieces = [(0, 0, 0, 1, at, rows // 4, 1, False) for at in range(rows // 2, rows, rows // 4)]
    n = len(pieces)
    hbm = pl.BlockSpec(memory_space=pltpu.HBM)
    vmem = pl.BlockSpec(memory_space=pltpu.VMEM)
    dma = pltpu.SemaphoreType.DMA
    low, wide = (count, width), (count, heads)
    scratch = [pltpu.VMEM(ffn_shard.shape, BF16), dma((n, 5)), dma((n, 4)), dma((1, 2)), dma, dma]
    scratch += [pltpu.VMEM((1,) + cot_block.shape, BF16), dma((1, 2)), dma((1, 2)), dma((1, 2))]
    scratch += [
        pltpu.VMEM((2,) + low, BF16),
        pltpu.VMEM((2, 2) + wide, BF16),
        pltpu.VMEM((4, 2, heads // 2, width), BF16),
        pltpu.VMEM((1, 2, width, hidden // 2), BF16),
        pltpu.VMEM((1, 2, hidden // 2, width), BF16),
        pltpu.VMEM(low, BF16),
        pltpu.VMEM(wide, BF16),
        pltpu.VMEM(wide, BF16),
        pltpu.VMEM((2, pairs, 8, 2 * count), F32),
        pltpu.VMEM(low, F32),
        pltpu.VMEM(low, F32),
        pltpu.VMEM(low, BF16),
        pltpu.VMEM(low, F32),
        pltpu.VMEM((count, hidden), BF16),
        pltpu.VMEM((2,) + low, F32),
        pltpu.VMEM(low, F32),
        pltpu.VMEM((2, count, hidden // 2), BF16),
        pltpu.VMEM(low, BF16),
        pltpu.VMEM(wide, BF16),
        pltpu.VMEM(wide, BF16),
        pltpu.VMEM((2, 2) + wide, BF16),
        pltpu.VMEM((count, LANES), F32),
        pltpu.VMEM(low, BF16),
        pltpu.VMEM((3,) + low, BF16),
        pltpu.VMEM((3,) + low, BF16),
        pltpu.VMEM((2,) + low, BF16),
        pltpu.VMEM((2, quarter, width), BF16),
        pltpu.VMEM((3, quarter, width), BF16),
        pltpu.VMEM(low, BF16),
        pltpu.VMEM((quarter, width), BF16),
    ]
    scratch += [pltpu.VMEM((blocks + 2, 2, rows_of, width), BF16), pltpu.VMEM((blocks + 2, 2, rows_of, half), BF16)]
    scratch += [pltpu.VMEM((blocks, 2, rows_of, half), BF16)]
    scratch += [dma((blocks + 2,)), dma((blocks + 2,)), dma((blocks, 2)), dma((blocks, 2)), dma((blocks,)), dma((blocks,))]
    scratch += [
        dma((6,)),
        dma((3,)),
        dma((4, 2, 2)),
        dma((CHUNKS, 2)),
        dma((CHUNKS, 2)),
        dma((2, CHUNKS, 2)),
        dma((2, 2)),
        dma((CHUNKS, 2)),
        dma((CHUNKS, 2)),
        dma((CHUNKS, 2)),
        dma((2,)),
    ]
    out_shape = [
        jax.ShapeDtypeStruct(low, F32),
        jax.ShapeDtypeStruct(low, F32),
        jax.ShapeDtypeStruct((16, width), F32),
        jax.ShapeDtypeStruct((quarter, width), BF16),
        jax.ShapeDtypeStruct(cross_shape, BF16),
        jax.ShapeDtypeStruct((blocks, rows_of, half), BF16),
    ]
    args = [values.act_three, values.x1, values.query, w_cross, w_in, w_mlp]
    return pl.pallas_call(
        functools.partial(mid_kernel, tuple(pieces), pairs, scale),
        in_specs=[hbm] * 9 + [vmem] * 7,
        out_specs=[hbm, hbm, vmem, hbm, hbm, vmem],
        out_shape=out_shape,
        scratch_shapes=scratch,
        compiler_params=pltpu.CompilerParams(
            collective_id=2, has_side_effects=True, vmem_limit_bytes=TAIL_LIMIT
        ),
        name="middle",
    )(*args, ffn_shard, cot_block, values.base, *vecs, picks)


def finish_kernel(*refs):
    it = iter(refs)
    late, early, from_text, total = (next(it) for _ in range(4))
    rows_in = [next(it) for _ in range(2)]
    rows_out = [next(it) for _ in range(2)]
    o_qkv, o_out, o_in, o_mlp, o_cross, o_qv, o_outb, o_inb, o_mlpb, o_gain, o_shift = (next(it) for _ in range(11))
    held = [next(it) for _ in range(2)]
    b_in, b_mlp, b_out, b_qkv, b_cross, sem = it
    tower, dp, z, core, line, other, partner = spots()

    def bring(i, image_src, text_src, target):
        @pl.when(tower == 0)
        def _():
            pltpu.make_async_copy(image_src, target, sem.at[i]).start()

        @pl.when(tower == 1)
        def _():
            pltpu.make_async_copy(text_src, target, sem.at[i]).start()

    n = b_in.shape[0]
    bring(0, late.at[pl.ds(n, n)], early.at[pl.ds(0, n)], b_in)
    bring(1, late.at[pl.ds(0, n)], early.at[pl.ds(n, n)], b_mlp)
    bring(2, late.at[2 * n], late.at[2 * n], b_out)
    bring(3, late.at[pl.ds(2 * n + 1, 3)], late.at[pl.ds(2 * n + 1, 3)], b_qkv)
    bring(4, from_text, early.at[pl.ds(2 * n, 2)], b_cross)
    for i in range(2):
        pltpu.make_async_copy(rows_in[i], held[i], sem.at[5 + i]).start()

    width = total.shape[2]
    heads = width // 2
    first = total[0]
    o_outb[...] = first[0:1, :]
    o_mlpb[...] = first[1:2, :]
    for i in range(3):
        o_gain[i] = first[2 + i : 3 + i, :]
        o_shift[i] = first[5 + i : 6 + i, :]
    for side in range(2):
        lanes = slice(side * heads, (side + 1) * heads)
        o_qv[0, 0:1, lanes] = total[side, 8:9, :heads]
        o_qv[0, 1:2, lanes] = total[side, 8:9, heads:]
        for b in range(2):
            at = (2 * side + b) * width
            o_inb[0:1, at : at + width] = total[side, 9 + b : 10 + b, :]

    def mine(block):
        cut = block.shape[1] // 2
        wide = block.astype(F32)
        return jnp.where(core == 0, wide[:, :cut], wide[:, cut:])

    for i in range(2):
        pltpu.make_async_copy(rows_in[i], held[i], sem.at[5 + i]).wait()
        pltpu.make_async_copy(held[i], rows_out[i].at[0], sem.at[7 + i]).start()
    half = b_in.shape[2]
    cols = b_in.shape[1]
    pltpu.make_async_copy(late.at[pl.ds(0, n)], b_in, sem.at[0]).wait()
    for i in range(n // 2):
        pair = b_in[2 * i : 2 * i + 2].reshape(2 * cols, half)
        o_in[0, :, 2 * i * cols : 2 * (i + 1) * cols] = mine(pair).T
    pltpu.make_async_copy(late.at[pl.ds(0, n)], b_mlp, sem.at[1]).wait()
    for i in range(n // 2):
        pair = b_mlp[2 * i : 2 * i + 2].reshape(2 * cols, half)
        o_mlp[0, :, 2 * i * cols : 2 * (i + 1) * cols] = mine(pair).T
    pltpu.make_async_copy(late.at[0], b_out, sem.at[2]).wait()
    o_out[0] = mine(b_out[...])
    pltpu.make_async_copy(late.at[pl.ds(0, 3)], b_qkv, sem.at[3]).wait()
    for a in range(3):
        o_qkv[0, a] = mine(b_qkv[a]).T
    pltpu.make_async_copy(late.at[pl.ds(0, 2)], b_cross, sem.at[4]).wait()
    for a in range(2):
        o_cross[0, a] = mine(b_cross[a]).T
    for i in range(2):
        pltpu.make_async_copy(held[i], rows_out[i].at[0], sem.at[7 + i]).wait()


def finish(late, early, from_text, total, token_rows):
    hbm = pl.BlockSpec(memory_space=pltpu.HBM)
    vmem = pl.BlockSpec(memory_space=pltpu.VMEM)
    struct = jax.ShapeDtypeStruct
    width = total.shape[2]
    blocks, cols, half = early.shape
    n = (blocks - 2) // 2
    ffn, cut = n * cols, half // 2
    out_shape = [struct((1,) + x.shape, BF16) for x in token_rows]
    out_shape += [
        struct((1, 3, cut, cols), F32),
        struct((1, cols, cut), F32),
        struct((1, cut, ffn), F32),
        struct((1, cut, ffn), F32),
        struct((1, 2, cut, cols), F32),
        struct((1, 2, width), F32),
        struct((1, width), F32),
        struct((1, 4 * width), F32),
        struct((1, width), F32),
        struct((3, 1, width), F32),
        struct((3, 1, width), F32),
    ]
    scratch = [pltpu.VMEM(x.shape, BF16) for x in token_rows]
    scratch += [pltpu.VMEM(x + (cols, half), BF16) for x in ((n,), (n,), (), (3,), (2,))]
    scratch += [pltpu.SemaphoreType.DMA((9,))]
    results = pl.pallas_call(
        finish_kernel,
        in_specs=[hbm] * 3 + [vmem] + [hbm] * 2,
        out_specs=[hbm] * 2 + [vmem] * 11,
        out_shape=out_shape,
        scratch_shapes=scratch,
        compiler_params=pltpu.CompilerParams(vmem_limit_bytes=VMEM_LIMIT),
        name="finish",
    )(late, early, from_text, total, *token_rows)
    turned = {5: (1, 2), 11: (0, 1), 12: (0, 1)}
    return tuple(jnp.swapaxes(x, *turned[i]) if i in turned else x for i, x in enumerate(results))


def split_heads(flat):
    return jnp.swapaxes(flat.reshape(flat.shape[0], -1, HDIM), 0, 1)


def join_heads(split):
    return jnp.swapaxes(split, 0, 1).reshape(split.shape[1], -1)


def batch_dot(left, right, left_dim, right_dim):
    return lax.dot_general(left, right, (((left_dim,), (right_dim,)), ((0,), (0,))), preferred_element_type=F32)


def attend_plain(queries, keys, vals, allowed, scale):
    queries, keys, vals = (split_heads(x) for x in (queries, keys, vals))
    scores = jnp.where(allowed, batch_dot(queries, keys, 2, 2) * scale, NEG)
    top = jnp.max(scores, axis=-1, keepdims=True)
    tops = top + jnp.log(jnp.sum(jnp.exp(scores - top), axis=-1, keepdims=True))
    weights = jnp.exp(scores - tops).astype(BF16)
    return (join_heads(batch_dot(weights, vals, 2, 1)).astype(BF16), tops)


def attend_back_plain(queries, keys, vals, grads, tops, allowed, scale):
    queries, keys, vals, grads = (split_heads(x) for x in (queries, keys, vals, grads))
    scores = jnp.where(allowed, batch_dot(queries, keys, 2, 2) * scale, NEG)
    weights = jnp.exp(scores - tops)
    grad_w = batch_dot(grads, vals, 2, 2)
    grad_s = (weights * (grad_w - jnp.sum(weights * grad_w, axis=-1, keepdims=True))).astype(BF16)
    return (
        join_heads(batch_dot(grad_s, keys, 2, 1) * scale).astype(BF16),
        join_heads(batch_dot(grad_s, queries, 1, 1) * scale).astype(BF16),
        join_heads(batch_dot(weights.astype(BF16), grads, 1, 1)).astype(BF16),
    )


def gather_plain(shards):
    core = lax.rem(lax.axis_index(DP), 2)
    outs = []
    for i, s in enumerate(shards):
        if i == 2:
            s = jnp.concatenate([lax.ppermute(s, TOWER, [(0, 1)]), s], axis=0)
        full = lax.all_gather(s, MP, axis=1, tiled=False)
        outs.append(lax.dynamic_slice_in_dim(full, 2 * core, 2, 1))
    return outs


def reduce_plain(grads, smalls):
    dp = lax.axis_index(DP)
    core = lax.rem(dp, 2)
    outs = []
    for g in grads:
        n, _, rows, wide = g.shape
        full = jnp.zeros((n, 4, rows, wide), BF16)
        full = lax.dynamic_update_slice(full, g, (0, 2 * core, 0, 0))
        part = lax.psum_scatter(full, MP, scatter_dimension=1, tiled=False)
        part = lax.psum_scatter(part, DP, scatter_dimension=2, tiled=True)
        outs.append(part)
    if smalls is None:
        return outs
    both = jnp.zeros((2,) + smalls.shape, F32)
    both = lax.dynamic_update_slice(both, smalls[None], (core, 0, 0))
    return outs + [lax.psum(both, (DP, MP))]


def body(
    tower_in,
    out_cot,
    segment_ids,
    row_image,
    attn_qkv,
    attn_out,
    mlp_in,
    mlp_out,
    cross_proj,
    qv_bias,
    out_bias,
    mlp_bias_in,
    mlp_bias_out,
    norm_gain,
    norm_bias,
):
    lines = lax.axis_size(DP) // 2
    depth = lax.axis_size(MP)
    devices = lax.axis_size(DP)
    is_enc = lax.axis_index(TOWER) == 0
    dp = lax.axis_index(DP)
    z = lax.axis_index(MP)
    core = lax.rem(dp, 2)
    side = lax.rem(z, 2)
    group = z // 2
    direct = lines == 2
    assert depth == 4
    quarter = tower_in.shape[1]
    tokens = 2 * quarter
    assert tokens == PATCH
    width = tower_in.shape[2]
    head_cols = 2 * attn_qkv.shape[3]
    hidden = 2 * mlp_in.shape[2]
    scale_qk = HDIM ** (-0.5)

    out_moves, back_moves = [], []
    for d in range(devices):
        for place in range(depth):
            here = d * depth + place
            there = (d - d % 2 + place % 2) * depth + 2 * (d % 2) + place // 2
            out_moves.append((here, there))
            back_moves.append((there, here))

    def swap_cores(x):
        return lax.ppermute(x, DP, [(i, i ^ 1) for i in range(devices)])

    def both_cores(own):
        other = swap_cores(own)
        return jnp.where(core == 0, jnp.concatenate([own, other], -2), jnp.concatenate([other, own], -2))

    def own_rows(full):
        return lax.dynamic_slice_in_dim(full, core * quarter, quarter, full.ndim - 2)

    def lowered(part):
        return lax.reduce_precision(part, 8, 7).astype(BF16)

    def add_lowered(low):
        return low.astype(F32) + swap_cores(low).astype(F32)

    def add_cores(part):
        return add_lowered(lowered(part))

    def only_image(run, *operands):
        def idle(*inputs):
            return jax.tree.map(lambda x: jnp.zeros(x.shape, x.dtype), jax.eval_shape(run, *inputs))

        return lax.cond(is_enc, run, idle, *operands)

    shards = [
        jnp.swapaxes(attn_qkv[0], 1, 2),
        attn_out,
        jnp.swapaxes(cross_proj[0], 1, 2),
        mlp_in,
        mlp_out,
    ]
    rows = segment_ids.shape[0] // 2

    bias_qv = lax.dynamic_slice_in_dim(qv_bias[0], core * head_cols, head_cols, 1)
    bias_packed = jnp.concatenate([bias_qv[0], jnp.zeros_like(bias_qv[0]), bias_qv[1]])
    bias_in = lax.dynamic_slice_in_dim(mlp_bias_in[0], core * hidden, hidden, 0)
    gains = norm_gain[0]
    shifts = norm_bias[0]

    def feed_forward(values):
        act = norm_rows(values, gains[1], shifts[1]).astype(BF16)
        pre = jnp.concatenate([dot_plain(act, w_in[0]), dot_plain(act, w_in[1])], axis=1) + bias_in
        hid = gelu_tanh(pre).astype(BF16)
        return (act, pre, hid, lowered(dot_plain(hid, w_mlp)))

    if direct:
        tall_gains, tall_shifts = (jnp.swapaxes(x, 0, 1) for x in (norm_gain, norm_bias))
        vecs = (tall_gains, tall_shifts, out_bias, mlp_bias_out, mlp_bias_in, qv_bias[0])
        gathered, stream_low, notes, first = head(
            shards, [tower_in[0]], segment_ids, row_image, vecs, scale_qk
        )
        seg_col, seg_row, picks = notes
    else:
        gathered = gather_plain(shards)
        stream_low = both_cores(lax.ppermute(tower_in[0], (DP, MP), out_moves))
        cot_low = both_cores(lax.ppermute(out_cot[0], (DP, MP), out_moves))
        segs = jnp.where(core == group, segment_ids, swap_cores(segment_ids))
        segs = lax.dynamic_slice_in_dim(segs, rows * side, rows, 0)
        marks = (segs + LTXT * jnp.arange(rows, dtype=jnp.int32)[:, None]).reshape(tokens)
        images_of = jnp.where(core == group, row_image, swap_cores(row_image))
        images_of = jnp.repeat(lax.dynamic_slice_in_dim(images_of, rows * side, rows, 0), LTXT)
        places = jnp.arange(tokens)
        allowed = (places[None, :] <= places[:, None]) & (marks[None, :] == marks[:, None])
        allowed = jnp.logical_or(allowed, is_enc)
        sees = images_of[:, None] == jnp.arange(2 * tokens)[None, :] // tokens
    w_qkv = gathered[0].reshape(3 * head_cols, width)
    w_out = gathered[1].reshape(head_cols, width)
    w_cross = gathered[2].reshape(4, head_cols, width)
    w_in = gathered[3][0]
    w_mlp = gathered[4].reshape(hidden, width)
    stream = stream_low.astype(F32)

    if not direct:
        act_one = norm_rows(stream, gains[0], shifts[0]).astype(BF16)
        packed = (dot_rows(act_one, w_qkv) + bias_packed).astype(BF16)
        parts = [packed[:, i * head_cols : (i + 1) * head_cols] for i in range(3)]
        mixed, tops = attend_plain(*parts, allowed, scale_qk)
        stream_one = stream + add_cores(dot_plain(mixed, w_out)) + out_bias[0]
        act_enc, pre_enc, hid_enc, part_enc = feed_forward(stream_one)
        out_enc = stream_one + add_lowered(part_enc) + mlp_bias_out[0]
        base_three = jnp.where(is_enc, out_enc, stream_one)
        act_three = norm_rows(base_three, gains[2], shifts[2]).astype(BF16)
        cross_q = dot_rows(act_three, w_cross[2]).astype(BF16)

    if direct:
        back_in_three, upstream, smalls, tower_rows, g_cross, early = middle(
            first, gathered[2], gathered[3], gathered[4], mlp_out, out_cot[0], vecs, picks, scale_qk
        )
        values = Tail(
            d_three=back_in_three,
            base=first.base,
            upstream=upstream,
            gains=tall_gains,
            smalls=smalls,
            w_mlp=w_mlp,
            pre=first.pre,
            hid=first.hid,
            act=first.act,
            w_in=w_in,
            x1=first.x1,
            w_out=w_out,
            mixed=first.mixed,
            packed=first.packed,
            tops=first.tops,
            seg_col=seg_col,
            seg_row=seg_row,
            a_one=first.a_one,
            w_qkv=w_qkv,
            x0=stream_low,
        )
        late, total, grad_in, from_text, tower_out = tail(values, g_cross, tower_rows, scale_qk)
        return finish(late, early, from_text, total, [tower_out, grad_in])
    else:
        near_half = lax.ppermute(own_rows(act_three), TOWER, [(0, 1)])
        far_half = lax.ppermute(near_half, MP, [(i, i ^ 1) for i in range(depth)])
        halves = jnp.where(side == 0, jnp.stack([near_half, far_half]), jnp.stack([far_half, near_half]))
        images = both_cores(halves)

        flat_images = images.reshape(2 * tokens, width)
        cross_k = dot_rows(flat_images, w_cross[0]).astype(BF16)
        cross_v = dot_rows(flat_images, w_cross[1]).astype(BF16)
        cross_mix, cross_tops = attend_plain(cross_q, cross_k, cross_v, sees, scale_qk)
        stream_two = stream_one + add_cores(dot_plain(cross_mix, w_cross[3]))

        act_dec, pre_dec, hid_dec, part_dec = feed_forward(stream_two)
        out_dec = stream_two + add_lowered(part_dec) + mlp_bias_out[0]
        tower_rows = own_rows(jnp.where(is_enc, base_three, out_dec).astype(BF16))

        def feed_back(grad_low, pre):
            grad_hid = dot_rows(grad_low, w_mlp)
            _, pullback = jax.vjp(gelu_tanh, pre)
            grad_pre = pullback(grad_hid)[0].astype(BF16)
            cols = hidden // 2
            part = dot_rows(grad_pre[:, :cols], w_in[0]) + dot_rows(grad_pre[:, cols:], w_in[1])
            return (grad_pre, lowered(part))

        def feed_grads(grad_low, act, grad_pre, hid):
            g_in = dot_first(grad_pre, act).astype(BF16)
            g_mlp = dot_first(hid, grad_low).astype(BF16)
            return (
                g_in.reshape(1, 2, hidden // 2, width),
                g_mlp.reshape(1, 2, hidden // 2, width),
            )

        cot = cot_low.astype(F32)
        grad_pre_dec, back_in = feed_back(cot_low, pre_dec)
        back_a, gain_a, shift_a = norm_back(stream_two, gains[1], add_lowered(back_in))
        grad_two = cot + back_a
        grad_two_low = grad_two.astype(BF16)

        grad_mix = dot_rows(grad_two_low, w_cross[3]).astype(BF16)
        grad_q, flat_k, flat_v = attend_back_plain(
            cross_q, cross_k, cross_v, grad_mix, cross_tops, sees, scale_qk
        )
        part_images = dot_plain(flat_k, w_cross[0]) + dot_plain(flat_v, w_cross[1])
        part_low = part_images.astype(BF16).reshape(2, 2, quarter, width)
        give = lax.dynamic_index_in_dim(part_low, 1 - core, 1, keepdims=False)
        keep = lax.dynamic_index_in_dim(part_low, core, 1, keepdims=False)
        pair_sum = (keep.astype(F32) + swap_cores(give).astype(F32)).astype(BF16)
        give = lax.dynamic_index_in_dim(pair_sum, 1 - side, 0, keepdims=False)
        keep = lax.dynamic_index_in_dim(pair_sum, side, 0, keepdims=False)
        got = lax.ppermute(give, MP, [(i, i ^ 1) for i in range(depth)])
        image_sum = (keep.astype(F32) + got.astype(F32)).astype(BF16)
        image_half = lax.ppermute(image_sum, TOWER, [(1, 0)])
        later = lax.optimization_barrier(
            (cot_low, act_dec, grad_pre_dec, hid_dec, flat_k, flat_v, grad_q, cross_mix, image_sum)
        )
        g_in_dec, g_mlp_dec = feed_grads(later[0], later[1], later[2], later[3])
        g_cross = jnp.concatenate(
            [
                dot_first(later[4], flat_images).astype(BF16),
                dot_first(later[5], flat_images).astype(BF16),
                dot_first(later[6], act_three).astype(BF16),
                dot_first(later[7], grad_two_low).astype(BF16),
            ],
            axis=0,
        ).reshape(4, 2, head_cols // 2, width)
        image_back = both_cores(image_half).astype(F32)
        query_back = add_cores(dot_plain(grad_q, w_cross[2]))
        back_in_three = jnp.where(is_enc, image_back, query_back)
        text_smalls = (
            jnp.zeros((16, width), F32)
            .at[1]
            .set(jnp.sum(cot_low, axis=0, dtype=F32))
            .at[3]
            .set(gain_a)
            .at[6]
            .set(shift_a)
            .at[9:11]
            .set(jnp.sum(grad_pre_dec, axis=0, dtype=F32).reshape(2, width))
        )
        smalls = jnp.where(is_enc, 0.0, text_smalls)
        tower_out = lax.ppermute(tower_rows, (DP, MP), back_moves)
        back_three, gain_three, shift_three = norm_back(
            base_three, gains[2], back_in_three
        )
        grad_enc = cot + back_three
        grad_enc_low = grad_enc.astype(BF16)

        grad_pre_enc, back_in = feed_back(grad_enc_low, pre_enc)
        g_in, g_mlp = feed_grads(grad_enc_low, act_enc, grad_pre_enc, hid_enc)
        back_b, gain_b, shift_b = norm_back(stream_one, gains[1], add_lowered(back_in))
        grad_one = jnp.where(is_enc, grad_enc + back_b, grad_two + back_three)
        grad_one_low = grad_one.astype(BF16)

        g_out = dot_first(mixed, grad_one_low).astype(BF16).reshape(1, 2, head_cols // 2, width)
        grad_mixed = dot_rows(grad_one_low, w_out).astype(BF16)
        grad_packed = jnp.concatenate(
            attend_back_plain(*parts, grad_mixed, tops, allowed, scale_qk), axis=1
        )
        g_qkv = dot_first(grad_packed, act_one).astype(BF16).reshape(3, 2, head_cols // 2, width)
        back_in = add_cores(dot_plain(grad_packed, w_qkv))
        back_one, gain_one, shift_one = norm_back(stream, gains[0], back_in)
        grad_in = own_rows((grad_one + back_one).astype(BF16))
        grad_in = lax.ppermute(grad_in, (DP, MP), back_moves)

        grad_pre_sum = jnp.sum(grad_pre_enc, axis=0, dtype=F32).reshape(2, width)
        packed_sum = jnp.sum(grad_packed, axis=0, dtype=F32)
        smalls = jnp.concatenate(
            [
                jnp.sum(grad_one_low, axis=0, dtype=F32)[None],
                jnp.where(is_enc, jnp.sum(grad_enc_low, axis=0, dtype=F32), smalls[1])[None],
                gain_one[None],
                jnp.where(is_enc, gain_b, smalls[3])[None],
                gain_three[None],
                shift_one[None],
                jnp.where(is_enc, shift_b, smalls[6])[None],
                shift_three[None],
                jnp.concatenate([packed_sum[:head_cols], packed_sum[2 * head_cols :]])[None],
                jnp.where(is_enc, grad_pre_sum, smalls[9:11]),
                smalls[11:],
            ]
        )
        g_in = jnp.where(is_enc, g_in, g_in_dec)
        g_mlp = jnp.where(is_enc, g_mlp, g_mlp_dec)
        s_in, s_mlp, s_out, s_qkv, s_cross, total = reduce_plain([g_in, g_mlp, g_out, g_qkv, g_cross], smalls)
        s_cross = jnp.where(is_enc, lax.ppermute(s_cross[:2], TOWER, [(1, 0)]), s_cross[2:])

    def turned(x):
        return jnp.swapaxes(x, 1, 2).astype(F32)

    cross_pair = jnp.stack(
        [
            s_cross[0].T,
            s_cross[1].T,
        ]
    ).astype(F32)
    first = total[0]
    qv_total = jnp.stack(
        [
            total[:, 8, :head_cols].reshape(-1),
            total[:, 8, head_cols:].reshape(-1),
        ]
    )
    in_total = total[:, 9:11].reshape(-1)
    return (
        tower_out[None],
        grad_in[None],
        turned(s_qkv)[None],
        s_out.astype(F32),
        turned(s_in),
        s_mlp.astype(F32),
        cross_pair[None],
        qv_total[None],
        first[0:1],
        in_total[None],
        first[1:2],
        first[2:5][None],
        first[5:8][None],
    )


def solution(mesh):
    return jax.shard_map(
        body,
        mesh=mesh,
        in_specs=(
            P(TOWER, (DP, MP), None),
            P(TOWER, (DP, MP), None),
            P(DP, None),
            P(DP),
            P(TOWER, None, None, MP),
            P(TOWER, MP, None),
            P(TOWER, None, MP),
            P(TOWER, MP, None),
            P(TOWER, None, None, MP),
            P(TOWER, None, None),
            P(TOWER, None),
            P(TOWER, None),
            P(TOWER, None),
            P(TOWER, None, None),
            P(TOWER, None, None),
        ),
        out_specs=(
            P(TOWER, (DP, MP), None),
            P(TOWER, (DP, MP), None),
            P(TOWER, None, DP, MP),
            P(TOWER, MP, DP),
            P(TOWER, DP, MP),
            P(TOWER, MP, DP),
            P(TOWER, None, DP, MP),
            P(TOWER, None, None),
            P(TOWER, None),
            P(TOWER, None),
            P(TOWER, None),
            P(TOWER, None, None),
            P(TOWER, None, None),
        ),
        check_vma=False,
    )
```

```python
import functools
from typing import Any, NamedTuple

import jax
import jax.numpy as jnp
from jax import lax
from jax.experimental import pallas as pl
from jax.experimental.pallas import tpu as pltpu
from jax.sharding import PartitionSpec as P

TOWER = "tower"
DP = "dp"
MP = "mp"
HDIM = 64
PATCH = 576
LTXT = 64
EPS = 1e-06
NEG = -1e30
LANES = 128
MESH = pl.DeviceIdType.MESH
F32 = jnp.float32
BF16 = jnp.bfloat16
VMEM_LIMIT = 60 * 1024 * 1024
TAIL_LIMIT = 67043328


def norm_parts(values):
    center = values - jnp.mean(values, axis=-1, keepdims=True)
    spread = jnp.mean(center * center, axis=-1, keepdims=True)
    scale = lax.rsqrt(spread + EPS)
    return (center * scale, scale)


def norm_rows(values, gain_vec, shift_vec):
    unit, _ = norm_parts(values)
    return unit * gain_vec + shift_vec


def norm_back(values, gain_vec, grad_normed):
    unit, scale = norm_parts(values)
    inner = grad_normed * gain_vec
    mean_one = jnp.mean(inner, axis=-1, keepdims=True)
    mean_two = jnp.mean(inner * unit, axis=-1, keepdims=True)
    back = (inner - mean_one - unit * mean_two) * scale
    return (back, jnp.sum(grad_normed * unit, axis=0), jnp.sum(grad_normed, axis=0))


def gelu_tanh(values):
    return jax.nn.gelu(values, approximate=True)


def dot_rows(left, right):
    return lax.dot_general(left, right, (((1,), (1,)), ((), ())), preferred_element_type=F32)


def dot_first(left, right):
    return lax.dot_general(left, right, (((0,), (0,)), ((), ())), preferred_element_type=F32)


def dot_plain(left, right):
    return lax.dot_general(left, right, (((1,), (0,)), ((), ())), preferred_element_type=F32)


def spots():
    tower = lax.axis_index(TOWER)
    dp = lax.axis_index(DP)
    z = lax.axis_index(MP)
    core = lax.rem(dp, 2)
    line = dp // 2
    return tower, dp, z, core, line, dp + 2 - 4 * line, dp + 1 - 2 * core


def greet(target):
    pl.semaphore_signal(pltpu.get_barrier_semaphore(), inc=1, device_id=target, device_id_type=MESH)


def weight_steps(pieces, srcs, outs, stages, sems, less):
    send_sem, recv_sem, local_sem, twin_send, twin_recv = sems
    tower, dp, z, core, line, other, partner = spots()
    place = z + core * (3 - 2 * z)
    ahead = z + 1 - 2 * core
    behind = z - 1 + 2 * core
    slot_of = (core, 1 - core)
    holder = place <= 1
    far_src = [k for k, p in enumerate(pieces) if p[7]]

    def spot(piece, slot, half):
        which, first, _, count, start, size, _, _ = piece
        part = size // 2
        return outs[which].at[pl.ds(first, count), slot, pl.ds(start + half * part, part), :]

    def own(piece):
        which, _, first, count, start, size, _, far = piece
        part = size // 2
        if far:
            return spot(piece, lax.rem(z, 2), line)
        return srcs[which].at[pl.ds(first, count), pl.ds(start + line * part, part), :]

    def move(k, source, slot, half, kind, arrive, target):
        return pltpu.make_async_remote_copy(
            src_ref=source,
            dst_ref=spot(pieces[k], slot, half),
            send_sem=send_sem.at[k, kind],
            recv_sem=recv_sem.at[k, arrive],
            device_id=target,
            device_id_type=MESH,
        )

    def twin_copy():
        which = pieces[far_src[0]][0]
        return pltpu.make_async_remote_copy(
            src_ref=srcs[which],
            dst_ref=outs[which].at[pl.ds(0, srcs[which].shape[0]), lax.rem(z, 2)],
            send_sem=twin_send,
            recv_sem=twin_recv,
            device_id={TOWER: 1 - tower},
            device_id_type=MESH,
        )

    def local_in(i):
        return pltpu.make_async_copy(srcs[i], stages[i], local_sem.at[i, 0])

    def local_out(i):
        first = outs[i].shape[0] - srcs[i].shape[0]
        return pltpu.make_async_copy(
            stages[i], outs[i].at[pl.ds(first, srcs[i].shape[0]), lax.rem(z, 2)], local_sem.at[i, 1]
        )

    def gate(piece, cond):
        return cond if piece[6] is None else jnp.logical_and(cond, tower == piece[6])

    def send_own(k, seat):
        piece = pieces[k]

        if seat == 0:

            @pl.when(gate(piece, place == 0))
            def _():
                move(k, own(piece), slot_of[0], line, 0, 0, {MP: ahead}).start()

        else:

            @pl.when(gate(piece, place == 1))
            def _():
                move(k, own(piece), slot_of[1], line, 1, 1, {MP: ahead}).start()
                move(k, own(piece), slot_of[1], line, 2, 1, {MP: behind}).start()

    orders = {t: [k for k, p in enumerate(pieces) if p[6] in (None, t)] for t in (0, 1)}

    def launch(t, at, seat):
        if at >= len(orders[t]):
            return
        k = orders[t][at]

        @pl.when(jnp.logical_and(place == seat, tower == t))
        def _():
            if far_src and k == far_src[0]:
                twin_copy().wait_recv()
            send_own(k, seat)

    def own_sent(k):
        piece = pieces[k]

        @pl.when(gate(piece, place == 0))
        def _():
            move(k, own(piece), slot_of[0], line, 0, 0, {MP: z}).wait_send()

        @pl.when(gate(piece, place == 1))
        def _():
            move(k, own(piece), slot_of[1], line, 1, 1, {MP: z}).wait_send()
            move(k, own(piece), slot_of[1], line, 2, 1, {MP: z}).wait_send()

    def begin():
        if far_src:

            @pl.when(jnp.logical_and(holder, tower == 0))
            def _():
                twin_copy().start()

        for t in (0, 1):
            for seat in (0, 1):
                for start in range(WINDOW - less * seat):
                    launch(t, start, seat)

    def keeps(i):
        flags = {p[6] for p in pieces if p[0] == i}
        flag = None if len(flags) > 1 else flags.pop()
        return holder if flag is None else jnp.logical_and(holder, tower == flag)

    def begin_local():
        for i in range(len(srcs)):

            @pl.when(keeps(i))
            def _(i=i):
                local_in(i).start()

        for i in range(len(srcs)):

            @pl.when(keeps(i))
            def _(i=i):
                local_in(i).wait()
                local_out(i).start()

    def pass_on(k):
        piece = pieces[k]

        @pl.when(gate(piece, place >= 1))
        def _():
            here = spot(piece, slot_of[0], line)
            move(k, here, slot_of[0], line, 0, 0, {MP: z}).wait_recv()
            move(k, here, slot_of[0], line, 3, 2, {DP: other}).start()

        @pl.when(gate(piece, jnp.logical_and(place >= 1, place <= 2)))
        def _():
            here = spot(piece, slot_of[0], line)
            move(k, here, slot_of[0], line, 0, 0, {MP: ahead}).start()

        @pl.when(gate(piece, place != 1))
        def _():
            here = spot(piece, slot_of[1], line)
            move(k, here, slot_of[1], line, 1, 1, {MP: z}).wait_recv()
            move(k, here, slot_of[1], line, 4, 3, {DP: other}).start()

        @pl.when(gate(piece, place == 2))
        def _():
            here = spot(piece, slot_of[1], line)
            move(k, here, slot_of[1], line, 1, 1, {MP: ahead}).start()

        own_sent(k)
        for t in (0, 1):
            if k in orders[t]:
                for seat in (0, 1):
                    launch(t, orders[t].index(k) + WINDOW - less * seat, seat)

    def arrived(k):
        piece = pieces[k]

        @pl.when(gate(piece, place >= 1))
        def _():
            move(k, spot(piece, slot_of[0], 1 - line), slot_of[0], 1 - line, 3, 2, {DP: dp}).wait_recv()

        @pl.when(gate(piece, place != 1))
        def _():
            move(k, spot(piece, slot_of[1], 1 - line), slot_of[1], 1 - line, 4, 3, {DP: dp}).wait_recv()

    def sent(k):
        piece = pieces[k]

        @pl.when(gate(piece, jnp.logical_or(place == 1, place == 2)))
        def _():
            move(k, spot(piece, slot_of[0], line), slot_of[0], line, 0, 0, {MP: z}).wait_send()

        @pl.when(gate(piece, place == 2))
        def _():
            move(k, spot(piece, slot_of[1], line), slot_of[1], line, 1, 1, {MP: z}).wait_send()

        @pl.when(gate(piece, place >= 1))
        def _():
            move(k, spot(piece, slot_of[0], line), slot_of[0], line, 3, 2, {DP: dp}).wait_send()

        @pl.when(gate(piece, place != 1))
        def _():
            move(k, spot(piece, slot_of[1], line), slot_of[1], line, 4, 3, {DP: dp}).wait_send()

    def end_local(i):
        @pl.when(keeps(i))
        def _():
            local_out(i).wait()

    def end_twin():
        @pl.when(jnp.logical_and(holder, tower == 0))
        def _():
            twin_copy().wait_send()

    return begin, begin_local, pass_on, arrived, sent, end_local, end_twin


def token_steps(blocks, outs, stage, sems):
    send_sem, recv_sem, local_sem = sems
    tower, dp, z, core, line, other, partner = spots()
    stays = z == 3 * core
    size = blocks[0].shape[0]

    def rows(which_core):
        return pl.ds(pl.multiple_of(which_core * size, 16), size)

    def away(i):
        target = {DP: 2 * line + lax.rem(z, 2), MP: 2 * core + z // 2}
        return pltpu.make_async_remote_copy(
            src_ref=blocks[i],
            dst_ref=outs[i].at[rows(lax.rem(z, 2)), :],
            send_sem=send_sem.at[i, 0],
            recv_sem=recv_sem.at[i, 0],
            device_id=target,
            device_id_type=MESH,
        )

    def across(i, which_core):
        return pltpu.make_async_remote_copy(
            src_ref=outs[i].at[rows(which_core), :],
            dst_ref=outs[i].at[rows(which_core), :],
            send_sem=send_sem.at[i, 1],
            recv_sem=recv_sem.at[i, 1],
            device_id={DP: partner},
            device_id_type=MESH,
        )

    def begin(i):
        @pl.when(jnp.logical_not(stays))
        def _():
            away(i).start()

        @pl.when(stays)
        def _():
            first = pltpu.make_async_copy(blocks[i], stage.at[i], local_sem.at[i, 0])
            first.start()
            first.wait()
            second = pltpu.make_async_copy(stage.at[i], outs[i].at[rows(core), :], local_sem.at[i, 1])
            second.start()
            second.wait()
            across(i, core).start()

    def relay(i):
        @pl.when(jnp.logical_not(stays))
        def _():
            away(i).wait_recv()
            across(i, core).start()

    def finish(i):
        across(i, 1 - core).wait_recv()
        across(i, core).wait_send()

        @pl.when(jnp.logical_not(stays))
        def _():
            away(i).wait_send()

    return begin, relay, finish


TILE = 32
LAG = 1
WINDOW = 2


def barrier_all(peers, options):
    for cond, target in peers:
        if cond is None:
            greet(target)
        else:
            pl.when(cond)(functools.partial(greet, target))
    for cond, count in options:

        @pl.when(cond)
        def _(count=count):
            pl.semaphore_wait(pltpu.get_barrier_semaphore(), count)


def fold_rows(tile):
    return jnp.sum(tile.reshape(tile.shape[0] // 8, 8, tile.shape[1]), axis=0)


def row_tiles(total, run, carry, first=0, unroll=1):
    tile = next(t for t, by in ((64, 192), (96, 96), (48, 48), (32, 32)) if total % by == 0)
    turns = total // tile

    def step(i, kept):
        return run(pl.ds(pl.multiple_of(first + i * tile, 16), tile), kept)

    return lax.fori_loop(0, turns, step, carry, unroll=unroll)


def norm_back_tile(values, gain, grads):
    unit, scale = norm_parts(values)
    inner = grads * gain
    mean_one = jnp.mean(inner, axis=-1, keepdims=True)
    mean_two = jnp.mean(inner * unit, axis=-1, keepdims=True)
    return ((inner - mean_one - unit * mean_two) * scale, fold_rows(grads * unit), fold_rows(grads))


def gelu_both(v):
    rate = 0.7978845608028654
    square = v * v
    bend = jnp.tanh(rate * (v + 0.044715 * (square * v)))
    lifted = 0.5 * (1.0 + bend)
    slope = lifted + 0.5 * v * (1.0 - bend * bend) * (rate * (1.0 + 3.0 * 0.044715 * square))
    return (v * lifted, slope)


def low_lanes_of(count):
    return lax.broadcasted_iota(jnp.int32, (count, LANES), 1) < HDIM


def stack_all(block, low):
    wide = block.astype(F32)
    return jnp.concatenate([jnp.where(low, wide, 0.0), jnp.where(low, 0.0, wide)], axis=0)


def merge_all(both, low):
    count = both.shape[0] // 2
    return jnp.where(low, both[:count], both[count:])


def lane_block(index):
    return pl.ds(pl.multiple_of(index * LANES, LANES), LANES)


def scores_of(keys, queries, mask):
    scores = dot_rows(keys, queries)
    if mask is None:
        return scores
    block = mask[...]
    return scores + jnp.concatenate([block, block], axis=1)


def forward_heads(queries, keys, vals, mask, low):
    scores = scores_of(keys, queries, mask)
    top = jnp.max(scores, axis=0, keepdims=True)
    grown = jnp.exp(scores - top)
    total = jnp.sum(grown, axis=0, keepdims=True)
    weights = (grown * (1.0 / total)).astype(BF16)
    return (merge_all(dot_first(weights, vals), low), top + jnp.log(total))


def backward_heads(queries, keys, vals, grads, tops, mask, low, scale):
    weights = jnp.exp(scores_of(keys, queries, mask) - tops)
    grad_w = dot_rows(vals, grads)
    row_dot = jnp.sum(weights * grad_w, axis=0, keepdims=True)
    grad_s = (weights * (grad_w - row_dot)).astype(BF16)
    grad_q = merge_all(dot_first(keys, grad_s).T, low) * scale
    return (grad_q, dot_plain(grad_s, queries), dot_plain(weights.astype(BF16), grads))


def fill_mask(mask, col, row, is_dec):
    count = mask.shape[0]

    def tile(rows, kept):
        shape = (rows.size, count)
        key_at = lax.broadcasted_iota(jnp.int32, shape, 0) + rows.start
        query_at = lax.broadcasted_iota(jnp.int32, shape, 1)
        allowed = jnp.logical_and(key_at <= query_at, col[rows, 0:1] == row[0:1, :])
        mask[rows, :] = jnp.where(jnp.logical_or(allowed, jnp.logical_not(is_dec)), 0.0, NEG)
        return kept

    row_tiles(count, tile, 0)


def self_forward(packed, mask, out, tops, pairs, scale):
    low = low_lanes_of(packed.shape[0])

    @pl.loop(0, pairs)
    def _(pair):
        queries = (stack_all(packed[:, lane_block(pair)], low) * scale).astype(BF16)
        mixed, top = forward_heads(
            queries, packed[:, lane_block(pairs + pair)], packed[:, lane_block(2 * pairs + pair)], mask, low
        )
        out[:, lane_block(pair)] = mixed.astype(BF16)
        tops[pair, 0:1, :] = top


def self_backward(packed, grads, tops, mask, out, pairs, scale, between):
    low = low_lanes_of(packed.shape[0])

    @pl.loop(0, pairs)
    def _(pair):
        queries = (stack_all(packed[:, lane_block(pair)], low) * scale).astype(BF16)
        head_grads = stack_all(grads[:, lane_block(pair)], low).astype(BF16)
        grad_q, grad_k, grad_v = backward_heads(
            queries,
            packed[:, lane_block(pairs + pair)],
            packed[:, lane_block(2 * pairs + pair)],
            head_grads,
            tops[pair, 0:1, :],
            mask,
            low,
            scale,
        )
        out[:, lane_block(pair)] = grad_q.astype(BF16)
        out[:, lane_block(pairs + pair)] = grad_k.astype(BF16)
        out[:, lane_block(2 * pairs + pair)] = grad_v.astype(BF16)
        pl.when(pair == 1)(between)


def cross_forward(image, query, keys, vals, picks, out, tops, pairs, scale):
    low = low_lanes_of(query.shape[0])

    @pl.loop(0, pairs)
    def _(pair):
        cols = lane_block(pair)
        queries = (stack_all(query[:, cols], low) * scale).astype(BF16)
        mixed, top = forward_heads(queries, keys[image, :, cols], vals[image, :, cols], None, low)
        kept = jnp.where(picks[...] == image, mixed, out[:, cols].astype(F32))
        out[:, cols] = kept.astype(BF16)
        tops[image, pair, 0:1, :] = top


def cross_backward(query, keys, vals, grads, picks, tops, dq, dk, dv, sum_q, pairs, scale):
    low = low_lanes_of(query.shape[0])

    @pl.loop(0, pairs)
    def _(pair):
        cols = lane_block(pair)
        queries = (stack_all(query[:, cols], low) * scale).astype(BF16)
        sum_q[...] = jnp.zeros_like(sum_q)

        @pl.loop(0, 2)
        def _(image):
            own = jnp.where(picks[...] == image, grads[:, cols].astype(F32), 0.0)
            grad_q, grad_k, grad_v = backward_heads(
                queries,
                keys[image, :, cols],
                vals[image, :, cols],
                stack_all(own, low).astype(BF16),
                tops[image, pair, 0:1, :],
                None,
                low,
                scale,
            )
            sum_q[...] += grad_q
            dk[image, :, cols] = grad_k.astype(BF16)
            dv[image, :, cols] = grad_v.astype(BF16)

        dq[:, cols] = sum_q[...].astype(BF16)


class Reducer:
    def __init__(self, grads, near, far, outs, sems, window, first, last, near_last):
        self.grads, self.near, self.far, self.outs = grads, near, far, outs
        self.y_send, self.y_recv, self.z_send, self.z_recv, self.c_send, self.c_recv = sems
        self.tower, self.dp, self.z, self.core, self.line, self.other, self.partner = spots()
        self.place = self.z + self.core * (3 - 2 * self.z)
        self.holder = self.place <= 1
        self.slot = lax.rem(self.z, 2)
        self.half = grads.shape[3] // 2
        self.rows = grads.shape[2]
        self.window, self.first, self.last, self.near_last = window, first, last, near_last

    def lanes(self, line):
        return pl.ds(pl.multiple_of(line * self.half, LANES), self.half)

    def to_line(self, k):
        return pltpu.make_async_remote_copy(
            src_ref=self.grads.at[k, :, :, self.lanes(1 - self.line)],
            dst_ref=self.near.at[k],
            send_sem=self.y_send.at[k],
            recv_sem=self.y_recv.at[k],
            device_id={DP: self.other},
            device_id_type=MESH,
        )

    def send(self, source, target, k, sent, got, where):
        return pltpu.make_async_remote_copy(
            src_ref=source,
            dst_ref=target,
            send_sem=self.z_send.at[k, sent],
            recv_sem=self.z_recv.at[k, got],
            device_id={MP: where},
            device_id_type=MESH,
        )

    def inward(self, k):
        return self.send(self.near.at[k], self.far.at[k], k, 0, 0, 2 - self.core)

    def beside(self, k):
        return self.send(self.near.at[k, 1 - self.slot], self.far.at[k, 0], k, 0, 0, 4 * self.core + 1 - self.z)

    def onward(self, k, shard):
        return self.send(self.near.at[k, shard], self.far.at[k, 1], k, shard, 1, 2 * self.core + shard)

    def to_core(self, k):
        return pltpu.make_async_remote_copy(
            src_ref=self.outs.at[k],
            dst_ref=self.outs.at[k],
            send_sem=self.c_send.at[k],
            recv_sem=self.c_recv.at[k],
            device_id={DP: self.partner},
            device_id_type=MESH,
        )

    def launch(self, k):
        self.to_line(k).start()

    def tiles(self, run):
        @pl.loop(0, self.rows // TILE)
        def _(i):
            run(pl.ds(pl.multiple_of(i * TILE, TILE), TILE))

    def add_near(self, k, more=True):
        self.to_line(k).wait_send()
        self.to_line(k).wait_recv()
        if more:
            pl.when(k + self.window < self.near_last)(lambda: self.launch(k + self.window))

        def run(rows):
            for b in range(2):
                total = self.grads[k, b, rows, self.lanes(self.line)].astype(F32) + self.near[k, b, rows, :].astype(F32)
                self.near[k, b, rows, :] = total.astype(BF16)

        self.tiles(run)
        if more:
            pl.when(k < self.last)(lambda: self.hop(k))

    def hop(self, k):
        pl.when(self.place == 3)(self.inward(k).start)
        pl.when(self.holder)(self.beside(k).start)

    def add_mid(self, k):
        @pl.when(self.place == 2)
        def _():
            self.inward(k).wait_recv()

            def run(rows):
                for b in range(2):
                    total = self.near[k, b, rows, :].astype(F32) + self.far[k, b, rows, :].astype(F32)
                    self.near[k, b, rows, :] = total.astype(BF16)

            self.tiles(run)
            for shard in range(2):
                self.onward(k, shard).start()

    def add_far(self, k):
        @pl.when(self.holder)
        def _():
            self.beside(k).wait_recv()
            self.onward(k, 0).wait_recv()

            def run(rows):
                total = self.near[k, self.slot, rows, :].astype(F32)
                for seat in range(2):
                    total = total + self.far[k, seat, rows, :].astype(F32)
                self.outs[k, rows, :] = total.astype(BF16)

            self.tiles(run)
            self.to_core(k).start()

    def step(self, k, mid=1):
        self.add_near(k)
        if mid:
            pl.when(k - LAG >= self.first)(lambda: self.add_mid(k - LAG))

    def drain(self, begin):
        @pl.loop(begin, max(self.near_last, self.last + 2 * LAG))
        def _(i):
            pl.when(i < self.near_last)(lambda: self.add_near(i))
            j = i - LAG
            pl.when(jnp.logical_and(j >= self.first, j < self.last))(lambda: self.add_mid(j))
            n = j - LAG
            pl.when(jnp.logical_and(n < self.last, n >= self.first))(lambda: self.add_far(n))

    def far_before(self, begin):
        @pl.loop(self.first, jnp.maximum(self.first, begin - 2 * LAG))
        def _(k):
            self.add_far(k)

    def close(self):
        @pl.loop(self.first, self.last)
        def _(k):
            pl.when(self.place == 3)(self.inward(k).wait_send)

            @pl.when(self.place == 2)
            def _():
                for shard in range(2):
                    self.onward(k, shard).wait_send()

            @pl.when(self.holder)
            def _():
                self.beside(k).wait_send()
                self.to_core(k).wait_send()

            @pl.when(jnp.logical_not(self.holder))
            def _():
                self.to_core(k).wait_recv()


class Tail(NamedTuple):
    seg_col: Any
    seg_row: Any
    d_three: Any
    base: Any
    upstream: Any
    gains: Any
    smalls: Any
    hid: Any
    w_mlp: Any
    pre: Any
    act: Any
    w_in: Any
    x1: Any
    w_out: Any
    mixed: Any
    packed: Any
    tops: Any
    a_one: Any
    w_qkv: Any
    x0: Any


IMAGE_ONLY = Tail._fields[7:13]


def tail_kernel(pairs, scale, *refs):
    it = iter(refs)
    hbm = Tail(*[next(it) for _ in Tail._fields])
    cross_in, tower_rows = next(it), next(it)
    outs = next(it)
    small_out, grad_out, from_text, tower_out = next(it), next(it), next(it), next(it)
    vm = Tail(*[next(it) for _ in Tail._fields])
    grads, near, far = next(it), next(it), next(it)
    g_f32, g_low, grad_hid, grad_pre, d_packed, mix_grad = (next(it) for _ in range(6))
    part_send, part_recv, mask, smalls, small_near, small_all, own_grad = (next(it) for _ in range(7))
    load_sem, red_sems, part_sem, small_sem, move_sem, twin_sem = next(it), [next(it) for _ in range(6)], next(it), next(it), next(it), next(it)
    tower, dp, z, core, line, other, partner = spots()
    is_enc = tower == 0
    is_dec = tower == 1
    stays = z == 3 * core
    tokens, width = g_f32.shape
    rows_txt = tokens // LTXT
    quarter = tokens // 2
    heads = mix_grad.shape[1]
    rows_of = grads.shape[2]
    ffn_blocks = width // rows_of
    text_first = 2 * ffn_blocks - 2

    home = {DP: 2 * line + z // 2, MP: 2 * lax.rem(z, 2) + core}
    guest = {DP: 2 * line + lax.rem(z, 2), MP: 2 * core + z // 2}
    moved = jnp.logical_not(stays)
    peers = [(None, {DP: other}), (None, {DP: partner}), (is_enc, {TOWER: 1 - tower})]
    peers += [(None, {MP: lax.rem(z + away, 4)}) for away in range(1, 4)]
    peers += [(moved, home), (moved, guest)]
    barrier_all(
        peers,
        [
            (jnp.logical_and(is_enc, stays), 5),
            (jnp.logical_and(is_enc, moved), 7),
            (jnp.logical_and(is_dec, stays), 6),
            (jnp.logical_and(is_dec, moved), 8),
        ],
    )

    def load(i):
        return pltpu.make_async_copy(hbm[i], vm[i], load_sem.at[i])

    def on_side(i, run):
        if Tail._fields[i] in IMAGE_ONLY:
            pl.when(is_enc)(run)
        else:
            run()

    pl.when(is_dec)(lambda: pltpu.make_async_copy(cross_in, near.at[pl.ds(text_first, 2)], load_sem.at[len(hbm)]).start())
    for i in range(len(hbm)):
        on_side(i, load(i).start)

    def need(*wanted):
        for i, ref in enumerate(vm):
            if any(ref is one for one in wanted):
                on_side(i, load(i).wait)

    first_block = text_first * tower
    blocks = grads.shape[0]
    red = Reducer(grads, near, far, outs, red_sems, 2 + tower, first_block, blocks, blocks)

    def twin_copy():
        return pltpu.make_async_remote_copy(
            src_ref=outs.at[pl.ds(text_first, 2)],
            dst_ref=from_text,
            send_sem=twin_sem.at[0],
            recv_sem=twin_sem.at[1],
            device_id={TOWER: 1 - tower},
            device_id_type=MESH,
        )

    cross_load = pltpu.make_async_copy(cross_in, near.at[pl.ds(text_first, 2)], load_sem.at[len(hbm)])

    @pl.when(is_dec)
    def _():
        cross_load.wait()
        red.hop(text_first)
        red.hop(text_first + 1)

    def home_move(source, target, k):
        return pltpu.make_async_remote_copy(
            src_ref=source,
            dst_ref=target,
            send_sem=move_sem.at[k, 0],
            recv_sem=move_sem.at[k, 1],
            device_id=home,
            device_id_type=MESH,
        )

    @pl.when(moved)
    def _():
        home_move(tower_rows, tower_out, 0).start()

    @pl.when(stays)
    def _():
        pltpu.make_async_copy(tower_rows, own_grad, move_sem.at[0, 0]).start()
        pltpu.make_async_copy(tower_rows, own_grad, move_sem.at[0, 0]).wait()
        pltpu.make_async_copy(own_grad, tower_out, move_sem.at[0, 1]).start()
        pltpu.make_async_copy(own_grad, tower_out, move_sem.at[0, 1]).wait()

    def part_copy(k):
        return pltpu.make_async_remote_copy(
            src_ref=part_send.at[k],
            dst_ref=part_recv.at[k],
            send_sem=part_sem.at[k, 0],
            recv_sem=part_sem.at[k, 1],
            device_id={DP: partner},
            device_id_type=MESH,
        )

    zero = jnp.zeros((8, width), F32)
    need(vm.seg_col, vm.seg_row)
    fill_mask(mask, vm.seg_col, vm.seg_row, is_dec)
    need(vm.d_three, vm.base, vm.upstream, vm.gains, vm.smalls)
    smalls[...] = vm.smalls[...]

    def put(row, value):
        smalls[pl.ds(row, 1), :] = jnp.sum(value, axis=0, keepdims=True)

    def third(rows, kept):
        back, dg, db = norm_back_tile(vm.base[rows, :], vm.gains[2], vm.d_three[rows, :])
        total = vm.upstream[rows, :] + back
        g_f32[rows, :] = total
        low = total.astype(BF16)
        g_low[rows, :] = low
        return (kept[0] + dg, kept[1] + db, kept[2] + fold_rows(low.astype(F32)))

    dg, db, bias = row_tiles(tokens, third, (zero, zero, zero), 0, 3)
    put(4, dg)
    put(7, db)

    @pl.when(is_enc)
    def _():
        put(1, bias)
        need(vm.hid)

        @pl.loop(0, 2)
        def _(b):
            made = dot_first(vm.hid[:, pl.ds(pl.multiple_of(b * width, LANES), width)], g_low[...]).astype(BF16)
            grads[0:ffn_blocks, b] = made.reshape(ffn_blocks, rows_of, width)

        red.launch(0)
        need(vm.w_mlp, vm.pre)

        @pl.loop(0, 2)
        def _(b):
            cols = pl.ds(pl.multiple_of(b * width, LANES), width)
            grad_hid[...] = dot_rows(g_low[...], vm.w_mlp[cols, :])

            def bend(rows, kept):
                low = (grad_hid[rows, :] * gelu_both(vm.pre[rows, cols])[1]).astype(BF16)
                grad_pre[b, rows, :] = low
                return kept + fold_rows(low.astype(F32))

            put(9 + b, row_tiles(tokens, bend, zero))

        red.launch(1)
        need(vm.act, vm.w_in)

        @pl.loop(0, 2)
        def _(b):
            made = dot_first(grad_pre[b], vm.act[...]).astype(BF16)
            grads[ffn_blocks : 2 * ffn_blocks, b] = made.reshape(ffn_blocks, rows_of, width)

        red.step(0)
        grad_hid[...] = jnp.zeros_like(grad_hid)

        @pl.loop(0, 2)
        def _(b):
            grad_hid[...] += dot_rows(grad_pre[b], vm.w_in[b])

        def lower(rows, kept):
            part_send[0, rows, :] = grad_hid[rows, :].astype(BF16)
            return kept

        row_tiles(tokens, lower, 0)
        part_copy(0).start()
        need(vm.x1)
        part_copy(0).wait()

        def second(rows, kept):
            grad = part_send[0, rows, :].astype(F32) + part_recv[0, rows, :].astype(F32)
            back, dg, db = norm_back_tile(vm.x1[rows, :], vm.gains[1], grad)
            total = g_f32[rows, :] + back
            g_f32[rows, :] = total
            low = total.astype(BF16)
            g_low[rows, :] = low
            return (kept[0] + dg, kept[1] + db, kept[2] + fold_rows(low.astype(F32)))

        dg, db, bias_two = row_tiles(tokens, second, (zero, zero, zero), 0, 3)
        put(3, dg)
        put(6, db)
        put(0, bias_two)
        red.step(1)

    @pl.when(is_dec)
    def _():
        put(0, bias)

    need(vm.w_out, vm.mixed, vm.packed, vm.tops)
    mix_grad[...] = dot_rows(g_low[...], vm.w_out[...]).astype(BF16)
    grads[2 * ffn_blocks] = dot_first(vm.mixed[...], g_low[...]).astype(BF16).reshape(grads.shape[1:])


    @pl.when(is_enc)
    def _():
        red.step(2)

    @pl.when(is_dec)
    def _():
        red.launch(2 * ffn_blocks)

    def between():
        @pl.when(is_enc)
        def _():
            red.step(3)

    self_backward(vm.packed, mix_grad, vm.tops, mask, d_packed, pairs, scale, between)


    @pl.when(is_enc)
    def _():
        red.step(4)

    @pl.when(is_dec)
    def _():
        red.add_mid(text_first)

    now = 5 + (2 * ffn_blocks - 5) * tower


    need(vm.a_one, vm.w_qkv, vm.x0)

    @pl.loop(0, 3)
    def _(a):
        cols = pl.ds(pl.multiple_of(a * heads, LANES), heads)
        made = dot_first(d_packed[:, cols], vm.a_one[...]).astype(BF16)
        grads[2 * ffn_blocks + 1 + a] = made.reshape(grads.shape[1:])


    @pl.when(is_dec)
    def _():
        red.launch(2 * ffn_blocks + 1)
        red.launch(2 * ffn_blocks + 2)

    red.step(now)
    grad_hid[...] = jnp.zeros_like(grad_hid)

    @pl.loop(0, 3)
    def _(a):
        cols = pl.ds(pl.multiple_of(a * heads, LANES), heads)
        grad_hid[...] += dot_plain(d_packed[:, cols], vm.w_qkv[cols, :])


    def lower_two(rows, kept):
        part_send[1, rows, :] = grad_hid[rows, :].astype(BF16)
        return (
            kept[0] + fold_rows(d_packed[rows, pl.ds(0, heads)].astype(F32)),
            kept[1] + fold_rows(d_packed[rows, pl.ds(2 * heads, heads)].astype(F32)),
        )

    small_zero = jnp.zeros((8, heads), F32)
    q_sum, v_sum = row_tiles(tokens, lower_two, (small_zero, small_zero))
    part_copy(1).start()
    pl.when(is_enc)(lambda: red.step(now + 1))
    smalls[8:9, :] = jnp.concatenate(
        [jnp.sum(q_sum, axis=0, keepdims=True), jnp.sum(v_sum, axis=0, keepdims=True)], axis=1
    )
    part_copy(1).wait()

    def first(rows, kept):
        grad = part_send[1, rows, :].astype(F32) + part_recv[1, rows, :].astype(F32)
        back, dg, db = norm_back_tile(vm.x0[rows, :].astype(F32), vm.gains[0], grad)
        part_send[1, rows, :] = (g_f32[rows, :] + back).astype(BF16)
        return (kept[0] + dg, kept[1] + db)

    dg, db = row_tiles(tokens, first, (zero, zero), 0, 3)
    put(2, dg)
    put(5, db)
    mine = pl.ds(pl.multiple_of(core * quarter, TILE), quarter)

    def own_copy(rows, kept):
        shifted = pl.ds(pl.multiple_of(core * quarter + rows.start, 32), rows.size)
        own_grad[rows, :] = part_send[1, shifted, :]
        return kept

    row_tiles(quarter, own_copy, 0)

    small_line = pltpu.make_async_remote_copy(
        src_ref=smalls,
        dst_ref=small_near,
        send_sem=small_sem.at[0],
        recv_sem=small_sem.at[1],
        device_id={DP: other},
        device_id_type=MESH,
    )
    small_line.start()

    @pl.when(moved)
    def _():
        home_move(own_grad, grad_out, 1).start()

    @pl.when(stays)
    def _():
        pltpu.make_async_copy(own_grad, grad_out, move_sem.at[1, 0]).start()


    def small_pair(sender, away):
        return pltpu.make_async_remote_copy(
            src_ref=small_all.at[sender],
            dst_ref=small_all.at[sender],
            send_sem=small_sem.at[1 + away],
            recv_sem=small_sem.at[4 + away],
            device_id={MP: lax.rem(z + away, 4)},
            device_id_type=MESH,
        )

    def small_core(which):
        return pltpu.make_async_remote_copy(
            src_ref=small_out.at[which],
            dst_ref=small_out.at[which],
            send_sem=small_sem.at[8],
            recv_sem=small_sem.at[9],
            device_id={DP: partner},
            device_id_type=MESH,
        )

    after = now + 2 - tower
    red.step(after)
    small_line.wait()
    small_all[z] = smalls[...] + small_near[...]


    for away in range(1, 4):
        small_pair(z, away).start()

    red.step(after + 1)
    for away in range(1, 4):
        small_pair(lax.rem(z + 4 - away, 4), away).wait_recv()
    small_out[core] = ((small_all[0] + small_all[1]) + small_all[2]) + small_all[3]
    small_core(core).start()
    red.far_before(after + 2)
    red.drain(after + 2)
    red.close()
    pl.when(is_dec)(twin_copy().start)

    for away in range(1, 4):
        small_pair(z, away).wait_send()

    @pl.when(moved)
    def _():
        home_move(tower_rows, tower_out, 0).wait()
        home_move(own_grad, grad_out, 1).wait()

    @pl.when(stays)
    def _():
        pltpu.make_async_copy(own_grad, grad_out, move_sem.at[1, 0]).wait()

    pl.when(is_dec)(twin_copy().wait_send)
    pl.when(is_enc)(twin_copy().wait_recv)
    small_core(core).wait_send()
    small_core(1 - core).wait_recv()


def tail(values, cross_grad, tower_rows, scale):
    tokens, width = values.base.shape
    heads = values.mixed.shape[1]
    pairs = heads // LANES
    hidden = values.pre.shape[1]
    quarter = tokens // 2
    half = width // 2
    rows_of = heads // 2
    blocks = 2 * (width // rows_of) + 4
    assert hidden == 2 * width and cross_grad.shape[0] == 2
    hbm = pl.BlockSpec(memory_space=pltpu.HBM)
    vmem = pl.BlockSpec(memory_space=pltpu.VMEM)
    n_in = len(values)
    scratch = [pltpu.VMEM(x.shape, x.dtype) for x in values]
    scratch += [pltpu.VMEM((blocks, 2, rows_of, width), BF16)]
    scratch += [pltpu.VMEM((blocks, 2, rows_of, half), BF16)] * 2
    scratch += [
        pltpu.VMEM((tokens, width), F32),
        pltpu.VMEM((tokens, width), BF16),
        pltpu.VMEM((tokens, width), F32),
        pltpu.VMEM((2, tokens, hidden // 2), BF16),
        pltpu.VMEM((tokens, 3 * heads), BF16),
        pltpu.VMEM((tokens, heads), BF16),
        pltpu.VMEM((2, tokens, width), BF16),
        pltpu.VMEM((2, tokens, width), BF16),
        pltpu.VMEM((tokens, tokens), F32),
        pltpu.VMEM(values.smalls.shape, F32),
        pltpu.VMEM(values.smalls.shape, F32),
        pltpu.VMEM((4,) + values.smalls.shape, F32),
        pltpu.VMEM((quarter, width), BF16),
    ]
    dma = pltpu.SemaphoreType.DMA
    scratch += [dma((n_in + 1,)), dma((blocks,)), dma((blocks,)), dma((blocks, 2)), dma((blocks, 2)), dma((blocks,)), dma((blocks,))]
    scratch += [dma((2, 2)), dma((10,)), dma((2, 2)), dma((2,))]
    out_shape = [jax.ShapeDtypeStruct((blocks, rows_of, half), BF16)]
    out_shape += [
        jax.ShapeDtypeStruct((2,) + values.smalls.shape, F32),
        jax.ShapeDtypeStruct((quarter, width), BF16),
        jax.ShapeDtypeStruct((2, heads // 2, half), BF16),
        jax.ShapeDtypeStruct((quarter, width), BF16),
    ]
    return pl.pallas_call(
        functools.partial(tail_kernel, pairs, scale),
        in_specs=[hbm] * (n_in + 2),
        out_specs=[vmem] * 2 + [hbm] * 3,
        out_shape=out_shape,
        scratch_shapes=scratch,
        compiler_params=pltpu.CompilerParams(
            collective_id=1, has_side_effects=True, vmem_limit_bytes=TAIL_LIMIT
        ),
        name="tail",
    )(*values, cross_grad, tower_rows)


class Head(NamedTuple):
    packed: Any
    mixed: Any
    tops: Any
    a_one: Any
    x1: Any
    base: Any
    act_three: Any
    act: Any
    pre: Any
    hid: Any
    query: Any


def head_kernel(pieces, pairs, scale, *refs):
    it = iter(refs)
    srcs = [next(it) for _ in range(5)]
    blocks = [next(it)]
    seg_ref, image_ref = next(it), next(it)
    gains, shifts, out_b, ffn_out_b, ffn_in_b, qv_b = (next(it) for _ in range(6))
    outs = [next(it) for _ in range(5)]
    tokens = [next(it)]
    seg_out = [next(it) for _ in range(3)]
    hbm = Head(*[next(it) for _ in Head._fields])
    stages = [next(it) for _ in range(5)]
    weight_sems = [next(it) for _ in range(5)]
    token_stage = next(it)
    token_sems = [next(it) for _ in range(3)]
    w_qkv, w_out, w_q, w_in, w_mlp = (next(it) for _ in range(5))
    vm = Head(*[next(it) for _ in Head._fields])
    part_send, part_recv, raw, mask = next(it), next(it), next(it), next(it)
    seg_sem, load_sem, store_sem, part_sem = (next(it) for _ in range(4))
    tower, dp, z, core, line, other, partner = spots()
    is_enc = tower == 0
    is_dec = tower == 1
    stays = z == 3 * core
    moved = jnp.logical_not(stays)
    count, width = vm.x1.shape
    rows_txt = count // LTXT
    heads = vm.mixed.shape[1]
    at_end = jnp.logical_or(z == 0, z == 3)

    peers = [(z > 0, {MP: z - 1}), (z < 3, {MP: z + 1})]
    peers += [(None, {DP: other}), (None, {TOWER: 1 - tower}), (None, {DP: partner})]
    peers += [
        (moved, {DP: 2 * line + lax.rem(z, 2), MP: 2 * core + z // 2}),
        (moved, {DP: 2 * line + z // 2, MP: 2 * lax.rem(z, 2) + core}),
    ]
    barrier_all(
        peers,
        [(stays, 4), (jnp.logical_and(at_end, moved), 6), (jnp.logical_not(at_end), 7)],
    )

    begin, begin_local, pass_on, arrived, sent, end_local, end_twin = weight_steps(
        pieces, srcs, outs, stages, weight_sems, 1
    )
    token_begin, token_relay, token_finish = token_steps(blocks, tokens, token_stage, token_sems)
    token_begin(0)
    begin()

    has_notes = core == z // 2

    def note_send(i):
        return pltpu.make_async_remote_copy(
            src_ref=seg_out[i],
            dst_ref=seg_out[i],
            send_sem=seg_sem.at[i, 0],
            recv_sem=seg_sem.at[i, 1],
            device_id={DP: partner},
            device_id_type=MESH,
        )

    @pl.when(has_notes)
    def _():
        rows = seg_ref.shape[0] // 2
        side = lax.rem(z, 2)
        segs = jnp.where(side == 0, seg_ref[0:rows, :], seg_ref[rows : 2 * rows, :])
        marks = segs + LTXT * lax.broadcasted_iota(jnp.int32, segs.shape, 0)
        tall = jnp.concatenate([marks.astype(F32), jnp.zeros((16 - rows, LTXT), F32)], axis=0).T
        seg_out[1][...] = jnp.zeros_like(seg_out[1])
        for r in range(rows):
            at = pl.ds(r * LTXT, LTXT)
            seg_out[0][at, :] = jnp.broadcast_to(tall[:, r : r + 1], (LTXT, LANES)).astype(jnp.int32)
            seg_out[1][0:1, at] = marks[r : r + 1, :]
            seg_out[2][at, :] = jnp.full((LTXT, LANES), image_ref[side * rows + r], jnp.int32)
        for i in range(3):
            note_send(i).start()

    begin_local()
    token_relay(0)

    def load(i, target, source):
        return pltpu.make_async_copy(source, target, load_sem.at[i])

    def store(ref):
        i = [x is ref for x in vm].index(True)
        return pltpu.make_async_copy(vm[i], hbm[i], store_sem.at[i])

    def part_copy(k):
        return pltpu.make_async_remote_copy(
            src_ref=part_send.at[k],
            dst_ref=part_recv.at[k],
            send_sem=part_sem.at[k, 0],
            recv_sem=part_sem.at[k, 1],
            device_id={DP: partner},
            device_id_type=MESH,
        )

    def last_copy(i):
        rows = pl.ds(pl.multiple_of(i * (count // 2), 32), count // 2)
        return pltpu.make_async_remote_copy(
            src_ref=part_send.at[1, rows, :],
            dst_ref=part_recv.at[1, rows, :],
            send_sem=part_sem.at[1 + i, 0],
            recv_sem=part_sem.at[1 + i, 1],
            device_id={DP: partner},
            device_id_type=MESH,
        )

    def normed(source, target, which):
        gain, shift = gains[which], shifts[which]

        def tile(rows, kept):
            unit, _ = norm_parts(source[rows, :].astype(F32))
            target[rows, :] = (unit * gain + shift).astype(BF16)
            return kept

        row_tiles(count, tile, 0, 0, 3)

    def chosen(which, flag, far=False):
        return [k for k, p in enumerate(pieces) if p[0] == which and p[6] == flag and p[7] == far]

    enc_in, enc_mlp, dec_in = chosen(3, 0), chosen(4, 0), chosen(3, 1) + chosen(4, 1)
    k_qkv, k_out, k_own, k_far = chosen(0, None), chosen(1, None), chosen(2, 1), chosen(2, 1, True)
    waiting = {0: enc_in + enc_mlp, 1: k_own + k_far + dec_in}

    def relay(enc=0, dec=0):
        for t, count in ((0, enc), (1, dec)):
            for k in waiting[t][:count]:
                pass_on(k)
            waiting[t] = waiting[t][count:]

    token_finish(0)
    normed(tokens[0], vm.a_one, 0)
    store(vm.a_one).start()
    for k in k_qkv + k_out:
        pass_on(k)
    for k in k_qkv:
        arrived(k)
    end_local(0)
    load(0, w_qkv, outs[0]).start()
    load(0, w_qkv, outs[0]).wait()

    @pl.loop(0, 3)
    def _(part):
        cols = pl.ds(pl.multiple_of(part * heads, LANES), heads)
        own = pl.ds(pl.multiple_of(core * heads, LANES), heads)
        bias = jnp.where(part == 1, 0.0, qv_b[pl.ds(part // 2, 1), own])
        made = dot_rows(vm.a_one[...], w_qkv[part].reshape(heads, width)) + bias
        vm.packed[:, cols] = made.astype(BF16)

    store(vm.packed).start()

    @pl.when(has_notes)
    def _():
        for i in range(3):
            note_send(i).wait_send()

    @pl.when(jnp.logical_not(has_notes))
    def _():
        for i in range(3):
            note_send(i).wait_recv()

    relay(1, 1)
    fill_mask(mask, seg_out[0], seg_out[1], is_dec)
    self_forward(vm.packed, mask, vm.mixed, vm.tops, pairs, scale)
    store(vm.mixed).start()
    store(vm.tops).start()
    for k in k_out:
        arrived(k)
    end_local(1)
    load(1, w_out, outs[1]).start()
    relay(1, 1)
    load(1, w_out, outs[1]).wait()
    part_send[0] = dot_plain(vm.mixed[...], w_out[0].reshape(heads, width)).astype(BF16)
    part_copy(0).start()
    relay(1, 1)
    part_copy(0).wait()

    def add_one(rows, kept):
        total = part_send[0, rows, :].astype(F32) + part_recv[0, rows, :].astype(F32)
        vm.x1[rows, :] = tokens[0][rows, :].astype(F32) + total + out_b[...]
        return kept

    row_tiles(count, add_one, 0)
    store(vm.x1).start()

    @pl.when(is_enc)
    def _():
        relay(1)
        normed(vm.x1, vm.act, 1)
        store(vm.act).start()
        relay(1)
        for k in enc_in:
            arrived(k)
        end_local(3)
        load(3, w_in, outs[3]).start()
        load(3, w_in, outs[3]).wait()
        relay(1)

        @pl.loop(0, 2)
        def _(b):
            cols = pl.ds(pl.multiple_of(b * width, LANES), width)
            raw[...] = dot_plain(vm.act[...], w_in[0, b])
            bias = ffn_in_b[0:1, pl.ds(pl.multiple_of((2 * core + b) * width, LANES), width)]

            def bend(rows, kept):
                pre = raw[rows, :] + bias
                vm.pre[rows, cols] = pre
                vm.hid[rows, cols] = gelu_tanh(pre).astype(BF16)
                return kept

            row_tiles(count, bend, 0)

        relay(1)
        store(vm.pre).start()
        store(vm.hid).start()
        cut = width // 2
        raw[...] = jnp.zeros_like(raw)
        end_local(4)

        def half_load(i):
            rows = pl.ds(i * cut, cut)
            return load(4, w_mlp.at[:, :, rows, :], outs[4].at[:, :, rows, :])

        for k in enc_mlp[:2]:
            arrived(k)
        half_load(0).start()
        relay(len(waiting[0]))
        half_load(0).wait()

        @pl.loop(0, 2)
        def _(b):
            raw[...] += dot_plain(vm.hid[:, pl.ds(pl.multiple_of(b * width, LANES), cut)], w_mlp[0, b, 0:cut, :])

        for k in enc_mlp[2:]:
            arrived(k)
        half_load(1).start()
        half_load(1).wait()
        half = count // 2

        @pl.loop(0, 2)
        def _(i):
            rows = pl.ds(pl.multiple_of(i * half, 32), half)
            made = raw[rows, :]
            for b in range(2):
                made = made + dot_plain(vm.hid[rows, pl.ds(b * width + cut, cut)], w_mlp[0, b, cut:width, :])
            part_send[1, rows, :] = made.astype(BF16)
            last_copy(i).start()

        def add_two(rows, kept):
            total = part_send[1, rows, :].astype(F32) + part_recv[1, rows, :].astype(F32)
            value = vm.x1[rows, :] + total + ffn_out_b[...]
            vm.base[rows, :] = value
            unit, _ = norm_parts(value)
            vm.act_three[rows, :] = (unit * gains[2] + shifts[2]).astype(BF16)
            return kept

        @pl.loop(0, 2)
        def _(i):
            last_copy(i).wait()
            row_tiles(half, add_two, 0, i * half)


    @pl.when(is_dec)
    def _():
        def same(rows, kept):
            vm.base[rows, :] = vm.x1[rows, :]
            return kept

        row_tiles(count, same, 0)
        normed(vm.base, vm.act_three, 2)

    store(vm.act_three).start()
    store(vm.base).start()

    @pl.when(is_dec)
    def _():
        relay(0, 2)
        for k in k_own:
            arrived(k)
        end_local(2)
        load(2, w_q, outs[2].at[2]).start()
        load(2, w_q, outs[2].at[2]).wait()
        vm.query[...] = dot_rows(vm.act_three[...], w_q[...].reshape(heads, width)).astype(BF16)
        store(vm.query).start()
        relay(0, len(waiting[1]))
        for k in k_far + dec_in:
            arrived(k)
        end_local(3)
        end_local(4)

    for k in range(len(pieces)):
        sent(k)
    end_twin()
    for ref in vm:
        if ref is vm.act or ref is vm.pre or ref is vm.hid:
            pl.when(is_enc)(store(ref).wait)
        elif ref is vm.query:
            pl.when(is_dec)(store(ref).wait)
        else:
            store(ref).wait()


def head(shards, blocks, segment_ids, row_image, vecs, scale):
    qkv, out, cross, ffn_in, ffn_out = shards
    heads = 2 * out.shape[1]
    width = out.shape[2]
    pairs = heads // LANES
    count = 2 * blocks[0].shape[0]
    hidden = 2 * ffn_in.shape[2]

    def cuts(i, flag):
        blocks_of, rows, _ = shards[i].shape
        cut = rows if rows <= 192 else rows // 4
        return [(i, a, a, 1, at, cut, flag, False) for a in range(blocks_of) for at in range(0, rows, cut)]

    pieces = cuts(0, None) + cuts(1, None)
    rows = cross.shape[1]
    pieces += [(2, 2 + a, a, 1, 0, rows, 1, False) for a in range(2)] + [(2, a, a, 1, 0, rows, 1, True) for a in range(2)]
    pieces += cuts(3, 0) + cuts(4, 0) + cuts(3, 1) + cuts(4, 1)[:2]
    n = len(pieces)
    hbm = pl.BlockSpec(memory_space=pltpu.HBM)
    vmem = pl.BlockSpec(memory_space=pltpu.VMEM)
    struct = jax.ShapeDtypeStruct
    made = Head(
        packed=struct((count, 3 * heads), BF16),
        mixed=struct((count, heads), BF16),
        tops=struct((pairs, 8, 2 * count), F32),
        a_one=struct((count, width), BF16),
        x1=struct((count, width), F32),
        base=struct((count, width), F32),
        act_three=struct((count, width), BF16),
        act=struct((count, width), BF16),
        pre=struct((count, hidden), F32),
        hid=struct((count, hidden), BF16),
        query=struct((count, heads), BF16),
    )
    out_shape = [
        jax.ShapeDtypeStruct(((2 if i == 2 else 1) * x.shape[0], 2) + x.shape[1:], BF16) for i, x in enumerate(shards)
    ]
    out_shape += [jax.ShapeDtypeStruct((count, width), BF16)]
    out_shape += [struct((count, LANES), jnp.int32), struct((8, count), jnp.int32), struct((count, LANES), jnp.int32)]
    out_shape += list(made)
    dma = pltpu.SemaphoreType.DMA
    scratch = [pltpu.VMEM(x.shape, BF16) for x in shards]
    scratch += [dma((n, 5)), dma((n, 4)), dma((5, 2)), dma, dma]
    scratch += [pltpu.VMEM((1,) + blocks[0].shape, BF16), dma((1, 2)), dma((1, 2)), dma((1, 2))]
    scratch += [
        pltpu.VMEM((3, 2) + qkv.shape[1:], BF16),
        pltpu.VMEM((1, 2) + out.shape[1:], BF16),
        pltpu.VMEM((2,) + cross.shape[1:], BF16),
        pltpu.VMEM((1, 2) + ffn_in.shape[1:], BF16),
        pltpu.VMEM((1, 2) + ffn_out.shape[1:], BF16),
    ]
    scratch += [pltpu.VMEM(x.shape, x.dtype) for x in made]
    scratch += [
        pltpu.VMEM((2, count, width), BF16),
        pltpu.VMEM((2, count, width), BF16),
        pltpu.VMEM((count, width), F32),
        pltpu.VMEM((count, count), F32),
        dma((3, 2)),
        dma((5,)),
        dma((len(made),)),
        dma((3, 2)),
    ]
    results = pl.pallas_call(
        functools.partial(head_kernel, tuple(pieces), pairs, scale),
        in_specs=[hbm] * 6 + [vmem, pl.BlockSpec(memory_space=pltpu.SMEM)] + [vmem] * 6,
        out_specs=[hbm] * 5 + [vmem] + [vmem] * 3 + [hbm] * len(made),
        out_shape=out_shape,
        scratch_shapes=scratch,
        compiler_params=pltpu.CompilerParams(
            collective_id=0, has_side_effects=True, vmem_limit_bytes=VMEM_LIMIT
        ),
        name="head",
    )(*shards, *blocks, segment_ids, row_image, *vecs)
    return results[:5], results[5], results[6:9], Head(*results[9:])


CHUNKS = 6


def mid_kernel(pieces, pairs, scale, *refs):
    it = iter(refs)
    act_three, x1, query_in, w_cross_in, w_in_in, w_mlp_in, ffn_shard, cot_block, base = (next(it) for _ in range(9))
    gains, shifts, out_b, ffn_out_b, ffn_in_b, qv_b, picks = (next(it) for _ in range(7))
    d_three, upstream, smalls, tower_out, cross_out = (next(it) for _ in range(5))
    outs = next(it)
    stages = [next(it)]
    weight_sems = [next(it) for _ in range(5)]
    token_stage = next(it)
    token_sems = [next(it) for _ in range(3)]
    images, kv, w_cross, w_in, w_mlp = (next(it) for _ in range(5))
    act_txt, query, mixed, tops, y1, y2, act, pre, hid = (next(it) for _ in range(9))
    grad_hid, raw, grad_pre, g_low, mix_grad, dq, dkv, sum_q = (next(it) for _ in range(8))
    keys, vals, dk, dv = kv.at[0], kv.at[1], dkv.at[0], dkv.at[1]
    cot, part_send, part_recv, halves, half_near, sums, image_grad, own_rows = (next(it) for _ in range(8))
    grads, near, far = (next(it) for _ in range(3))
    red_sems = [next(it) for _ in range(6)]
    load_sem, store_sem, part_sem, twin_sem, side_sem, core_sem, half_sem, sum_sem, back_sem, give_sem, home_sem = it
    tower, dp, z, core, line, other, partner = spots()
    is_enc = tower == 0
    is_dec = tower == 1
    stays = z == 3 * core
    moved = jnp.logical_not(stays)
    side = lax.rem(z, 2)
    across_chip = z + 1 - 2 * side
    count, width = y1.shape
    quarter = count // 2
    chunk = quarter // CHUNKS
    heads = mixed.shape[1]

    home = {DP: 2 * line + z // 2, MP: 2 * lax.rem(z, 2) + core}
    guest = {DP: 2 * line + lax.rem(z, 2), MP: 2 * core + z // 2}
    peers = [(None, {DP: other}), (None, {DP: partner}), (None, {TOWER: 1 - tower})]
    peers += [(None, {MP: lax.rem(z + away, 4)}) for away in range(1, 4)]
    peers += [(moved, home), (moved, guest)]
    barrier_all(peers, [(stays, 6), (moved, 8)])

    def remote(source, target, sends, recvs, where):
        return pltpu.make_async_remote_copy(
            src_ref=source,
            dst_ref=target,
            send_sem=sends,
            recv_sem=recvs,
            device_id=where,
            device_id_type=MESH,
        )

    def span(which_core, i):
        return pl.ds(pl.multiple_of(which_core * quarter + i * chunk, 16), chunk)

    def twin_copy(i):
        rows = span(core, i)
        return remote(
            act_three.at[rows, :], images.at[side, rows, :], twin_sem.at[i, 0], twin_sem.at[i, 1], {TOWER: 1 - tower}
        )

    def side_copy(i, image):
        here = images.at[image, span(core, i), :]
        return remote(here, here, side_sem.at[i, 0], side_sem.at[i, 1], {MP: across_chip})

    def core_copy(i, image, which_core, far_image):
        here = images.at[image, span(which_core, i), :]
        return remote(here, here, core_sem.at[far_image, i, 0], core_sem.at[far_image, i, 1], {DP: partner})

    @pl.when(is_enc)
    def _():
        for i in range(CHUNKS):
            twin_copy(i).start()

    token_begin, token_relay, token_finish = token_steps([cot_block], [cot], token_stage, token_sems)
    pl.when(is_enc)(functools.partial(token_begin, 0))
    begin, begin_local, pass_on, arrived, sent, end_local, _ = weight_steps(
        pieces, [ffn_shard], [w_mlp], stages, weight_sems, 0
    )

    def load(i, source, target):
        return pltpu.make_async_copy(source, target, load_sem.at[i])

    held = pl.ds(0, ffn_shard.shape[1] // 2)
    early = [load(5, w_mlp_in.at[:, :, held, :], w_mlp.at[:, :, held, :])]
    text_loads = [
        load(0, w_cross_in, w_cross),
        load(1, query_in, query),
        load(2, x1, y1),
        load(3, w_in_in, w_in),
        load(4, act_three, act_txt),
    ]

    def part_copy(k, h):
        rows = pl.ds(pl.multiple_of(h * quarter, 32), quarter)
        return remote(
            part_send.at[k % 3, rows, :],
            part_recv.at[k % 3, rows, :],
            part_sem.at[k, h, 0],
            part_sem.at[k, h, 1],
            {DP: partner},
        )

    rows_copy = pltpu.make_async_copy(own_rows, tower_out, home_sem.at[0])

    def back_copy(i):
        rows = pl.ds(i * chunk, chunk)
        return remote(
            sums.at[1, rows, :], image_grad.at[span(core, i), :], back_sem.at[i, 0], back_sem.at[i, 1], {TOWER: 1 - tower}
        )

    def back_core(i, which_core):
        here = image_grad.at[span(which_core, i), :]
        return remote(here, here, give_sem.at[i, 0], give_sem.at[i, 1], {DP: partner})

    store_grad = pltpu.make_async_copy(y2, upstream, store_sem.at[0])
    store_three = pltpu.make_async_copy(raw, d_three, store_sem.at[1])
    zero = jnp.zeros((8, width), F32)
    blocks, rows_of = outs.shape[0], outs.shape[1]
    ffn_blocks = width // rows_of
    red = Reducer(grads, near, far, outs, red_sems, 4, 0, blocks, blocks + 2)

    @pl.when(is_enc)
    def _():
        smalls[...] = jnp.zeros_like(smalls)
        mine = pl.ds(pl.multiple_of(core * quarter, TILE), quarter)
        take = load(2, base.at[mine, :], y1.at[pl.ds(0, quarter), :])
        take.start()
        take.wait()

        def lower(rows, kept):
            own_rows[rows, :] = y1[rows, :].astype(BF16)
            return kept

        row_tiles(quarter, lower, 0)
        rows_copy.start()
        token_relay(0)
        token_finish(0)

        def lift(rows, kept):
            y2[rows, :] = cot[rows, :].astype(F32)
            return kept

        row_tiles(count, lift, 0)
        store_grad.start()
        for i in range(CHUNKS):
            back_copy(i).wait_recv()
            back_core(i, core).start()
        for i in range(CHUNKS):
            back_core(i, 1 - core).wait_recv()

        def lift_three(rows, kept):
            raw[rows, :] = image_grad[rows, :].astype(F32)
            return kept

        row_tiles(count, lift_three, 0)
        store_three.start()
        for i in range(CHUNKS):
            twin_copy(i).wait_send()
            back_core(i, core).wait_send()

    @pl.when(is_dec)
    def _():
        begin()
        for one in early + text_loads:
            one.start()
        for one in early:
            one.wait()
        begin_local()
        smalls[...] = jnp.zeros_like(smalls)

        def put(row, value):
            smalls[pl.ds(row, 1), :] = jnp.sum(value, axis=0, keepdims=True)

        for i in range(CHUNKS):
            twin_copy(i).wait_recv()
            side_copy(i, side).start()
            core_copy(i, side, core, 0).start()
        for k in range(len(pieces)):
            pass_on(k)
        for one in text_loads[:2]:
            one.wait()
        mixed[...] = jnp.zeros_like(mixed)
        for i in range(CHUNKS):
            core_copy(i, side, 1 - core, 0).wait_recv()

        @pl.loop(0, 2)
        def _(turn):
            image = side + turn * (1 - 2 * side)

            @pl.when(turn == 1)
            def _():
                for i in range(CHUNKS):
                    side_copy(i, 1 - side).wait_recv()
                    core_copy(i, 1 - side, core, 1).start()
                token_begin(0)
                for i in range(CHUNKS):
                    core_copy(i, 1 - side, 1 - core, 1).wait_recv()

            @pl.loop(0, 2)
            def _(part):
                kv[part, image] = dot_rows(images[image], w_cross[part].reshape(heads, width)).astype(BF16)

            cross_forward(image, query, keys, vals, picks, mixed, tops, pairs, scale)

        token_relay(0)

        def half_part(k, made):
            @pl.loop(0, 2)
            def _(h):
                rows = pl.ds(pl.multiple_of(h * quarter, 32), quarter)
                part_send[k % 3, rows, :] = made(rows).astype(BF16)
                part_copy(k, h).start()

        def add_halves(k, run, carry):
            def half(h, kept):
                part_copy(k, h).wait()
                return row_tiles(quarter, run, kept, h * quarter)

            return lax.fori_loop(0, 2, half, carry)

        half_part(0, lambda rows: dot_plain(mixed[rows, :], w_cross[3].reshape(heads, width)))
        for one in text_loads[2:]:
            one.wait()
        gain, shift = gains[1], shifts[1]

        def add_cross(rows, kept):
            total = part_send[0, rows, :].astype(F32) + part_recv[0, rows, :].astype(F32)
            value = y1[rows, :] + total
            y2[rows, :] = value
            unit, _ = norm_parts(value)
            act[rows, :] = (unit * gain + shift).astype(BF16)
            return kept

        token_finish(0)
        for k in range(len(pieces)):
            arrived(k)
        end_local(0)

        @pl.loop(0, 2)
        def _(b):
            grad_hid[b] = dot_rows(cot[...], w_mlp[0, b])

        add_halves(0, add_cross, 0)

        @pl.loop(0, 2)
        def _(b):
            cols = pl.ds(pl.multiple_of(b * width, LANES), width)
            pre[...] = dot_plain(act[...], w_in[0, b])
            bias = ffn_in_b[0:1, pl.ds(pl.multiple_of((2 * core + b) * width, LANES), width)]

            def bend(rows, kept):
                lifted, slope = gelu_both(pre[rows, :] + bias)
                hid[rows, cols] = lifted.astype(BF16)
                low = (grad_hid[b, rows, :] * slope).astype(BF16)
                grad_pre[b, rows, :] = low
                return kept + fold_rows(low.astype(F32))

            put(9 + b, row_tiles(count, bend, zero))

        half_part(2, lambda rows: dot_rows(grad_pre[0, rows, :], w_in[0, 0]) + dot_rows(grad_pre[1, rows, :], w_in[0, 1]))

        @pl.loop(0, 2)
        def _(b):
            made = dot_first(grad_pre[b], act[...]).astype(BF16)
            grads[0:ffn_blocks, b] = made.reshape(ffn_blocks, rows_of, width)

        red.launch(0)
        red.launch(1)

        def second(rows, kept):
            low_cot = cot[rows, :].astype(F32)
            grad = part_send[2, rows, :].astype(F32) + part_recv[2, rows, :].astype(F32)
            back, dg, db = norm_back_tile(y2[rows, :], gain, grad)
            total = low_cot + back
            raw[rows, :] = total
            g_low[rows, :] = total.astype(BF16)
            return (kept[0] + dg, kept[1] + db, kept[2] + fold_rows(low_cot))

        dg, db, cot_sum = add_halves(2, second, (zero, zero, zero))
        put(3, dg)
        put(6, db)
        put(1, cot_sum)

        mix_grad[...] = dot_rows(g_low[...], w_cross[3].reshape(heads, width)).astype(BF16)
        cross_backward(query, keys, vals, mix_grad, picks, tops, dq, dk, dv, sum_q, pairs, scale)

        def half_copy(image, far_image):
            return remote(
                halves.at[image, pl.ds(pl.multiple_of((1 - core) * quarter, TILE), quarter), :],
                half_near.at[far_image],
                half_sem.at[far_image, 0],
                half_sem.at[far_image, 1],
                {DP: partner},
            )

        @pl.loop(0, 2)
        def _(i):
            image = side + (1 - i) * (1 - 2 * side)
            made = dot_plain(dkv[0, image], w_cross[0].reshape(heads, width))
            made = made + dot_plain(dkv[1, image], w_cross[1].reshape(heads, width))
            halves[image] = made.astype(BF16)
            half_copy(image, 1 - i).start()

        for k in range(2):
            red.add_near(k, False)
            red.launch(k + 2)

        def sum_copy(i):
            rows = pl.ds(i * chunk, chunk)
            return remote(
                sums.at[0, rows, :], sums.at[2, rows, :], sum_sem.at[i, 0], sum_sem.at[i, 1], {MP: across_chip}
            )

        half_copy(1 - side, 1).wait_recv()
        for i in range(CHUNKS):

            def add_far(rows, kept):
                at = pl.ds(pl.multiple_of(i * chunk + rows.start, 16), rows.size)
                own = pl.ds(pl.multiple_of(core * quarter + i * chunk + rows.start, 16), rows.size)
                total = halves[1 - side, own, :].astype(F32) + half_near[1, at, :].astype(F32)
                sums[0, at, :] = total.astype(BF16)
                return kept

            row_tiles(chunk, add_far, 0)
            sum_copy(i).start()
        @pl.loop(0, 2)
        def _(b):
            cols = pl.ds(pl.multiple_of(b * width, LANES), width)
            made = dot_first(hid[:, cols], cot[...]).astype(BF16)
            grads[ffn_blocks : 2 * ffn_blocks, b] = made.reshape(ffn_blocks, rows_of, width)

        red.launch(4)
        red.launch(5)
        half_copy(side, 0).wait_recv()
        for i in range(CHUNKS):
            sum_copy(i).wait_recv()

            def add_own(rows, kept):
                at = pl.ds(pl.multiple_of(i * chunk + rows.start, 16), rows.size)
                own = pl.ds(pl.multiple_of(core * quarter + i * chunk + rows.start, 16), rows.size)
                total = halves[side, own, :].astype(F32) + half_near[0, at, :].astype(F32)
                sums[1, at, :] = (total + sums[2, at, :].astype(F32)).astype(BF16)
                return kept

            row_tiles(chunk, add_own, 0)
            back_copy(i).start()

        half_part(3, lambda rows: dot_plain(dq[rows, :], w_cross[2].reshape(heads, width)))
        red.hop(0)
        red.hop(1)
        red.step(2, 0)

        def keep_two(rows, kept):
            y1[rows, :] = raw[rows, :]
            return kept

        row_tiles(count, keep_two, 0)
        pltpu.make_async_copy(y1, upstream, store_sem.at[0]).start()

        def lift_query(rows, kept):
            raw[rows, :] = part_send[0, rows, :].astype(F32) + part_recv[0, rows, :].astype(F32)
            return kept

        add_halves(3, lift_query, 0)
        store_three.start()
        pre[...] = jnp.zeros_like(pre)

        @pl.loop(0, 2)
        def _(b):
            pre[...] += dot_plain(hid[:, pl.ds(pl.multiple_of(b * width, LANES), width)], w_mlp[0, b])

        for h in range(2):
            rows = pl.ds(h * quarter, quarter)
            part_send[1, rows, :] = pre[rows, :].astype(BF16)
            part_copy(1, h).start()
        red.add_mid(0)
        red.step(3, 0)
        red.add_mid(1)
        grads[2 * ffn_blocks] = dot_first(dq[...], act_txt[...]).astype(BF16).reshape(grads.shape[1:])
        grads[2 * ffn_blocks + 1] = dot_first(mixed[...], g_low[...]).astype(BF16).reshape(grads.shape[1:])
        red.add_mid(2)
        red.step(4)

        @pl.loop(0, 2)
        def _(which):
            made = dot_first(dkv[which, 0], images[0]) + dot_first(dkv[which, 1], images[1])
            grads[blocks + which] = made.astype(BF16).reshape(grads.shape[1:])

        red.step(5)
        for h in range(2):
            part_copy(1, h).wait()

        def add_last(rows, kept):
            own = pl.ds(pl.multiple_of(core * quarter + rows.start, 32), rows.size)
            total = part_send[1, own, :].astype(F32) + part_recv[1, own, :].astype(F32)
            own_rows[rows, :] = (y2[own, :] + total + ffn_out_b[...]).astype(BF16)
            return kept

        row_tiles(quarter, add_last, 0)
        rows_copy.start()
        red.far_before(6)
        red.drain(6)
        store_cross = pltpu.make_async_copy(near.at[pl.ds(blocks, 2)], cross_out, store_sem.at[2])
        store_cross.start()
        red.close()
        store_cross.wait()
        for i in range(CHUNKS):
            side_copy(i, side).wait_send()
            core_copy(i, side, core, 0).wait_send()
            core_copy(i, 1 - side, core, 1).wait_send()
            sum_copy(i).wait_send()
            back_copy(i).wait_send()
        half_copy(1 - side, 1).wait_send()
        half_copy(side, 0).wait_send()
        for k in range(len(pieces)):
            sent(k)

    rows_copy.wait()
    store_grad.wait()
    store_three.wait()


def middle(values, w_cross, w_in, w_mlp, ffn_shard, cot_block, vecs, picks, scale):
    count, width = values.base.shape
    heads = values.mixed.shape[1]
    pairs = heads // LANES
    hidden = values.hid.shape[1]
    quarter = count // 2
    half = width // 2
    chunk = quarter // CHUNKS
    assert chunk * CHUNKS == quarter
    rows_of = heads // 2
    blocks = 2 * (width // rows_of) + 2
    assert hidden == 2 * width
    cross_shape = (2, 2, rows_of, half)
    rows = ffn_shard.shape[1]
    pieces = [(0, 0, 0, 1, at, rows // 4, 1, False) for at in range(rows // 2, rows, rows // 4)]
    n = len(pieces)
    hbm = pl.BlockSpec(memory_space=pltpu.HBM)
    vmem = pl.BlockSpec(memory_space=pltpu.VMEM)
    dma = pltpu.SemaphoreType.DMA
    low, wide = (count, width), (count, heads)
    scratch = [pltpu.VMEM(ffn_shard.shape, BF16), dma((n, 5)), dma((n, 4)), dma((1, 2)), dma, dma]
    scratch += [pltpu.VMEM((1,) + cot_block.shape, BF16), dma((1, 2)), dma((1, 2)), dma((1, 2))]
    scratch += [
        pltpu.VMEM((2,) + low, BF16),
        pltpu.VMEM((2, 2) + wide, BF16),
        pltpu.VMEM((4, 2, heads // 2, width), BF16),
        pltpu.VMEM((1, 2, width, hidden // 2), BF16),
        pltpu.VMEM((1, 2, hidden // 2, width), BF16),
        pltpu.VMEM(low, BF16),
        pltpu.VMEM(wide, BF16),
        pltpu.VMEM(wide, BF16),
        pltpu.VMEM((2, pairs, 8, 2 * count), F32),
        pltpu.VMEM(low, F32),
        pltpu.VMEM(low, F32),
        pltpu.VMEM(low, BF16),
        pltpu.VMEM(low, F32),
        pltpu.VMEM((count, hidden), BF16),
        pltpu.VMEM((2,) + low, F32),
        pltpu.VMEM(low, F32),
        pltpu.VMEM((2, count, hidden // 2), BF16),
        pltpu.VMEM(low, BF16),
        pltpu.VMEM(wide, BF16),
        pltpu.VMEM(wide, BF16),
        pltpu.VMEM((2, 2) + wide, BF16),
        pltpu.VMEM((count, LANES), F32),
        pltpu.VMEM(low, BF16),
        pltpu.VMEM((3,) + low, BF16),
        pltpu.VMEM((3,) + low, BF16),
        pltpu.VMEM((2,) + low, BF16),
        pltpu.VMEM((2, quarter, width), BF16),
        pltpu.VMEM((3, quarter, width), BF16),
        pltpu.VMEM(low, BF16),
        pltpu.VMEM((quarter, width), BF16),
    ]
    scratch += [pltpu.VMEM((blocks + 2, 2, rows_of, width), BF16), pltpu.VMEM((blocks + 2, 2, rows_of, half), BF16)]
    scratch += [pltpu.VMEM((blocks, 2, rows_of, half), BF16)]
    scratch += [dma((blocks + 2,)), dma((blocks + 2,)), dma((blocks, 2)), dma((blocks, 2)), dma((blocks,)), dma((blocks,))]
    scratch += [
        dma((6,)),
        dma((3,)),
        dma((4, 2, 2)),
        dma((CHUNKS, 2)),
        dma((CHUNKS, 2)),
        dma((2, CHUNKS, 2)),
        dma((2, 2)),
        dma((CHUNKS, 2)),
        dma((CHUNKS, 2)),
        dma((CHUNKS, 2)),
        dma((2,)),
    ]
    out_shape = [
        jax.ShapeDtypeStruct(low, F32),
        jax.ShapeDtypeStruct(low, F32),
        jax.ShapeDtypeStruct((16, width), F32),
        jax.ShapeDtypeStruct((quarter, width), BF16),
        jax.ShapeDtypeStruct(cross_shape, BF16),
        jax.ShapeDtypeStruct((blocks, rows_of, half), BF16),
    ]
    args = [values.act_three, values.x1, values.query, w_cross, w_in, w_mlp]
    return pl.pallas_call(
        functools.partial(mid_kernel, tuple(pieces), pairs, scale),
        in_specs=[hbm] * 9 + [vmem] * 7,
        out_specs=[hbm, hbm, vmem, hbm, hbm, vmem],
        out_shape=out_shape,
        scratch_shapes=scratch,
        compiler_params=pltpu.CompilerParams(
            collective_id=2, has_side_effects=True, vmem_limit_bytes=TAIL_LIMIT
        ),
        name="middle",
    )(*args, ffn_shard, cot_block, values.base, *vecs, picks)


def finish_kernel(*refs):
    it = iter(refs)
    late, early, from_text, total = (next(it) for _ in range(4))
    rows_in = [next(it) for _ in range(2)]
    rows_out = [next(it) for _ in range(2)]
    o_qkv, o_out, o_in, o_mlp, o_cross, o_qv, o_outb, o_inb, o_mlpb, o_gain, o_shift = (next(it) for _ in range(11))
    held = [next(it) for _ in range(2)]
    b_in, b_mlp, b_out, b_qkv, b_cross, sem = it
    tower, dp, z, core, line, other, partner = spots()

    def bring(i, image_src, text_src, target):
        @pl.when(tower == 0)
        def _():
            pltpu.make_async_copy(image_src, target, sem.at[i]).start()

        @pl.when(tower == 1)
        def _():
            pltpu.make_async_copy(text_src, target, sem.at[i]).start()

    n = b_in.shape[0]
    bring(0, late.at[pl.ds(n, n)], early.at[pl.ds(0, n)], b_in)
    bring(1, late.at[pl.ds(0, n)], early.at[pl.ds(n, n)], b_mlp)
    bring(2, late.at[2 * n], late.at[2 * n], b_out)
    bring(3, late.at[pl.ds(2 * n + 1, 3)], late.at[pl.ds(2 * n + 1, 3)], b_qkv)
    bring(4, from_text, early.at[pl.ds(2 * n, 2)], b_cross)
    for i in range(2):
        pltpu.make_async_copy(rows_in[i], held[i], sem.at[5 + i]).start()

    width = total.shape[2]
    heads = width // 2
    first = total[0]
    o_outb[...] = first[0:1, :]
    o_mlpb[...] = first[1:2, :]
    for i in range(3):
        o_gain[i] = first[2 + i : 3 + i, :]
        o_shift[i] = first[5 + i : 6 + i, :]
    for side in range(2):
        lanes = slice(side * heads, (side + 1) * heads)
        o_qv[0, 0:1, lanes] = total[side, 8:9, :heads]
        o_qv[0, 1:2, lanes] = total[side, 8:9, heads:]
        for b in range(2):
            at = (2 * side + b) * width
            o_inb[0:1, at : at + width] = total[side, 9 + b : 10 + b, :]

    def mine(block):
        cut = block.shape[1] // 2
        wide = block.astype(F32)
        return jnp.where(core == 0, wide[:, :cut], wide[:, cut:])

    for i in range(2):
        pltpu.make_async_copy(rows_in[i], held[i], sem.at[5 + i]).wait()
        pltpu.make_async_copy(held[i], rows_out[i].at[0], sem.at[7 + i]).start()
    half = b_in.shape[2]
    cols = b_in.shape[1]
    pltpu.make_async_copy(late.at[pl.ds(0, n)], b_in, sem.at[0]).wait()
    for i in range(n // 2):
        pair = b_in[2 * i : 2 * i + 2].reshape(2 * cols, half)
        o_in[0, :, 2 * i * cols : 2 * (i + 1) * cols] = mine(pair).T
    pltpu.make_async_copy(late.at[pl.ds(0, n)], b_mlp, sem.at[1]).wait()
    for i in range(n // 2):
        pair = b_mlp[2 * i : 2 * i + 2].reshape(2 * cols, half)
        o_mlp[0, :, 2 * i * cols : 2 * (i + 1) * cols] = mine(pair).T
    pltpu.make_async_copy(late.at[0], b_out, sem.at[2]).wait()
    o_out[0] = mine(b_out[...])
    pltpu.make_async_copy(late.at[pl.ds(0, 3)], b_qkv, sem.at[3]).wait()
    for a in range(3):
        o_qkv[0, a] = mine(b_qkv[a]).T
    pltpu.make_async_copy(late.at[pl.ds(0, 2)], b_cross, sem.at[4]).wait()
    for a in range(2):
        o_cross[0, a] = mine(b_cross[a]).T
    for i in range(2):
        pltpu.make_async_copy(held[i], rows_out[i].at[0], sem.at[7 + i]).wait()


def finish(late, early, from_text, total, token_rows):
    hbm = pl.BlockSpec(memory_space=pltpu.HBM)
    vmem = pl.BlockSpec(memory_space=pltpu.VMEM)
    struct = jax.ShapeDtypeStruct
    width = total.shape[2]
    blocks, cols, half = early.shape
    n = (blocks - 2) // 2
    ffn, cut = n * cols, half // 2
    out_shape = [struct((1,) + x.shape, BF16) for x in token_rows]
    out_shape += [
        struct((1, 3, cut, cols), F32),
        struct((1, cols, cut), F32),
        struct((1, cut, ffn), F32),
        struct((1, cut, ffn), F32),
        struct((1, 2, cut, cols), F32),
        struct((1, 2, width), F32),
        struct((1, width), F32),
        struct((1, 4 * width), F32),
        struct((1, width), F32),
        struct((3, 1, width), F32),
        struct((3, 1, width), F32),
    ]
    scratch = [pltpu.VMEM(x.shape, BF16) for x in token_rows]
    scratch += [pltpu.VMEM(x + (cols, half), BF16) for x in ((n,), (n,), (), (3,), (2,))]
    scratch += [pltpu.SemaphoreType.DMA((9,))]
    results = pl.pallas_call(
        finish_kernel,
        in_specs=[hbm] * 3 + [vmem] + [hbm] * 2,
        out_specs=[hbm] * 2 + [vmem] * 11,
        out_shape=out_shape,
        scratch_shapes=scratch,
        compiler_params=pltpu.CompilerParams(vmem_limit_bytes=VMEM_LIMIT),
        name="finish",
    )(late, early, from_text, total, *token_rows)
    turned = {5: (1, 2), 11: (0, 1), 12: (0, 1)}
    return tuple(jnp.swapaxes(x, *turned[i]) if i in turned else x for i, x in enumerate(results))


def split_heads(flat):
    return jnp.swapaxes(flat.reshape(flat.shape[0], -1, HDIM), 0, 1)


def join_heads(split):
    return jnp.swapaxes(split, 0, 1).reshape(split.shape[1], -1)


def batch_dot(left, right, left_dim, right_dim):
    return lax.dot_general(left, right, (((left_dim,), (right_dim,)), ((0,), (0,))), preferred_element_type=F32)


def attend_plain(queries, keys, vals, allowed, scale):
    queries, keys, vals = (split_heads(x) for x in (queries, keys, vals))
    scores = jnp.where(allowed, batch_dot(queries, keys, 2, 2) * scale, NEG)
    top = jnp.max(scores, axis=-1, keepdims=True)
    tops = top + jnp.log(jnp.sum(jnp.exp(scores - top), axis=-1, keepdims=True))
    weights = jnp.exp(scores - tops).astype(BF16)
    return (join_heads(batch_dot(weights, vals, 2, 1)).astype(BF16), tops)


def attend_back_plain(queries, keys, vals, grads, tops, allowed, scale):
    queries, keys, vals, grads = (split_heads(x) for x in (queries, keys, vals, grads))
    scores = jnp.where(allowed, batch_dot(queries, keys, 2, 2) * scale, NEG)
    weights = jnp.exp(scores - tops)
    grad_w = batch_dot(grads, vals, 2, 2)
    grad_s = (weights * (grad_w - jnp.sum(weights * grad_w, axis=-1, keepdims=True))).astype(BF16)
    return (
        join_heads(batch_dot(grad_s, keys, 2, 1) * scale).astype(BF16),
        join_heads(batch_dot(grad_s, queries, 1, 1) * scale).astype(BF16),
        join_heads(batch_dot(weights.astype(BF16), grads, 1, 1)).astype(BF16),
    )


def gather_plain(shards):
    core = lax.rem(lax.axis_index(DP), 2)
    outs = []
    for i, s in enumerate(shards):
        if i == 2:
            s = jnp.concatenate([lax.ppermute(s, TOWER, [(0, 1)]), s], axis=0)
        full = lax.all_gather(s, MP, axis=1, tiled=False)
        outs.append(lax.dynamic_slice_in_dim(full, 2 * core, 2, 1))
    return outs


def reduce_plain(grads, smalls):
    dp = lax.axis_index(DP)
    core = lax.rem(dp, 2)
    outs = []
    for g in grads:
        n, _, rows, wide = g.shape
        full = jnp.zeros((n, 4, rows, wide), BF16)
        full = lax.dynamic_update_slice(full, g, (0, 2 * core, 0, 0))
        part = lax.psum_scatter(full, MP, scatter_dimension=1, tiled=False)
        part = lax.psum_scatter(part, DP, scatter_dimension=2, tiled=True)
        outs.append(part)
    if smalls is None:
        return outs
    both = jnp.zeros((2,) + smalls.shape, F32)
    both = lax.dynamic_update_slice(both, smalls[None], (core, 0, 0))
    return outs + [lax.psum(both, (DP, MP))]


def body(
    tower_in,
    out_cot,
    segment_ids,
    row_image,
    attn_qkv,
    attn_out,
    mlp_in,
    mlp_out,
    cross_proj,
    qv_bias,
    out_bias,
    mlp_bias_in,
    mlp_bias_out,
    norm_gain,
    norm_bias,
):
    lines = lax.axis_size(DP) // 2
    depth = lax.axis_size(MP)
    devices = lax.axis_size(DP)
    is_enc = lax.axis_index(TOWER) == 0
    dp = lax.axis_index(DP)
    z = lax.axis_index(MP)
    core = lax.rem(dp, 2)
    side = lax.rem(z, 2)
    group = z // 2
    direct = lines == 2
    assert depth == 4
    quarter = tower_in.shape[1]
    tokens = 2 * quarter
    assert tokens == PATCH
    width = tower_in.shape[2]
    head_cols = 2 * attn_qkv.shape[3]
    hidden = 2 * mlp_in.shape[2]
    scale_qk = HDIM ** (-0.5)

    out_moves, back_moves = [], []
    for d in range(devices):
        for place in range(depth):
            here = d * depth + place
            there = (d - d % 2 + place % 2) * depth + 2 * (d % 2) + place // 2
            out_moves.append((here, there))
            back_moves.append((there, here))

    def swap_cores(x):
        return lax.ppermute(x, DP, [(i, i ^ 1) for i in range(devices)])

    def both_cores(own):
        other = swap_cores(own)
        return jnp.where(core == 0, jnp.concatenate([own, other], -2), jnp.concatenate([other, own], -2))

    def own_rows(full):
        return lax.dynamic_slice_in_dim(full, core * quarter, quarter, full.ndim - 2)

    def lowered(part):
        return lax.reduce_precision(part, 8, 7).astype(BF16)

    def add_lowered(low):
        return low.astype(F32) + swap_cores(low).astype(F32)

    def add_cores(part):
        return add_lowered(lowered(part))

    def only_image(run, *operands):
        def idle(*inputs):
            return jax.tree.map(lambda x: jnp.zeros(x.shape, x.dtype), jax.eval_shape(run, *inputs))

        return lax.cond(is_enc, run, idle, *operands)

    shards = [
        jnp.swapaxes(attn_qkv[0], 1, 2),
        attn_out,
        jnp.swapaxes(cross_proj[0], 1, 2),
        mlp_in,
        mlp_out,
    ]
    rows = segment_ids.shape[0] // 2

    bias_qv = lax.dynamic_slice_in_dim(qv_bias[0], core * head_cols, head_cols, 1)
    bias_packed = jnp.concatenate([bias_qv[0], jnp.zeros_like(bias_qv[0]), bias_qv[1]])
    bias_in = lax.dynamic_slice_in_dim(mlp_bias_in[0], core * hidden, hidden, 0)
    gains = norm_gain[0]
    shifts = norm_bias[0]

    def feed_forward(values):
        act = norm_rows(values, gains[1], shifts[1]).astype(BF16)
        pre = jnp.concatenate([dot_plain(act, w_in[0]), dot_plain(act, w_in[1])], axis=1) + bias_in
        hid = gelu_tanh(pre).astype(BF16)
        return (act, pre, hid, lowered(dot_plain(hid, w_mlp)))

    if direct:
        tall_gains, tall_shifts = (jnp.swapaxes(x, 0, 1) for x in (norm_gain, norm_bias))
        vecs = (tall_gains, tall_shifts, out_bias, mlp_bias_out, mlp_bias_in, qv_bias[0])
        gathered, stream_low, notes, first = head(
            shards, [tower_in[0]], segment_ids, row_image, vecs, scale_qk
        )
        seg_col, seg_row, picks = notes
    else:
        gathered = gather_plain(shards)
        stream_low = both_cores(lax.ppermute(tower_in[0], (DP, MP), out_moves))
        cot_low = both_cores(lax.ppermute(out_cot[0], (DP, MP), out_moves))
        segs = jnp.where(core == group, segment_ids, swap_cores(segment_ids))
        segs = lax.dynamic_slice_in_dim(segs, rows * side, rows, 0)
        marks = (segs + LTXT * jnp.arange(rows, dtype=jnp.int32)[:, None]).reshape(tokens)
        images_of = jnp.where(core == group, row_image, swap_cores(row_image))
        images_of = jnp.repeat(lax.dynamic_slice_in_dim(images_of, rows * side, rows, 0), LTXT)
        places = jnp.arange(tokens)
        allowed = (places[None, :] <= places[:, None]) & (marks[None, :] == marks[:, None])
        allowed = jnp.logical_or(allowed, is_enc)
        sees = images_of[:, None] == jnp.arange(2 * tokens)[None, :] // tokens
    w_qkv = gathered[0].reshape(3 * head_cols, width)
    w_out = gathered[1].reshape(head_cols, width)
    w_cross = gathered[2].reshape(4, head_cols, width)
    w_in = gathered[3][0]
    w_mlp = gathered[4].reshape(hidden, width)
    stream = stream_low.astype(F32)

    if not direct:
        act_one = norm_rows(stream, gains[0], shifts[0]).astype(BF16)
        packed = (dot_rows(act_one, w_qkv) + bias_packed).astype(BF16)
        parts = [packed[:, i * head_cols : (i + 1) * head_cols] for i in range(3)]
        mixed, tops = attend_plain(*parts, allowed, scale_qk)
        stream_one = stream + add_cores(dot_plain(mixed, w_out)) + out_bias[0]
        act_enc, pre_enc, hid_enc, part_enc = feed_forward(stream_one)
        out_enc = stream_one + add_lowered(part_enc) + mlp_bias_out[0]
        base_three = jnp.where(is_enc, out_enc, stream_one)
        act_three = norm_rows(base_three, gains[2], shifts[2]).astype(BF16)
        cross_q = dot_rows(act_three, w_cross[2]).astype(BF16)

    if direct:
        back_in_three, upstream, smalls, tower_rows, g_cross, early = middle(
            first, gathered[2], gathered[3], gathered[4], mlp_out, out_cot[0], vecs, picks, scale_qk
        )
        values = Tail(
            d_three=back_in_three,
            base=first.base,
            upstream=upstream,
            gains=tall_gains,
            smalls=smalls,
            w_mlp=w_mlp,
            pre=first.pre,
            hid=first.hid,
            act=first.act,
            w_in=w_in,
            x1=first.x1,
            w_out=w_out,
            mixed=first.mixed,
            packed=first.packed,
            tops=first.tops,
            seg_col=seg_col,
            seg_row=seg_row,
            a_one=first.a_one,
            w_qkv=w_qkv,
            x0=stream_low,
        )
        late, total, grad_in, from_text, tower_out = tail(values, g_cross, tower_rows, scale_qk)
        return finish(late, early, from_text, total, [tower_out, grad_in])
    else:
        near_half = lax.ppermute(own_rows(act_three), TOWER, [(0, 1)])
        far_half = lax.ppermute(near_half, MP, [(i, i ^ 1) for i in range(depth)])
        halves = jnp.where(side == 0, jnp.stack([near_half, far_half]), jnp.stack([far_half, near_half]))
        images = both_cores(halves)

        flat_images = images.reshape(2 * tokens, width)
        cross_k = dot_rows(flat_images, w_cross[0]).astype(BF16)
        cross_v = dot_rows(flat_images, w_cross[1]).astype(BF16)
        cross_mix, cross_tops = attend_plain(cross_q, cross_k, cross_v, sees, scale_qk)
        stream_two = stream_one + add_cores(dot_plain(cross_mix, w_cross[3]))

        act_dec, pre_dec, hid_dec, part_dec = feed_forward(stream_two)
        out_dec = stream_two + add_lowered(part_dec) + mlp_bias_out[0]
        tower_rows = own_rows(jnp.where(is_enc, base_three, out_dec).astype(BF16))

        def feed_back(grad_low, pre):
            grad_hid = dot_rows(grad_low, w_mlp)
            _, pullback = jax.vjp(gelu_tanh, pre)
            grad_pre = pullback(grad_hid)[0].astype(BF16)
            cols = hidden // 2
            part = dot_rows(grad_pre[:, :cols], w_in[0]) + dot_rows(grad_pre[:, cols:], w_in[1])
            return (grad_pre, lowered(part))

        def feed_grads(grad_low, act, grad_pre, hid):
            g_in = dot_first(grad_pre, act).astype(BF16)
            g_mlp = dot_first(hid, grad_low).astype(BF16)
            return (
                g_in.reshape(1, 2, hidden // 2, width),
                g_mlp.reshape(1, 2, hidden // 2, width),
            )

        cot = cot_low.astype(F32)
        grad_pre_dec, back_in = feed_back(cot_low, pre_dec)
        back_a, gain_a, shift_a = norm_back(stream_two, gains[1], add_lowered(back_in))
        grad_two = cot + back_a
        grad_two_low = grad_two.astype(BF16)

        grad_mix = dot_rows(grad_two_low, w_cross[3]).astype(BF16)
        grad_q, flat_k, flat_v = attend_back_plain(
            cross_q, cross_k, cross_v, grad_mix, cross_tops, sees, scale_qk
        )
        part_images = dot_plain(flat_k, w_cross[0]) + dot_plain(flat_v, w_cross[1])
        part_low = part_images.astype(BF16).reshape(2, 2, quarter, width)
        give = lax.dynamic_index_in_dim(part_low, 1 - core, 1, keepdims=False)
        keep = lax.dynamic_index_in_dim(part_low, core, 1, keepdims=False)
        pair_sum = (keep.astype(F32) + swap_cores(give).astype(F32)).astype(BF16)
        give = lax.dynamic_index_in_dim(pair_sum, 1 - side, 0, keepdims=False)
        keep = lax.dynamic_index_in_dim(pair_sum, side, 0, keepdims=False)
        got = lax.ppermute(give, MP, [(i, i ^ 1) for i in range(depth)])
        image_sum = (keep.astype(F32) + got.astype(F32)).astype(BF16)
        image_half = lax.ppermute(image_sum, TOWER, [(1, 0)])
        later = lax.optimization_barrier(
            (cot_low, act_dec, grad_pre_dec, hid_dec, flat_k, flat_v, grad_q, cross_mix, image_sum)
        )
        g_in_dec, g_mlp_dec = feed_grads(later[0], later[1], later[2], later[3])
        g_cross = jnp.concatenate(
            [
                dot_first(later[4], flat_images).astype(BF16),
                dot_first(later[5], flat_images).astype(BF16),
                dot_first(later[6], act_three).astype(BF16),
                dot_first(later[7], grad_two_low).astype(BF16),
            ],
            axis=0,
        ).reshape(4, 2, head_cols // 2, width)
        image_back = both_cores(image_half).astype(F32)
        query_back = add_cores(dot_plain(grad_q, w_cross[2]))
        back_in_three = jnp.where(is_enc, image_back, query_back)
        text_smalls = (
            jnp.zeros((16, width), F32)
            .at[1]
            .set(jnp.sum(cot_low, axis=0, dtype=F32))
            .at[3]
            .set(gain_a)
            .at[6]
            .set(shift_a)
            .at[9:11]
            .set(jnp.sum(grad_pre_dec, axis=0, dtype=F32).reshape(2, width))
        )
        smalls = jnp.where(is_enc, 0.0, text_smalls)
        tower_out = lax.ppermute(tower_rows, (DP, MP), back_moves)
        back_three, gain_three, shift_three = norm_back(
            base_three, gains[2], back_in_three
        )
        grad_enc = cot + back_three
        grad_enc_low = grad_enc.astype(BF16)

        grad_pre_enc, back_in = feed_back(grad_enc_low, pre_enc)
        g_in, g_mlp = feed_grads(grad_enc_low, act_enc, grad_pre_enc, hid_enc)
        back_b, gain_b, shift_b = norm_back(stream_one, gains[1], add_lowered(back_in))
        grad_one = jnp.where(is_enc, grad_enc + back_b, grad_two + back_three)
        grad_one_low = grad_one.astype(BF16)

        g_out = dot_first(mixed, grad_one_low).astype(BF16).reshape(1, 2, head_cols // 2, width)
        grad_mixed = dot_rows(grad_one_low, w_out).astype(BF16)
        grad_packed = jnp.concatenate(
            attend_back_plain(*parts, grad_mixed, tops, allowed, scale_qk), axis=1
        )
        g_qkv = dot_first(grad_packed, act_one).astype(BF16).reshape(3, 2, head_cols // 2, width)
        back_in = add_cores(dot_plain(grad_packed, w_qkv))
        back_one, gain_one, shift_one = norm_back(stream, gains[0], back_in)
        grad_in = own_rows((grad_one + back_one).astype(BF16))
        grad_in = lax.ppermute(grad_in, (DP, MP), back_moves)

        grad_pre_sum = jnp.sum(grad_pre_enc, axis=0, dtype=F32).reshape(2, width)
        packed_sum = jnp.sum(grad_packed, axis=0, dtype=F32)
        smalls = jnp.concatenate(
            [
                jnp.sum(grad_one_low, axis=0, dtype=F32)[None],
                jnp.where(is_enc, jnp.sum(grad_enc_low, axis=0, dtype=F32), smalls[1])[None],
                gain_one[None],
                jnp.where(is_enc, gain_b, smalls[3])[None],
                gain_three[None],
                shift_one[None],
                jnp.where(is_enc, shift_b, smalls[6])[None],
                shift_three[None],
                jnp.concatenate([packed_sum[:head_cols], packed_sum[2 * head_cols :]])[None],
                jnp.where(is_enc, grad_pre_sum, smalls[9:11]),
                smalls[11:],
            ]
        )
        g_in = jnp.where(is_enc, g_in, g_in_dec)
        g_mlp = jnp.where(is_enc, g_mlp, g_mlp_dec)
        s_in, s_mlp, s_out, s_qkv, s_cross, total = reduce_plain([g_in, g_mlp, g_out, g_qkv, g_cross], smalls)
        s_cross = jnp.where(is_enc, lax.ppermute(s_cross[:2], TOWER, [(1, 0)]), s_cross[2:])

    def turned(x):
        return jnp.swapaxes(x, 1, 2).astype(F32)

    cross_pair = jnp.stack(
        [
            s_cross[0].T,
            s_cross[1].T,
        ]
    ).astype(F32)
    first = total[0]
    qv_total = jnp.stack(
        [
            total[:, 8, :head_cols].reshape(-1),
            total[:, 8, head_cols:].reshape(-1),
        ]
    )
    in_total = total[:, 9:11].reshape(-1)
    return (
        tower_out[None],
        grad_in[None],
        turned(s_qkv)[None],
        s_out.astype(F32),
        turned(s_in),
        s_mlp.astype(F32),
        cross_pair[None],
        qv_total[None],
        first[0:1],
        in_total[None],
        first[1:2],
        first[2:5][None],
        first[5:8][None],
    )


def solution(mesh):
    return jax.shard_map(
        body,
        mesh=mesh,
        in_specs=(
            P(TOWER, (DP, MP), None),
            P(TOWER, (DP, MP), None),
            P(DP, None),
            P(DP),
            P(TOWER, None, None, MP),
            P(TOWER, MP, None),
            P(TOWER, None, MP),
            P(TOWER, MP, None),
            P(TOWER, None, None, MP),
            P(TOWER, None, None),
            P(TOWER, None),
            P(TOWER, None),
            P(TOWER, None),
            P(TOWER, None, None),
            P(TOWER, None, None),
        ),
        out_specs=(
            P(TOWER, (DP, MP), None),
            P(TOWER, (DP, MP), None),
            P(TOWER, None, DP, MP),
            P(TOWER, MP, DP),
            P(TOWER, DP, MP),
            P(TOWER, MP, DP),
            P(TOWER, None, DP, MP),
            P(TOWER, None, None),
            P(TOWER, None),
            P(TOWER, None),
            P(TOWER, None),
            P(TOWER, None, None),
            P(TOWER, None, None),
        ),
        check_vma=False,
    )
```

```python
import functools
from typing import Any, NamedTuple

import jax
import jax.numpy as jnp
from jax import lax
from jax.experimental import pallas as pl
from jax.experimental.pallas import tpu as pltpu
from jax.sharding import PartitionSpec as P

TOWER = "tower"
DP = "dp"
MP = "mp"
HDIM = 64
PATCH = 576
LTXT = 64
EPS = 1e-06
NEG = -1e30
LANES = 128
MESH = pl.DeviceIdType.MESH
F32 = jnp.float32
BF16 = jnp.bfloat16
VMEM_LIMIT = 60 * 1024 * 1024
TAIL_LIMIT = 67043328


def norm_parts(values):
    center = values - jnp.mean(values, axis=-1, keepdims=True)
    spread = jnp.mean(center * center, axis=-1, keepdims=True)
    scale = lax.rsqrt(spread + EPS)
    return (center * scale, scale)


def norm_rows(values, gain_vec, shift_vec):
    unit, _ = norm_parts(values)
    return unit * gain_vec + shift_vec


def norm_back(values, gain_vec, grad_normed):
    unit, scale = norm_parts(values)
    inner = grad_normed * gain_vec
    mean_one = jnp.mean(inner, axis=-1, keepdims=True)
    mean_two = jnp.mean(inner * unit, axis=-1, keepdims=True)
    back = (inner - mean_one - unit * mean_two) * scale
    return (back, jnp.sum(grad_normed * unit, axis=0), jnp.sum(grad_normed, axis=0))


def gelu_tanh(values):
    return jax.nn.gelu(values, approximate=True)


def dot_rows(left, right):
    return lax.dot_general(left, right, (((1,), (1,)), ((), ())), preferred_element_type=F32)


def dot_first(left, right):
    return lax.dot_general(left, right, (((0,), (0,)), ((), ())), preferred_element_type=F32)


def dot_plain(left, right):
    return lax.dot_general(left, right, (((1,), (0,)), ((), ())), preferred_element_type=F32)


def spots():
    tower = lax.axis_index(TOWER)
    dp = lax.axis_index(DP)
    z = lax.axis_index(MP)
    core = lax.rem(dp, 2)
    line = dp // 2
    return tower, dp, z, core, line, dp + 2 - 4 * line, dp + 1 - 2 * core


def greet(target):
    pl.semaphore_signal(pltpu.get_barrier_semaphore(), inc=1, device_id=target, device_id_type=MESH)


def weight_steps(pieces, srcs, outs, stages, sems, less):
    send_sem, recv_sem, local_sem, twin_send, twin_recv = sems
    tower, dp, z, core, line, other, partner = spots()
    place = z + core * (3 - 2 * z)
    ahead = z + 1 - 2 * core
    behind = z - 1 + 2 * core
    slot_of = (core, 1 - core)
    holder = place <= 1
    far_src = [k for k, p in enumerate(pieces) if p[7]]

    def spot(piece, slot, half):
        which, first, _, count, start, size, _, _ = piece
        part = size // 2
        return outs[which].at[pl.ds(first, count), slot, pl.ds(start + half * part, part), :]

    def own(piece):
        which, _, first, count, start, size, _, far = piece
        part = size // 2
        if far:
            return spot(piece, lax.rem(z, 2), line)
        return srcs[which].at[pl.ds(first, count), pl.ds(start + line * part, part), :]

    def move(k, source, slot, half, kind, arrive, target):
        return pltpu.make_async_remote_copy(
            src_ref=source,
            dst_ref=spot(pieces[k], slot, half),
            send_sem=send_sem.at[k, kind],
            recv_sem=recv_sem.at[k, arrive],
            device_id=target,
            device_id_type=MESH,
        )

    def twin_copy():
        which = pieces[far_src[0]][0]
        return pltpu.make_async_remote_copy(
            src_ref=srcs[which],
            dst_ref=outs[which].at[pl.ds(0, srcs[which].shape[0]), lax.rem(z, 2)],
            send_sem=twin_send,
            recv_sem=twin_recv,
            device_id={TOWER: 1 - tower},
            device_id_type=MESH,
        )

    def local_in(i):
        return pltpu.make_async_copy(srcs[i], stages[i], local_sem.at[i, 0])

    def local_out(i):
        first = outs[i].shape[0] - srcs[i].shape[0]
        return pltpu.make_async_copy(
            stages[i], outs[i].at[pl.ds(first, srcs[i].shape[0]), lax.rem(z, 2)], local_sem.at[i, 1]
        )

    def gate(piece, cond):
        return cond if piece[6] is None else jnp.logical_and(cond, tower == piece[6])

    def send_own(k, seat):
        piece = pieces[k]

        if seat == 0:

            @pl.when(gate(piece, place == 0))
            def _():
                move(k, own(piece), slot_of[0], line, 0, 0, {MP: ahead}).start()

        else:

            @pl.when(gate(piece, place == 1))
            def _():
                move(k, own(piece), slot_of[1], line, 1, 1, {MP: ahead}).start()
                move(k, own(piece), slot_of[1], line, 2, 1, {MP: behind}).start()

    orders = {t: [k for k, p in enumerate(pieces) if p[6] in (None, t)] for t in (0, 1)}

    def launch(t, at, seat):
        if at >= len(orders[t]):
            return
        k = orders[t][at]

        @pl.when(jnp.logical_and(place == seat, tower == t))
        def _():
            if far_src and k == far_src[0]:
                twin_copy().wait_recv()
            send_own(k, seat)

    def own_sent(k):
        piece = pieces[k]

        @pl.when(gate(piece, place == 0))
        def _():
            move(k, own(piece), slot_of[0], line, 0, 0, {MP: z}).wait_send()

        @pl.when(gate(piece, place == 1))
        def _():
            move(k, own(piece), slot_of[1], line, 1, 1, {MP: z}).wait_send()
            move(k, own(piece), slot_of[1], line, 2, 1, {MP: z}).wait_send()

    def begin():
        if far_src:

            @pl.when(jnp.logical_and(holder, tower == 0))
            def _():
                twin_copy().start()

        for t in (0, 1):
            for seat in (0, 1):
                for start in range(WINDOW - less * seat):
                    launch(t, start, seat)

    def keeps(i):
        flags = {p[6] for p in pieces if p[0] == i}
        flag = None if len(flags) > 1 else flags.pop()
        return holder if flag is None else jnp.logical_and(holder, tower == flag)

    def begin_local():
        for i in range(len(srcs)):

            @pl.when(keeps(i))
            def _(i=i):
                local_in(i).start()

        for i in range(len(srcs)):

            @pl.when(keeps(i))
            def _(i=i):
                local_in(i).wait()
                local_out(i).start()

    def pass_on(k):
        piece = pieces[k]

        @pl.when(gate(piece, place >= 1))
        def _():
            here = spot(piece, slot_of[0], line)
            move(k, here, slot_of[0], line, 0, 0, {MP: z}).wait_recv()
            move(k, here, slot_of[0], line, 3, 2, {DP: other}).start()

        @pl.when(gate(piece, jnp.logical_and(place >= 1, place <= 2)))
        def _():
            here = spot(piece, slot_of[0], line)
            move(k, here, slot_of[0], line, 0, 0, {MP: ahead}).start()

        @pl.when(gate(piece, place != 1))
        def _():
            here = spot(piece, slot_of[1], line)
            move(k, here, slot_of[1], line, 1, 1, {MP: z}).wait_recv()
            move(k, here, slot_of[1], line, 4, 3, {DP: other}).start()

        @pl.when(gate(piece, place == 2))
        def _():
            here = spot(piece, slot_of[1], line)
            move(k, here, slot_of[1], line, 1, 1, {MP: ahead}).start()

        own_sent(k)
        for t in (0, 1):
            if k in orders[t]:
                for seat in (0, 1):
                    launch(t, orders[t].index(k) + WINDOW - less * seat, seat)

    def arrived(k):
        piece = pieces[k]

        @pl.when(gate(piece, place >= 1))
        def _():
            move(k, spot(piece, slot_of[0], 1 - line), slot_of[0], 1 - line, 3, 2, {DP: dp}).wait_recv()

        @pl.when(gate(piece, place != 1))
        def _():
            move(k, spot(piece, slot_of[1], 1 - line), slot_of[1], 1 - line, 4, 3, {DP: dp}).wait_recv()

    def sent(k):
        piece = pieces[k]

        @pl.when(gate(piece, jnp.logical_or(place == 1, place == 2)))
        def _():
            move(k, spot(piece, slot_of[0], line), slot_of[0], line, 0, 0, {MP: z}).wait_send()

        @pl.when(gate(piece, place == 2))
        def _():
            move(k, spot(piece, slot_of[1], line), slot_of[1], line, 1, 1, {MP: z}).wait_send()

        @pl.when(gate(piece, place >= 1))
        def _():
            move(k, spot(piece, slot_of[0], line), slot_of[0], line, 3, 2, {DP: dp}).wait_send()

        @pl.when(gate(piece, place != 1))
        def _():
            move(k, spot(piece, slot_of[1], line), slot_of[1], line, 4, 3, {DP: dp}).wait_send()

    def end_local(i):
        @pl.when(keeps(i))
        def _():
            local_out(i).wait()

    def end_twin():
        @pl.when(jnp.logical_and(holder, tower == 0))
        def _():
            twin_copy().wait_send()

    return begin, begin_local, pass_on, arrived, sent, end_local, end_twin


def token_steps(blocks, outs, stage, sems):
    send_sem, recv_sem, local_sem = sems
    tower, dp, z, core, line, other, partner = spots()
    stays = z == 3 * core
    size = blocks[0].shape[0]

    def rows(which_core):
        return pl.ds(pl.multiple_of(which_core * size, 16), size)

    def away(i):
        target = {DP: 2 * line + lax.rem(z, 2), MP: 2 * core + z // 2}
        return pltpu.make_async_remote_copy(
            src_ref=blocks[i],
            dst_ref=outs[i].at[rows(lax.rem(z, 2)), :],
            send_sem=send_sem.at[i, 0],
            recv_sem=recv_sem.at[i, 0],
            device_id=target,
            device_id_type=MESH,
        )

    def across(i, which_core):
        return pltpu.make_async_remote_copy(
            src_ref=outs[i].at[rows(which_core), :],
            dst_ref=outs[i].at[rows(which_core), :],
            send_sem=send_sem.at[i, 1],
            recv_sem=recv_sem.at[i, 1],
            device_id={DP: partner},
            device_id_type=MESH,
        )

    def begin(i):
        @pl.when(jnp.logical_not(stays))
        def _():
            away(i).start()

        @pl.when(stays)
        def _():
            first = pltpu.make_async_copy(blocks[i], stage.at[i], local_sem.at[i, 0])
            first.start()
            first.wait()
            second = pltpu.make_async_copy(stage.at[i], outs[i].at[rows(core), :], local_sem.at[i, 1])
            second.start()
            second.wait()
            across(i, core).start()

    def relay(i):
        @pl.when(jnp.logical_not(stays))
        def _():
            away(i).wait_recv()
            across(i, core).start()

    def finish(i):
        across(i, 1 - core).wait_recv()
        across(i, core).wait_send()

        @pl.when(jnp.logical_not(stays))
        def _():
            away(i).wait_send()

    return begin, relay, finish


TILE = 32
LAG = 1
WINDOW = 2


def barrier_all(peers, options):
    for cond, target in peers:
        if cond is None:
            greet(target)
        else:
            pl.when(cond)(functools.partial(greet, target))
    for cond, count in options:

        @pl.when(cond)
        def _(count=count):
            pl.semaphore_wait(pltpu.get_barrier_semaphore(), count)


def fold_rows(tile):
    return jnp.sum(tile.reshape(tile.shape[0] // 8, 8, tile.shape[1]), axis=0)


def row_tiles(total, run, carry, first=0, unroll=1):
    tile = next(t for t, by in ((64, 192), (96, 96), (48, 48), (32, 32)) if total % by == 0)
    turns = total // tile

    def step(i, kept):
        return run(pl.ds(pl.multiple_of(first + i * tile, 16), tile), kept)

    return lax.fori_loop(0, turns, step, carry, unroll=unroll)


def norm_back_tile(values, gain, grads):
    unit, scale = norm_parts(values)
    inner = grads * gain
    mean_one = jnp.mean(inner, axis=-1, keepdims=True)
    mean_two = jnp.mean(inner * unit, axis=-1, keepdims=True)
    return ((inner - mean_one - unit * mean_two) * scale, fold_rows(grads * unit), fold_rows(grads))


def gelu_both(v):
    rate = 0.7978845608028654
    square = v * v
    bend = jnp.tanh(rate * (v + 0.044715 * (square * v)))
    lifted = 0.5 * (1.0 + bend)
    slope = lifted + 0.5 * v * (1.0 - bend * bend) * (rate * (1.0 + 3.0 * 0.044715 * square))
    return (v * lifted, slope)


def low_lanes_of(count):
    return lax.broadcasted_iota(jnp.int32, (count, LANES), 1) < HDIM


def stack_all(block, low):
    wide = block.astype(F32)
    return jnp.concatenate([jnp.where(low, wide, 0.0), jnp.where(low, 0.0, wide)], axis=0)


def merge_all(both, low):
    count = both.shape[0] // 2
    return jnp.where(low, both[:count], both[count:])


def lane_block(index):
    return pl.ds(pl.multiple_of(index * LANES, LANES), LANES)


def scores_of(keys, queries, mask):
    scores = dot_rows(keys, queries)
    if mask is None:
        return scores
    block = mask[...]
    return scores + jnp.concatenate([block, block], axis=1)


def forward_heads(queries, keys, vals, mask, low):
    scores = scores_of(keys, queries, mask)
    top = jnp.max(scores, axis=0, keepdims=True)
    grown = jnp.exp(scores - top)
    total = jnp.sum(grown, axis=0, keepdims=True)
    weights = (grown * (1.0 / total)).astype(BF16)
    return (merge_all(dot_first(weights, vals), low), top + jnp.log(total))


def backward_heads(queries, keys, vals, grads, tops, mask, low, scale):
    weights = jnp.exp(scores_of(keys, queries, mask) - tops)
    grad_w = dot_rows(vals, grads)
    row_dot = jnp.sum(weights * grad_w, axis=0, keepdims=True)
    grad_s = (weights * (grad_w - row_dot)).astype(BF16)
    grad_q = merge_all(dot_first(keys, grad_s).T, low) * scale
    return (grad_q, dot_plain(grad_s, queries), dot_plain(weights.astype(BF16), grads))


def fill_mask(mask, col, row, is_dec):
    count = mask.shape[0]

    def tile(rows, kept):
        shape = (rows.size, count)
        key_at = lax.broadcasted_iota(jnp.int32, shape, 0) + rows.start
        query_at = lax.broadcasted_iota(jnp.int32, shape, 1)
        allowed = jnp.logical_and(key_at <= query_at, col[rows, 0:1] == row[0:1, :])
        mask[rows, :] = jnp.where(jnp.logical_or(allowed, jnp.logical_not(is_dec)), 0.0, NEG)
        return kept

    row_tiles(count, tile, 0)


def self_forward(packed, mask, out, tops, pairs, scale):
    low = low_lanes_of(packed.shape[0])

    @pl.loop(0, pairs)
    def _(pair):
        queries = (stack_all(packed[:, lane_block(pair)], low) * scale).astype(BF16)
        mixed, top = forward_heads(
            queries, packed[:, lane_block(pairs + pair)], packed[:, lane_block(2 * pairs + pair)], mask, low
        )
        out[:, lane_block(pair)] = mixed.astype(BF16)
        tops[pair, 0:1, :] = top


def self_backward(packed, grads, tops, mask, out, pairs, scale, between):
    low = low_lanes_of(packed.shape[0])

    @pl.loop(0, pairs)
    def _(pair):
        queries = (stack_all(packed[:, lane_block(pair)], low) * scale).astype(BF16)
        head_grads = stack_all(grads[:, lane_block(pair)], low).astype(BF16)
        grad_q, grad_k, grad_v = backward_heads(
            queries,
            packed[:, lane_block(pairs + pair)],
            packed[:, lane_block(2 * pairs + pair)],
            head_grads,
            tops[pair, 0:1, :],
            mask,
            low,
            scale,
        )
        out[:, lane_block(pair)] = grad_q.astype(BF16)
        out[:, lane_block(pairs + pair)] = grad_k.astype(BF16)
        out[:, lane_block(2 * pairs + pair)] = grad_v.astype(BF16)
        pl.when(pair == 1)(between)


def cross_forward(image, query, keys, vals, picks, out, tops, pairs, scale):
    low = low_lanes_of(query.shape[0])

    @pl.loop(0, pairs)
    def _(pair):
        cols = lane_block(pair)
        queries = (stack_all(query[:, cols], low) * scale).astype(BF16)
        mixed, top = forward_heads(queries, keys[image, :, cols], vals[image, :, cols], None, low)
        kept = jnp.where(picks[...] == image, mixed, out[:, cols].astype(F32))
        out[:, cols] = kept.astype(BF16)
        tops[image, pair, 0:1, :] = top


def cross_backward(query, keys, vals, grads, picks, tops, dq, dk, dv, sum_q, pairs, scale):
    low = low_lanes_of(query.shape[0])

    @pl.loop(0, pairs)
    def _(pair):
        cols = lane_block(pair)
        queries = (stack_all(query[:, cols], low) * scale).astype(BF16)
        sum_q[...] = jnp.zeros_like(sum_q)

        @pl.loop(0, 2)
        def _(image):
            own = jnp.where(picks[...] == image, grads[:, cols].astype(F32), 0.0)
            grad_q, grad_k, grad_v = backward_heads(
                queries,
                keys[image, :, cols],
                vals[image, :, cols],
                stack_all(own, low).astype(BF16),
                tops[image, pair, 0:1, :],
                None,
                low,
                scale,
            )
            sum_q[...] += grad_q
            dk[image, :, cols] = grad_k.astype(BF16)
            dv[image, :, cols] = grad_v.astype(BF16)

        dq[:, cols] = sum_q[...].astype(BF16)


class Reducer:
    def __init__(self, grads, near, far, outs, sems, window, first, last, near_last):
        self.grads, self.near, self.far, self.outs = grads, near, far, outs
        self.y_send, self.y_recv, self.z_send, self.z_recv, self.c_send, self.c_recv = sems
        self.tower, self.dp, self.z, self.core, self.line, self.other, self.partner = spots()
        self.place = self.z + self.core * (3 - 2 * self.z)
        self.holder = self.place <= 1
        self.slot = lax.rem(self.z, 2)
        self.half = grads.shape[3] // 2
        self.rows = grads.shape[2]
        self.window, self.first, self.last, self.near_last = window, first, last, near_last

    def lanes(self, line):
        return pl.ds(pl.multiple_of(line * self.half, LANES), self.half)

    def to_line(self, k):
        return pltpu.make_async_remote_copy(
            src_ref=self.grads.at[k, :, :, self.lanes(1 - self.line)],
            dst_ref=self.near.at[k],
            send_sem=self.y_send.at[k],
            recv_sem=self.y_recv.at[k],
            device_id={DP: self.other},
            device_id_type=MESH,
        )

    def send(self, source, target, k, sent, got, where):
        return pltpu.make_async_remote_copy(
            src_ref=source,
            dst_ref=target,
            send_sem=self.z_send.at[k, sent],
            recv_sem=self.z_recv.at[k, got],
            device_id={MP: where},
            device_id_type=MESH,
        )

    def inward(self, k):
        return self.send(self.near.at[k], self.far.at[k], k, 0, 0, 2 - self.core)

    def beside(self, k):
        return self.send(self.near.at[k, 1 - self.slot], self.far.at[k, 0], k, 0, 0, 4 * self.core + 1 - self.z)

    def onward(self, k, shard):
        return self.send(self.near.at[k, shard], self.far.at[k, 1], k, shard, 1, 2 * self.core + shard)

    def to_core(self, k):
        return pltpu.make_async_remote_copy(
            src_ref=self.outs.at[k],
            dst_ref=self.outs.at[k],
            send_sem=self.c_send.at[k],
            recv_sem=self.c_recv.at[k],
            device_id={DP: self.partner},
            device_id_type=MESH,
        )

    def launch(self, k):
        self.to_line(k).start()

    def tiles(self, run):
        @pl.loop(0, self.rows // TILE)
        def _(i):
            run(pl.ds(pl.multiple_of(i * TILE, TILE), TILE))

    def add_near(self, k, more=True):
        self.to_line(k).wait_send()
        self.to_line(k).wait_recv()
        if more:
            pl.when(k + self.window < self.near_last)(lambda: self.launch(k + self.window))

        def run(rows):
            for b in range(2):
                total = self.grads[k, b, rows, self.lanes(self.line)].astype(F32) + self.near[k, b, rows, :].astype(F32)
                self.near[k, b, rows, :] = total.astype(BF16)

        self.tiles(run)
        if more:
            pl.when(k < self.last)(lambda: self.hop(k))

    def hop(self, k):
        pl.when(self.place == 3)(self.inward(k).start)
        pl.when(self.holder)(self.beside(k).start)

    def add_mid(self, k):
        @pl.when(self.place == 2)
        def _():
            self.inward(k).wait_recv()

            def run(rows):
                for b in range(2):
                    total = self.near[k, b, rows, :].astype(F32) + self.far[k, b, rows, :].astype(F32)
                    self.near[k, b, rows, :] = total.astype(BF16)

            self.tiles(run)
            for shard in range(2):
                self.onward(k, shard).start()

    def add_far(self, k):
        @pl.when(self.holder)
        def _():
            self.beside(k).wait_recv()
            self.onward(k, 0).wait_recv()

            def run(rows):
                total = self.near[k, self.slot, rows, :].astype(F32)
                for seat in range(2):
                    total = total + self.far[k, seat, rows, :].astype(F32)
                self.outs[k, rows, :] = total.astype(BF16)

            self.tiles(run)
            self.to_core(k).start()

    def step(self, k, mid=1):
        self.add_near(k)
        if mid:
            pl.when(k - LAG >= self.first)(lambda: self.add_mid(k - LAG))

    def drain(self, begin):
        @pl.loop(begin, max(self.near_last, self.last + 2 * LAG))
        def _(i):
            pl.when(i < self.near_last)(lambda: self.add_near(i))
            j = i - LAG
            pl.when(jnp.logical_and(j >= self.first, j < self.last))(lambda: self.add_mid(j))
            n = j - LAG
            pl.when(jnp.logical_and(n < self.last, n >= self.first))(lambda: self.add_far(n))

    def far_before(self, begin):
        @pl.loop(self.first, jnp.maximum(self.first, begin - 2 * LAG))
        def _(k):
            self.add_far(k)

    def close(self, got):
        @pl.loop(self.first, self.last)
        def _(k):
            pl.when(self.place == 3)(self.inward(k).wait_send)

            @pl.when(self.place == 2)
            def _():
                for shard in range(2):
                    self.onward(k, shard).wait_send()

            @pl.when(self.holder)
            def _():
                self.beside(k).wait_send()
                self.to_core(k).wait_send()

            @pl.when(jnp.logical_and(jnp.logical_not(self.holder), k >= got))
            def _():
                self.to_core(k).wait_recv()


class Tail(NamedTuple):
    seg_col: Any
    seg_row: Any
    d_three: Any
    base: Any
    upstream: Any
    gains: Any
    smalls: Any
    hid: Any
    w_mlp: Any
    pre: Any
    act: Any
    w_in: Any
    x1: Any
    w_out: Any
    mixed: Any
    packed: Any
    tops: Any
    a_one: Any
    w_qkv: Any
    x0: Any


IMAGE_ONLY = Tail._fields[7:13]


def tail_kernel(pairs, scale, *refs):
    it = iter(refs)
    hbm = Tail(*[next(it) for _ in Tail._fields])
    cross_in, tower_rows = next(it), next(it)
    outs = next(it)
    small_out, grad_out, from_text, tower_out = next(it), next(it), next(it), next(it)
    vm = Tail(*[next(it) for _ in Tail._fields])
    grads, near, far = next(it), next(it), next(it)
    g_f32, g_low, grad_hid, grad_pre, d_packed, mix_grad = (next(it) for _ in range(6))
    part_send, part_recv, mask, smalls, small_near, small_all, own_grad = (next(it) for _ in range(7))
    load_sem, red_sems, part_sem, small_sem, move_sem, twin_sem = next(it), [next(it) for _ in range(6)], next(it), next(it), next(it), next(it)
    tower, dp, z, core, line, other, partner = spots()
    is_enc = tower == 0
    is_dec = tower == 1
    stays = z == 3 * core
    tokens, width = g_f32.shape
    rows_txt = tokens // LTXT
    quarter = tokens // 2
    heads = mix_grad.shape[1]
    rows_of = grads.shape[2]
    ffn_blocks = width // rows_of
    text_first = 2 * ffn_blocks - 2

    home = {DP: 2 * line + z // 2, MP: 2 * lax.rem(z, 2) + core}
    guest = {DP: 2 * line + lax.rem(z, 2), MP: 2 * core + z // 2}
    moved = jnp.logical_not(stays)
    peers = [(None, {DP: other}), (None, {DP: partner}), (is_enc, {TOWER: 1 - tower})]
    peers += [(None, {MP: lax.rem(z + away, 4)}) for away in range(1, 4)]
    peers += [(moved, home), (moved, guest)]
    def load(i):
        return pltpu.make_async_copy(hbm[i], vm[i], load_sem.at[i])

    def on_side(i, run):
        if Tail._fields[i] in IMAGE_ONLY:
            pl.when(is_enc)(run)
        else:
            run()

    pl.when(is_dec)(lambda: pltpu.make_async_copy(cross_in, near.at[pl.ds(text_first, 2)], load_sem.at[len(hbm)]).start())
    for i in range(len(hbm)):
        on_side(i, load(i).start)

    barrier_all(
        peers,
        [
            (jnp.logical_and(is_enc, stays), 5),
            (jnp.logical_and(is_enc, moved), 7),
            (jnp.logical_and(is_dec, stays), 6),
            (jnp.logical_and(is_dec, moved), 8),
        ],
    )

    def need(*wanted):
        for i, ref in enumerate(vm):
            if any(ref is one for one in wanted):
                on_side(i, load(i).wait)

    first_block = text_first * tower
    blocks = grads.shape[0]
    red = Reducer(grads, near, far, outs, red_sems, 2 + 2 * tower, first_block, blocks, blocks)

    def twin_copy():
        return pltpu.make_async_remote_copy(
            src_ref=outs.at[pl.ds(text_first, 2)],
            dst_ref=from_text,
            send_sem=twin_sem.at[0],
            recv_sem=twin_sem.at[1],
            device_id={TOWER: 1 - tower},
            device_id_type=MESH,
        )

    cross_load = pltpu.make_async_copy(cross_in, near.at[pl.ds(text_first, 2)], load_sem.at[len(hbm)])

    @pl.when(is_dec)
    def _():
        cross_load.wait()
        red.hop(text_first)
        red.hop(text_first + 1)

    def home_move(source, target, k):
        return pltpu.make_async_remote_copy(
            src_ref=source,
            dst_ref=target,
            send_sem=move_sem.at[k, 0],
            recv_sem=move_sem.at[k, 1],
            device_id=home,
            device_id_type=MESH,
        )

    @pl.when(moved)
    def _():
        home_move(tower_rows, tower_out, 0).start()

    @pl.when(stays)
    def _():
        pltpu.make_async_copy(tower_rows, own_grad, move_sem.at[0, 0]).start()
        pltpu.make_async_copy(tower_rows, own_grad, move_sem.at[0, 0]).wait()
        pltpu.make_async_copy(own_grad, tower_out, move_sem.at[0, 1]).start()
        pltpu.make_async_copy(own_grad, tower_out, move_sem.at[0, 1]).wait()

    def part_copy(k):
        return pltpu.make_async_remote_copy(
            src_ref=part_send.at[k],
            dst_ref=part_recv.at[k],
            send_sem=part_sem.at[k, 0],
            recv_sem=part_sem.at[k, 1],
            device_id={DP: partner},
            device_id_type=MESH,
        )

    zero = jnp.zeros((8, width), F32)
    need(vm.seg_col, vm.seg_row)
    fill_mask(mask, vm.seg_col, vm.seg_row, is_dec)
    need(vm.d_three, vm.base, vm.upstream, vm.gains, vm.smalls)
    smalls[...] = vm.smalls[...]

    def put(row, value):
        smalls[pl.ds(row, 1), :] = jnp.sum(value, axis=0, keepdims=True)

    def third(rows, kept):
        back, dg, db = norm_back_tile(vm.base[rows, :], vm.gains[2], vm.d_three[rows, :])
        total = vm.upstream[rows, :] + back
        g_f32[rows, :] = total
        low = total.astype(BF16)
        g_low[rows, :] = low
        return (kept[0] + dg, kept[1] + db, kept[2] + fold_rows(low.astype(F32)))

    dg, db, bias = row_tiles(tokens, third, (zero, zero, zero), 0, 3)
    put(4, dg)
    put(7, db)

    @pl.when(is_enc)
    def _():
        put(1, bias)
        need(vm.hid)

        @pl.loop(0, 2)
        def _(b):
            made = dot_first(vm.hid[:, pl.ds(pl.multiple_of(b * width, LANES), width)], g_low[...]).astype(BF16)
            grads[0:ffn_blocks, b] = made.reshape(ffn_blocks, rows_of, width)

        red.launch(0)
        need(vm.w_mlp, vm.pre)

        @pl.loop(0, 2)
        def _(b):
            cols = pl.ds(pl.multiple_of(b * width, LANES), width)
            grad_hid[...] = dot_rows(g_low[...], vm.w_mlp[cols, :])

            def bend(rows, kept):
                low = (grad_hid[rows, :] * gelu_both(vm.pre[rows, cols])[1]).astype(BF16)
                grad_pre[b, rows, :] = low
                return kept + fold_rows(low.astype(F32))

            put(9 + b, row_tiles(tokens, bend, zero))

        red.launch(1)
        need(vm.act, vm.w_in)

        @pl.loop(0, 2)
        def _(b):
            made = dot_first(grad_pre[b], vm.act[...]).astype(BF16)
            grads[ffn_blocks : 2 * ffn_blocks, b] = made.reshape(ffn_blocks, rows_of, width)

        red.step(0)
        grad_hid[...] = jnp.zeros_like(grad_hid)

        @pl.loop(0, 2)
        def _(b):
            grad_hid[...] += dot_rows(grad_pre[b], vm.w_in[b])

        def lower(rows, kept):
            part_send[0, rows, :] = grad_hid[rows, :].astype(BF16)
            return kept

        row_tiles(tokens, lower, 0)
        part_copy(0).start()
        need(vm.x1)
        part_copy(0).wait()

        def second(rows, kept):
            grad = part_send[0, rows, :].astype(F32) + part_recv[0, rows, :].astype(F32)
            back, dg, db = norm_back_tile(vm.x1[rows, :], vm.gains[1], grad)
            total = g_f32[rows, :] + back
            g_f32[rows, :] = total
            low = total.astype(BF16)
            g_low[rows, :] = low
            return (kept[0] + dg, kept[1] + db, kept[2] + fold_rows(low.astype(F32)))

        dg, db, bias_two = row_tiles(tokens, second, (zero, zero, zero), 0, 3)
        put(3, dg)
        put(6, db)
        put(0, bias_two)
        red.step(1)

    @pl.when(is_dec)
    def _():
        put(0, bias)

    need(vm.w_out, vm.mixed, vm.packed, vm.tops)
    mix_grad[...] = dot_rows(g_low[...], vm.w_out[...]).astype(BF16)
    grads[2 * ffn_blocks] = dot_first(vm.mixed[...], g_low[...]).astype(BF16).reshape(grads.shape[1:])


    @pl.when(is_enc)
    def _():
        red.step(2)

    @pl.when(is_dec)
    def _():
        red.launch(2 * ffn_blocks)

    def between():
        @pl.when(is_enc)
        def _():
            red.step(3)

    self_backward(vm.packed, mix_grad, vm.tops, mask, d_packed, pairs, scale, between)


    @pl.when(is_enc)
    def _():
        red.step(4)

    @pl.when(is_dec)
    def _():
        red.add_mid(text_first)

    now = 5 + (2 * ffn_blocks - 5) * tower


    need(vm.a_one, vm.w_qkv, vm.x0)

    @pl.loop(0, 3)
    def _(a):
        cols = pl.ds(pl.multiple_of(a * heads, LANES), heads)
        made = dot_first(d_packed[:, cols], vm.a_one[...]).astype(BF16)
        grads[2 * ffn_blocks + 1 + a] = made.reshape(grads.shape[1:])
        pl.when(is_dec)(lambda: red.launch(2 * ffn_blocks + 1 + a))

    red.step(now)
    grad_hid[...] = jnp.zeros_like(grad_hid)

    @pl.loop(0, 3)
    def _(a):
        cols = pl.ds(pl.multiple_of(a * heads, LANES), heads)
        grad_hid[...] += dot_plain(d_packed[:, cols], vm.w_qkv[cols, :])


    def lower_two(rows, kept):
        part_send[1, rows, :] = grad_hid[rows, :].astype(BF16)
        return (
            kept[0] + fold_rows(d_packed[rows, pl.ds(0, heads)].astype(F32)),
            kept[1] + fold_rows(d_packed[rows, pl.ds(2 * heads, heads)].astype(F32)),
        )

    small_zero = jnp.zeros((8, heads), F32)
    q_sum, v_sum = row_tiles(tokens, lower_two, (small_zero, small_zero))
    part_copy(1).start()
    pl.when(is_enc)(lambda: red.step(now + 1))
    smalls[8:9, :] = jnp.concatenate(
        [jnp.sum(q_sum, axis=0, keepdims=True), jnp.sum(v_sum, axis=0, keepdims=True)], axis=1
    )
    part_copy(1).wait()

    def first(rows, kept):
        grad = part_send[1, rows, :].astype(F32) + part_recv[1, rows, :].astype(F32)
        back, dg, db = norm_back_tile(vm.x0[rows, :].astype(F32), vm.gains[0], grad)
        part_send[1, rows, :] = (g_f32[rows, :] + back).astype(BF16)
        return (kept[0] + dg, kept[1] + db)

    dg, db = row_tiles(tokens, first, (zero, zero), 0, 3)
    put(2, dg)
    put(5, db)
    mine = pl.ds(pl.multiple_of(core * quarter, TILE), quarter)

    def own_copy(rows, kept):
        shifted = pl.ds(pl.multiple_of(core * quarter + rows.start, 32), rows.size)
        own_grad[rows, :] = part_send[1, shifted, :]
        return kept

    row_tiles(quarter, own_copy, 0)

    small_line = pltpu.make_async_remote_copy(
        src_ref=smalls,
        dst_ref=small_near,
        send_sem=small_sem.at[0],
        recv_sem=small_sem.at[1],
        device_id={DP: other},
        device_id_type=MESH,
    )
    small_line.start()

    @pl.when(moved)
    def _():
        home_move(own_grad, grad_out, 1).start()

    @pl.when(stays)
    def _():
        pltpu.make_async_copy(own_grad, grad_out, move_sem.at[1, 0]).start()


    def small_pair(sender, away):
        return pltpu.make_async_remote_copy(
            src_ref=small_all.at[sender],
            dst_ref=small_all.at[sender],
            send_sem=small_sem.at[1 + away],
            recv_sem=small_sem.at[4 + away],
            device_id={MP: lax.rem(z + away, 4)},
            device_id_type=MESH,
        )

    def small_core(which):
        return pltpu.make_async_remote_copy(
            src_ref=small_out.at[which],
            dst_ref=small_out.at[which],
            send_sem=small_sem.at[8],
            recv_sem=small_sem.at[9],
            device_id={DP: partner},
            device_id_type=MESH,
        )

    after = now + 2 - tower
    red.step(after)
    small_line.wait()
    small_all[z] = smalls[...] + small_near[...]


    for away in range(1, 4):
        small_pair(z, away).start()

    red.step(after + 1)
    for away in range(1, 4):
        small_pair(lax.rem(z + 4 - away, 4), away).wait_recv()
    small_out[core] = ((small_all[0] + small_all[1]) + small_all[2]) + small_all[3]
    small_core(core).start()
    red.far_before(after + 2)

    @pl.when(is_dec)
    def _():
        @pl.when(jnp.logical_not(red.holder))
        def _():
            for k in range(2):
                red.to_core(text_first + k).wait_recv()

        twin_copy().start()

    red.drain(after + 2)
    red.close((text_first + 2) * tower)

    for away in range(1, 4):
        small_pair(z, away).wait_send()

    @pl.when(moved)
    def _():
        home_move(tower_rows, tower_out, 0).wait()
        home_move(own_grad, grad_out, 1).wait()

    @pl.when(stays)
    def _():
        pltpu.make_async_copy(own_grad, grad_out, move_sem.at[1, 0]).wait()

    pl.when(is_dec)(twin_copy().wait_send)
    pl.when(is_enc)(twin_copy().wait_recv)
    small_core(core).wait_send()
    small_core(1 - core).wait_recv()


def tail(values, cross_grad, tower_rows, scale):
    tokens, width = values.base.shape
    heads = values.mixed.shape[1]
    pairs = heads // LANES
    hidden = values.pre.shape[1]
    quarter = tokens // 2
    half = width // 2
    rows_of = heads // 2
    blocks = 2 * (width // rows_of) + 4
    assert hidden == 2 * width and cross_grad.shape[0] == 2
    hbm = pl.BlockSpec(memory_space=pltpu.HBM)
    vmem = pl.BlockSpec(memory_space=pltpu.VMEM)
    n_in = len(values)
    scratch = [pltpu.VMEM(x.shape, x.dtype) for x in values]
    scratch += [pltpu.VMEM((blocks, 2, rows_of, width), BF16)]
    scratch += [pltpu.VMEM((blocks, 2, rows_of, half), BF16)] * 2
    scratch += [
        pltpu.VMEM((tokens, width), F32),
        pltpu.VMEM((tokens, width), BF16),
        pltpu.VMEM((tokens, width), F32),
        pltpu.VMEM((2, tokens, hidden // 2), BF16),
        pltpu.VMEM((tokens, 3 * heads), BF16),
        pltpu.VMEM((tokens, heads), BF16),
        pltpu.VMEM((2, tokens, width), BF16),
        pltpu.VMEM((2, tokens, width), BF16),
        pltpu.VMEM((tokens, tokens), F32),
        pltpu.VMEM(values.smalls.shape, F32),
        pltpu.VMEM(values.smalls.shape, F32),
        pltpu.VMEM((4,) + values.smalls.shape, F32),
        pltpu.VMEM((quarter, width), BF16),
    ]
    dma = pltpu.SemaphoreType.DMA
    scratch += [dma((n_in + 1,)), dma((blocks,)), dma((blocks,)), dma((blocks, 2)), dma((blocks, 2)), dma((blocks,)), dma((blocks,))]
    scratch += [dma((2, 2)), dma((10,)), dma((2, 2)), dma((2,))]
    out_shape = [jax.ShapeDtypeStruct((blocks, rows_of, half), BF16)]
    out_shape += [
        jax.ShapeDtypeStruct((2,) + values.smalls.shape, F32),
        jax.ShapeDtypeStruct((quarter, width), BF16),
        jax.ShapeDtypeStruct((2, heads // 2, half), BF16),
        jax.ShapeDtypeStruct((quarter, width), BF16),
    ]
    return pl.pallas_call(
        functools.partial(tail_kernel, pairs, scale),
        in_specs=[hbm] * (n_in + 2),
        out_specs=[vmem] * 2 + [hbm] * 3,
        out_shape=out_shape,
        scratch_shapes=scratch,
        compiler_params=pltpu.CompilerParams(
            collective_id=1, has_side_effects=True, vmem_limit_bytes=TAIL_LIMIT
        ),
        name="tail",
    )(*values, cross_grad, tower_rows)


class Head(NamedTuple):
    packed: Any
    mixed: Any
    tops: Any
    a_one: Any
    x1: Any
    base: Any
    act_three: Any
    act: Any
    pre: Any
    hid: Any
    query: Any


def head_kernel(pieces, pairs, scale, *refs):
    it = iter(refs)
    srcs = [next(it) for _ in range(5)]
    blocks = [next(it)]
    seg_ref, image_ref = next(it), next(it)
    gains, shifts, out_b, ffn_out_b, ffn_in_b, qv_b = (next(it) for _ in range(6))
    outs = [next(it) for _ in range(5)]
    tokens = [next(it)]
    seg_out = [next(it) for _ in range(3)]
    hbm = Head(*[next(it) for _ in Head._fields])
    stages = [next(it) for _ in range(5)]
    weight_sems = [next(it) for _ in range(5)]
    token_stage = next(it)
    token_sems = [next(it) for _ in range(3)]
    w_qkv, w_out, w_q, w_in, w_mlp = (next(it) for _ in range(5))
    vm = Head(*[next(it) for _ in Head._fields])
    part_send, part_recv, raw, mask = next(it), next(it), next(it), next(it)
    seg_sem, load_sem, store_sem, part_sem = (next(it) for _ in range(4))
    tower, dp, z, core, line, other, partner = spots()
    is_enc = tower == 0
    is_dec = tower == 1
    stays = z == 3 * core
    moved = jnp.logical_not(stays)
    count, width = vm.x1.shape
    rows_txt = count // LTXT
    heads = vm.mixed.shape[1]
    at_end = jnp.logical_or(z == 0, z == 3)

    peers = [(z > 0, {MP: z - 1}), (z < 3, {MP: z + 1})]
    peers += [(None, {DP: other}), (None, {TOWER: 1 - tower}), (None, {DP: partner})]
    peers += [
        (moved, {DP: 2 * line + lax.rem(z, 2), MP: 2 * core + z // 2}),
        (moved, {DP: 2 * line + z // 2, MP: 2 * lax.rem(z, 2) + core}),
    ]
    barrier_all(
        peers,
        [(stays, 4), (jnp.logical_and(at_end, moved), 6), (jnp.logical_not(at_end), 7)],
    )

    begin, begin_local, pass_on, arrived, sent, end_local, end_twin = weight_steps(
        pieces, srcs, outs, stages, weight_sems, 1
    )
    token_begin, token_relay, token_finish = token_steps(blocks, tokens, token_stage, token_sems)
    token_begin(0)
    begin()

    has_notes = core == z // 2

    def note_send(i):
        return pltpu.make_async_remote_copy(
            src_ref=seg_out[i],
            dst_ref=seg_out[i],
            send_sem=seg_sem.at[i, 0],
            recv_sem=seg_sem.at[i, 1],
            device_id={DP: partner},
            device_id_type=MESH,
        )

    @pl.when(has_notes)
    def _():
        rows = seg_ref.shape[0] // 2
        side = lax.rem(z, 2)
        segs = jnp.where(side == 0, seg_ref[0:rows, :], seg_ref[rows : 2 * rows, :])
        marks = segs + LTXT * lax.broadcasted_iota(jnp.int32, segs.shape, 0)
        tall = jnp.concatenate([marks.astype(F32), jnp.zeros((16 - rows, LTXT), F32)], axis=0).T
        seg_out[1][...] = jnp.zeros_like(seg_out[1])
        for r in range(rows):
            at = pl.ds(r * LTXT, LTXT)
            seg_out[0][at, :] = jnp.broadcast_to(tall[:, r : r + 1], (LTXT, LANES)).astype(jnp.int32)
            seg_out[1][0:1, at] = marks[r : r + 1, :]
            seg_out[2][at, :] = jnp.full((LTXT, LANES), image_ref[side * rows + r], jnp.int32)
        for i in range(3):
            note_send(i).start()

    begin_local()
    token_relay(0)

    def load(i, target, source):
        return pltpu.make_async_copy(source, target, load_sem.at[i])

    def store(ref):
        i = [x is ref for x in vm].index(True)
        return pltpu.make_async_copy(vm[i], hbm[i], store_sem.at[i])

    def part_copy(k):
        return pltpu.make_async_remote_copy(
            src_ref=part_send.at[k],
            dst_ref=part_recv.at[k],
            send_sem=part_sem.at[k, 0],
            recv_sem=part_sem.at[k, 1],
            device_id={DP: partner},
            device_id_type=MESH,
        )

    def last_copy(i):
        rows = pl.ds(pl.multiple_of(i * (count // 2), 32), count // 2)
        return pltpu.make_async_remote_copy(
            src_ref=part_send.at[1, rows, :],
            dst_ref=part_recv.at[1, rows, :],
            send_sem=part_sem.at[1 + i, 0],
            recv_sem=part_sem.at[1 + i, 1],
            device_id={DP: partner},
            device_id_type=MESH,
        )

    def normed(source, target, which):
        gain, shift = gains[which], shifts[which]

        def tile(rows, kept):
            unit, _ = norm_parts(source[rows, :].astype(F32))
            target[rows, :] = (unit * gain + shift).astype(BF16)
            return kept

        row_tiles(count, tile, 0, 0, 3)

    def chosen(which, flag, far=False):
        return [k for k, p in enumerate(pieces) if p[0] == which and p[6] == flag and p[7] == far]

    enc_in, enc_mlp, dec_in = chosen(3, 0), chosen(4, 0), chosen(3, 1) + chosen(4, 1)
    k_qkv, k_out, k_own, k_far = chosen(0, None), chosen(1, None), chosen(2, 1), chosen(2, 1, True)
    waiting = {0: enc_in + enc_mlp, 1: k_own + k_far + dec_in}

    def relay(enc=0, dec=0):
        for t, count in ((0, enc), (1, dec)):
            for k in waiting[t][:count]:
                pass_on(k)
            waiting[t] = waiting[t][count:]

    token_finish(0)
    normed(tokens[0], vm.a_one, 0)
    store(vm.a_one).start()
    for k in k_qkv + k_out:
        pass_on(k)
    for k in k_qkv:
        arrived(k)
    end_local(0)
    load(0, w_qkv, outs[0]).start()
    load(0, w_qkv, outs[0]).wait()

    @pl.loop(0, 3)
    def _(part):
        cols = pl.ds(pl.multiple_of(part * heads, LANES), heads)
        own = pl.ds(pl.multiple_of(core * heads, LANES), heads)
        bias = jnp.where(part == 1, 0.0, qv_b[pl.ds(part // 2, 1), own])
        made = dot_rows(vm.a_one[...], w_qkv[part].reshape(heads, width)) + bias
        vm.packed[:, cols] = made.astype(BF16)

    store(vm.packed).start()

    @pl.when(has_notes)
    def _():
        for i in range(3):
            note_send(i).wait_send()

    @pl.when(jnp.logical_not(has_notes))
    def _():
        for i in range(3):
            note_send(i).wait_recv()

    relay(1, 1)
    fill_mask(mask, seg_out[0], seg_out[1], is_dec)
    self_forward(vm.packed, mask, vm.mixed, vm.tops, pairs, scale)
    store(vm.mixed).start()
    store(vm.tops).start()
    for k in k_out:
        arrived(k)
    end_local(1)
    load(1, w_out, outs[1]).start()
    relay(1, 1)
    load(1, w_out, outs[1]).wait()
    part_send[0] = dot_plain(vm.mixed[...], w_out[0].reshape(heads, width)).astype(BF16)
    part_copy(0).start()
    relay(1, 1)
    part_copy(0).wait()

    def add_one(rows, kept):
        total = part_send[0, rows, :].astype(F32) + part_recv[0, rows, :].astype(F32)
        vm.x1[rows, :] = tokens[0][rows, :].astype(F32) + total + out_b[...]
        return kept

    row_tiles(count, add_one, 0)
    store(vm.x1).start()

    @pl.when(is_enc)
    def _():
        relay(1)
        normed(vm.x1, vm.act, 1)
        store(vm.act).start()
        relay(1)
        for k in enc_in:
            arrived(k)
        end_local(3)
        load(3, w_in, outs[3]).start()
        load(3, w_in, outs[3]).wait()
        relay(1)

        @pl.loop(0, 2)
        def _(b):
            cols = pl.ds(pl.multiple_of(b * width, LANES), width)
            raw[...] = dot_plain(vm.act[...], w_in[0, b])
            bias = ffn_in_b[0:1, pl.ds(pl.multiple_of((2 * core + b) * width, LANES), width)]

            def bend(rows, kept):
                pre = raw[rows, :] + bias
                vm.pre[rows, cols] = pre
                vm.hid[rows, cols] = gelu_tanh(pre).astype(BF16)
                return kept

            row_tiles(count, bend, 0)

        relay(1)
        store(vm.pre).start()
        store(vm.hid).start()
        cut = width // 2
        raw[...] = jnp.zeros_like(raw)
        end_local(4)

        def half_load(i):
            rows = pl.ds(i * cut, cut)
            return load(4, w_mlp.at[:, :, rows, :], outs[4].at[:, :, rows, :])

        for k in enc_mlp[:2]:
            arrived(k)
        half_load(0).start()
        relay(len(waiting[0]))
        half_load(0).wait()

        @pl.loop(0, 2)
        def _(b):
            raw[...] += dot_plain(vm.hid[:, pl.ds(pl.multiple_of(b * width, LANES), cut)], w_mlp[0, b, 0:cut, :])

        for k in enc_mlp[2:]:
            arrived(k)
        half_load(1).start()
        half_load(1).wait()
        half = count // 2

        @pl.loop(0, 2)
        def _(i):
            rows = pl.ds(pl.multiple_of(i * half, 32), half)
            made = raw[rows, :]
            for b in range(2):
                made = made + dot_plain(vm.hid[rows, pl.ds(b * width + cut, cut)], w_mlp[0, b, cut:width, :])
            part_send[1, rows, :] = made.astype(BF16)
            last_copy(i).start()

        def add_two(rows, kept):
            total = part_send[1, rows, :].astype(F32) + part_recv[1, rows, :].astype(F32)
            value = vm.x1[rows, :] + total + ffn_out_b[...]
            vm.base[rows, :] = value
            unit, _ = norm_parts(value)
            vm.act_three[rows, :] = (unit * gains[2] + shifts[2]).astype(BF16)
            return kept

        @pl.loop(0, 2)
        def _(i):
            last_copy(i).wait()
            row_tiles(half, add_two, 0, i * half)


    @pl.when(is_dec)
    def _():
        def same(rows, kept):
            vm.base[rows, :] = vm.x1[rows, :]
            return kept

        row_tiles(count, same, 0)
        normed(vm.base, vm.act_three, 2)

    store(vm.act_three).start()
    store(vm.base).start()

    @pl.when(is_dec)
    def _():
        relay(0, 2)
        for k in k_own:
            arrived(k)
        end_local(2)
        load(2, w_q, outs[2].at[2]).start()
        load(2, w_q, outs[2].at[2]).wait()
        vm.query[...] = dot_rows(vm.act_three[...], w_q[...].reshape(heads, width)).astype(BF16)
        store(vm.query).start()
        relay(0, len(waiting[1]))
        for k in k_far + dec_in:
            arrived(k)
        end_local(3)
        end_local(4)

    for k in range(len(pieces)):
        sent(k)
    end_twin()
    for ref in vm:
        if ref is vm.act or ref is vm.pre or ref is vm.hid:
            pl.when(is_enc)(store(ref).wait)
        elif ref is vm.query:
            pl.when(is_dec)(store(ref).wait)
        else:
            store(ref).wait()


def head(shards, blocks, segment_ids, row_image, vecs, scale):
    qkv, out, cross, ffn_in, ffn_out = shards
    heads = 2 * out.shape[1]
    width = out.shape[2]
    pairs = heads // LANES
    count = 2 * blocks[0].shape[0]
    hidden = 2 * ffn_in.shape[2]

    def cuts(i, flag):
        blocks_of, rows, _ = shards[i].shape
        cut = rows if rows <= 192 else rows // 4
        return [(i, a, a, 1, at, cut, flag, False) for a in range(blocks_of) for at in range(0, rows, cut)]

    pieces = cuts(0, None) + cuts(1, None)
    rows = cross.shape[1]
    pieces += [(2, 2 + a, a, 1, 0, rows, 1, False) for a in range(2)] + [(2, a, a, 1, 0, rows, 1, True) for a in range(2)]
    pieces += cuts(3, 0) + cuts(4, 0) + cuts(3, 1) + cuts(4, 1)[:2]
    n = len(pieces)
    hbm = pl.BlockSpec(memory_space=pltpu.HBM)
    vmem = pl.BlockSpec(memory_space=pltpu.VMEM)
    struct = jax.ShapeDtypeStruct
    made = Head(
        packed=struct((count, 3 * heads), BF16),
        mixed=struct((count, heads), BF16),
        tops=struct((pairs, 8, 2 * count), F32),
        a_one=struct((count, width), BF16),
        x1=struct((count, width), F32),
        base=struct((count, width), F32),
        act_three=struct((count, width), BF16),
        act=struct((count, width), BF16),
        pre=struct((count, hidden), F32),
        hid=struct((count, hidden), BF16),
        query=struct((count, heads), BF16),
    )
    out_shape = [
        jax.ShapeDtypeStruct(((2 if i == 2 else 1) * x.shape[0], 2) + x.shape[1:], BF16) for i, x in enumerate(shards)
    ]
    out_shape += [jax.ShapeDtypeStruct((count, width), BF16)]
    out_shape += [struct((count, LANES), jnp.int32), struct((8, count), jnp.int32), struct((count, LANES), jnp.int32)]
    out_shape += list(made)
    dma = pltpu.SemaphoreType.DMA
    scratch = [pltpu.VMEM(x.shape, BF16) for x in shards]
    scratch += [dma((n, 5)), dma((n, 4)), dma((5, 2)), dma, dma]
    scratch += [pltpu.VMEM((1,) + blocks[0].shape, BF16), dma((1, 2)), dma((1, 2)), dma((1, 2))]
    scratch += [
        pltpu.VMEM((3, 2) + qkv.shape[1:], BF16),
        pltpu.VMEM((1, 2) + out.shape[1:], BF16),
        pltpu.VMEM((2,) + cross.shape[1:], BF16),
        pltpu.VMEM((1, 2) + ffn_in.shape[1:], BF16),
        pltpu.VMEM((1, 2) + ffn_out.shape[1:], BF16),
    ]
    scratch += [pltpu.VMEM(x.shape, x.dtype) for x in made]
    scratch += [
        pltpu.VMEM((2, count, width), BF16),
        pltpu.VMEM((2, count, width), BF16),
        pltpu.VMEM((count, width), F32),
        pltpu.VMEM((count, count), F32),
        dma((3, 2)),
        dma((5,)),
        dma((len(made),)),
        dma((3, 2)),
    ]
    results = pl.pallas_call(
        functools.partial(head_kernel, tuple(pieces), pairs, scale),
        in_specs=[hbm] * 6 + [vmem, pl.BlockSpec(memory_space=pltpu.SMEM)] + [vmem] * 6,
        out_specs=[hbm] * 5 + [vmem] + [vmem] * 3 + [hbm] * len(made),
        out_shape=out_shape,
        scratch_shapes=scratch,
        compiler_params=pltpu.CompilerParams(
            collective_id=0, has_side_effects=True, vmem_limit_bytes=VMEM_LIMIT
        ),
        name="head",
    )(*shards, *blocks, segment_ids, row_image, *vecs)
    return results[:5], results[5], results[6:9], Head(*results[9:])


CHUNKS = 6


def mid_kernel(pieces, pairs, scale, *refs):
    it = iter(refs)
    act_three, x1, query_in, w_cross_in, w_in_in, w_mlp_in, ffn_shard, cot_block, base = (next(it) for _ in range(9))
    gains, shifts, out_b, ffn_out_b, ffn_in_b, qv_b, picks = (next(it) for _ in range(7))
    d_three, upstream, smalls, tower_out, cross_out = (next(it) for _ in range(5))
    outs = next(it)
    stages = [next(it)]
    weight_sems = [next(it) for _ in range(5)]
    token_stage = next(it)
    token_sems = [next(it) for _ in range(3)]
    images, kv, w_cross, w_in, w_mlp = (next(it) for _ in range(5))
    act_txt, query, mixed, tops, y1, y2, act, pre, hid = (next(it) for _ in range(9))
    grad_hid, raw, grad_pre, g_low, mix_grad, dq, dkv, sum_q = (next(it) for _ in range(8))
    keys, vals, dk, dv = kv.at[0], kv.at[1], dkv.at[0], dkv.at[1]
    cot, part_send, part_recv, halves, half_near, sums, image_grad, own_rows = (next(it) for _ in range(8))
    grads, near, far = (next(it) for _ in range(3))
    red_sems = [next(it) for _ in range(6)]
    load_sem, store_sem, part_sem, twin_sem, side_sem, core_sem, half_sem, sum_sem, back_sem, give_sem, home_sem = it
    tower, dp, z, core, line, other, partner = spots()
    is_enc = tower == 0
    is_dec = tower == 1
    stays = z == 3 * core
    moved = jnp.logical_not(stays)
    side = lax.rem(z, 2)
    across_chip = z + 1 - 2 * side
    count, width = y1.shape
    quarter = count // 2
    chunk = quarter // CHUNKS
    heads = mixed.shape[1]

    home = {DP: 2 * line + z // 2, MP: 2 * lax.rem(z, 2) + core}
    guest = {DP: 2 * line + lax.rem(z, 2), MP: 2 * core + z // 2}
    peers = [(None, {DP: other}), (None, {DP: partner}), (None, {TOWER: 1 - tower})]
    peers += [(None, {MP: lax.rem(z + away, 4)}) for away in range(1, 4)]
    peers += [(moved, home), (moved, guest)]
    barrier_all(peers, [(stays, 6), (moved, 8)])

    def remote(source, target, sends, recvs, where):
        return pltpu.make_async_remote_copy(
            src_ref=source,
            dst_ref=target,
            send_sem=sends,
            recv_sem=recvs,
            device_id=where,
            device_id_type=MESH,
        )

    def span(which_core, i):
        return pl.ds(pl.multiple_of(which_core * quarter + i * chunk, 16), chunk)

    def twin_copy(i):
        rows = span(core, i)
        return remote(
            act_three.at[rows, :], images.at[side, rows, :], twin_sem.at[i, 0], twin_sem.at[i, 1], {TOWER: 1 - tower}
        )

    def side_copy(i, image):
        here = images.at[image, span(core, i), :]
        return remote(here, here, side_sem.at[i, 0], side_sem.at[i, 1], {MP: across_chip})

    def core_copy(i, image, which_core, far_image):
        here = images.at[image, span(which_core, i), :]
        return remote(here, here, core_sem.at[far_image, i, 0], core_sem.at[far_image, i, 1], {DP: partner})

    @pl.when(is_enc)
    def _():
        for i in range(CHUNKS):
            twin_copy(i).start()

    token_begin, token_relay, token_finish = token_steps([cot_block], [cot], token_stage, token_sems)
    pl.when(is_enc)(functools.partial(token_begin, 0))
    begin, begin_local, pass_on, arrived, sent, end_local, _ = weight_steps(
        pieces, [ffn_shard], [w_mlp], stages, weight_sems, 0
    )

    def load(i, source, target):
        return pltpu.make_async_copy(source, target, load_sem.at[i])

    held = pl.ds(0, ffn_shard.shape[1] // 2)
    early = [load(5, w_mlp_in.at[:, :, held, :], w_mlp.at[:, :, held, :])]
    text_loads = [
        load(0, w_cross_in, w_cross),
        load(1, query_in, query),
        load(2, x1, y1),
        load(3, w_in_in, w_in),
        load(4, act_three, act_txt),
    ]

    def part_copy(k, h):
        rows = pl.ds(pl.multiple_of(h * quarter, 32), quarter)
        return remote(
            part_send.at[k % 3, rows, :],
            part_recv.at[k % 3, rows, :],
            part_sem.at[k, h, 0],
            part_sem.at[k, h, 1],
            {DP: partner},
        )

    rows_copy = pltpu.make_async_copy(own_rows, tower_out, home_sem.at[0])

    def back_copy(i):
        rows = pl.ds(i * chunk, chunk)
        return remote(
            sums.at[1, rows, :], image_grad.at[span(core, i), :], back_sem.at[i, 0], back_sem.at[i, 1], {TOWER: 1 - tower}
        )

    def back_core(i, which_core):
        here = image_grad.at[span(which_core, i), :]
        return remote(here, here, give_sem.at[i, 0], give_sem.at[i, 1], {DP: partner})

    store_grad = pltpu.make_async_copy(y2, upstream, store_sem.at[0])
    store_three = pltpu.make_async_copy(raw, d_three, store_sem.at[1])
    zero = jnp.zeros((8, width), F32)
    blocks, rows_of = outs.shape[0], outs.shape[1]
    ffn_blocks = width // rows_of
    red = Reducer(grads, near, far, outs, red_sems, 4, 0, blocks, blocks + 2)

    @pl.when(is_enc)
    def _():
        smalls[...] = jnp.zeros_like(smalls)
        mine = pl.ds(pl.multiple_of(core * quarter, TILE), quarter)
        take = load(2, base.at[mine, :], y1.at[pl.ds(0, quarter), :])
        take.start()
        take.wait()

        def lower(rows, kept):
            own_rows[rows, :] = y1[rows, :].astype(BF16)
            return kept

        row_tiles(quarter, lower, 0)
        rows_copy.start()
        token_relay(0)
        token_finish(0)

        def lift(rows, kept):
            y2[rows, :] = cot[rows, :].astype(F32)
            return kept

        row_tiles(count, lift, 0)
        store_grad.start()
        for i in range(CHUNKS):
            back_copy(i).wait_recv()
            back_core(i, core).start()
        for i in range(CHUNKS):
            back_core(i, 1 - core).wait_recv()

        def lift_three(rows, kept):
            raw[rows, :] = image_grad[rows, :].astype(F32)
            return kept

        row_tiles(count, lift_three, 0)
        store_three.start()
        for i in range(CHUNKS):
            twin_copy(i).wait_send()
            back_core(i, core).wait_send()

    @pl.when(is_dec)
    def _():
        begin()
        for one in early + text_loads:
            one.start()
        for one in early:
            one.wait()
        begin_local()
        smalls[...] = jnp.zeros_like(smalls)

        def put(row, value):
            smalls[pl.ds(row, 1), :] = jnp.sum(value, axis=0, keepdims=True)

        for i in range(CHUNKS):
            twin_copy(i).wait_recv()
            side_copy(i, side).start()
            core_copy(i, side, core, 0).start()
        for k in range(len(pieces)):
            pass_on(k)
        for one in text_loads[:2]:
            one.wait()
        mixed[...] = jnp.zeros_like(mixed)
        for i in range(CHUNKS):
            core_copy(i, side, 1 - core, 0).wait_recv()

        @pl.loop(0, 2)
        def _(turn):
            image = side + turn * (1 - 2 * side)

            @pl.when(turn == 1)
            def _():
                for i in range(CHUNKS):
                    side_copy(i, 1 - side).wait_recv()
                    core_copy(i, 1 - side, core, 1).start()
                token_begin(0)
                for i in range(CHUNKS):
                    core_copy(i, 1 - side, 1 - core, 1).wait_recv()

            @pl.loop(0, 2)
            def _(part):
                kv[part, image] = dot_rows(images[image], w_cross[part].reshape(heads, width)).astype(BF16)

            cross_forward(image, query, keys, vals, picks, mixed, tops, pairs, scale)

        token_relay(0)

        def half_part(k, made):
            @pl.loop(0, 2)
            def _(h):
                rows = pl.ds(pl.multiple_of(h * quarter, 32), quarter)
                part_send[k % 3, rows, :] = made(rows).astype(BF16)
                part_copy(k, h).start()

        def add_halves(k, run, carry):
            def half(h, kept):
                part_copy(k, h).wait()
                return row_tiles(quarter, run, kept, h * quarter)

            return lax.fori_loop(0, 2, half, carry)

        half_part(0, lambda rows: dot_plain(mixed[rows, :], w_cross[3].reshape(heads, width)))
        for one in text_loads[2:]:
            one.wait()
        gain, shift = gains[1], shifts[1]

        def add_cross(rows, kept):
            total = part_send[0, rows, :].astype(F32) + part_recv[0, rows, :].astype(F32)
            value = y1[rows, :] + total
            y2[rows, :] = value
            unit, _ = norm_parts(value)
            act[rows, :] = (unit * gain + shift).astype(BF16)
            return kept

        token_finish(0)
        for k in range(len(pieces)):
            arrived(k)
        end_local(0)

        @pl.loop(0, 2)
        def _(b):
            grad_hid[b] = dot_rows(cot[...], w_mlp[0, b])

        add_halves(0, add_cross, 0)

        @pl.loop(0, 2)
        def _(b):
            cols = pl.ds(pl.multiple_of(b * width, LANES), width)
            pre[...] = dot_plain(act[...], w_in[0, b])
            bias = ffn_in_b[0:1, pl.ds(pl.multiple_of((2 * core + b) * width, LANES), width)]

            def bend(rows, kept):
                lifted, slope = gelu_both(pre[rows, :] + bias)
                hid[rows, cols] = lifted.astype(BF16)
                low = (grad_hid[b, rows, :] * slope).astype(BF16)
                grad_pre[b, rows, :] = low
                return kept + fold_rows(low.astype(F32))

            put(9 + b, row_tiles(count, bend, zero))

        half_part(2, lambda rows: dot_rows(grad_pre[0, rows, :], w_in[0, 0]) + dot_rows(grad_pre[1, rows, :], w_in[0, 1]))

        @pl.loop(0, 2)
        def _(b):
            made = dot_first(grad_pre[b], act[...]).astype(BF16)
            grads[0:ffn_blocks, b] = made.reshape(ffn_blocks, rows_of, width)

        red.launch(0)
        red.launch(1)

        def second(rows, kept):
            low_cot = cot[rows, :].astype(F32)
            grad = part_send[2, rows, :].astype(F32) + part_recv[2, rows, :].astype(F32)
            back, dg, db = norm_back_tile(y2[rows, :], gain, grad)
            total = low_cot + back
            raw[rows, :] = total
            g_low[rows, :] = total.astype(BF16)
            return (kept[0] + dg, kept[1] + db, kept[2] + fold_rows(low_cot))

        dg, db, cot_sum = add_halves(2, second, (zero, zero, zero))
        put(3, dg)
        put(6, db)
        put(1, cot_sum)

        mix_grad[...] = dot_rows(g_low[...], w_cross[3].reshape(heads, width)).astype(BF16)
        cross_backward(query, keys, vals, mix_grad, picks, tops, dq, dk, dv, sum_q, pairs, scale)

        def half_copy(image, far_image):
            return remote(
                halves.at[image, pl.ds(pl.multiple_of((1 - core) * quarter, TILE), quarter), :],
                half_near.at[far_image],
                half_sem.at[far_image, 0],
                half_sem.at[far_image, 1],
                {DP: partner},
            )

        @pl.loop(0, 2)
        def _(i):
            image = side + (1 - i) * (1 - 2 * side)
            made = dot_plain(dkv[0, image], w_cross[0].reshape(heads, width))
            made = made + dot_plain(dkv[1, image], w_cross[1].reshape(heads, width))
            halves[image] = made.astype(BF16)
            half_copy(image, 1 - i).start()

        for k in range(2):
            red.add_near(k, False)
            red.launch(k + 2)

        def sum_copy(i):
            rows = pl.ds(i * chunk, chunk)
            return remote(
                sums.at[0, rows, :], sums.at[2, rows, :], sum_sem.at[i, 0], sum_sem.at[i, 1], {MP: across_chip}
            )

        half_copy(1 - side, 1).wait_recv()
        for i in range(CHUNKS):

            def add_far(rows, kept):
                at = pl.ds(pl.multiple_of(i * chunk + rows.start, 16), rows.size)
                own = pl.ds(pl.multiple_of(core * quarter + i * chunk + rows.start, 16), rows.size)
                total = halves[1 - side, own, :].astype(F32) + half_near[1, at, :].astype(F32)
                sums[0, at, :] = total.astype(BF16)
                return kept

            row_tiles(chunk, add_far, 0)
            sum_copy(i).start()
        @pl.loop(0, 2)
        def _(b):
            cols = pl.ds(pl.multiple_of(b * width, LANES), width)
            made = dot_first(hid[:, cols], cot[...]).astype(BF16)
            grads[ffn_blocks : 2 * ffn_blocks, b] = made.reshape(ffn_blocks, rows_of, width)

        red.launch(4)
        red.launch(5)
        half_copy(side, 0).wait_recv()
        for i in range(CHUNKS):
            sum_copy(i).wait_recv()

            def add_own(rows, kept):
                at = pl.ds(pl.multiple_of(i * chunk + rows.start, 16), rows.size)
                own = pl.ds(pl.multiple_of(core * quarter + i * chunk + rows.start, 16), rows.size)
                total = halves[side, own, :].astype(F32) + half_near[0, at, :].astype(F32)
                sums[1, at, :] = (total + sums[2, at, :].astype(F32)).astype(BF16)
                return kept

            row_tiles(chunk, add_own, 0)
            back_copy(i).start()

        half_part(3, lambda rows: dot_plain(dq[rows, :], w_cross[2].reshape(heads, width)))
        red.hop(0)
        red.hop(1)
        red.step(2, 0)

        def keep_two(rows, kept):
            y1[rows, :] = raw[rows, :]
            return kept

        row_tiles(count, keep_two, 0)
        pltpu.make_async_copy(y1, upstream, store_sem.at[0]).start()

        def lift_query(rows, kept):
            raw[rows, :] = part_send[0, rows, :].astype(F32) + part_recv[0, rows, :].astype(F32)
            return kept

        add_halves(3, lift_query, 0)
        store_three.start()
        pre[...] = jnp.zeros_like(pre)

        @pl.loop(0, 2)
        def _(b):
            pre[...] += dot_plain(hid[:, pl.ds(pl.multiple_of(b * width, LANES), width)], w_mlp[0, b])

        for h in range(2):
            rows = pl.ds(h * quarter, quarter)
            part_send[1, rows, :] = pre[rows, :].astype(BF16)
            part_copy(1, h).start()
        red.add_mid(0)
        red.step(3, 0)
        red.add_mid(1)
        grads[2 * ffn_blocks] = dot_first(dq[...], act_txt[...]).astype(BF16).reshape(grads.shape[1:])
        grads[2 * ffn_blocks + 1] = dot_first(mixed[...], g_low[...]).astype(BF16).reshape(grads.shape[1:])
        red.add_mid(2)
        red.step(4)

        @pl.loop(0, 2)
        def _(which):
            made = dot_first(dkv[which, 0], images[0]) + dot_first(dkv[which, 1], images[1])
            grads[blocks + which] = made.astype(BF16).reshape(grads.shape[1:])

        red.step(5)
        for h in range(2):
            part_copy(1, h).wait()

        def add_last(rows, kept):
            own = pl.ds(pl.multiple_of(core * quarter + rows.start, 32), rows.size)
            total = part_send[1, own, :].astype(F32) + part_recv[1, own, :].astype(F32)
            own_rows[rows, :] = (y2[own, :] + total + ffn_out_b[...]).astype(BF16)
            return kept

        row_tiles(quarter, add_last, 0)
        rows_copy.start()
        red.far_before(6)
        red.drain(6)
        store_cross = pltpu.make_async_copy(near.at[pl.ds(blocks, 2)], cross_out, store_sem.at[2])
        store_cross.start()
        red.close(0)
        store_cross.wait()
        for i in range(CHUNKS):
            side_copy(i, side).wait_send()
            core_copy(i, side, core, 0).wait_send()
            core_copy(i, 1 - side, core, 1).wait_send()
            sum_copy(i).wait_send()
            back_copy(i).wait_send()
        half_copy(1 - side, 1).wait_send()
        half_copy(side, 0).wait_send()
        for k in range(len(pieces)):
            sent(k)

    rows_copy.wait()
    store_grad.wait()
    store_three.wait()


def middle(values, w_cross, w_in, w_mlp, ffn_shard, cot_block, vecs, picks, scale):
    count, width = values.base.shape
    heads = values.mixed.shape[1]
    pairs = heads // LANES
    hidden = values.hid.shape[1]
    quarter = count // 2
    half = width // 2
    chunk = quarter // CHUNKS
    assert chunk * CHUNKS == quarter
    rows_of = heads // 2
    blocks = 2 * (width // rows_of) + 2
    assert hidden == 2 * width
    cross_shape = (2, 2, rows_of, half)
    rows = ffn_shard.shape[1]
    pieces = [(0, 0, 0, 1, at, rows // 4, 1, False) for at in range(rows // 2, rows, rows // 4)]
    n = len(pieces)
    hbm = pl.BlockSpec(memory_space=pltpu.HBM)
    vmem = pl.BlockSpec(memory_space=pltpu.VMEM)
    dma = pltpu.SemaphoreType.DMA
    low, wide = (count, width), (count, heads)
    scratch = [pltpu.VMEM(ffn_shard.shape, BF16), dma((n, 5)), dma((n, 4)), dma((1, 2)), dma, dma]
    scratch += [pltpu.VMEM((1,) + cot_block.shape, BF16), dma((1, 2)), dma((1, 2)), dma((1, 2))]
    scratch += [
        pltpu.VMEM((2,) + low, BF16),
        pltpu.VMEM((2, 2) + wide, BF16),
        pltpu.VMEM((4, 2, heads // 2, width), BF16),
        pltpu.VMEM((1, 2, width, hidden // 2), BF16),
        pltpu.VMEM((1, 2, hidden // 2, width), BF16),
        pltpu.VMEM(low, BF16),
        pltpu.VMEM(wide, BF16),
        pltpu.VMEM(wide, BF16),
        pltpu.VMEM((2, pairs, 8, 2 * count), F32),
        pltpu.VMEM(low, F32),
        pltpu.VMEM(low, F32),
        pltpu.VMEM(low, BF16),
        pltpu.VMEM(low, F32),
        pltpu.VMEM((count, hidden), BF16),
        pltpu.VMEM((2,) + low, F32),
        pltpu.VMEM(low, F32),
        pltpu.VMEM((2, count, hidden // 2), BF16),
        pltpu.VMEM(low, BF16),
        pltpu.VMEM(wide, BF16),
        pltpu.VMEM(wide, BF16),
        pltpu.VMEM((2, 2) + wide, BF16),
        pltpu.VMEM((count, LANES), F32),
        pltpu.VMEM(low, BF16),
        pltpu.VMEM((3,) + low, BF16),
        pltpu.VMEM((3,) + low, BF16),
        pltpu.VMEM((2,) + low, BF16),
        pltpu.VMEM((2, quarter, width), BF16),
        pltpu.VMEM((3, quarter, width), BF16),
        pltpu.VMEM(low, BF16),
        pltpu.VMEM((quarter, width), BF16),
    ]
    scratch += [pltpu.VMEM((blocks + 2, 2, rows_of, width), BF16), pltpu.VMEM((blocks + 2, 2, rows_of, half), BF16)]
    scratch += [pltpu.VMEM((blocks, 2, rows_of, half), BF16)]
    scratch += [dma((blocks + 2,)), dma((blocks + 2,)), dma((blocks, 2)), dma((blocks, 2)), dma((blocks,)), dma((blocks,))]
    scratch += [
        dma((6,)),
        dma((3,)),
        dma((4, 2, 2)),
        dma((CHUNKS, 2)),
        dma((CHUNKS, 2)),
        dma((2, CHUNKS, 2)),
        dma((2, 2)),
        dma((CHUNKS, 2)),
        dma((CHUNKS, 2)),
        dma((CHUNKS, 2)),
        dma((2,)),
    ]
    out_shape = [
        jax.ShapeDtypeStruct(low, F32),
        jax.ShapeDtypeStruct(low, F32),
        jax.ShapeDtypeStruct((16, width), F32),
        jax.ShapeDtypeStruct((quarter, width), BF16),
        jax.ShapeDtypeStruct(cross_shape, BF16),
        jax.ShapeDtypeStruct((blocks, rows_of, half), BF16),
    ]
    args = [values.act_three, values.x1, values.query, w_cross, w_in, w_mlp]
    return pl.pallas_call(
        functools.partial(mid_kernel, tuple(pieces), pairs, scale),
        in_specs=[hbm] * 9 + [vmem] * 7,
        out_specs=[hbm, hbm, vmem, hbm, hbm, vmem],
        out_shape=out_shape,
        scratch_shapes=scratch,
        compiler_params=pltpu.CompilerParams(
            collective_id=2, has_side_effects=True, vmem_limit_bytes=TAIL_LIMIT
        ),
        name="middle",
    )(*args, ffn_shard, cot_block, values.base, *vecs, picks)


def finish_kernel(*refs):
    it = iter(refs)
    late, early, from_text, total = (next(it) for _ in range(4))
    rows_in = [next(it) for _ in range(2)]
    rows_out = [next(it) for _ in range(2)]
    o_qkv, o_out, o_in, o_mlp, o_cross, o_qv, o_outb, o_inb, o_mlpb, o_gain, o_shift = (next(it) for _ in range(11))
    held = [next(it) for _ in range(2)]
    b_in, b_mlp, b_out, b_qkv, b_cross, sem = it
    tower, dp, z, core, line, other, partner = spots()

    def bring(i, image_src, text_src, target):
        @pl.when(tower == 0)
        def _():
            pltpu.make_async_copy(image_src, target, sem.at[i]).start()

        @pl.when(tower == 1)
        def _():
            pltpu.make_async_copy(text_src, target, sem.at[i]).start()

    n = b_in.shape[0]
    bring(0, late.at[pl.ds(n, n)], early.at[pl.ds(0, n)], b_in)
    bring(1, late.at[pl.ds(0, n)], early.at[pl.ds(n, n)], b_mlp)
    bring(2, late.at[2 * n], late.at[2 * n], b_out)
    bring(3, late.at[pl.ds(2 * n + 1, 3)], late.at[pl.ds(2 * n + 1, 3)], b_qkv)
    bring(4, from_text, early.at[pl.ds(2 * n, 2)], b_cross)
    for i in range(2):
        pltpu.make_async_copy(rows_in[i], held[i], sem.at[5 + i]).start()

    width = total.shape[2]
    heads = width // 2
    first = total[0]
    o_outb[...] = first[0:1, :]
    o_mlpb[...] = first[1:2, :]
    for i in range(3):
        o_gain[i] = first[2 + i : 3 + i, :]
        o_shift[i] = first[5 + i : 6 + i, :]
    for side in range(2):
        lanes = slice(side * heads, (side + 1) * heads)
        o_qv[0, 0:1, lanes] = total[side, 8:9, :heads]
        o_qv[0, 1:2, lanes] = total[side, 8:9, heads:]
        for b in range(2):
            at = (2 * side + b) * width
            o_inb[0:1, at : at + width] = total[side, 9 + b : 10 + b, :]

    def mine(block):
        cut = block.shape[1] // 2
        wide = block.astype(F32)
        return jnp.where(core == 0, wide[:, :cut], wide[:, cut:])

    for i in range(2):
        pltpu.make_async_copy(rows_in[i], held[i], sem.at[5 + i]).wait()
        pltpu.make_async_copy(held[i], rows_out[i].at[0], sem.at[7 + i]).start()
    half = b_in.shape[2]
    cols = b_in.shape[1]
    pltpu.make_async_copy(late.at[pl.ds(0, n)], b_in, sem.at[0]).wait()
    for i in range(n // 2):
        pair = b_in[2 * i : 2 * i + 2].reshape(2 * cols, half)
        o_in[0, :, 2 * i * cols : 2 * (i + 1) * cols] = mine(pair).T
    pltpu.make_async_copy(late.at[pl.ds(0, n)], b_mlp, sem.at[1]).wait()
    for i in range(n // 2):
        pair = b_mlp[2 * i : 2 * i + 2].reshape(2 * cols, half)
        o_mlp[0, :, 2 * i * cols : 2 * (i + 1) * cols] = mine(pair).T
    pltpu.make_async_copy(late.at[0], b_out, sem.at[2]).wait()
    o_out[0] = mine(b_out[...])
    pltpu.make_async_copy(late.at[pl.ds(0, 3)], b_qkv, sem.at[3]).wait()
    for a in range(3):
        o_qkv[0, a] = mine(b_qkv[a]).T
    pltpu.make_async_copy(late.at[pl.ds(0, 2)], b_cross, sem.at[4]).wait()
    for a in range(2):
        o_cross[0, a] = mine(b_cross[a]).T
    for i in range(2):
        pltpu.make_async_copy(held[i], rows_out[i].at[0], sem.at[7 + i]).wait()


def finish(late, early, from_text, total, token_rows):
    hbm = pl.BlockSpec(memory_space=pltpu.HBM)
    vmem = pl.BlockSpec(memory_space=pltpu.VMEM)
    struct = jax.ShapeDtypeStruct
    width = total.shape[2]
    blocks, cols, half = early.shape
    n = (blocks - 2) // 2
    ffn, cut = n * cols, half // 2
    out_shape = [struct((1,) + x.shape, BF16) for x in token_rows]
    out_shape += [
        struct((1, 3, cut, cols), F32),
        struct((1, cols, cut), F32),
        struct((1, cut, ffn), F32),
        struct((1, cut, ffn), F32),
        struct((1, 2, cut, cols), F32),
        struct((1, 2, width), F32),
        struct((1, width), F32),
        struct((1, 4 * width), F32),
        struct((1, width), F32),
        struct((3, 1, width), F32),
        struct((3, 1, width), F32),
    ]
    scratch = [pltpu.VMEM(x.shape, BF16) for x in token_rows]
    scratch += [pltpu.VMEM(x + (cols, half), BF16) for x in ((n,), (n,), (), (3,), (2,))]
    scratch += [pltpu.SemaphoreType.DMA((9,))]
    results = pl.pallas_call(
        finish_kernel,
        in_specs=[hbm] * 3 + [vmem] + [hbm] * 2,
        out_specs=[hbm] * 2 + [vmem] * 11,
        out_shape=out_shape,
        scratch_shapes=scratch,
        compiler_params=pltpu.CompilerParams(vmem_limit_bytes=VMEM_LIMIT),
        name="finish",
    )(late, early, from_text, total, *token_rows)
    turned = {5: (1, 2), 11: (0, 1), 12: (0, 1)}
    return tuple(jnp.swapaxes(x, *turned[i]) if i in turned else x for i, x in enumerate(results))


def split_heads(flat):
    return jnp.swapaxes(flat.reshape(flat.shape[0], -1, HDIM), 0, 1)


def join_heads(split):
    return jnp.swapaxes(split, 0, 1).reshape(split.shape[1], -1)


def batch_dot(left, right, left_dim, right_dim):
    return lax.dot_general(left, right, (((left_dim,), (right_dim,)), ((0,), (0,))), preferred_element_type=F32)


def attend_plain(queries, keys, vals, allowed, scale):
    queries, keys, vals = (split_heads(x) for x in (queries, keys, vals))
    scores = jnp.where(allowed, batch_dot(queries, keys, 2, 2) * scale, NEG)
    top = jnp.max(scores, axis=-1, keepdims=True)
    tops = top + jnp.log(jnp.sum(jnp.exp(scores - top), axis=-1, keepdims=True))
    weights = jnp.exp(scores - tops).astype(BF16)
    return (join_heads(batch_dot(weights, vals, 2, 1)).astype(BF16), tops)


def attend_back_plain(queries, keys, vals, grads, tops, allowed, scale):
    queries, keys, vals, grads = (split_heads(x) for x in (queries, keys, vals, grads))
    scores = jnp.where(allowed, batch_dot(queries, keys, 2, 2) * scale, NEG)
    weights = jnp.exp(scores - tops)
    grad_w = batch_dot(grads, vals, 2, 2)
    grad_s = (weights * (grad_w - jnp.sum(weights * grad_w, axis=-1, keepdims=True))).astype(BF16)
    return (
        join_heads(batch_dot(grad_s, keys, 2, 1) * scale).astype(BF16),
        join_heads(batch_dot(grad_s, queries, 1, 1) * scale).astype(BF16),
        join_heads(batch_dot(weights.astype(BF16), grads, 1, 1)).astype(BF16),
    )


def gather_plain(shards):
    core = lax.rem(lax.axis_index(DP), 2)
    outs = []
    for i, s in enumerate(shards):
        if i == 2:
            s = jnp.concatenate([lax.ppermute(s, TOWER, [(0, 1)]), s], axis=0)
        full = lax.all_gather(s, MP, axis=1, tiled=False)
        outs.append(lax.dynamic_slice_in_dim(full, 2 * core, 2, 1))
    return outs


def reduce_plain(grads, smalls):
    dp = lax.axis_index(DP)
    core = lax.rem(dp, 2)
    outs = []
    for g in grads:
        n, _, rows, wide = g.shape
        full = jnp.zeros((n, 4, rows, wide), BF16)
        full = lax.dynamic_update_slice(full, g, (0, 2 * core, 0, 0))
        part = lax.psum_scatter(full, MP, scatter_dimension=1, tiled=False)
        part = lax.psum_scatter(part, DP, scatter_dimension=2, tiled=True)
        outs.append(part)
    if smalls is None:
        return outs
    both = jnp.zeros((2,) + smalls.shape, F32)
    both = lax.dynamic_update_slice(both, smalls[None], (core, 0, 0))
    return outs + [lax.psum(both, (DP, MP))]


def body(
    tower_in,
    out_cot,
    segment_ids,
    row_image,
    attn_qkv,
    attn_out,
    mlp_in,
    mlp_out,
    cross_proj,
    qv_bias,
    out_bias,
    mlp_bias_in,
    mlp_bias_out,
    norm_gain,
    norm_bias,
):
    lines = lax.axis_size(DP) // 2
    depth = lax.axis_size(MP)
    devices = lax.axis_size(DP)
    is_enc = lax.axis_index(TOWER) == 0
    dp = lax.axis_index(DP)
    z = lax.axis_index(MP)
    core = lax.rem(dp, 2)
    side = lax.rem(z, 2)
    group = z // 2
    direct = lines == 2
    assert depth == 4
    quarter = tower_in.shape[1]
    tokens = 2 * quarter
    assert tokens == PATCH
    width = tower_in.shape[2]
    head_cols = 2 * attn_qkv.shape[3]
    hidden = 2 * mlp_in.shape[2]
    scale_qk = HDIM ** (-0.5)

    out_moves, back_moves = [], []
    for d in range(devices):
        for place in range(depth):
            here = d * depth + place
            there = (d - d % 2 + place % 2) * depth + 2 * (d % 2) + place // 2
            out_moves.append((here, there))
            back_moves.append((there, here))

    def swap_cores(x):
        return lax.ppermute(x, DP, [(i, i ^ 1) for i in range(devices)])

    def both_cores(own):
        other = swap_cores(own)
        return jnp.where(core == 0, jnp.concatenate([own, other], -2), jnp.concatenate([other, own], -2))

    def own_rows(full):
        return lax.dynamic_slice_in_dim(full, core * quarter, quarter, full.ndim - 2)

    def lowered(part):
        return lax.reduce_precision(part, 8, 7).astype(BF16)

    def add_lowered(low):
        return low.astype(F32) + swap_cores(low).astype(F32)

    def add_cores(part):
        return add_lowered(lowered(part))

    def only_image(run, *operands):
        def idle(*inputs):
            return jax.tree.map(lambda x: jnp.zeros(x.shape, x.dtype), jax.eval_shape(run, *inputs))

        return lax.cond(is_enc, run, idle, *operands)

    shards = [
        jnp.swapaxes(attn_qkv[0], 1, 2),
        attn_out,
        jnp.swapaxes(cross_proj[0], 1, 2),
        mlp_in,
        mlp_out,
    ]
    rows = segment_ids.shape[0] // 2

    bias_qv = lax.dynamic_slice_in_dim(qv_bias[0], core * head_cols, head_cols, 1)
    bias_packed = jnp.concatenate([bias_qv[0], jnp.zeros_like(bias_qv[0]), bias_qv[1]])
    bias_in = lax.dynamic_slice_in_dim(mlp_bias_in[0], core * hidden, hidden, 0)
    gains = norm_gain[0]
    shifts = norm_bias[0]

    def feed_forward(values):
        act = norm_rows(values, gains[1], shifts[1]).astype(BF16)
        pre = jnp.concatenate([dot_plain(act, w_in[0]), dot_plain(act, w_in[1])], axis=1) + bias_in
        hid = gelu_tanh(pre).astype(BF16)
        return (act, pre, hid, lowered(dot_plain(hid, w_mlp)))

    if direct:
        tall_gains, tall_shifts = (jnp.swapaxes(x, 0, 1) for x in (norm_gain, norm_bias))
        vecs = (tall_gains, tall_shifts, out_bias, mlp_bias_out, mlp_bias_in, qv_bias[0])
        gathered, stream_low, notes, first = head(
            shards, [tower_in[0]], segment_ids, row_image, vecs, scale_qk
        )
        seg_col, seg_row, picks = notes
    else:
        gathered = gather_plain(shards)
        stream_low = both_cores(lax.ppermute(tower_in[0], (DP, MP), out_moves))
        cot_low = both_cores(lax.ppermute(out_cot[0], (DP, MP), out_moves))
        segs = jnp.where(core == group, segment_ids, swap_cores(segment_ids))
        segs = lax.dynamic_slice_in_dim(segs, rows * side, rows, 0)
        marks = (segs + LTXT * jnp.arange(rows, dtype=jnp.int32)[:, None]).reshape(tokens)
        images_of = jnp.where(core == group, row_image, swap_cores(row_image))
        images_of = jnp.repeat(lax.dynamic_slice_in_dim(images_of, rows * side, rows, 0), LTXT)
        places = jnp.arange(tokens)
        allowed = (places[None, :] <= places[:, None]) & (marks[None, :] == marks[:, None])
        allowed = jnp.logical_or(allowed, is_enc)
        sees = images_of[:, None] == jnp.arange(2 * tokens)[None, :] // tokens
    w_qkv = gathered[0].reshape(3 * head_cols, width)
    w_out = gathered[1].reshape(head_cols, width)
    w_cross = gathered[2].reshape(4, head_cols, width)
    w_in = gathered[3][0]
    w_mlp = gathered[4].reshape(hidden, width)
    stream = stream_low.astype(F32)

    if not direct:
        act_one = norm_rows(stream, gains[0], shifts[0]).astype(BF16)
        packed = (dot_rows(act_one, w_qkv) + bias_packed).astype(BF16)
        parts = [packed[:, i * head_cols : (i + 1) * head_cols] for i in range(3)]
        mixed, tops = attend_plain(*parts, allowed, scale_qk)
        stream_one = stream + add_cores(dot_plain(mixed, w_out)) + out_bias[0]
        act_enc, pre_enc, hid_enc, part_enc = feed_forward(stream_one)
        out_enc = stream_one + add_lowered(part_enc) + mlp_bias_out[0]
        base_three = jnp.where(is_enc, out_enc, stream_one)
        act_three = norm_rows(base_three, gains[2], shifts[2]).astype(BF16)
        cross_q = dot_rows(act_three, w_cross[2]).astype(BF16)

    if direct:
        back_in_three, upstream, smalls, tower_rows, g_cross, early = middle(
            first, gathered[2], gathered[3], gathered[4], mlp_out, out_cot[0], vecs, picks, scale_qk
        )
        values = Tail(
            d_three=back_in_three,
            base=first.base,
            upstream=upstream,
            gains=tall_gains,
            smalls=smalls,
            w_mlp=w_mlp,
            pre=first.pre,
            hid=first.hid,
            act=first.act,
            w_in=w_in,
            x1=first.x1,
            w_out=w_out,
            mixed=first.mixed,
            packed=first.packed,
            tops=first.tops,
            seg_col=seg_col,
            seg_row=seg_row,
            a_one=first.a_one,
            w_qkv=w_qkv,
            x0=stream_low,
        )
        late, total, grad_in, from_text, tower_out = tail(values, g_cross, tower_rows, scale_qk)
        return finish(late, early, from_text, total, [tower_out, grad_in])
    else:
        near_half = lax.ppermute(own_rows(act_three), TOWER, [(0, 1)])
        far_half = lax.ppermute(near_half, MP, [(i, i ^ 1) for i in range(depth)])
        halves = jnp.where(side == 0, jnp.stack([near_half, far_half]), jnp.stack([far_half, near_half]))
        images = both_cores(halves)

        flat_images = images.reshape(2 * tokens, width)
        cross_k = dot_rows(flat_images, w_cross[0]).astype(BF16)
        cross_v = dot_rows(flat_images, w_cross[1]).astype(BF16)
        cross_mix, cross_tops = attend_plain(cross_q, cross_k, cross_v, sees, scale_qk)
        stream_two = stream_one + add_cores(dot_plain(cross_mix, w_cross[3]))

        act_dec, pre_dec, hid_dec, part_dec = feed_forward(stream_two)
        out_dec = stream_two + add_lowered(part_dec) + mlp_bias_out[0]
        tower_rows = own_rows(jnp.where(is_enc, base_three, out_dec).astype(BF16))

        def feed_back(grad_low, pre):
            grad_hid = dot_rows(grad_low, w_mlp)
            _, pullback = jax.vjp(gelu_tanh, pre)
            grad_pre = pullback(grad_hid)[0].astype(BF16)
            cols = hidden // 2
            part = dot_rows(grad_pre[:, :cols], w_in[0]) + dot_rows(grad_pre[:, cols:], w_in[1])
            return (grad_pre, lowered(part))

        def feed_grads(grad_low, act, grad_pre, hid):
            g_in = dot_first(grad_pre, act).astype(BF16)
            g_mlp = dot_first(hid, grad_low).astype(BF16)
            return (
                g_in.reshape(1, 2, hidden // 2, width),
                g_mlp.reshape(1, 2, hidden // 2, width),
            )

        cot = cot_low.astype(F32)
        grad_pre_dec, back_in = feed_back(cot_low, pre_dec)
        back_a, gain_a, shift_a = norm_back(stream_two, gains[1], add_lowered(back_in))
        grad_two = cot + back_a
        grad_two_low = grad_two.astype(BF16)

        grad_mix = dot_rows(grad_two_low, w_cross[3]).astype(BF16)
        grad_q, flat_k, flat_v = attend_back_plain(
            cross_q, cross_k, cross_v, grad_mix, cross_tops, sees, scale_qk
        )
        part_images = dot_plain(flat_k, w_cross[0]) + dot_plain(flat_v, w_cross[1])
        part_low = part_images.astype(BF16).reshape(2, 2, quarter, width)
        give = lax.dynamic_index_in_dim(part_low, 1 - core, 1, keepdims=False)
        keep = lax.dynamic_index_in_dim(part_low, core, 1, keepdims=False)
        pair_sum = (keep.astype(F32) + swap_cores(give).astype(F32)).astype(BF16)
        give = lax.dynamic_index_in_dim(pair_sum, 1 - side, 0, keepdims=False)
        keep = lax.dynamic_index_in_dim(pair_sum, side, 0, keepdims=False)
        got = lax.ppermute(give, MP, [(i, i ^ 1) for i in range(depth)])
        image_sum = (keep.astype(F32) + got.astype(F32)).astype(BF16)
        image_half = lax.ppermute(image_sum, TOWER, [(1, 0)])
        later = lax.optimization_barrier(
            (cot_low, act_dec, grad_pre_dec, hid_dec, flat_k, flat_v, grad_q, cross_mix, image_sum)
        )
        g_in_dec, g_mlp_dec = feed_grads(later[0], later[1], later[2], later[3])
        g_cross = jnp.concatenate(
            [
                dot_first(later[4], flat_images).astype(BF16),
                dot_first(later[5], flat_images).astype(BF16),
                dot_first(later[6], act_three).astype(BF16),
                dot_first(later[7], grad_two_low).astype(BF16),
            ],
            axis=0,
        ).reshape(4, 2, head_cols // 2, width)
        image_back = both_cores(image_half).astype(F32)
        query_back = add_cores(dot_plain(grad_q, w_cross[2]))
        back_in_three = jnp.where(is_enc, image_back, query_back)
        text_smalls = (
            jnp.zeros((16, width), F32)
            .at[1]
            .set(jnp.sum(cot_low, axis=0, dtype=F32))
            .at[3]
            .set(gain_a)
            .at[6]
            .set(shift_a)
            .at[9:11]
            .set(jnp.sum(grad_pre_dec, axis=0, dtype=F32).reshape(2, width))
        )
        smalls = jnp.where(is_enc, 0.0, text_smalls)
        tower_out = lax.ppermute(tower_rows, (DP, MP), back_moves)
        back_three, gain_three, shift_three = norm_back(
            base_three, gains[2], back_in_three
        )
        grad_enc = cot + back_three
        grad_enc_low = grad_enc.astype(BF16)

        grad_pre_enc, back_in = feed_back(grad_enc_low, pre_enc)
        g_in, g_mlp = feed_grads(grad_enc_low, act_enc, grad_pre_enc, hid_enc)
        back_b, gain_b, shift_b = norm_back(stream_one, gains[1], add_lowered(back_in))
        grad_one = jnp.where(is_enc, grad_enc + back_b, grad_two + back_three)
        grad_one_low = grad_one.astype(BF16)

        g_out = dot_first(mixed, grad_one_low).astype(BF16).reshape(1, 2, head_cols // 2, width)
        grad_mixed = dot_rows(grad_one_low, w_out).astype(BF16)
        grad_packed = jnp.concatenate(
            attend_back_plain(*parts, grad_mixed, tops, allowed, scale_qk), axis=1
        )
        g_qkv = dot_first(grad_packed, act_one).astype(BF16).reshape(3, 2, head_cols // 2, width)
        back_in = add_cores(dot_plain(grad_packed, w_qkv))
        back_one, gain_one, shift_one = norm_back(stream, gains[0], back_in)
        grad_in = own_rows((grad_one + back_one).astype(BF16))
        grad_in = lax.ppermute(grad_in, (DP, MP), back_moves)

        grad_pre_sum = jnp.sum(grad_pre_enc, axis=0, dtype=F32).reshape(2, width)
        packed_sum = jnp.sum(grad_packed, axis=0, dtype=F32)
        smalls = jnp.concatenate(
            [
                jnp.sum(grad_one_low, axis=0, dtype=F32)[None],
                jnp.where(is_enc, jnp.sum(grad_enc_low, axis=0, dtype=F32), smalls[1])[None],
                gain_one[None],
                jnp.where(is_enc, gain_b, smalls[3])[None],
                gain_three[None],
                shift_one[None],
                jnp.where(is_enc, shift_b, smalls[6])[None],
                shift_three[None],
                jnp.concatenate([packed_sum[:head_cols], packed_sum[2 * head_cols :]])[None],
                jnp.where(is_enc, grad_pre_sum, smalls[9:11]),
                smalls[11:],
            ]
        )
        g_in = jnp.where(is_enc, g_in, g_in_dec)
        g_mlp = jnp.where(is_enc, g_mlp, g_mlp_dec)
        s_in, s_mlp, s_out, s_qkv, s_cross, total = reduce_plain([g_in, g_mlp, g_out, g_qkv, g_cross], smalls)
        s_cross = jnp.where(is_enc, lax.ppermute(s_cross[:2], TOWER, [(1, 0)]), s_cross[2:])

    def turned(x):
        return jnp.swapaxes(x, 1, 2).astype(F32)

    cross_pair = jnp.stack(
        [
            s_cross[0].T,
            s_cross[1].T,
        ]
    ).astype(F32)
    first = total[0]
    qv_total = jnp.stack(
        [
            total[:, 8, :head_cols].reshape(-1),
            total[:, 8, head_cols:].reshape(-1),
        ]
    )
    in_total = total[:, 9:11].reshape(-1)
    return (
        tower_out[None],
        grad_in[None],
        turned(s_qkv)[None],
        s_out.astype(F32),
        turned(s_in),
        s_mlp.astype(F32),
        cross_pair[None],
        qv_total[None],
        first[0:1],
        in_total[None],
        first[1:2],
        first[2:5][None],
        first[5:8][None],
    )


def solution(mesh):
    return jax.shard_map(
        body,
        mesh=mesh,
        in_specs=(
            P(TOWER, (DP, MP), None),
            P(TOWER, (DP, MP), None),
            P(DP, None),
            P(DP),
            P(TOWER, None, None, MP),
            P(TOWER, MP, None),
            P(TOWER, None, MP),
            P(TOWER, MP, None),
            P(TOWER, None, None, MP),
            P(TOWER, None, None),
            P(TOWER, None),
            P(TOWER, None),
            P(TOWER, None),
            P(TOWER, None, None),
            P(TOWER, None, None),
        ),
        out_specs=(
            P(TOWER, (DP, MP), None),
            P(TOWER, (DP, MP), None),
            P(TOWER, None, DP, MP),
            P(TOWER, MP, DP),
            P(TOWER, DP, MP),
            P(TOWER, MP, DP),
            P(TOWER, None, DP, MP),
            P(TOWER, None, None),
            P(TOWER, None),
            P(TOWER, None),
            P(TOWER, None),
            P(TOWER, None, None),
            P(TOWER, None, None),
        ),
        check_vma=False,
    )
```

```python
import functools
from typing import Any, NamedTuple

import jax
import jax.numpy as jnp
from jax import lax
from jax.experimental import pallas as pl
from jax.experimental.pallas import tpu as pltpu
from jax.sharding import PartitionSpec as P

TOWER = "tower"
DP = "dp"
MP = "mp"
HDIM = 64
PATCH = 576
LTXT = 64
EPS = 1e-06
NEG = -1e30
LANES = 128
MESH = pl.DeviceIdType.MESH
F32 = jnp.float32
BF16 = jnp.bfloat16
VMEM_LIMIT = 60 * 1024 * 1024
TAIL_LIMIT = 67043328


def norm_parts(values):
    center = values - jnp.mean(values, axis=-1, keepdims=True)
    spread = jnp.mean(center * center, axis=-1, keepdims=True)
    scale = lax.rsqrt(spread + EPS)
    return (center * scale, scale)


def norm_rows(values, gain_vec, shift_vec):
    unit, _ = norm_parts(values)
    return unit * gain_vec + shift_vec


def norm_back(values, gain_vec, grad_normed):
    unit, scale = norm_parts(values)
    inner = grad_normed * gain_vec
    mean_one = jnp.mean(inner, axis=-1, keepdims=True)
    mean_two = jnp.mean(inner * unit, axis=-1, keepdims=True)
    back = (inner - mean_one - unit * mean_two) * scale
    return (back, jnp.sum(grad_normed * unit, axis=0), jnp.sum(grad_normed, axis=0))


def gelu_tanh(values):
    return jax.nn.gelu(values, approximate=True)


def dot_rows(left, right):
    return lax.dot_general(left, right, (((1,), (1,)), ((), ())), preferred_element_type=F32)


def dot_first(left, right):
    return lax.dot_general(left, right, (((0,), (0,)), ((), ())), preferred_element_type=F32)


def dot_plain(left, right):
    return lax.dot_general(left, right, (((1,), (0,)), ((), ())), preferred_element_type=F32)


def spots():
    tower = lax.axis_index(TOWER)
    dp = lax.axis_index(DP)
    z = lax.axis_index(MP)
    core = lax.rem(dp, 2)
    line = dp // 2
    return tower, dp, z, core, line, dp + 2 - 4 * line, dp + 1 - 2 * core


def greet(target):
    pl.semaphore_signal(pltpu.get_barrier_semaphore(), inc=1, device_id=target, device_id_type=MESH)


def weight_steps(pieces, srcs, outs, stages, sems, less):
    send_sem, recv_sem, local_sem, twin_send, twin_recv = sems
    tower, dp, z, core, line, other, partner = spots()
    place = z + core * (3 - 2 * z)
    ahead = z + 1 - 2 * core
    behind = z - 1 + 2 * core
    slot_of = (core, 1 - core)
    holder = place <= 1
    far_src = [k for k, p in enumerate(pieces) if p[7]]

    def spot(piece, slot, half):
        which, first, _, count, start, size, _, _ = piece
        part = size // 2
        return outs[which].at[pl.ds(first, count), slot, pl.ds(start + half * part, part), :]

    def own(piece):
        which, _, first, count, start, size, _, far = piece
        part = size // 2
        if far:
            return spot(piece, lax.rem(z, 2), line)
        return srcs[which].at[pl.ds(first, count), pl.ds(start + line * part, part), :]

    def move(k, source, slot, half, kind, arrive, target):
        return pltpu.make_async_remote_copy(
            src_ref=source,
            dst_ref=spot(pieces[k], slot, half),
            send_sem=send_sem.at[k, kind],
            recv_sem=recv_sem.at[k, arrive],
            device_id=target,
            device_id_type=MESH,
        )

    def twin_copy():
        which = pieces[far_src[0]][0]
        return pltpu.make_async_remote_copy(
            src_ref=srcs[which],
            dst_ref=outs[which].at[pl.ds(0, srcs[which].shape[0]), lax.rem(z, 2)],
            send_sem=twin_send,
            recv_sem=twin_recv,
            device_id={TOWER: 1 - tower},
            device_id_type=MESH,
        )

    def local_in(i):
        return pltpu.make_async_copy(srcs[i], stages[i], local_sem.at[i, 0])

    def local_out(i):
        first = outs[i].shape[0] - srcs[i].shape[0]
        return pltpu.make_async_copy(
            stages[i], outs[i].at[pl.ds(first, srcs[i].shape[0]), lax.rem(z, 2)], local_sem.at[i, 1]
        )

    def gate(piece, cond):
        return cond if piece[6] is None else jnp.logical_and(cond, tower == piece[6])

    def send_own(k, seat):
        piece = pieces[k]

        if seat == 0:

            @pl.when(gate(piece, place == 0))
            def _():
                move(k, own(piece), slot_of[0], line, 0, 0, {MP: ahead}).start()

        else:

            @pl.when(gate(piece, place == 1))
            def _():
                move(k, own(piece), slot_of[1], line, 1, 1, {MP: ahead}).start()
                move(k, own(piece), slot_of[1], line, 2, 1, {MP: behind}).start()

    orders = {t: [k for k, p in enumerate(pieces) if p[6] in (None, t)] for t in (0, 1)}

    def launch(t, at, seat):
        if at >= len(orders[t]):
            return
        k = orders[t][at]

        @pl.when(jnp.logical_and(place == seat, tower == t))
        def _():
            if far_src and k == far_src[0]:
                twin_copy().wait_recv()
            send_own(k, seat)

    def own_sent(k):
        piece = pieces[k]

        @pl.when(gate(piece, place == 0))
        def _():
            move(k, own(piece), slot_of[0], line, 0, 0, {MP: z}).wait_send()

        @pl.when(gate(piece, place == 1))
        def _():
            move(k, own(piece), slot_of[1], line, 1, 1, {MP: z}).wait_send()
            move(k, own(piece), slot_of[1], line, 2, 1, {MP: z}).wait_send()

    def begin():
        if far_src:

            @pl.when(jnp.logical_and(holder, tower == 0))
            def _():
                twin_copy().start()

        for t in (0, 1):
            for seat in (0, 1):
                for start in range(WINDOW - less * seat):
                    launch(t, start, seat)

    def keeps(i):
        flags = {p[6] for p in pieces if p[0] == i}
        flag = None if len(flags) > 1 else flags.pop()
        return holder if flag is None else jnp.logical_and(holder, tower == flag)

    def begin_local():
        for i in range(len(srcs)):

            @pl.when(keeps(i))
            def _(i=i):
                local_in(i).start()

        for i in range(len(srcs)):

            @pl.when(keeps(i))
            def _(i=i):
                local_in(i).wait()
                local_out(i).start()

    def pass_on(k):
        piece = pieces[k]

        @pl.when(gate(piece, place >= 1))
        def _():
            here = spot(piece, slot_of[0], line)
            move(k, here, slot_of[0], line, 0, 0, {MP: z}).wait_recv()
            move(k, here, slot_of[0], line, 3, 2, {DP: other}).start()

        @pl.when(gate(piece, jnp.logical_and(place >= 1, place <= 2)))
        def _():
            here = spot(piece, slot_of[0], line)
            move(k, here, slot_of[0], line, 0, 0, {MP: ahead}).start()

        @pl.when(gate(piece, place != 1))
        def _():
            here = spot(piece, slot_of[1], line)
            move(k, here, slot_of[1], line, 1, 1, {MP: z}).wait_recv()
            move(k, here, slot_of[1], line, 4, 3, {DP: other}).start()

        @pl.when(gate(piece, place == 2))
        def _():
            here = spot(piece, slot_of[1], line)
            move(k, here, slot_of[1], line, 1, 1, {MP: ahead}).start()

        own_sent(k)
        for t in (0, 1):
            if k in orders[t]:
                for seat in (0, 1):
                    launch(t, orders[t].index(k) + WINDOW - less * seat, seat)

    def arrived(k):
        piece = pieces[k]

        @pl.when(gate(piece, place >= 1))
        def _():
            move(k, spot(piece, slot_of[0], 1 - line), slot_of[0], 1 - line, 3, 2, {DP: dp}).wait_recv()

        @pl.when(gate(piece, place != 1))
        def _():
            move(k, spot(piece, slot_of[1], 1 - line), slot_of[1], 1 - line, 4, 3, {DP: dp}).wait_recv()

    def sent(k):
        piece = pieces[k]

        @pl.when(gate(piece, jnp.logical_or(place == 1, place == 2)))
        def _():
            move(k, spot(piece, slot_of[0], line), slot_of[0], line, 0, 0, {MP: z}).wait_send()

        @pl.when(gate(piece, place == 2))
        def _():
            move(k, spot(piece, slot_of[1], line), slot_of[1], line, 1, 1, {MP: z}).wait_send()

        @pl.when(gate(piece, place >= 1))
        def _():
            move(k, spot(piece, slot_of[0], line), slot_of[0], line, 3, 2, {DP: dp}).wait_send()

        @pl.when(gate(piece, place != 1))
        def _():
            move(k, spot(piece, slot_of[1], line), slot_of[1], line, 4, 3, {DP: dp}).wait_send()

    def end_local(i):
        @pl.when(keeps(i))
        def _():
            local_out(i).wait()

    def end_twin():
        @pl.when(jnp.logical_and(holder, tower == 0))
        def _():
            twin_copy().wait_send()

    return begin, begin_local, pass_on, arrived, sent, end_local, end_twin


def token_steps(blocks, outs, stage, sems):
    send_sem, recv_sem, local_sem = sems
    tower, dp, z, core, line, other, partner = spots()
    stays = z == 3 * core
    size = blocks[0].shape[0]

    def rows(which_core):
        return pl.ds(pl.multiple_of(which_core * size, 16), size)

    def away(i):
        target = {DP: 2 * line + lax.rem(z, 2), MP: 2 * core + z // 2}
        return pltpu.make_async_remote_copy(
            src_ref=blocks[i],
            dst_ref=outs[i].at[rows(lax.rem(z, 2)), :],
            send_sem=send_sem.at[i, 0],
            recv_sem=recv_sem.at[i, 0],
            device_id=target,
            device_id_type=MESH,
        )

    def across(i, which_core):
        return pltpu.make_async_remote_copy(
            src_ref=outs[i].at[rows(which_core), :],
            dst_ref=outs[i].at[rows(which_core), :],
            send_sem=send_sem.at[i, 1],
            recv_sem=recv_sem.at[i, 1],
            device_id={DP: partner},
            device_id_type=MESH,
        )

    def begin(i):
        @pl.when(jnp.logical_not(stays))
        def _():
            away(i).start()

        @pl.when(stays)
        def _():
            first = pltpu.make_async_copy(blocks[i], stage.at[i], local_sem.at[i, 0])
            first.start()
            first.wait()
            second = pltpu.make_async_copy(stage.at[i], outs[i].at[rows(core), :], local_sem.at[i, 1])
            second.start()
            second.wait()
            across(i, core).start()

    def relay(i):
        @pl.when(jnp.logical_not(stays))
        def _():
            away(i).wait_recv()
            across(i, core).start()

    def finish(i):
        across(i, 1 - core).wait_recv()
        across(i, core).wait_send()

        @pl.when(jnp.logical_not(stays))
        def _():
            away(i).wait_send()

    return begin, relay, finish


TILE = 32
LAG = 1
WINDOW = 2


def barrier_all(peers, options):
    for cond, target in peers:
        if cond is None:
            greet(target)
        else:
            pl.when(cond)(functools.partial(greet, target))
    for cond, count in options:

        @pl.when(cond)
        def _(count=count):
            pl.semaphore_wait(pltpu.get_barrier_semaphore(), count)


def fold_rows(tile):
    return jnp.sum(tile.reshape(tile.shape[0] // 8, 8, tile.shape[1]), axis=0)


def row_tiles(total, run, carry, first=0, unroll=1):
    tile = next(t for t, by in ((64, 192), (96, 96), (48, 48), (32, 32)) if total % by == 0)
    turns = total // tile

    def step(i, kept):
        return run(pl.ds(pl.multiple_of(first + i * tile, 16), tile), kept)

    return lax.fori_loop(0, turns, step, carry, unroll=unroll)


def norm_back_tile(values, gain, grads):
    unit, scale = norm_parts(values)
    inner = grads * gain
    mean_one = jnp.mean(inner, axis=-1, keepdims=True)
    mean_two = jnp.mean(inner * unit, axis=-1, keepdims=True)
    return ((inner - mean_one - unit * mean_two) * scale, fold_rows(grads * unit), fold_rows(grads))


def gelu_both(v):
    rate = 0.7978845608028654
    square = v * v
    bend = jnp.tanh(rate * (v + 0.044715 * (square * v)))
    lifted = 0.5 * (1.0 + bend)
    slope = lifted + 0.5 * v * (1.0 - bend * bend) * (rate * (1.0 + 3.0 * 0.044715 * square))
    return (v * lifted, slope)


def low_lanes_of(count):
    return lax.broadcasted_iota(jnp.int32, (count, LANES), 1) < HDIM


def stack_all(block, low):
    wide = block.astype(F32)
    return jnp.concatenate([jnp.where(low, wide, 0.0), jnp.where(low, 0.0, wide)], axis=0)


def merge_all(both, low):
    count = both.shape[0] // 2
    return jnp.where(low, both[:count], both[count:])


def lane_block(index):
    return pl.ds(pl.multiple_of(index * LANES, LANES), LANES)


def scores_of(keys, queries, mask):
    scores = dot_rows(keys, queries)
    if mask is None:
        return scores
    block = mask[...]
    return scores + jnp.concatenate([block, block], axis=1)


def forward_heads(queries, keys, vals, mask, low):
    scores = scores_of(keys, queries, mask)
    top = jnp.max(scores, axis=0, keepdims=True)
    grown = jnp.exp(scores - top)
    total = jnp.sum(grown, axis=0, keepdims=True)
    weights = (grown * (1.0 / total)).astype(BF16)
    return (merge_all(dot_first(weights, vals), low), top + jnp.log(total))


def backward_heads(queries, keys, vals, grads, tops, mask, low, scale):
    weights = jnp.exp(scores_of(keys, queries, mask) - tops)
    grad_w = dot_rows(vals, grads)
    row_dot = jnp.sum(weights * grad_w, axis=0, keepdims=True)
    grad_s = (weights * (grad_w - row_dot)).astype(BF16)
    grad_q = merge_all(dot_first(keys, grad_s).T, low) * scale
    return (grad_q, dot_plain(grad_s, queries), dot_plain(weights.astype(BF16), grads))


def fill_mask(mask, col, row, is_dec):
    count = mask.shape[0]

    def tile(rows, kept):
        shape = (rows.size, count)
        key_at = lax.broadcasted_iota(jnp.int32, shape, 0) + rows.start
        query_at = lax.broadcasted_iota(jnp.int32, shape, 1)
        allowed = jnp.logical_and(key_at <= query_at, col[rows, 0:1] == row[0:1, :])
        mask[rows, :] = jnp.where(jnp.logical_or(allowed, jnp.logical_not(is_dec)), 0.0, NEG)
        return kept

    row_tiles(count, tile, 0)


def self_forward(packed, mask, out, tops, pairs, scale):
    low = low_lanes_of(packed.shape[0])

    @pl.loop(0, pairs)
    def _(pair):
        queries = (stack_all(packed[:, lane_block(pair)], low) * scale).astype(BF16)
        mixed, top = forward_heads(
            queries, packed[:, lane_block(pairs + pair)], packed[:, lane_block(2 * pairs + pair)], mask, low
        )
        out[:, lane_block(pair)] = mixed.astype(BF16)
        tops[pair, 0:1, :] = top


def self_backward(packed, grads, tops, mask, out, pairs, scale, between):
    low = low_lanes_of(packed.shape[0])

    @pl.loop(0, pairs)
    def _(pair):
        queries = (stack_all(packed[:, lane_block(pair)], low) * scale).astype(BF16)
        head_grads = stack_all(grads[:, lane_block(pair)], low).astype(BF16)
        grad_q, grad_k, grad_v = backward_heads(
            queries,
            packed[:, lane_block(pairs + pair)],
            packed[:, lane_block(2 * pairs + pair)],
            head_grads,
            tops[pair, 0:1, :],
            mask,
            low,
            scale,
        )
        out[:, lane_block(pair)] = grad_q.astype(BF16)
        out[:, lane_block(pairs + pair)] = grad_k.astype(BF16)
        out[:, lane_block(2 * pairs + pair)] = grad_v.astype(BF16)
        pl.when(pair == 1)(between)


def cross_forward(image, query, keys, vals, picks, out, tops, pairs, scale):
    low = low_lanes_of(query.shape[0])

    @pl.loop(0, pairs)
    def _(pair):
        cols = lane_block(pair)
        queries = (stack_all(query[:, cols], low) * scale).astype(BF16)
        mixed, top = forward_heads(queries, keys[image, :, cols], vals[image, :, cols], None, low)
        kept = jnp.where(picks[...] == image, mixed, out[:, cols].astype(F32))
        out[:, cols] = kept.astype(BF16)
        tops[image, pair, 0:1, :] = top


def cross_backward(query, keys, vals, grads, picks, tops, dq, dk, dv, sum_q, pairs, scale):
    low = low_lanes_of(query.shape[0])

    @pl.loop(0, pairs)
    def _(pair):
        cols = lane_block(pair)
        queries = (stack_all(query[:, cols], low) * scale).astype(BF16)
        sum_q[...] = jnp.zeros_like(sum_q)

        @pl.loop(0, 2)
        def _(image):
            own = jnp.where(picks[...] == image, grads[:, cols].astype(F32), 0.0)
            grad_q, grad_k, grad_v = backward_heads(
                queries,
                keys[image, :, cols],
                vals[image, :, cols],
                stack_all(own, low).astype(BF16),
                tops[image, pair, 0:1, :],
                None,
                low,
                scale,
            )
            sum_q[...] += grad_q
            dk[image, :, cols] = grad_k.astype(BF16)
            dv[image, :, cols] = grad_v.astype(BF16)

        dq[:, cols] = sum_q[...].astype(BF16)


class Reducer:
    def __init__(self, grads, near, far, outs, sems, window, first, last, near_last):
        self.grads, self.near, self.far, self.outs = grads, near, far, outs
        self.y_send, self.y_recv, self.z_send, self.z_recv, self.c_send, self.c_recv = sems
        self.tower, self.dp, self.z, self.core, self.line, self.other, self.partner = spots()
        self.place = self.z + self.core * (3 - 2 * self.z)
        self.holder = self.place <= 1
        self.slot = lax.rem(self.z, 2)
        self.half = grads.shape[3] // 2
        self.rows = grads.shape[2]
        self.window, self.first, self.last, self.near_last = window, first, last, near_last

    def lanes(self, line):
        return pl.ds(pl.multiple_of(line * self.half, LANES), self.half)

    def to_line(self, k):
        return pltpu.make_async_remote_copy(
            src_ref=self.grads.at[k, :, :, self.lanes(1 - self.line)],
            dst_ref=self.near.at[k],
            send_sem=self.y_send.at[k],
            recv_sem=self.y_recv.at[k],
            device_id={DP: self.other},
            device_id_type=MESH,
        )

    def send(self, source, target, k, sent, got, where):
        return pltpu.make_async_remote_copy(
            src_ref=source,
            dst_ref=target,
            send_sem=self.z_send.at[k, sent],
            recv_sem=self.z_recv.at[k, got],
            device_id={MP: where},
            device_id_type=MESH,
        )

    def inward(self, k):
        return self.send(self.near.at[k], self.far.at[k], k, 0, 0, 2 - self.core)

    def beside(self, k):
        return self.send(self.near.at[k, 1 - self.slot], self.far.at[k, 0], k, 0, 0, 4 * self.core + 1 - self.z)

    def onward(self, k, shard):
        return self.send(self.near.at[k, shard], self.far.at[k, 1], k, shard, 1, 2 * self.core + shard)

    def to_core(self, k):
        return pltpu.make_async_remote_copy(
            src_ref=self.outs.at[k],
            dst_ref=self.outs.at[k],
            send_sem=self.c_send.at[k],
            recv_sem=self.c_recv.at[k],
            device_id={DP: self.partner},
            device_id_type=MESH,
        )

    def launch(self, k):
        self.to_line(k).start()

    def tiles(self, run):
        @pl.loop(0, self.rows // TILE)
        def _(i):
            run(pl.ds(pl.multiple_of(i * TILE, TILE), TILE))

    def add_near(self, k, more=True):
        self.to_line(k).wait_send()
        self.to_line(k).wait_recv()
        if more:
            pl.when(k + self.window < self.near_last)(lambda: self.launch(k + self.window))

        def run(rows):
            for b in range(2):
                total = self.grads[k, b, rows, self.lanes(self.line)].astype(F32) + self.near[k, b, rows, :].astype(F32)
                self.near[k, b, rows, :] = total.astype(BF16)

        self.tiles(run)
        if more:
            pl.when(k < self.last)(lambda: self.hop(k))

    def hop(self, k):
        pl.when(self.place == 3)(self.inward(k).start)
        pl.when(self.holder)(self.beside(k).start)

    def add_mid(self, k):
        @pl.when(self.place == 2)
        def _():
            self.inward(k).wait_recv()

            def run(rows):
                for b in range(2):
                    total = self.near[k, b, rows, :].astype(F32) + self.far[k, b, rows, :].astype(F32)
                    self.near[k, b, rows, :] = total.astype(BF16)

            self.tiles(run)
            for shard in range(2):
                self.onward(k, shard).start()

    def add_far(self, k):
        @pl.when(self.holder)
        def _():
            self.beside(k).wait_recv()
            self.onward(k, 0).wait_recv()

            def run(rows):
                total = self.near[k, self.slot, rows, :].astype(F32)
                for seat in range(2):
                    total = total + self.far[k, seat, rows, :].astype(F32)
                self.outs[k, rows, :] = total.astype(BF16)

            self.tiles(run)
            self.to_core(k).start()

    def step(self, k, mid=1):
        self.add_near(k)
        if mid:
            pl.when(k - LAG >= self.first)(lambda: self.add_mid(k - LAG))

    def drain(self, begin):
        @pl.loop(begin, max(self.near_last, self.last + 2 * LAG))
        def _(i):
            pl.when(i < self.near_last)(lambda: self.add_near(i))
            j = i - LAG
            pl.when(jnp.logical_and(j >= self.first, j < self.last))(lambda: self.add_mid(j))
            n = j - LAG
            pl.when(jnp.logical_and(n < self.last, n >= self.first))(lambda: self.add_far(n))

    def far_before(self, begin):
        @pl.loop(self.first, jnp.maximum(self.first, begin - 2 * LAG))
        def _(k):
            self.add_far(k)

    def close(self, got):
        @pl.loop(self.first, self.last)
        def _(k):
            pl.when(self.place == 3)(self.inward(k).wait_send)

            @pl.when(self.place == 2)
            def _():
                for shard in range(2):
                    self.onward(k, shard).wait_send()

            @pl.when(self.holder)
            def _():
                self.beside(k).wait_send()
                self.to_core(k).wait_send()

            @pl.when(jnp.logical_and(jnp.logical_not(self.holder), k >= got))
            def _():
                self.to_core(k).wait_recv()


class Tail(NamedTuple):
    seg_col: Any
    seg_row: Any
    d_three: Any
    base: Any
    upstream: Any
    gains: Any
    smalls: Any
    hid: Any
    w_mlp: Any
    pre: Any
    act: Any
    w_in: Any
    x1: Any
    w_out: Any
    mixed: Any
    packed: Any
    tops: Any
    a_one: Any
    w_qkv: Any
    x0: Any


IMAGE_ONLY = Tail._fields[7:13]


def tail_kernel(pairs, scale, *refs):
    it = iter(refs)
    hbm = Tail(*[next(it) for _ in Tail._fields])
    cross_in, tower_rows = next(it), next(it)
    outs = next(it)
    small_out, grad_out, from_text, tower_out = next(it), next(it), next(it), next(it)
    vm = Tail(*[next(it) for _ in Tail._fields])
    grads, near, far = next(it), next(it), next(it)
    g_f32, g_low, grad_hid, grad_pre, d_packed, mix_grad = (next(it) for _ in range(6))
    part_send, part_recv, mask, smalls, small_near, small_all, own_grad = (next(it) for _ in range(7))
    load_sem, red_sems, part_sem, small_sem, move_sem, twin_sem = next(it), [next(it) for _ in range(6)], next(it), next(it), next(it), next(it)
    tower, dp, z, core, line, other, partner = spots()
    is_enc = tower == 0
    is_dec = tower == 1
    stays = z == 3 * core
    tokens, width = g_f32.shape
    rows_txt = tokens // LTXT
    quarter = tokens // 2
    heads = mix_grad.shape[1]
    rows_of = grads.shape[2]
    ffn_blocks = width // rows_of
    text_first = 2 * ffn_blocks - 2

    home = {DP: 2 * line + z // 2, MP: 2 * lax.rem(z, 2) + core}
    guest = {DP: 2 * line + lax.rem(z, 2), MP: 2 * core + z // 2}
    moved = jnp.logical_not(stays)
    peers = [(None, {DP: other}), (None, {DP: partner}), (is_enc, {TOWER: 1 - tower})]
    peers += [(None, {MP: lax.rem(z + away, 4)}) for away in range(1, 4)]
    peers += [(moved, home), (moved, guest)]
    def load(i):
        return pltpu.make_async_copy(hbm[i], vm[i], load_sem.at[i])

    def on_side(i, run):
        if Tail._fields[i] in IMAGE_ONLY:
            pl.when(is_enc)(run)
        else:
            run()

    pl.when(is_dec)(lambda: pltpu.make_async_copy(cross_in, near.at[pl.ds(text_first, 2)], load_sem.at[len(hbm)]).start())
    for i in range(len(hbm)):
        on_side(i, load(i).start)

    barrier_all(
        peers,
        [
            (jnp.logical_and(is_enc, stays), 5),
            (jnp.logical_and(is_enc, moved), 7),
            (jnp.logical_and(is_dec, stays), 6),
            (jnp.logical_and(is_dec, moved), 8),
        ],
    )

    def need(*wanted):
        for i, ref in enumerate(vm):
            if any(ref is one for one in wanted):
                on_side(i, load(i).wait)

    first_block = text_first * tower
    blocks = grads.shape[0]
    red = Reducer(grads, near, far, outs, red_sems, 2 + 2 * tower, first_block, blocks, blocks)

    def twin_copy():
        return pltpu.make_async_remote_copy(
            src_ref=outs.at[pl.ds(text_first, 2)],
            dst_ref=from_text,
            send_sem=twin_sem.at[0],
            recv_sem=twin_sem.at[1],
            device_id={TOWER: 1 - tower},
            device_id_type=MESH,
        )

    cross_load = pltpu.make_async_copy(cross_in, near.at[pl.ds(text_first, 2)], load_sem.at[len(hbm)])

    @pl.when(is_dec)
    def _():
        cross_load.wait()
        red.hop(text_first)
        red.hop(text_first + 1)

    def home_move(source, target, k):
        return pltpu.make_async_remote_copy(
            src_ref=source,
            dst_ref=target,
            send_sem=move_sem.at[k, 0],
            recv_sem=move_sem.at[k, 1],
            device_id=home,
            device_id_type=MESH,
        )

    @pl.when(moved)
    def _():
        home_move(tower_rows, tower_out, 0).start()

    @pl.when(stays)
    def _():
        pltpu.make_async_copy(tower_rows, own_grad, move_sem.at[0, 0]).start()
        pltpu.make_async_copy(tower_rows, own_grad, move_sem.at[0, 0]).wait()
        pltpu.make_async_copy(own_grad, tower_out, move_sem.at[0, 1]).start()
        pltpu.make_async_copy(own_grad, tower_out, move_sem.at[0, 1]).wait()

    def part_copy(k):
        return pltpu.make_async_remote_copy(
            src_ref=part_send.at[k],
            dst_ref=part_recv.at[k],
            send_sem=part_sem.at[k, 0],
            recv_sem=part_sem.at[k, 1],
            device_id={DP: partner},
            device_id_type=MESH,
        )

    zero = jnp.zeros((8, width), F32)
    need(vm.seg_col, vm.seg_row)
    fill_mask(mask, vm.seg_col, vm.seg_row, is_dec)
    need(vm.d_three, vm.base, vm.upstream, vm.gains, vm.smalls)
    smalls[...] = vm.smalls[...]

    def put(row, value):
        smalls[pl.ds(row, 1), :] = jnp.sum(value, axis=0, keepdims=True)

    def third(rows, kept):
        back, dg, db = norm_back_tile(vm.base[rows, :], vm.gains[2], vm.d_three[rows, :])
        total = vm.upstream[rows, :] + back
        g_f32[rows, :] = total
        low = total.astype(BF16)
        g_low[rows, :] = low
        return (kept[0] + dg, kept[1] + db, kept[2] + fold_rows(low.astype(F32)))

    dg, db, bias = row_tiles(tokens, third, (zero, zero, zero), 0, 3)
    put(4, dg)
    put(7, db)

    @pl.when(is_enc)
    def _():
        put(1, bias)
        need(vm.hid)

        @pl.loop(0, 2)
        def _(b):
            made = dot_first(vm.hid[:, pl.ds(pl.multiple_of(b * width, LANES), width)], g_low[...]).astype(BF16)
            grads[0:ffn_blocks, b] = made.reshape(ffn_blocks, rows_of, width)

        red.launch(0)
        need(vm.w_mlp, vm.pre)

        @pl.loop(0, 2)
        def _(b):
            cols = pl.ds(pl.multiple_of(b * width, LANES), width)
            grad_hid[...] = dot_rows(g_low[...], vm.w_mlp[cols, :])

            def bend(rows, kept):
                low = (grad_hid[rows, :] * gelu_both(vm.pre[rows, cols])[1]).astype(BF16)
                grad_pre[b, rows, :] = low
                return kept + fold_rows(low.astype(F32))

            put(9 + b, row_tiles(tokens, bend, zero))

        red.launch(1)
        need(vm.act, vm.w_in)

        @pl.loop(0, 2)
        def _(b):
            made = dot_first(grad_pre[b], vm.act[...]).astype(BF16)
            grads[ffn_blocks : 2 * ffn_blocks, b] = made.reshape(ffn_blocks, rows_of, width)

        red.step(0)
        grad_hid[...] = jnp.zeros_like(grad_hid)

        @pl.loop(0, 2)
        def _(b):
            grad_hid[...] += dot_rows(grad_pre[b], vm.w_in[b])

        def lower(rows, kept):
            part_send[0, rows, :] = grad_hid[rows, :].astype(BF16)
            return kept

        row_tiles(tokens, lower, 0)
        part_copy(0).start()
        need(vm.x1)
        part_copy(0).wait()

        def second(rows, kept):
            grad = part_send[0, rows, :].astype(F32) + part_recv[0, rows, :].astype(F32)
            back, dg, db = norm_back_tile(vm.x1[rows, :], vm.gains[1], grad)
            total = g_f32[rows, :] + back
            g_f32[rows, :] = total
            low = total.astype(BF16)
            g_low[rows, :] = low
            return (kept[0] + dg, kept[1] + db, kept[2] + fold_rows(low.astype(F32)))

        dg, db, bias_two = row_tiles(tokens, second, (zero, zero, zero), 0, 3)
        put(3, dg)
        put(6, db)
        put(0, bias_two)
        red.step(1)

    @pl.when(is_dec)
    def _():
        put(0, bias)

    need(vm.w_out, vm.mixed, vm.packed, vm.tops)
    mix_grad[...] = dot_rows(g_low[...], vm.w_out[...]).astype(BF16)
    grads[2 * ffn_blocks] = dot_first(vm.mixed[...], g_low[...]).astype(BF16).reshape(grads.shape[1:])


    @pl.when(is_enc)
    def _():
        red.step(2)

    @pl.when(is_dec)
    def _():
        red.launch(2 * ffn_blocks)

    def between():
        @pl.when(is_enc)
        def _():
            red.step(3)

    self_backward(vm.packed, mix_grad, vm.tops, mask, d_packed, pairs, scale, between)


    @pl.when(is_enc)
    def _():
        red.step(4)

    @pl.when(is_dec)
    def _():
        red.add_mid(text_first)

    now = 5 + (2 * ffn_blocks - 5) * tower


    need(vm.a_one, vm.w_qkv, vm.x0)

    @pl.loop(0, 3)
    def _(a):
        cols = pl.ds(pl.multiple_of(a * heads, LANES), heads)
        made = dot_first(d_packed[:, cols], vm.a_one[...]).astype(BF16)
        grads[2 * ffn_blocks + 1 + a] = made.reshape(grads.shape[1:])
        pl.when(is_dec)(lambda: red.launch(2 * ffn_blocks + 1 + a))

    red.step(now)
    grad_hid[...] = jnp.zeros_like(grad_hid)

    @pl.loop(0, 3)
    def _(a):
        cols = pl.ds(pl.multiple_of(a * heads, LANES), heads)
        grad_hid[...] += dot_plain(d_packed[:, cols], vm.w_qkv[cols, :])


    def lower_two(rows, kept):
        part_send[1, rows, :] = grad_hid[rows, :].astype(BF16)
        return (
            kept[0] + fold_rows(d_packed[rows, pl.ds(0, heads)].astype(F32)),
            kept[1] + fold_rows(d_packed[rows, pl.ds(2 * heads, heads)].astype(F32)),
        )

    small_zero = jnp.zeros((8, heads), F32)
    q_sum, v_sum = row_tiles(tokens, lower_two, (small_zero, small_zero))
    part_copy(1).start()
    pl.when(is_enc)(lambda: red.step(now + 1))
    smalls[8:9, :] = jnp.concatenate(
        [jnp.sum(q_sum, axis=0, keepdims=True), jnp.sum(v_sum, axis=0, keepdims=True)], axis=1
    )
    part_copy(1).wait()

    def first(rows, kept):
        grad = part_send[1, rows, :].astype(F32) + part_recv[1, rows, :].astype(F32)
        back, dg, db = norm_back_tile(vm.x0[rows, :].astype(F32), vm.gains[0], grad)
        part_send[1, rows, :] = (g_f32[rows, :] + back).astype(BF16)
        return (kept[0] + dg, kept[1] + db)

    dg, db = row_tiles(tokens, first, (zero, zero), 0, 3)
    put(2, dg)
    put(5, db)
    mine = pl.ds(pl.multiple_of(core * quarter, TILE), quarter)

    def own_copy(rows, kept):
        shifted = pl.ds(pl.multiple_of(core * quarter + rows.start, 32), rows.size)
        own_grad[rows, :] = part_send[1, shifted, :]
        return kept

    row_tiles(quarter, own_copy, 0)

    small_line = pltpu.make_async_remote_copy(
        src_ref=smalls,
        dst_ref=small_near,
        send_sem=small_sem.at[0],
        recv_sem=small_sem.at[1],
        device_id={DP: other},
        device_id_type=MESH,
    )
    small_line.start()

    @pl.when(moved)
    def _():
        home_move(own_grad, grad_out, 1).start()

    @pl.when(stays)
    def _():
        pltpu.make_async_copy(own_grad, grad_out, move_sem.at[1, 0]).start()


    def small_pair(sender, away):
        return pltpu.make_async_remote_copy(
            src_ref=small_all.at[sender],
            dst_ref=small_all.at[sender],
            send_sem=small_sem.at[1 + away],
            recv_sem=small_sem.at[4 + away],
            device_id={MP: lax.rem(z + away, 4)},
            device_id_type=MESH,
        )

    def small_core(which):
        return pltpu.make_async_remote_copy(
            src_ref=small_out.at[which],
            dst_ref=small_out.at[which],
            send_sem=small_sem.at[8],
            recv_sem=small_sem.at[9],
            device_id={DP: partner},
            device_id_type=MESH,
        )

    after = now + 2 - tower
    red.step(after)
    small_line.wait()
    small_all[z] = smalls[...] + small_near[...]


    for away in range(1, 4):
        small_pair(z, away).start()

    red.step(after + 1)
    for away in range(1, 4):
        small_pair(lax.rem(z + 4 - away, 4), away).wait_recv()
    small_out[core] = ((small_all[0] + small_all[1]) + small_all[2]) + small_all[3]
    small_core(core).start()
    red.far_before(after + 2)

    @pl.when(is_dec)
    def _():
        @pl.when(jnp.logical_not(red.holder))
        def _():
            for k in range(2):
                red.to_core(text_first + k).wait_recv()

        twin_copy().start()

    red.drain(after + 2)
    red.close((text_first + 2) * tower)

    for away in range(1, 4):
        small_pair(z, away).wait_send()

    @pl.when(moved)
    def _():
        home_move(tower_rows, tower_out, 0).wait()
        home_move(own_grad, grad_out, 1).wait()

    @pl.when(stays)
    def _():
        pltpu.make_async_copy(own_grad, grad_out, move_sem.at[1, 0]).wait()

    pl.when(is_dec)(twin_copy().wait_send)
    pl.when(is_enc)(twin_copy().wait_recv)
    small_core(core).wait_send()
    small_core(1 - core).wait_recv()


def tail(values, cross_grad, tower_rows, scale):
    tokens, width = values.base.shape
    heads = values.mixed.shape[1]
    pairs = heads // LANES
    hidden = values.pre.shape[1]
    quarter = tokens // 2
    half = width // 2
    rows_of = heads // 2
    blocks = 2 * (width // rows_of) + 4
    assert hidden == 2 * width and cross_grad.shape[0] == 2
    hbm = pl.BlockSpec(memory_space=pltpu.HBM)
    vmem = pl.BlockSpec(memory_space=pltpu.VMEM)
    n_in = len(values)
    scratch = [pltpu.VMEM(x.shape, x.dtype) for x in values]
    scratch += [pltpu.VMEM((blocks, 2, rows_of, width), BF16)]
    scratch += [pltpu.VMEM((blocks, 2, rows_of, half), BF16)] * 2
    scratch += [
        pltpu.VMEM((tokens, width), F32),
        pltpu.VMEM((tokens, width), BF16),
        pltpu.VMEM((tokens, width), F32),
        pltpu.VMEM((2, tokens, hidden // 2), BF16),
        pltpu.VMEM((tokens, 3 * heads), BF16),
        pltpu.VMEM((tokens, heads), BF16),
        pltpu.VMEM((2, tokens, width), BF16),
        pltpu.VMEM((2, tokens, width), BF16),
        pltpu.VMEM((tokens, tokens), F32),
        pltpu.VMEM(values.smalls.shape, F32),
        pltpu.VMEM(values.smalls.shape, F32),
        pltpu.VMEM((4,) + values.smalls.shape, F32),
        pltpu.VMEM((quarter, width), BF16),
    ]
    dma = pltpu.SemaphoreType.DMA
    scratch += [dma((n_in + 1,)), dma((blocks,)), dma((blocks,)), dma((blocks, 2)), dma((blocks, 2)), dma((blocks,)), dma((blocks,))]
    scratch += [dma((2, 2)), dma((10,)), dma((2, 2)), dma((2,))]
    out_shape = [jax.ShapeDtypeStruct((blocks, rows_of, half), BF16)]
    out_shape += [
        jax.ShapeDtypeStruct((2,) + values.smalls.shape, F32),
        jax.ShapeDtypeStruct((quarter, width), BF16),
        jax.ShapeDtypeStruct((2, heads // 2, half), BF16),
        jax.ShapeDtypeStruct((quarter, width), BF16),
    ]
    return pl.pallas_call(
        functools.partial(tail_kernel, pairs, scale),
        in_specs=[hbm] * (n_in + 2),
        out_specs=[vmem] * 2 + [hbm] * 3,
        out_shape=out_shape,
        scratch_shapes=scratch,
        compiler_params=pltpu.CompilerParams(
            collective_id=1, has_side_effects=True, vmem_limit_bytes=TAIL_LIMIT
        ),
        name="tail",
    )(*values, cross_grad, tower_rows)


class Head(NamedTuple):
    packed: Any
    mixed: Any
    tops: Any
    a_one: Any
    x1: Any
    base: Any
    act_three: Any
    act: Any
    pre: Any
    hid: Any
    query: Any


def head_kernel(pieces, pairs, scale, *refs):
    it = iter(refs)
    srcs = [next(it) for _ in range(5)]
    blocks = [next(it)]
    seg_ref, image_ref = next(it), next(it)
    gains, shifts, out_b, ffn_out_b, ffn_in_b, qv_b = (next(it) for _ in range(6))
    outs = [next(it) for _ in range(5)]
    tokens = [next(it)]
    seg_out = [next(it) for _ in range(3)]
    hbm = Head(*[next(it) for _ in Head._fields])
    stages = [next(it) for _ in range(5)]
    weight_sems = [next(it) for _ in range(5)]
    token_stage = next(it)
    token_sems = [next(it) for _ in range(3)]
    w_qkv, w_out, w_q, w_in, w_mlp = (next(it) for _ in range(5))
    vm = Head(*[next(it) for _ in Head._fields])
    part_send, part_recv, raw, mask = next(it), next(it), next(it), next(it)
    seg_sem, load_sem, store_sem, part_sem = (next(it) for _ in range(4))
    tower, dp, z, core, line, other, partner = spots()
    is_enc = tower == 0
    is_dec = tower == 1
    stays = z == 3 * core
    moved = jnp.logical_not(stays)
    count, width = vm.x1.shape
    rows_txt = count // LTXT
    heads = vm.mixed.shape[1]
    at_end = jnp.logical_or(z == 0, z == 3)

    peers = [(z > 0, {MP: z - 1}), (z < 3, {MP: z + 1})]
    peers += [(None, {DP: other}), (None, {TOWER: 1 - tower}), (None, {DP: partner})]
    peers += [
        (moved, {DP: 2 * line + lax.rem(z, 2), MP: 2 * core + z // 2}),
        (moved, {DP: 2 * line + z // 2, MP: 2 * lax.rem(z, 2) + core}),
    ]
    barrier_all(
        peers,
        [(stays, 4), (jnp.logical_and(at_end, moved), 6), (jnp.logical_not(at_end), 7)],
    )

    begin, begin_local, pass_on, arrived, sent, end_local, end_twin = weight_steps(
        pieces, srcs, outs, stages, weight_sems, 1
    )
    token_begin, token_relay, token_finish = token_steps(blocks, tokens, token_stage, token_sems)
    token_begin(0)
    begin()

    has_notes = core == z // 2

    def note_send(i):
        return pltpu.make_async_remote_copy(
            src_ref=seg_out[i],
            dst_ref=seg_out[i],
            send_sem=seg_sem.at[i, 0],
            recv_sem=seg_sem.at[i, 1],
            device_id={DP: partner},
            device_id_type=MESH,
        )

    @pl.when(has_notes)
    def _():
        rows = seg_ref.shape[0] // 2
        side = lax.rem(z, 2)
        segs = jnp.where(side == 0, seg_ref[0:rows, :], seg_ref[rows : 2 * rows, :])
        marks = segs + LTXT * lax.broadcasted_iota(jnp.int32, segs.shape, 0)
        tall = jnp.concatenate([marks.astype(F32), jnp.zeros((16 - rows, LTXT), F32)], axis=0).T
        seg_out[1][...] = jnp.zeros_like(seg_out[1])
        for r in range(rows):
            at = pl.ds(r * LTXT, LTXT)
            seg_out[0][at, :] = jnp.broadcast_to(tall[:, r : r + 1], (LTXT, LANES)).astype(jnp.int32)
            seg_out[1][0:1, at] = marks[r : r + 1, :]
            seg_out[2][at, :] = jnp.full((LTXT, LANES), image_ref[side * rows + r], jnp.int32)
        for i in range(3):
            note_send(i).start()

    begin_local()
    token_relay(0)

    def load(i, target, source):
        return pltpu.make_async_copy(source, target, load_sem.at[i])

    def store(ref):
        i = [x is ref for x in vm].index(True)
        return pltpu.make_async_copy(vm[i], hbm[i], store_sem.at[i])

    def part_copy(k):
        return pltpu.make_async_remote_copy(
            src_ref=part_send.at[k],
            dst_ref=part_recv.at[k],
            send_sem=part_sem.at[k, 0],
            recv_sem=part_sem.at[k, 1],
            device_id={DP: partner},
            device_id_type=MESH,
        )

    def last_copy(i):
        rows = pl.ds(pl.multiple_of(i * (count // 2), 32), count // 2)
        return pltpu.make_async_remote_copy(
            src_ref=part_send.at[1, rows, :],
            dst_ref=part_recv.at[1, rows, :],
            send_sem=part_sem.at[1 + i, 0],
            recv_sem=part_sem.at[1 + i, 1],
            device_id={DP: partner},
            device_id_type=MESH,
        )

    def normed(source, target, which):
        gain, shift = gains[which], shifts[which]

        def tile(rows, kept):
            unit, _ = norm_parts(source[rows, :].astype(F32))
            target[rows, :] = (unit * gain + shift).astype(BF16)
            return kept

        row_tiles(count, tile, 0, 0, 3)

    def chosen(which, flag, far=False):
        return [k for k, p in enumerate(pieces) if p[0] == which and p[6] == flag and p[7] == far]

    enc_in, enc_mlp, dec_in = chosen(3, 0), chosen(4, 0), chosen(3, 1) + chosen(4, 1)
    k_qkv, k_out, k_own, k_far = chosen(0, None), chosen(1, None), chosen(2, 1), chosen(2, 1, True)
    waiting = {0: enc_in + enc_mlp, 1: k_own + k_far + dec_in}

    def relay(enc=0, dec=0):
        for t, count in ((0, enc), (1, dec)):
            for k in waiting[t][:count]:
                pass_on(k)
            waiting[t] = waiting[t][count:]

    token_finish(0)
    normed(tokens[0], vm.a_one, 0)
    store(vm.a_one).start()
    for k in k_qkv + k_out:
        pass_on(k)
    for k in k_qkv:
        arrived(k)
    end_local(0)
    load(0, w_qkv, outs[0]).start()
    load(0, w_qkv, outs[0]).wait()

    @pl.loop(0, 3)
    def _(part):
        cols = pl.ds(pl.multiple_of(part * heads, LANES), heads)
        own = pl.ds(pl.multiple_of(core * heads, LANES), heads)
        bias = jnp.where(part == 1, 0.0, qv_b[pl.ds(part // 2, 1), own])
        made = dot_rows(vm.a_one[...], w_qkv[part].reshape(heads, width)) + bias
        vm.packed[:, cols] = made.astype(BF16)

    store(vm.packed).start()

    @pl.when(has_notes)
    def _():
        for i in range(3):
            note_send(i).wait_send()

    @pl.when(jnp.logical_not(has_notes))
    def _():
        for i in range(3):
            note_send(i).wait_recv()

    relay(1, 1)
    fill_mask(mask, seg_out[0], seg_out[1], is_dec)
    self_forward(vm.packed, mask, vm.mixed, vm.tops, pairs, scale)
    store(vm.mixed).start()
    store(vm.tops).start()
    for k in k_out:
        arrived(k)
    end_local(1)
    load(1, w_out, outs[1]).start()
    relay(1, 1)
    load(1, w_out, outs[1]).wait()
    part_send[0] = dot_plain(vm.mixed[...], w_out[0].reshape(heads, width)).astype(BF16)
    part_copy(0).start()
    relay(1, 1)
    part_copy(0).wait()

    def add_one(rows, kept):
        total = part_send[0, rows, :].astype(F32) + part_recv[0, rows, :].astype(F32)
        vm.x1[rows, :] = tokens[0][rows, :].astype(F32) + total + out_b[...]
        return kept

    row_tiles(count, add_one, 0)
    store(vm.x1).start()

    @pl.when(is_enc)
    def _():
        relay(1)
        normed(vm.x1, vm.act, 1)
        store(vm.act).start()
        relay(1)
        for k in enc_in:
            arrived(k)
        end_local(3)
        load(3, w_in, outs[3]).start()
        load(3, w_in, outs[3]).wait()
        relay(1)

        @pl.loop(0, 2)
        def _(b):
            cols = pl.ds(pl.multiple_of(b * width, LANES), width)
            raw[...] = dot_plain(vm.act[...], w_in[0, b])
            bias = ffn_in_b[0:1, pl.ds(pl.multiple_of((2 * core + b) * width, LANES), width)]

            def bend(rows, kept):
                pre = raw[rows, :] + bias
                vm.pre[rows, cols] = pre
                vm.hid[rows, cols] = gelu_tanh(pre).astype(BF16)
                return kept

            row_tiles(count, bend, 0)

        relay(1)
        store(vm.pre).start()
        store(vm.hid).start()
        cut = width // 2
        raw[...] = jnp.zeros_like(raw)
        end_local(4)

        def half_load(i):
            rows = pl.ds(i * cut, cut)
            return load(4, w_mlp.at[:, :, rows, :], outs[4].at[:, :, rows, :])

        for k in enc_mlp[:2]:
            arrived(k)
        half_load(0).start()
        relay(len(waiting[0]))
        half_load(0).wait()

        @pl.loop(0, 2)
        def _(b):
            raw[...] += dot_plain(vm.hid[:, pl.ds(pl.multiple_of(b * width, LANES), cut)], w_mlp[0, b, 0:cut, :])

        for k in enc_mlp[2:]:
            arrived(k)
        half_load(1).start()
        half_load(1).wait()
        half = count // 2

        @pl.loop(0, 2)
        def _(i):
            rows = pl.ds(pl.multiple_of(i * half, 32), half)
            made = raw[rows, :]
            for b in range(2):
                made = made + dot_plain(vm.hid[rows, pl.ds(b * width + cut, cut)], w_mlp[0, b, cut:width, :])
            part_send[1, rows, :] = made.astype(BF16)
            last_copy(i).start()

        def add_two(rows, kept):
            total = part_send[1, rows, :].astype(F32) + part_recv[1, rows, :].astype(F32)
            value = vm.x1[rows, :] + total + ffn_out_b[...]
            vm.base[rows, :] = value
            unit, _ = norm_parts(value)
            vm.act_three[rows, :] = (unit * gains[2] + shifts[2]).astype(BF16)
            return kept

        @pl.loop(0, 2)
        def _(i):
            last_copy(i).wait()
            row_tiles(half, add_two, 0, i * half)


    @pl.when(is_dec)
    def _():
        def same(rows, kept):
            vm.base[rows, :] = vm.x1[rows, :]
            return kept

        row_tiles(count, same, 0)
        normed(vm.base, vm.act_three, 2)

    store(vm.act_three).start()
    store(vm.base).start()

    @pl.when(is_dec)
    def _():
        relay(0, 2)
        for k in k_own:
            arrived(k)
        end_local(2)
        load(2, w_q, outs[2].at[2]).start()
        load(2, w_q, outs[2].at[2]).wait()
        vm.query[...] = dot_rows(vm.act_three[...], w_q[...].reshape(heads, width)).astype(BF16)
        store(vm.query).start()
        relay(0, len(waiting[1]))
        for k in k_far + dec_in:
            arrived(k)
        end_local(3)
        end_local(4)

    for k in range(len(pieces)):
        sent(k)
    end_twin()
    for ref in vm:
        if ref is vm.act or ref is vm.pre or ref is vm.hid:
            pl.when(is_enc)(store(ref).wait)
        elif ref is vm.query:
            pl.when(is_dec)(store(ref).wait)
        else:
            store(ref).wait()


def head(shards, blocks, segment_ids, row_image, vecs, scale):
    qkv, out, cross, ffn_in, ffn_out = shards
    heads = 2 * out.shape[1]
    width = out.shape[2]
    pairs = heads // LANES
    count = 2 * blocks[0].shape[0]
    hidden = 2 * ffn_in.shape[2]

    def cuts(i, flag):
        blocks_of, rows, _ = shards[i].shape
        cut = rows if rows <= 192 else rows // 4
        return [(i, a, a, 1, at, cut, flag, False) for a in range(blocks_of) for at in range(0, rows, cut)]

    pieces = cuts(0, None) + cuts(1, None)
    rows = cross.shape[1]
    pieces += [(2, 2 + a, a, 1, 0, rows, 1, False) for a in range(2)] + [(2, a, a, 1, 0, rows, 1, True) for a in range(2)]
    pieces += cuts(3, 0) + cuts(4, 0) + cuts(3, 1) + cuts(4, 1)[:2]
    n = len(pieces)
    hbm = pl.BlockSpec(memory_space=pltpu.HBM)
    vmem = pl.BlockSpec(memory_space=pltpu.VMEM)
    struct = jax.ShapeDtypeStruct
    made = Head(
        packed=struct((count, 3 * heads), BF16),
        mixed=struct((count, heads), BF16),
        tops=struct((pairs, 8, 2 * count), F32),
        a_one=struct((count, width), BF16),
        x1=struct((count, width), F32),
        base=struct((count, width), F32),
        act_three=struct((count, width), BF16),
        act=struct((count, width), BF16),
        pre=struct((count, hidden), F32),
        hid=struct((count, hidden), BF16),
        query=struct((count, heads), BF16),
    )
    out_shape = [
        jax.ShapeDtypeStruct(((2 if i == 2 else 1) * x.shape[0], 2) + x.shape[1:], BF16) for i, x in enumerate(shards)
    ]
    out_shape += [jax.ShapeDtypeStruct((count, width), BF16)]
    out_shape += [struct((count, LANES), jnp.int32), struct((8, count), jnp.int32), struct((count, LANES), jnp.int32)]
    out_shape += list(made)
    dma = pltpu.SemaphoreType.DMA
    scratch = [pltpu.VMEM(x.shape, BF16) for x in shards]
    scratch += [dma((n, 5)), dma((n, 4)), dma((5, 2)), dma, dma]
    scratch += [pltpu.VMEM((1,) + blocks[0].shape, BF16), dma((1, 2)), dma((1, 2)), dma((1, 2))]
    scratch += [
        pltpu.VMEM((3, 2) + qkv.shape[1:], BF16),
        pltpu.VMEM((1, 2) + out.shape[1:], BF16),
        pltpu.VMEM((2,) + cross.shape[1:], BF16),
        pltpu.VMEM((1, 2) + ffn_in.shape[1:], BF16),
        pltpu.VMEM((1, 2) + ffn_out.shape[1:], BF16),
    ]
    scratch += [pltpu.VMEM(x.shape, x.dtype) for x in made]
    scratch += [
        pltpu.VMEM((2, count, width), BF16),
        pltpu.VMEM((2, count, width), BF16),
        pltpu.VMEM((count, width), F32),
        pltpu.VMEM((count, count), F32),
        dma((3, 2)),
        dma((5,)),
        dma((len(made),)),
        dma((3, 2)),
    ]
    results = pl.pallas_call(
        functools.partial(head_kernel, tuple(pieces), pairs, scale),
        in_specs=[hbm] * 6 + [vmem, pl.BlockSpec(memory_space=pltpu.SMEM)] + [vmem] * 6,
        out_specs=[hbm] * 5 + [vmem] + [vmem] * 3 + [hbm] * len(made),
        out_shape=out_shape,
        scratch_shapes=scratch,
        compiler_params=pltpu.CompilerParams(
            collective_id=0, has_side_effects=True, vmem_limit_bytes=VMEM_LIMIT
        ),
        name="head",
    )(*shards, *blocks, segment_ids, row_image, *vecs)
    return results[:5], results[5], results[6:9], Head(*results[9:])


CHUNKS = 6


def mid_kernel(pieces, pairs, scale, *refs):
    it = iter(refs)
    act_three, x1, query_in, w_cross_in, w_in_in, w_mlp_in, ffn_shard, cot_block, base = (next(it) for _ in range(9))
    gains, shifts, out_b, ffn_out_b, ffn_in_b, qv_b, picks = (next(it) for _ in range(7))
    d_three, upstream, smalls, tower_out, cross_out = (next(it) for _ in range(5))
    outs = next(it)
    stages = [next(it)]
    weight_sems = [next(it) for _ in range(5)]
    token_stage = next(it)
    token_sems = [next(it) for _ in range(3)]
    images, kv, w_cross, w_in, w_mlp = (next(it) for _ in range(5))
    act_txt, query, mixed, tops, y1, y2, act, pre, hid = (next(it) for _ in range(9))
    grad_hid, raw, grad_pre, g_low, mix_grad, dq, dkv, sum_q = (next(it) for _ in range(8))
    keys, vals, dk, dv = kv.at[0], kv.at[1], dkv.at[0], dkv.at[1]
    cot, part_send, part_recv, halves, half_near, sums, image_grad, own_rows = (next(it) for _ in range(8))
    grads, near, far = (next(it) for _ in range(3))
    red_sems = [next(it) for _ in range(6)]
    load_sem, store_sem, part_sem, twin_sem, side_sem, core_sem, half_sem, sum_sem, back_sem, give_sem, home_sem = it
    tower, dp, z, core, line, other, partner = spots()
    is_enc = tower == 0
    is_dec = tower == 1
    stays = z == 3 * core
    moved = jnp.logical_not(stays)
    side = lax.rem(z, 2)
    across_chip = z + 1 - 2 * side
    count, width = y1.shape
    quarter = count // 2
    chunk = quarter // CHUNKS
    heads = mixed.shape[1]

    home = {DP: 2 * line + z // 2, MP: 2 * lax.rem(z, 2) + core}
    guest = {DP: 2 * line + lax.rem(z, 2), MP: 2 * core + z // 2}
    peers = [(None, {DP: other}), (None, {DP: partner}), (None, {TOWER: 1 - tower})]
    peers += [(None, {MP: lax.rem(z + away, 4)}) for away in range(1, 4)]
    peers += [(moved, home), (moved, guest)]
    barrier_all(peers, [(stays, 6), (moved, 8)])

    def remote(source, target, sends, recvs, where):
        return pltpu.make_async_remote_copy(
            src_ref=source,
            dst_ref=target,
            send_sem=sends,
            recv_sem=recvs,
            device_id=where,
            device_id_type=MESH,
        )

    def span(which_core, i):
        return pl.ds(pl.multiple_of(which_core * quarter + i * chunk, 16), chunk)

    def twin_copy(i):
        rows = span(core, i)
        return remote(
            act_three.at[rows, :], images.at[side, rows, :], twin_sem.at[i, 0], twin_sem.at[i, 1], {TOWER: 1 - tower}
        )

    def side_copy(i, image):
        here = images.at[image, span(core, i), :]
        return remote(here, here, side_sem.at[i, 0], side_sem.at[i, 1], {MP: across_chip})

    def core_copy(i, image, which_core, far_image):
        here = images.at[image, span(which_core, i), :]
        return remote(here, here, core_sem.at[far_image, i, 0], core_sem.at[far_image, i, 1], {DP: partner})

    @pl.when(is_enc)
    def _():
        for i in range(CHUNKS):
            twin_copy(i).start()

    token_begin, token_relay, token_finish = token_steps([cot_block], [cot], token_stage, token_sems)
    pl.when(is_enc)(functools.partial(token_begin, 0))
    begin, begin_local, pass_on, arrived, sent, end_local, _ = weight_steps(
        pieces, [ffn_shard], [w_mlp], stages, weight_sems, 0
    )

    def load(i, source, target):
        return pltpu.make_async_copy(source, target, load_sem.at[i])

    held = pl.ds(0, ffn_shard.shape[1] // 2)
    early = [load(5, w_mlp_in.at[:, :, held, :], w_mlp.at[:, :, held, :])]
    text_loads = [
        load(0, w_cross_in, w_cross),
        load(1, query_in, query),
        load(2, x1, y1),
        load(3, w_in_in, w_in),
        load(4, act_three, act_txt),
    ]

    def part_copy(k, h):
        rows = pl.ds(pl.multiple_of(h * quarter, 32), quarter)
        return remote(
            part_send.at[k % 3, rows, :],
            part_recv.at[k % 3, rows, :],
            part_sem.at[k, h, 0],
            part_sem.at[k, h, 1],
            {DP: partner},
        )

    rows_copy = pltpu.make_async_copy(own_rows, tower_out, home_sem.at[0])

    def back_copy(i):
        rows = pl.ds(i * chunk, chunk)
        return remote(
            sums.at[1, rows, :], image_grad.at[span(core, i), :], back_sem.at[i, 0], back_sem.at[i, 1], {TOWER: 1 - tower}
        )

    def back_core(i, which_core):
        here = image_grad.at[span(which_core, i), :]
        return remote(here, here, give_sem.at[i, 0], give_sem.at[i, 1], {DP: partner})

    store_grad = pltpu.make_async_copy(y2, upstream, store_sem.at[0])
    store_three = pltpu.make_async_copy(raw, d_three, store_sem.at[1])
    zero = jnp.zeros((8, width), F32)
    blocks, rows_of = outs.shape[0], outs.shape[1]
    ffn_blocks = width // rows_of
    red = Reducer(grads, near, far, outs, red_sems, 4, 0, blocks, blocks + 2)

    @pl.when(is_enc)
    def _():
        smalls[...] = jnp.zeros_like(smalls)
        mine = pl.ds(pl.multiple_of(core * quarter, TILE), quarter)
        take = load(2, base.at[mine, :], y1.at[pl.ds(0, quarter), :])
        take.start()
        take.wait()

        def lower(rows, kept):
            own_rows[rows, :] = y1[rows, :].astype(BF16)
            return kept

        row_tiles(quarter, lower, 0)
        rows_copy.start()
        token_relay(0)
        token_finish(0)

        def lift(rows, kept):
            y2[rows, :] = cot[rows, :].astype(F32)
            return kept

        row_tiles(count, lift, 0)
        store_grad.start()
        for i in range(CHUNKS):
            back_copy(i).wait_recv()
            back_core(i, core).start()
        for i in range(CHUNKS):
            back_core(i, 1 - core).wait_recv()

        def lift_three(rows, kept):
            raw[rows, :] = image_grad[rows, :].astype(F32)
            return kept

        row_tiles(count, lift_three, 0)
        store_three.start()
        for i in range(CHUNKS):
            twin_copy(i).wait_send()
            back_core(i, core).wait_send()

    @pl.when(is_dec)
    def _():
        begin()
        for one in early + text_loads:
            one.start()
        for one in early:
            one.wait()
        begin_local()
        smalls[...] = jnp.zeros_like(smalls)

        def put(row, value):
            smalls[pl.ds(row, 1), :] = jnp.sum(value, axis=0, keepdims=True)

        for i in range(CHUNKS):
            twin_copy(i).wait_recv()
            side_copy(i, side).start()
            core_copy(i, side, core, 0).start()
        for k in range(len(pieces)):
            pass_on(k)
        for one in text_loads[:2]:
            one.wait()
        mixed[...] = jnp.zeros_like(mixed)
        for i in range(CHUNKS):
            core_copy(i, side, 1 - core, 0).wait_recv()

        @pl.loop(0, 2)
        def _(turn):
            image = side + turn * (1 - 2 * side)

            @pl.when(turn == 1)
            def _():
                for i in range(CHUNKS):
                    side_copy(i, 1 - side).wait_recv()
                    core_copy(i, 1 - side, core, 1).start()
                token_begin(0)
                for i in range(CHUNKS):
                    core_copy(i, 1 - side, 1 - core, 1).wait_recv()

            @pl.loop(0, 2)
            def _(part):
                kv[part, image] = dot_rows(images[image], w_cross[part].reshape(heads, width)).astype(BF16)

            cross_forward(image, query, keys, vals, picks, mixed, tops, pairs, scale)

        token_relay(0)

        def half_part(k, made):
            @pl.loop(0, 2)
            def _(h):
                rows = pl.ds(pl.multiple_of(h * quarter, 32), quarter)
                part_send[k % 3, rows, :] = made(rows).astype(BF16)
                part_copy(k, h).start()

        def add_halves(k, run, carry):
            def half(h, kept):
                part_copy(k, h).wait()
                return row_tiles(quarter, run, kept, h * quarter)

            return lax.fori_loop(0, 2, half, carry)

        half_part(0, lambda rows: dot_plain(mixed[rows, :], w_cross[3].reshape(heads, width)))
        for one in text_loads[2:]:
            one.wait()
        gain, shift = gains[1], shifts[1]

        def add_cross(rows, kept):
            total = part_send[0, rows, :].astype(F32) + part_recv[0, rows, :].astype(F32)
            value = y1[rows, :] + total
            y2[rows, :] = value
            unit, _ = norm_parts(value)
            act[rows, :] = (unit * gain + shift).astype(BF16)
            return kept

        token_finish(0)
        for k in range(len(pieces)):
            arrived(k)
        end_local(0)

        @pl.loop(0, 2)
        def _(b):
            grad_hid[b] = dot_rows(cot[...], w_mlp[0, b])

        add_halves(0, add_cross, 0)

        @pl.loop(0, 2)
        def _(b):
            cols = pl.ds(pl.multiple_of(b * width, LANES), width)
            pre[...] = dot_plain(act[...], w_in[0, b])
            bias = ffn_in_b[0:1, pl.ds(pl.multiple_of((2 * core + b) * width, LANES), width)]

            def bend(rows, kept):
                lifted, slope = gelu_both(pre[rows, :] + bias)
                hid[rows, cols] = lifted.astype(BF16)
                low = (grad_hid[b, rows, :] * slope).astype(BF16)
                grad_pre[b, rows, :] = low
                return kept + fold_rows(low.astype(F32))

            put(9 + b, row_tiles(count, bend, zero))

        half_part(2, lambda rows: dot_rows(grad_pre[0, rows, :], w_in[0, 0]) + dot_rows(grad_pre[1, rows, :], w_in[0, 1]))

        @pl.loop(0, 2)
        def _(b):
            made = dot_first(grad_pre[b], act[...]).astype(BF16)
            grads[0:ffn_blocks, b] = made.reshape(ffn_blocks, rows_of, width)

        red.launch(0)
        red.launch(1)

        def second(rows, kept):
            low_cot = cot[rows, :].astype(F32)
            grad = part_send[2, rows, :].astype(F32) + part_recv[2, rows, :].astype(F32)
            back, dg, db = norm_back_tile(y2[rows, :], gain, grad)
            total = low_cot + back
            raw[rows, :] = total
            g_low[rows, :] = total.astype(BF16)
            return (kept[0] + dg, kept[1] + db, kept[2] + fold_rows(low_cot))

        dg, db, cot_sum = add_halves(2, second, (zero, zero, zero))
        put(3, dg)
        put(6, db)
        put(1, cot_sum)

        mix_grad[...] = dot_rows(g_low[...], w_cross[3].reshape(heads, width)).astype(BF16)
        cross_backward(query, keys, vals, mix_grad, picks, tops, dq, dk, dv, sum_q, pairs, scale)

        def half_copy(image, far_image):
            return remote(
                halves.at[image, pl.ds(pl.multiple_of((1 - core) * quarter, TILE), quarter), :],
                half_near.at[far_image],
                half_sem.at[far_image, 0],
                half_sem.at[far_image, 1],
                {DP: partner},
            )

        @pl.loop(0, 2)
        def _(i):
            image = side + (1 - i) * (1 - 2 * side)
            made = dot_plain(dkv[0, image], w_cross[0].reshape(heads, width))
            made = made + dot_plain(dkv[1, image], w_cross[1].reshape(heads, width))
            halves[image] = made.astype(BF16)
            half_copy(image, 1 - i).start()

        def sum_copy(i):
            rows = pl.ds(i * chunk, chunk)
            return remote(
                sums.at[0, rows, :], sums.at[2, rows, :], sum_sem.at[i, 0], sum_sem.at[i, 1], {MP: across_chip}
            )

        half_copy(1 - side, 1).wait_recv()
        for i in range(CHUNKS):

            def add_far(rows, kept):
                at = pl.ds(pl.multiple_of(i * chunk + rows.start, 16), rows.size)
                own = pl.ds(pl.multiple_of(core * quarter + i * chunk + rows.start, 16), rows.size)
                total = halves[1 - side, own, :].astype(F32) + half_near[1, at, :].astype(F32)
                sums[0, at, :] = total.astype(BF16)
                return kept

            row_tiles(chunk, add_far, 0)
            sum_copy(i).start()
        for k in range(2):
            red.add_near(k, False)
            red.launch(k + 2)

        @pl.loop(0, 2)
        def _(b):
            cols = pl.ds(pl.multiple_of(b * width, LANES), width)
            made = dot_first(hid[:, cols], cot[...]).astype(BF16)
            grads[ffn_blocks : 2 * ffn_blocks, b] = made.reshape(ffn_blocks, rows_of, width)

        red.launch(4)
        red.launch(5)
        half_copy(side, 0).wait_recv()
        for i in range(CHUNKS):
            sum_copy(i).wait_recv()

            def add_own(rows, kept):
                at = pl.ds(pl.multiple_of(i * chunk + rows.start, 16), rows.size)
                own = pl.ds(pl.multiple_of(core * quarter + i * chunk + rows.start, 16), rows.size)
                total = halves[side, own, :].astype(F32) + half_near[0, at, :].astype(F32)
                sums[1, at, :] = (total + sums[2, at, :].astype(F32)).astype(BF16)
                return kept

            row_tiles(chunk, add_own, 0)
            back_copy(i).start()

        half_part(3, lambda rows: dot_plain(dq[rows, :], w_cross[2].reshape(heads, width)))
        red.hop(0)
        red.hop(1)
        red.step(2, 0)

        def keep_two(rows, kept):
            y1[rows, :] = raw[rows, :]
            return kept

        row_tiles(count, keep_two, 0)
        pltpu.make_async_copy(y1, upstream, store_sem.at[0]).start()

        def lift_query(rows, kept):
            raw[rows, :] = part_send[0, rows, :].astype(F32) + part_recv[0, rows, :].astype(F32)
            return kept

        add_halves(3, lift_query, 0)
        store_three.start()
        pre[...] = jnp.zeros_like(pre)

        @pl.loop(0, 2)
        def _(b):
            pre[...] += dot_plain(hid[:, pl.ds(pl.multiple_of(b * width, LANES), width)], w_mlp[0, b])

        for h in range(2):
            rows = pl.ds(h * quarter, quarter)
            part_send[1, rows, :] = pre[rows, :].astype(BF16)
            part_copy(1, h).start()
        red.add_mid(0)
        red.step(3, 0)
        red.add_mid(1)
        grads[2 * ffn_blocks] = dot_first(dq[...], act_txt[...]).astype(BF16).reshape(grads.shape[1:])
        grads[2 * ffn_blocks + 1] = dot_first(mixed[...], g_low[...]).astype(BF16).reshape(grads.shape[1:])
        red.add_mid(2)
        red.step(4)

        @pl.loop(0, 2)
        def _(which):
            made = dot_first(dkv[which, 0], images[0]) + dot_first(dkv[which, 1], images[1])
            grads[blocks + which] = made.astype(BF16).reshape(grads.shape[1:])

        red.step(5)
        for h in range(2):
            part_copy(1, h).wait()

        def add_last(rows, kept):
            own = pl.ds(pl.multiple_of(core * quarter + rows.start, 32), rows.size)
            total = part_send[1, own, :].astype(F32) + part_recv[1, own, :].astype(F32)
            own_rows[rows, :] = (y2[own, :] + total + ffn_out_b[...]).astype(BF16)
            return kept

        row_tiles(quarter, add_last, 0)
        rows_copy.start()
        red.far_before(6)
        red.drain(6)
        store_cross = pltpu.make_async_copy(near.at[pl.ds(blocks, 2)], cross_out, store_sem.at[2])
        store_cross.start()
        red.close(0)
        store_cross.wait()
        for i in range(CHUNKS):
            side_copy(i, side).wait_send()
            core_copy(i, side, core, 0).wait_send()
            core_copy(i, 1 - side, core, 1).wait_send()
            sum_copy(i).wait_send()
            back_copy(i).wait_send()
        half_copy(1 - side, 1).wait_send()
        half_copy(side, 0).wait_send()
        for k in range(len(pieces)):
            sent(k)

    rows_copy.wait()
    store_grad.wait()
    store_three.wait()


def middle(values, w_cross, w_in, w_mlp, ffn_shard, cot_block, vecs, picks, scale):
    count, width = values.base.shape
    heads = values.mixed.shape[1]
    pairs = heads // LANES
    hidden = values.hid.shape[1]
    quarter = count // 2
    half = width // 2
    chunk = quarter // CHUNKS
    assert chunk * CHUNKS == quarter
    rows_of = heads // 2
    blocks = 2 * (width // rows_of) + 2
    assert hidden == 2 * width
    cross_shape = (2, 2, rows_of, half)
    rows = ffn_shard.shape[1]
    pieces = [(0, 0, 0, 1, at, rows // 4, 1, False) for at in range(rows // 2, rows, rows // 4)]
    n = len(pieces)
    hbm = pl.BlockSpec(memory_space=pltpu.HBM)
    vmem = pl.BlockSpec(memory_space=pltpu.VMEM)
    dma = pltpu.SemaphoreType.DMA
    low, wide = (count, width), (count, heads)
    scratch = [pltpu.VMEM(ffn_shard.shape, BF16), dma((n, 5)), dma((n, 4)), dma((1, 2)), dma, dma]
    scratch += [pltpu.VMEM((1,) + cot_block.shape, BF16), dma((1, 2)), dma((1, 2)), dma((1, 2))]
    scratch += [
        pltpu.VMEM((2,) + low, BF16),
        pltpu.VMEM((2, 2) + wide, BF16),
        pltpu.VMEM((4, 2, heads // 2, width), BF16),
        pltpu.VMEM((1, 2, width, hidden // 2), BF16),
        pltpu.VMEM((1, 2, hidden // 2, width), BF16),
        pltpu.VMEM(low, BF16),
        pltpu.VMEM(wide, BF16),
        pltpu.VMEM(wide, BF16),
        pltpu.VMEM((2, pairs, 8, 2 * count), F32),
        pltpu.VMEM(low, F32),
        pltpu.VMEM(low, F32),
        pltpu.VMEM(low, BF16),
        pltpu.VMEM(low, F32),
        pltpu.VMEM((count, hidden), BF16),
        pltpu.VMEM((2,) + low, F32),
        pltpu.VMEM(low, F32),
        pltpu.VMEM((2, count, hidden // 2), BF16),
        pltpu.VMEM(low, BF16),
        pltpu.VMEM(wide, BF16),
        pltpu.VMEM(wide, BF16),
        pltpu.VMEM((2, 2) + wide, BF16),
        pltpu.VMEM((count, LANES), F32),
        pltpu.VMEM(low, BF16),
        pltpu.VMEM((3,) + low, BF16),
        pltpu.VMEM((3,) + low, BF16),
        pltpu.VMEM((2,) + low, BF16),
        pltpu.VMEM((2, quarter, width), BF16),
        pltpu.VMEM((3, quarter, width), BF16),
        pltpu.VMEM(low, BF16),
        pltpu.VMEM((quarter, width), BF16),
    ]
    scratch += [pltpu.VMEM((blocks + 2, 2, rows_of, width), BF16), pltpu.VMEM((blocks + 2, 2, rows_of, half), BF16)]
    scratch += [pltpu.VMEM((blocks, 2, rows_of, half), BF16)]
    scratch += [dma((blocks + 2,)), dma((blocks + 2,)), dma((blocks, 2)), dma((blocks, 2)), dma((blocks,)), dma((blocks,))]
    scratch += [
        dma((6,)),
        dma((3,)),
        dma((4, 2, 2)),
        dma((CHUNKS, 2)),
        dma((CHUNKS, 2)),
        dma((2, CHUNKS, 2)),
        dma((2, 2)),
        dma((CHUNKS, 2)),
        dma((CHUNKS, 2)),
        dma((CHUNKS, 2)),
        dma((2,)),
    ]
    out_shape = [
        jax.ShapeDtypeStruct(low, F32),
        jax.ShapeDtypeStruct(low, F32),
        jax.ShapeDtypeStruct((16, width), F32),
        jax.ShapeDtypeStruct((quarter, width), BF16),
        jax.ShapeDtypeStruct(cross_shape, BF16),
        jax.ShapeDtypeStruct((blocks, rows_of, half), BF16),
    ]
    args = [values.act_three, values.x1, values.query, w_cross, w_in, w_mlp]
    return pl.pallas_call(
        functools.partial(mid_kernel, tuple(pieces), pairs, scale),
        in_specs=[hbm] * 9 + [vmem] * 7,
        out_specs=[hbm, hbm, vmem, hbm, hbm, vmem],
        out_shape=out_shape,
        scratch_shapes=scratch,
        compiler_params=pltpu.CompilerParams(
            collective_id=2, has_side_effects=True, vmem_limit_bytes=TAIL_LIMIT
        ),
        name="middle",
    )(*args, ffn_shard, cot_block, values.base, *vecs, picks)


def finish_kernel(*refs):
    it = iter(refs)
    late, early, from_text, total = (next(it) for _ in range(4))
    rows_in = [next(it) for _ in range(2)]
    rows_out = [next(it) for _ in range(2)]
    o_qkv, o_out, o_in, o_mlp, o_cross, o_qv, o_outb, o_inb, o_mlpb, o_gain, o_shift = (next(it) for _ in range(11))
    held = [next(it) for _ in range(2)]
    b_in, b_mlp, b_out, b_qkv, b_cross, sem = it
    tower, dp, z, core, line, other, partner = spots()

    def bring(i, image_src, text_src, target):
        @pl.when(tower == 0)
        def _():
            pltpu.make_async_copy(image_src, target, sem.at[i]).start()

        @pl.when(tower == 1)
        def _():
            pltpu.make_async_copy(text_src, target, sem.at[i]).start()

    n = b_in.shape[0]
    bring(0, late.at[pl.ds(n, n)], early.at[pl.ds(0, n)], b_in)
    bring(1, late.at[pl.ds(0, n)], early.at[pl.ds(n, n)], b_mlp)
    bring(2, late.at[2 * n], late.at[2 * n], b_out)
    bring(3, late.at[pl.ds(2 * n + 1, 3)], late.at[pl.ds(2 * n + 1, 3)], b_qkv)
    bring(4, from_text, early.at[pl.ds(2 * n, 2)], b_cross)
    for i in range(2):
        pltpu.make_async_copy(rows_in[i], held[i], sem.at[5 + i]).start()

    width = total.shape[2]
    heads = width // 2
    first = total[0]
    o_outb[...] = first[0:1, :]
    o_mlpb[...] = first[1:2, :]
    for i in range(3):
        o_gain[i] = first[2 + i : 3 + i, :]
        o_shift[i] = first[5 + i : 6 + i, :]
    for side in range(2):
        lanes = slice(side * heads, (side + 1) * heads)
        o_qv[0, 0:1, lanes] = total[side, 8:9, :heads]
        o_qv[0, 1:2, lanes] = total[side, 8:9, heads:]
        for b in range(2):
            at = (2 * side + b) * width
            o_inb[0:1, at : at + width] = total[side, 9 + b : 10 + b, :]

    def mine(block):
        cut = block.shape[1] // 2
        wide = block.astype(F32)
        return jnp.where(core == 0, wide[:, :cut], wide[:, cut:])

    def mine_turned(block):
        tall = block.T
        cut = tall.shape[0] // 2
        return jnp.where(core == 0, tall[:cut].astype(F32), tall[cut:].astype(F32))

    for i in range(2):
        pltpu.make_async_copy(rows_in[i], held[i], sem.at[5 + i]).wait()
        pltpu.make_async_copy(held[i], rows_out[i].at[0], sem.at[7 + i]).start()
    half = b_in.shape[2]
    cols = b_in.shape[1]
    pltpu.make_async_copy(late.at[pl.ds(0, n)], b_in, sem.at[0]).wait()
    for i in range(n // 2):
        pair = b_in[2 * i : 2 * i + 2].reshape(2 * cols, half)
        o_in[0, :, 2 * i * cols : 2 * (i + 1) * cols] = mine_turned(pair)
    pltpu.make_async_copy(late.at[pl.ds(0, n)], b_mlp, sem.at[1]).wait()
    for i in range(n // 2):
        pair = b_mlp[2 * i : 2 * i + 2].reshape(2 * cols, half)
        o_mlp[0, :, 2 * i * cols : 2 * (i + 1) * cols] = mine_turned(pair)
    pltpu.make_async_copy(late.at[0], b_out, sem.at[2]).wait()
    o_out[0] = mine(b_out[...])
    pltpu.make_async_copy(late.at[pl.ds(0, 3)], b_qkv, sem.at[3]).wait()
    for a in range(3):
        o_qkv[0, a] = mine_turned(b_qkv[a])
    pltpu.make_async_copy(late.at[pl.ds(0, 2)], b_cross, sem.at[4]).wait()
    for a in range(2):
        o_cross[0, a] = mine_turned(b_cross[a])
    for i in range(2):
        pltpu.make_async_copy(held[i], rows_out[i].at[0], sem.at[7 + i]).wait()


def finish(late, early, from_text, total, token_rows):
    hbm = pl.BlockSpec(memory_space=pltpu.HBM)
    vmem = pl.BlockSpec(memory_space=pltpu.VMEM)
    struct = jax.ShapeDtypeStruct
    width = total.shape[2]
    blocks, cols, half = early.shape
    n = (blocks - 2) // 2
    ffn, cut = n * cols, half // 2
    out_shape = [struct((1,) + x.shape, BF16) for x in token_rows]
    out_shape += [
        struct((1, 3, cut, cols), F32),
        struct((1, cols, cut), F32),
        struct((1, cut, ffn), F32),
        struct((1, cut, ffn), F32),
        struct((1, 2, cut, cols), F32),
        struct((1, 2, width), F32),
        struct((1, width), F32),
        struct((1, 4 * width), F32),
        struct((1, width), F32),
        struct((3, 1, width), F32),
        struct((3, 1, width), F32),
    ]
    scratch = [pltpu.VMEM(x.shape, BF16) for x in token_rows]
    scratch += [pltpu.VMEM(x + (cols, half), BF16) for x in ((n,), (n,), (), (3,), (2,))]
    scratch += [pltpu.SemaphoreType.DMA((9,))]
    results = pl.pallas_call(
        finish_kernel,
        in_specs=[hbm] * 3 + [vmem] + [hbm] * 2,
        out_specs=[hbm] * 2 + [vmem] * 11,
        out_shape=out_shape,
        scratch_shapes=scratch,
        compiler_params=pltpu.CompilerParams(vmem_limit_bytes=VMEM_LIMIT),
        name="finish",
    )(late, early, from_text, total, *token_rows)
    turned = {5: (1, 2), 11: (0, 1), 12: (0, 1)}
    return tuple(jnp.swapaxes(x, *turned[i]) if i in turned else x for i, x in enumerate(results))


def split_heads(flat):
    return jnp.swapaxes(flat.reshape(flat.shape[0], -1, HDIM), 0, 1)


def join_heads(split):
    return jnp.swapaxes(split, 0, 1).reshape(split.shape[1], -1)


def batch_dot(left, right, left_dim, right_dim):
    return lax.dot_general(left, right, (((left_dim,), (right_dim,)), ((0,), (0,))), preferred_element_type=F32)


def attend_plain(queries, keys, vals, allowed, scale):
    queries, keys, vals = (split_heads(x) for x in (queries, keys, vals))
    scores = jnp.where(allowed, batch_dot(queries, keys, 2, 2) * scale, NEG)
    top = jnp.max(scores, axis=-1, keepdims=True)
    tops = top + jnp.log(jnp.sum(jnp.exp(scores - top), axis=-1, keepdims=True))
    weights = jnp.exp(scores - tops).astype(BF16)
    return (join_heads(batch_dot(weights, vals, 2, 1)).astype(BF16), tops)


def attend_back_plain(queries, keys, vals, grads, tops, allowed, scale):
    queries, keys, vals, grads = (split_heads(x) for x in (queries, keys, vals, grads))
    scores = jnp.where(allowed, batch_dot(queries, keys, 2, 2) * scale, NEG)
    weights = jnp.exp(scores - tops)
    grad_w = batch_dot(grads, vals, 2, 2)
    grad_s = (weights * (grad_w - jnp.sum(weights * grad_w, axis=-1, keepdims=True))).astype(BF16)
    return (
        join_heads(batch_dot(grad_s, keys, 2, 1) * scale).astype(BF16),
        join_heads(batch_dot(grad_s, queries, 1, 1) * scale).astype(BF16),
        join_heads(batch_dot(weights.astype(BF16), grads, 1, 1)).astype(BF16),
    )


def gather_plain(shards):
    core = lax.rem(lax.axis_index(DP), 2)
    outs = []
    for i, s in enumerate(shards):
        if i == 2:
            s = jnp.concatenate([lax.ppermute(s, TOWER, [(0, 1)]), s], axis=0)
        full = lax.all_gather(s, MP, axis=1, tiled=False)
        outs.append(lax.dynamic_slice_in_dim(full, 2 * core, 2, 1))
    return outs


def reduce_plain(grads, smalls):
    dp = lax.axis_index(DP)
    core = lax.rem(dp, 2)
    outs = []
    for g in grads:
        n, _, rows, wide = g.shape
        full = jnp.zeros((n, 4, rows, wide), BF16)
        full = lax.dynamic_update_slice(full, g, (0, 2 * core, 0, 0))
        part = lax.psum_scatter(full, MP, scatter_dimension=1, tiled=False)
        part = lax.psum_scatter(part, DP, scatter_dimension=2, tiled=True)
        outs.append(part)
    if smalls is None:
        return outs
    both = jnp.zeros((2,) + smalls.shape, F32)
    both = lax.dynamic_update_slice(both, smalls[None], (core, 0, 0))
    return outs + [lax.psum(both, (DP, MP))]


def body(
    tower_in,
    out_cot,
    segment_ids,
    row_image,
    attn_qkv,
    attn_out,
    mlp_in,
    mlp_out,
    cross_proj,
    qv_bias,
    out_bias,
    mlp_bias_in,
    mlp_bias_out,
    norm_gain,
    norm_bias,
):
    lines = lax.axis_size(DP) // 2
    depth = lax.axis_size(MP)
    devices = lax.axis_size(DP)
    is_enc = lax.axis_index(TOWER) == 0
    dp = lax.axis_index(DP)
    z = lax.axis_index(MP)
    core = lax.rem(dp, 2)
    side = lax.rem(z, 2)
    group = z // 2
    direct = lines == 2
    assert depth == 4
    quarter = tower_in.shape[1]
    tokens = 2 * quarter
    assert tokens == PATCH
    width = tower_in.shape[2]
    head_cols = 2 * attn_qkv.shape[3]
    hidden = 2 * mlp_in.shape[2]
    scale_qk = HDIM ** (-0.5)

    out_moves, back_moves = [], []
    for d in range(devices):
        for place in range(depth):
            here = d * depth + place
            there = (d - d % 2 + place % 2) * depth + 2 * (d % 2) + place // 2
            out_moves.append((here, there))
            back_moves.append((there, here))

    def swap_cores(x):
        return lax.ppermute(x, DP, [(i, i ^ 1) for i in range(devices)])

    def both_cores(own):
        other = swap_cores(own)
        return jnp.where(core == 0, jnp.concatenate([own, other], -2), jnp.concatenate([other, own], -2))

    def own_rows(full):
        return lax.dynamic_slice_in_dim(full, core * quarter, quarter, full.ndim - 2)

    def lowered(part):
        return lax.reduce_precision(part, 8, 7).astype(BF16)

    def add_lowered(low):
        return low.astype(F32) + swap_cores(low).astype(F32)

    def add_cores(part):
        return add_lowered(lowered(part))

    def only_image(run, *operands):
        def idle(*inputs):
            return jax.tree.map(lambda x: jnp.zeros(x.shape, x.dtype), jax.eval_shape(run, *inputs))

        return lax.cond(is_enc, run, idle, *operands)

    shards = [
        jnp.swapaxes(attn_qkv[0], 1, 2),
        attn_out,
        jnp.swapaxes(cross_proj[0], 1, 2),
        mlp_in,
        mlp_out,
    ]
    rows = segment_ids.shape[0] // 2

    bias_qv = lax.dynamic_slice_in_dim(qv_bias[0], core * head_cols, head_cols, 1)
    bias_packed = jnp.concatenate([bias_qv[0], jnp.zeros_like(bias_qv[0]), bias_qv[1]])
    bias_in = lax.dynamic_slice_in_dim(mlp_bias_in[0], core * hidden, hidden, 0)
    gains = norm_gain[0]
    shifts = norm_bias[0]

    def feed_forward(values):
        act = norm_rows(values, gains[1], shifts[1]).astype(BF16)
        pre = jnp.concatenate([dot_plain(act, w_in[0]), dot_plain(act, w_in[1])], axis=1) + bias_in
        hid = gelu_tanh(pre).astype(BF16)
        return (act, pre, hid, lowered(dot_plain(hid, w_mlp)))

    if direct:
        tall_gains, tall_shifts = (jnp.swapaxes(x, 0, 1) for x in (norm_gain, norm_bias))
        vecs = (tall_gains, tall_shifts, out_bias, mlp_bias_out, mlp_bias_in, qv_bias[0])
        gathered, stream_low, notes, first = head(
            shards, [tower_in[0]], segment_ids, row_image, vecs, scale_qk
        )
        seg_col, seg_row, picks = notes
    else:
        gathered = gather_plain(shards)
        stream_low = both_cores(lax.ppermute(tower_in[0], (DP, MP), out_moves))
        cot_low = both_cores(lax.ppermute(out_cot[0], (DP, MP), out_moves))
        segs = jnp.where(core == group, segment_ids, swap_cores(segment_ids))
        segs = lax.dynamic_slice_in_dim(segs, rows * side, rows, 0)
        marks = (segs + LTXT * jnp.arange(rows, dtype=jnp.int32)[:, None]).reshape(tokens)
        images_of = jnp.where(core == group, row_image, swap_cores(row_image))
        images_of = jnp.repeat(lax.dynamic_slice_in_dim(images_of, rows * side, rows, 0), LTXT)
        places = jnp.arange(tokens)
        allowed = (places[None, :] <= places[:, None]) & (marks[None, :] == marks[:, None])
        allowed = jnp.logical_or(allowed, is_enc)
        sees = images_of[:, None] == jnp.arange(2 * tokens)[None, :] // tokens
    w_qkv = gathered[0].reshape(3 * head_cols, width)
    w_out = gathered[1].reshape(head_cols, width)
    w_cross = gathered[2].reshape(4, head_cols, width)
    w_in = gathered[3][0]
    w_mlp = gathered[4].reshape(hidden, width)
    stream = stream_low.astype(F32)

    if not direct:
        act_one = norm_rows(stream, gains[0], shifts[0]).astype(BF16)
        packed = (dot_rows(act_one, w_qkv) + bias_packed).astype(BF16)
        parts = [packed[:, i * head_cols : (i + 1) * head_cols] for i in range(3)]
        mixed, tops = attend_plain(*parts, allowed, scale_qk)
        stream_one = stream + add_cores(dot_plain(mixed, w_out)) + out_bias[0]
        act_enc, pre_enc, hid_enc, part_enc = feed_forward(stream_one)
        out_enc = stream_one + add_lowered(part_enc) + mlp_bias_out[0]
        base_three = jnp.where(is_enc, out_enc, stream_one)
        act_three = norm_rows(base_three, gains[2], shifts[2]).astype(BF16)
        cross_q = dot_rows(act_three, w_cross[2]).astype(BF16)

    if direct:
        back_in_three, upstream, smalls, tower_rows, g_cross, early = middle(
            first, gathered[2], gathered[3], gathered[4], mlp_out, out_cot[0], vecs, picks, scale_qk
        )
        values = Tail(
            d_three=back_in_three,
            base=first.base,
            upstream=upstream,
            gains=tall_gains,
            smalls=smalls,
            w_mlp=w_mlp,
            pre=first.pre,
            hid=first.hid,
            act=first.act,
            w_in=w_in,
            x1=first.x1,
            w_out=w_out,
            mixed=first.mixed,
            packed=first.packed,
            tops=first.tops,
            seg_col=seg_col,
            seg_row=seg_row,
            a_one=first.a_one,
            w_qkv=w_qkv,
            x0=stream_low,
        )
        late, total, grad_in, from_text, tower_out = tail(values, g_cross, tower_rows, scale_qk)
        return finish(late, early, from_text, total, [tower_out, grad_in])
    else:
        near_half = lax.ppermute(own_rows(act_three), TOWER, [(0, 1)])
        far_half = lax.ppermute(near_half, MP, [(i, i ^ 1) for i in range(depth)])
        halves = jnp.where(side == 0, jnp.stack([near_half, far_half]), jnp.stack([far_half, near_half]))
        images = both_cores(halves)

        flat_images = images.reshape(2 * tokens, width)
        cross_k = dot_rows(flat_images, w_cross[0]).astype(BF16)
        cross_v = dot_rows(flat_images, w_cross[1]).astype(BF16)
        cross_mix, cross_tops = attend_plain(cross_q, cross_k, cross_v, sees, scale_qk)
        stream_two = stream_one + add_cores(dot_plain(cross_mix, w_cross[3]))

        act_dec, pre_dec, hid_dec, part_dec = feed_forward(stream_two)
        out_dec = stream_two + add_lowered(part_dec) + mlp_bias_out[0]
        tower_rows = own_rows(jnp.where(is_enc, base_three, out_dec).astype(BF16))

        def feed_back(grad_low, pre):
            grad_hid = dot_rows(grad_low, w_mlp)
            _, pullback = jax.vjp(gelu_tanh, pre)
            grad_pre = pullback(grad_hid)[0].astype(BF16)
            cols = hidden // 2
            part = dot_rows(grad_pre[:, :cols], w_in[0]) + dot_rows(grad_pre[:, cols:], w_in[1])
            return (grad_pre, lowered(part))

        def feed_grads(grad_low, act, grad_pre, hid):
            g_in = dot_first(grad_pre, act).astype(BF16)
            g_mlp = dot_first(hid, grad_low).astype(BF16)
            return (
                g_in.reshape(1, 2, hidden // 2, width),
                g_mlp.reshape(1, 2, hidden // 2, width),
            )

        cot = cot_low.astype(F32)
        grad_pre_dec, back_in = feed_back(cot_low, pre_dec)
        back_a, gain_a, shift_a = norm_back(stream_two, gains[1], add_lowered(back_in))
        grad_two = cot + back_a
        grad_two_low = grad_two.astype(BF16)

        grad_mix = dot_rows(grad_two_low, w_cross[3]).astype(BF16)
        grad_q, flat_k, flat_v = attend_back_plain(
            cross_q, cross_k, cross_v, grad_mix, cross_tops, sees, scale_qk
        )
        part_images = dot_plain(flat_k, w_cross[0]) + dot_plain(flat_v, w_cross[1])
        part_low = part_images.astype(BF16).reshape(2, 2, quarter, width)
        give = lax.dynamic_index_in_dim(part_low, 1 - core, 1, keepdims=False)
        keep = lax.dynamic_index_in_dim(part_low, core, 1, keepdims=False)
        pair_sum = (keep.astype(F32) + swap_cores(give).astype(F32)).astype(BF16)
        give = lax.dynamic_index_in_dim(pair_sum, 1 - side, 0, keepdims=False)
        keep = lax.dynamic_index_in_dim(pair_sum, side, 0, keepdims=False)
        got = lax.ppermute(give, MP, [(i, i ^ 1) for i in range(depth)])
        image_sum = (keep.astype(F32) + got.astype(F32)).astype(BF16)
        image_half = lax.ppermute(image_sum, TOWER, [(1, 0)])
        later = lax.optimization_barrier(
            (cot_low, act_dec, grad_pre_dec, hid_dec, flat_k, flat_v, grad_q, cross_mix, image_sum)
        )
        g_in_dec, g_mlp_dec = feed_grads(later[0], later[1], later[2], later[3])
        g_cross = jnp.concatenate(
            [
                dot_first(later[4], flat_images).astype(BF16),
                dot_first(later[5], flat_images).astype(BF16),
                dot_first(later[6], act_three).astype(BF16),
                dot_first(later[7], grad_two_low).astype(BF16),
            ],
            axis=0,
        ).reshape(4, 2, head_cols // 2, width)
        image_back = both_cores(image_half).astype(F32)
        query_back = add_cores(dot_plain(grad_q, w_cross[2]))
        back_in_three = jnp.where(is_enc, image_back, query_back)
        text_smalls = (
            jnp.zeros((16, width), F32)
            .at[1]
            .set(jnp.sum(cot_low, axis=0, dtype=F32))
            .at[3]
            .set(gain_a)
            .at[6]
            .set(shift_a)
            .at[9:11]
            .set(jnp.sum(grad_pre_dec, axis=0, dtype=F32).reshape(2, width))
        )
        smalls = jnp.where(is_enc, 0.0, text_smalls)
        tower_out = lax.ppermute(tower_rows, (DP, MP), back_moves)
        back_three, gain_three, shift_three = norm_back(
            base_three, gains[2], back_in_three
        )
        grad_enc = cot + back_three
        grad_enc_low = grad_enc.astype(BF16)

        grad_pre_enc, back_in = feed_back(grad_enc_low, pre_enc)
        g_in, g_mlp = feed_grads(grad_enc_low, act_enc, grad_pre_enc, hid_enc)
        back_b, gain_b, shift_b = norm_back(stream_one, gains[1], add_lowered(back_in))
        grad_one = jnp.where(is_enc, grad_enc + back_b, grad_two + back_three)
        grad_one_low = grad_one.astype(BF16)

        g_out = dot_first(mixed, grad_one_low).astype(BF16).reshape(1, 2, head_cols // 2, width)
        grad_mixed = dot_rows(grad_one_low, w_out).astype(BF16)
        grad_packed = jnp.concatenate(
            attend_back_plain(*parts, grad_mixed, tops, allowed, scale_qk), axis=1
        )
        g_qkv = dot_first(grad_packed, act_one).astype(BF16).reshape(3, 2, head_cols // 2, width)
        back_in = add_cores(dot_plain(grad_packed, w_qkv))
        back_one, gain_one, shift_one = norm_back(stream, gains[0], back_in)
        grad_in = own_rows((grad_one + back_one).astype(BF16))
        grad_in = lax.ppermute(grad_in, (DP, MP), back_moves)

        grad_pre_sum = jnp.sum(grad_pre_enc, axis=0, dtype=F32).reshape(2, width)
        packed_sum = jnp.sum(grad_packed, axis=0, dtype=F32)
        smalls = jnp.concatenate(
            [
                jnp.sum(grad_one_low, axis=0, dtype=F32)[None],
                jnp.where(is_enc, jnp.sum(grad_enc_low, axis=0, dtype=F32), smalls[1])[None],
                gain_one[None],
                jnp.where(is_enc, gain_b, smalls[3])[None],
                gain_three[None],
                shift_one[None],
                jnp.where(is_enc, shift_b, smalls[6])[None],
                shift_three[None],
                jnp.concatenate([packed_sum[:head_cols], packed_sum[2 * head_cols :]])[None],
                jnp.where(is_enc, grad_pre_sum, smalls[9:11]),
                smalls[11:],
            ]
        )
        g_in = jnp.where(is_enc, g_in, g_in_dec)
        g_mlp = jnp.where(is_enc, g_mlp, g_mlp_dec)
        s_in, s_mlp, s_out, s_qkv, s_cross, total = reduce_plain([g_in, g_mlp, g_out, g_qkv, g_cross], smalls)
        s_cross = jnp.where(is_enc, lax.ppermute(s_cross[:2], TOWER, [(1, 0)]), s_cross[2:])

    def turned(x):
        return jnp.swapaxes(x, 1, 2).astype(F32)

    cross_pair = jnp.stack(
        [
            s_cross[0].T,
            s_cross[1].T,
        ]
    ).astype(F32)
    first = total[0]
    qv_total = jnp.stack(
        [
            total[:, 8, :head_cols].reshape(-1),
            total[:, 8, head_cols:].reshape(-1),
        ]
    )
    in_total = total[:, 9:11].reshape(-1)
    return (
        tower_out[None],
        grad_in[None],
        turned(s_qkv)[None],
        s_out.astype(F32),
        turned(s_in),
        s_mlp.astype(F32),
        cross_pair[None],
        qv_total[None],
        first[0:1],
        in_total[None],
        first[1:2],
        first[2:5][None],
        first[5:8][None],
    )


def solution(mesh):
    return jax.shard_map(
        body,
        mesh=mesh,
        in_specs=(
            P(TOWER, (DP, MP), None),
            P(TOWER, (DP, MP), None),
            P(DP, None),
            P(DP),
            P(TOWER, None, None, MP),
            P(TOWER, MP, None),
            P(TOWER, None, MP),
            P(TOWER, MP, None),
            P(TOWER, None, None, MP),
            P(TOWER, None, None),
            P(TOWER, None),
            P(TOWER, None),
            P(TOWER, None),
            P(TOWER, None, None),
            P(TOWER, None, None),
        ),
        out_specs=(
            P(TOWER, (DP, MP), None),
            P(TOWER, (DP, MP), None),
            P(TOWER, None, DP, MP),
            P(TOWER, MP, DP),
            P(TOWER, DP, MP),
            P(TOWER, MP, DP),
            P(TOWER, None, DP, MP),
            P(TOWER, None, None),
            P(TOWER, None),
            P(TOWER, None),
            P(TOWER, None),
            P(TOWER, None, None),
            P(TOWER, None, None),
        ),
        check_vma=False,
    )
```
